32 devices in a mesh: dp: 8 (over z, x), tensor: 4 (over y, core).
Axes of the slice: x: 2, y: 2, z: 4, core: 2. Of those that a mesh axis runs over, the one named last changes fastest.
Arguments:
- hidden: bfloat16 [8192, 2048], P(('dp', 'tensor')), may hold values from -6 to 6
- teacher: bfloat16 [8192, 2048], P(('dp', 'tensor')), may hold values from -6 to 6
- valid_mask: int32 [8192], P(('dp', 'tensor')), may hold values from 0 to 1, as said below
- prefix_len: int32 [8], P('dp'), may hold values from 128 to 256
- ln1_gain: bfloat16 [2048], replicated, may hold values from 0.5 to 1.5
- ln1_bias: bfloat16 [2048], replicated, may hold values from -1.75 to 1.75
- ln2_gain: bfloat16 [2048], replicated, may hold values from 0.5 to 1.5
- ln2_bias: bfloat16 [2048], replicated, may hold values from -1.75 to 1.75
- qkv_weight: bfloat16 [2048, 6144], P(None, 'tensor'), may hold values from -0.1875 to 0.1875
- qkv_bias: bfloat16 [6144], P('tensor'), may hold values from -1.75 to 1.75
- out_weight: bfloat16 [2048, 2048], P('tensor'), may hold values from -0.5 to 0.5
- out_bias: bfloat16 [2048], replicated, may hold values from -1.75 to 1.75
- fc1_weight: bfloat16 [2048, 8192], P(None, 'tensor'), may hold values from -0.125 to 0.125
- fc1_bias: bfloat16 [8192], P('tensor'), may hold values from -1.75 to 1.75
- fc2_weight: bfloat16 [8192, 2048], P('tensor'), may hold values from -0.0625 to 0.0625
- fc2_bias: bfloat16 [2048], replicated, may hold values from -1.75 to 1.75
Outputs:
- output: bfloat16 [8192, 2048], P(('dp', 'tensor'))
- loss: float32 [], replicated
- input_grad: float32 [8192, 2048], P(('dp', 'tensor'))
- ln1_gain_grad: float32 [2048], replicated
- ln1_bias_grad: float32 [2048], replicated
- ln2_gain_grad: float32 [2048], replicated
- ln2_bias_grad: float32 [2048], replicated
- qkv_weight_grad: float32 [2048, 6144], P(None, 'tensor')
- qkv_bias_grad: float32 [6144], P('tensor')
- out_weight_grad: float32 [2048, 2048], P('tensor')
- out_bias_grad: float32 [2048], replicated
- fc1_weight_grad: float32 [2048, 8192], P(None, 'tensor')
- fc1_bias_grad: float32 [8192], P('tensor')
- fc2_weight_grad: float32 [8192, 2048], P('tensor')
- fc2_bias_grad: float32 [2048], replicated
The draws below stay inside these ranges and needn't reach their ends.
Inputs may be any that keep to these rules, and one draw needn't show every extreme that they name: `valid_mask`: 1 marks a token that counts in the loss, 0 one that does not; the first token of all counts.
All inputs are finite; a program needn't handle non-finite values.
Results may differ from the reference program's by a relative error of at most 0.006.
The reference program's roundings to bfloat16 on the way count: a program that leaves them out, or rounds other values in their place, can miss the bound.
Values may be sent and summed in bfloat16 or wider, within the bound.
No kernel may reach another device: no remote copies, remote signals or barrier semaphores. Data moves between devices by JAX's collectives and lax.ppermute only.
A program may use at most 256 MiB of HBM per device.

```python
import jax
import jax.numpy as jnp
from jax import lax

D = 2048
HEADS = 8
HD = 256
ROT = 64
FF = 8192
LEN = 1024
SEQS = 8
TOKENS = 8192


def draw_valid_mask(key, part):
    ticket = jax.random.randint(key, (TOKENS,), 0, 100)
    places = jnp.arange(TOKENS, dtype=jnp.int32)
    levels = 30 + 60 * places // TOKENS
    chosen = (ticket < levels) | (places == 0)
    return chosen.astype(jnp.int32)


def place_ends(result, own_key, smallest, high):
    place = [jax.random.randint(jax.random.fold_in(own_key, axis), (), 0, length) for axis, length in enumerate(result.shape)]
    main_axis = result.shape.index(max(result.shape))
    next_to = place[:main_axis] + [(place[main_axis] + 1) % result.shape[main_axis]] + place[main_axis + 1:]
    return result.at[tuple(place)].set(smallest).at[tuple(next_to)].set(high)


def steps_of(stream_key, extent, cuts, least, largest):
    level = 1.0
    for position, shards_of in cuts:
        steps = jax.random.uniform(jax.random.fold_in(jax.random.fold_in(stream_key, 6), position), (shards_of,), jnp.float32, least / len(cuts), largest / len(cuts))
        level = level * jnp.repeat(jnp.exp(steps), extent[position] // shards_of).reshape((-1,) + (1,) * (len(extent) - 1 - position))
    return level


def bell_draw(rng, dims, deviation, reach, shards=(), held_as=jnp.bfloat16):
    values = deviation * jax.random.normal(rng, dims, jnp.float32)
    if shards:
        values = values * steps_of(rng, dims, shards, -0.22, 0.18)
    return jnp.clip(values, -reach, reach).astype(held_as)


def setup_inputs(seed: int = 0) -> dict:
    seeds = jax.random.split(jax.random.key(seed), 17)
    return {
        "hidden": bell_draw(seeds[0], (TOKENS, D), 1.0, 6.0, ((0, 32),)),
        "teacher": bell_draw(seeds[1], (TOKENS, D), 1.0, 6.0, ((0, 32),)),
        "valid_mask": draw_valid_mask(jax.random.fold_in(seeds[16], 71), 0),
        "prefix_len": place_ends(jax.random.randint(seeds[3], (SEQS,), LEN // 8, LEN // 4 + 1), jax.random.fold_in(seeds[3], 1), LEN // 8, (LEN // 4 + 1) - 1).astype(jnp.int32),
        "ln1_gain": jnp.clip(1.0 + 0.1 * jax.random.normal(seeds[4], (D,), jnp.float32), 0.5, 1.5).astype(jnp.bfloat16),
        "ln1_bias": bell_draw(seeds[5], (D,), 0.3, 1.75),
        "ln2_gain": jnp.clip(1.0 + 0.1 * jax.random.normal(seeds[6], (D,), jnp.float32), 0.5, 1.5).astype(jnp.bfloat16),
        "ln2_bias": bell_draw(seeds[7], (D,), 0.3, 1.75),
        "qkv_weight": bell_draw(seeds[8], (D, 3 * D), (D // 2) ** -0.5, 0.1875, ((1, 4),)),
        "qkv_bias": bell_draw(seeds[9], (3 * D,), 0.3, 1.75, ((0, 4),)),
        "out_weight": bell_draw(seeds[10], (D, D), (D // 16) ** -0.5, 0.5, ((0, 4),)),
        "out_bias": bell_draw(seeds[11], (D,), 0.3, 1.75),
        "fc1_weight": bell_draw(seeds[12], (D, FF), D ** -0.5, 0.125, ((1, 4),)),
        "fc1_bias": bell_draw(seeds[13], (FF,), 0.3, 1.75, ((0, 4),)),
        "fc2_weight": bell_draw(seeds[14], (FF, D), FF ** -0.5, 0.0625, ((0, 4),)),
        "fc2_bias": bell_draw(seeds[15], (D,), 0.3, 1.75),
    }


@jax.custom_vjp
def low(v):
    return lax.optimization_barrier(v.astype(jnp.bfloat16)).astype(jnp.float32)

@jax.custom_vjp
def low_back(v):
    return v

def low_keep(v):
    return (low(v), None)

def low_pass(kept, grad):
    return (grad,)

def back_keep(v):
    return (v, None)

def back_low(kept, grad):
    return (low(grad),)
low.defvjp(low_keep, low_pass)
low_back.defvjp(back_keep, back_low)
EPSILON = 1e-05
HIGHEST = lax.Precision.HIGHEST

def layer_norm(features, gain, shift):
    average = lax.optimization_barrier(jnp.mean(features, axis=-1, keepdims=True))
    centered = features - average
    spread = lax.optimization_barrier(jnp.mean(centered * centered, axis=-1, keepdims=True))
    return centered * lax.rsqrt(spread + EPSILON) * gain + shift

def rotary_tables(length, rot_dims):
    half_dims = rot_dims // 2
    frequency = 10000.0 ** (-2.0 * jnp.arange(half_dims, dtype=jnp.float32) / rot_dims)
    angles = jnp.arange(length, dtype=jnp.float32)[:, None] * frequency[None, :]
    return (jnp.cos(angles)[:, None, :], jnp.sin(angles)[:, None, :])

def rotate_block(block, cosine_table, sine_table):
    half_dims = cosine_table.shape[-1]
    first_half = block[..., :half_dims]
    second_half = block[..., half_dims:2 * half_dims]
    return jnp.concatenate([first_half * cosine_table - second_half * sine_table, second_half * cosine_table + first_half * sine_table, block[..., 2 * half_dims:]], axis=-1)

def attend_sequence(packed):
    qkv_rows, prefix_end = packed
    cosine_table, sine_table = rotary_tables(LEN, ROT)
    split_qkv = qkv_rows.reshape(LEN, HEADS, 3, HD)
    queries = low(rotate_block(split_qkv[:, :, 0], cosine_table, sine_table))
    keys_rot = low(rotate_block(split_qkv[:, :, 1], cosine_table, sine_table))
    values = low(split_qkv[:, :, 2])
    scores = low_back(jnp.einsum('qhd,khd->hqk', queries, keys_rot, precision=HIGHEST) * HD ** (-0.5))
    places = jnp.arange(LEN, dtype=jnp.int32)
    allowed = (places[None, :] <= places[:, None]) | (places[None, :] < prefix_end)
    scores = jnp.where(allowed[None], scores, -jnp.inf)
    attention = jax.nn.softmax(scores, axis=-1)
    context = jnp.einsum('hqk,khd->qhd', low(attention), values, precision=HIGHEST)
    return low_back(low(context)).reshape(LEN, HEADS * HD)

def reference(hidden, teacher, valid_mask, prefix_len, ln1_gain, ln1_bias, ln2_gain, ln2_bias, qkv_weight, qkv_bias, out_weight, out_bias, fc1_weight, fc1_bias, fc2_weight, fc2_bias):
    teacher_f = teacher.astype(jnp.float32)
    mask_f = valid_mask.astype(jnp.float32)
    params = tuple((array_in.astype(jnp.float32) for array_in in (hidden, ln1_gain, ln1_bias, ln2_gain, ln2_bias, qkv_weight, qkv_bias, out_weight, out_bias, fc1_weight, fc1_bias, fc2_weight, fc2_bias)))

    def forward(hidden_f, gain_attn, shift_attn, gain_mlp, shift_mlp, weight_qkv, bias_qkv, weight_out, bias_out, weight_up, bias_up, weight_down, bias_down):
        norm_attn = low(layer_norm(hidden_f, gain_attn, shift_attn))
        norm_mlp = low(layer_norm(hidden_f, gain_mlp, shift_mlp))
        qkv_all = low_back(jnp.dot(norm_attn, weight_qkv, precision=HIGHEST) + bias_qkv)
        context = lax.map(jax.checkpoint(attend_sequence), (qkv_all.reshape(SEQS, LEN, 3 * D), prefix_len))
        context = context.reshape(TOKENS, D)
        hidden_pre = low_back(jnp.dot(norm_mlp, weight_up, precision=HIGHEST) + bias_up)
        active = low(jax.nn.gelu(hidden_pre, approximate=False))
        branch = low_back(jnp.dot(context, weight_out, precision=HIGHEST) + jnp.dot(active, weight_down, precision=HIGHEST))
        output_f = hidden_f + branch + bias_out + bias_down
        mismatch = output_f - teacher_f
        count_all = jnp.sum(mask_f)
        loss_value = jnp.sum(mask_f[:, None] * mismatch * mismatch) / (count_all * D)
        return (output_f, loss_value)
    (output_f, loss_value), pullback = jax.vjp(forward, *params)
    grads = pullback((jnp.zeros_like(output_f), jnp.full_like(loss_value, TOKENS * D)))
    return (output_f.astype(jnp.bfloat16), loss_value, grads[0], grads[1], grads[2], grads[3], grads[4], grads[5], grads[6], grads[7], grads[8], grads[9], grads[10], grads[11], grads[12])
```

```python
import jax
import jax.numpy as jnp
from jax import lax
from jax.sharding import PartitionSpec as P

D = 2048
HD = 256
ROT = 64
LEN = 1024
EPSILON = 1e-05
BF = jnp.bfloat16
F32 = jnp.float32


def rotary_tables(length, rot_dims):
    half_dims = rot_dims // 2
    frequency = 10000.0 ** (-2.0 * jnp.arange(half_dims, dtype=F32) / rot_dims)
    angles = jnp.arange(length, dtype=F32)[:, None] * frequency[None, :]
    return jnp.cos(angles), jnp.sin(angles)


def rotate_block(block, cosine_table, sine_table):
    half_dims = cosine_table.shape[-1]
    first_half = block[..., :half_dims]
    second_half = block[..., half_dims : 2 * half_dims]
    return jnp.concatenate(
        [
            first_half * cosine_table - second_half * sine_table,
            second_half * cosine_table + first_half * sine_table,
            block[..., 2 * half_dims :],
        ],
        axis=-1,
    )


def contract(left_side, right_side, left_dim, right_dim):
    return lax.dot_general(
        left_side,
        right_side,
        (((left_dim,), (right_dim,)), ((), ())),
        preferred_element_type=F32,
    )


def exact_gelu(pre_act):
    return jax.nn.gelu(pre_act, approximate=False)


def after(value, *earlier):
    return lax.optimization_barrier((value,) + earlier)[0]


def on_device(
    hidden,
    teacher,
    valid_mask,
    prefix_len,
    ln1_gain,
    ln1_bias,
    ln2_gain,
    ln2_bias,
    qkv_weight,
    qkv_bias,
    out_weight,
    out_bias,
    fc1_weight,
    fc1_bias,
    fc2_weight,
    fc2_bias,
):
    rows = hidden.shape[0]
    dp = lax.axis_size("dp")
    tp = lax.axis_size("tensor")
    ways = tp // 2
    line = dp // 2
    total_tokens = dp * tp * rows
    heads = qkv_weight.shape[1] // (3 * HD)
    dp_index = lax.axis_index("dp")
    tp_index = lax.axis_index("tensor")
    core, y = tp_index % 2, tp_index // 2
    side, place = dp_index % 2, dp_index // 2

    def to_core(v):
        return lax.ppermute(v, "tensor", [(t, t ^ 1) for t in range(tp)])

    def from_y(v, step):
        pairs = [(t, ((t // 2 - step) % ways) * 2 + t % 2) for t in range(tp)]
        return lax.ppermute(v, "tensor", pairs)

    def to_y(v, step):
        pairs = [(t, ((t // 2 + step) % ways) * 2 + t % 2) for t in range(tp)]
        return lax.ppermute(v, "tensor", pairs)

    def to_side(v):
        return lax.ppermute(v, "dp", [(d, d ^ 1) for d in range(dp)])

    def along(v, hops):
        return lax.ppermute(v, "dp", [(a * 2 + s, b * 2 + s) for a, b in hops for s in (0, 1)])

    def tensor_sum(v):
        v = v + to_core(v)
        bit = 2
        while bit < tp:
            v = v + lax.ppermute(v, "tensor", [(t, t ^ bit) for t in range(tp)])
            bit *= 2
        return v

    def dp_sum(v):
        bit = 1
        while bit < dp:
            v = v + lax.ppermute(v, "dp", [(d, d ^ bit) for d in range(dp)])
            bit *= 2
        return v

    block_ids = [
        ((y + step) % ways) * 2 + (core if mate == 0 else 1 - core)
        for step in range(ways)
        for mate in (0, 1)
    ]

    def gather_rows(own):
        parts = [own, to_core(own)]
        for step in range(1, ways):
            far = from_y(own, step)
            parts += [far, to_core(far)]
        return parts

    def own_side(v, axis):
        half = v.shape[axis] // 2
        return lax.dynamic_slice_in_dim(v, side * half, half, axis)

    def other_side(v, axis):
        half = v.shape[axis] // 2
        return lax.dynamic_slice_in_dim(v, (1 - side) * half, half, axis)

    gain_attn = ln1_gain.astype(F32)
    shift_attn = ln1_bias.astype(F32)
    gain_mlp = ln2_gain.astype(F32)
    shift_mlp = ln2_bias.astype(F32)
    mask_f = valid_mask.astype(F32)
    count_all = dp_sum(tensor_sum(jnp.full((8, 128), jnp.sum(mask_f), F32)))[0, 0]

    def normalize(features):
        average = jnp.mean(features, axis=-1, keepdims=True)
        centered = features - average
        spread = jnp.mean(centered * centered, axis=-1, keepdims=True)
        inverse = lax.rsqrt(spread + EPSILON)
        return centered * inverse, inverse

    hidden_near = jnp.concatenate(gather_rows(hidden), axis=0)
    hidden_far = jnp.concatenate(gather_rows(to_side(hidden)), axis=0)
    xhat, inverse = normalize(hidden_near.astype(F32))
    norm_attn = (xhat * gain_attn + shift_attn).astype(BF)
    norm_mlp = (xhat * gain_mlp + shift_mlp).astype(BF)
    qkv_all = jnp.dot(norm_attn, qkv_weight, preferred_element_type=F32) + qkv_bias.astype(F32)

    cosine_all, sine_all = rotary_tables(LEN, ROT)

    def in_order(table):
        return jnp.concatenate(
            [lax.dynamic_slice_in_dim(table, b * rows, rows, 0) for b in block_ids], axis=0
        )

    cosine_table = in_order(cosine_all)[:, None, :]
    sine_table = in_order(sine_all)[:, None, :]
    spots = jnp.concatenate([b * rows + jnp.arange(rows, dtype=jnp.int32) for b in block_ids])
    scale_factor = HD ** (-0.5)
    visible = (spots[None, :] <= spots[:, None]) | (spots[None, :] < prefix_len[0])

    split_qkv = qkv_all.reshape(LEN, heads, 3, HD)
    queries = rotate_block(split_qkv[:, :, 0], cosine_table, sine_table).astype(BF)
    keys_rot = rotate_block(split_qkv[:, :, 1], cosine_table, sine_table).astype(BF)
    values = split_qkv[:, :, 2].astype(BF)

    def masked_scores():
        scores = (
            jnp.einsum("qhd,khd->hqk", queries, keys_rot, preferred_element_type=F32)
            * scale_factor
        )
        return jnp.where(visible[None], scores, -jnp.inf)

    scores = masked_scores()
    top_score = jnp.max(scores, axis=-1, keepdims=True)
    log_total = top_score + jnp.log(jnp.sum(jnp.exp(scores - top_score), axis=-1, keepdims=True))
    attention_low = jnp.exp(scores - log_total).astype(BF)
    context = (
        jnp.einsum("hqk,khd->qhd", attention_low, values, preferred_element_type=F32)
        .astype(BF)
        .reshape(LEN, heads * HD)
    )
    hidden_pre = jnp.dot(norm_mlp, fc1_weight, preferred_element_type=F32) + fc1_bias.astype(F32)
    active = exact_gelu(hidden_pre).astype(BF)
    branch_part = jnp.dot(context, out_weight, preferred_element_type=F32) + jnp.dot(
        active, fc2_weight, preferred_element_type=F32
    )

    def scatter_rows(part):
        blocks = part.reshape(ways, 2, rows, D)
        mine = blocks[:, 0] + to_core(blocks[:, 1].astype(BF)).astype(F32)
        total = mine[0]
        for step in range(1, ways):
            total = total + to_y(mine[step].astype(BF), step).astype(F32)
        return total

    branch = scatter_rows(branch_part)
    output_f = hidden.astype(F32) + branch + out_bias.astype(F32) + fc2_bias.astype(F32)
    mismatch = output_f - teacher.astype(F32)
    error_part = jnp.sum(mask_f[:, None] * mismatch * mismatch)
    grad_out = mask_f[:, None] * mismatch * (2.0 * total_tokens / count_all)
    bias_part = jnp.sum(grad_out, axis=0)
    grad_low = grad_out.astype(BF)
    grad_near = jnp.concatenate(gather_rows(grad_low), axis=0)
    grad_far = jnp.concatenate(gather_rows(to_side(grad_low)), axis=0)

    xhat_far, _ = normalize(hidden_far.astype(F32))
    norm_attn_far = (xhat_far * gain_attn + shift_attn).astype(BF)
    norm_mlp_far = (xhat_far * gain_mlp + shift_mlp).astype(BF)
    fc1_half = own_side(fc1_weight, 1)
    fc2_half = own_side(fc2_weight, 0)
    pre_far = jnp.dot(norm_mlp_far, fc1_half, preferred_element_type=F32) + own_side(
        fc1_bias, 0
    ).astype(F32)
    active_far = exact_gelu(pre_far).astype(BF)
    context_far = to_side(other_side(context, 1))

    flight = {"in": [], "mid": [], "out": [], "side": []}

    def send(kind, value, move):
        past = flight[kind]
        if len(past) >= 2:
            value = after(value, past[-2])
        result = move(value)
        past.append(result)
        return result

    middle = (place == line // 2 - 1) | (place == line // 2)

    def line_total(part):
        held = part
        low = part.astype(BF)
        for hop in range(line // 2 - 1):
            got = send(
                "in",
                low,
                lambda v, h=hop: along(v, [(h, h + 1), (line - 1 - h, line - 2 - h)]),
            )
            low = (held + got.astype(F32)).astype(BF)
        got = send(
            "mid",
            low,
            lambda v: along(v, [(line // 2 - 1, line // 2), (line // 2, line // 2 - 1)]),
        )
        low = (low.astype(F32) + got.astype(F32)).astype(BF)
        for hop in reversed(range(line // 2 - 1)):
            got = send(
                "out",
                low,
                lambda v, h=hop: along(v, [(h + 1, h), (line - 2 - h, line - 1 - h)]),
            )
            low = jnp.where((place == hop) | (place == line - 1 - hop), got, low)
        return low

    def summed(part, chunks, axis):
        size = part.shape[0] // chunks
        mine, theirs = [], []
        for i in range(chunks):
            low = line_total(lax.slice_in_dim(part, i * size, (i + 1) * size, axis=0))
            mine.append(low)
            theirs.append(send("side", low, to_side))
        mine = jnp.concatenate(mine, axis=0)
        theirs = jnp.concatenate(theirs, axis=0)
        first = jnp.where(side == 0, mine, theirs).astype(F32)
        second = jnp.where(side == 0, theirs, mine).astype(F32)
        return jnp.concatenate([first, second], axis=axis)

    fc2_part = contract(own_side(active, 1), grad_near, 0, 0) + contract(
        active_far, grad_far, 0, 0
    )
    fc2_weight_grad = summed(fc2_part, 4, 0)
    out_part = contract(own_side(context, 1), grad_near, 0, 0) + contract(
        context_far, grad_far, 0, 0
    )
    out_weight_grad = summed(out_part, 1, 0)

    grad_inner = jax.vjp(exact_gelu, hidden_pre)[1](contract(grad_near, fc2_weight, 1, 1))[
        0
    ].astype(BF)
    grad_inner_far = jax.vjp(exact_gelu, pre_far)[1](contract(grad_far, fc2_half, 1, 1))[
        0
    ].astype(BF)
    fc1_part = contract(norm_mlp, own_side(grad_inner, 1), 0, 0) + contract(
        norm_mlp_far, grad_inner_far, 0, 0
    )
    fc1_weight_grad = summed(fc1_part, 4, 1)
    fc1_bias_part = jnp.sum(grad_inner, axis=0, dtype=F32)

    grad_context = contract(grad_near, out_weight, 1, 1).astype(BF).reshape(LEN, heads, HD)
    attention = jnp.exp(masked_scores() - log_total)
    grad_attention = jnp.einsum("qhd,khd->hqk", grad_context, values, preferred_element_type=F32)
    row_dots = jnp.sum(attention * grad_attention, axis=-1, keepdims=True)
    grad_scores = (attention * (grad_attention - row_dots)).astype(BF)
    grad_queries = (
        jnp.einsum("hqk,khd->qhd", grad_scores, keys_rot, preferred_element_type=F32)
        * scale_factor
    )
    grad_keys = (
        jnp.einsum("hqk,qhd->khd", grad_scores, queries, preferred_element_type=F32)
        * scale_factor
    )
    grad_values = jnp.einsum(
        "hqk,qhd->khd", attention.astype(BF), grad_context, preferred_element_type=F32
    )
    grad_qkv = (
        jnp.stack(
            [
                rotate_block(grad_queries, cosine_table, -sine_table),
                rotate_block(grad_keys, cosine_table, -sine_table),
                grad_values,
            ],
            axis=2,
        )
        .reshape(LEN, heads * 3 * HD)
        .astype(BF)
    )
    grad_qkv_far = to_side(other_side(grad_qkv, 1))
    qkv_part = contract(norm_attn, own_side(grad_qkv, 1), 0, 0) + contract(
        norm_attn_far, grad_qkv_far, 0, 0
    )
    qkv_weight_grad = summed(qkv_part, 4, 1)
    qkv_bias_part = jnp.sum(grad_qkv, axis=0, dtype=F32)

    grad_norm_mlp = contract(grad_inner, fc1_weight, 1, 1)
    grad_norm_attn = contract(grad_qkv, qkv_weight, 1, 1)

    def norm_back(gained):
        return inverse * (
            gained
            - jnp.mean(gained, axis=-1, keepdims=True)
            - xhat * jnp.mean(gained * xhat, axis=-1, keepdims=True)
        )

    grad_hidden = norm_back(grad_norm_attn * gain_attn + grad_norm_mlp * gain_mlp)
    input_grad = grad_out + scatter_rows(grad_hidden)
    tensor_parts = jnp.stack(
        [
            jnp.sum(grad_norm_attn * xhat, axis=0),
            jnp.sum(grad_norm_attn, axis=0),
            jnp.sum(grad_norm_mlp * xhat, axis=0),
            jnp.sum(grad_norm_mlp, axis=0),
            bias_part,
            jnp.full((D,), error_part, F32),
        ]
    ).reshape(-1)
    small = jnp.concatenate([tensor_sum(tensor_parts), fc1_bias_part, qkv_bias_part])
    small = dp_sum(small)
    vectors = small[: 6 * D].reshape(6, D)
    fc1_bias_grad = small[6 * D : 6 * D + fc1_bias_part.shape[0]]
    qkv_bias_grad = small[6 * D + fc1_bias_part.shape[0] :]
    loss_value = vectors[5, 0] / (count_all * D)
    return (
        output_f.astype(BF),
        loss_value,
        input_grad,
        vectors[0],
        vectors[1],
        vectors[2],
        vectors[3],
        qkv_weight_grad,
        qkv_bias_grad,
        out_weight_grad,
        vectors[4],
        fc1_weight_grad,
        fc1_bias_grad,
        fc2_weight_grad,
        vectors[4],
    )


def solution(mesh):
    tokens = P(("dp", "tensor"), None)
    columns, lanes, down, whole = P(None, "tensor"), P("tensor"), P("tensor", None), P()
    in_specs = (
        tokens,
        tokens,
        P(("dp", "tensor")),
        P("dp"),
        whole,
        whole,
        whole,
        whole,
        columns,
        lanes,
        down,
        whole,
        columns,
        lanes,
        down,
        whole,
    )
    out_specs = (
        tokens,
        whole,
        tokens,
        whole,
        whole,
        whole,
        whole,
        columns,
        lanes,
        down,
        whole,
        columns,
        lanes,
        down,
        whole,
    )
    return jax.shard_map(
        on_device, mesh=mesh, in_specs=in_specs, out_specs=out_specs, check_vma=False
    )
```

```python
import jax
import jax.numpy as jnp
from jax import lax
from jax.sharding import PartitionSpec as P

D = 2048
HD = 256
ROT = 64
LEN = 1024
EPSILON = 1e-05
BF = jnp.bfloat16
F32 = jnp.float32


def rotary_tables(length, rot_dims):
    half_dims = rot_dims // 2
    frequency = 10000.0 ** (-2.0 * jnp.arange(half_dims, dtype=F32) / rot_dims)
    angles = jnp.arange(length, dtype=F32)[:, None] * frequency[None, :]
    return jnp.cos(angles), jnp.sin(angles)


def rotate_block(block, cosine_table, sine_table):
    half_dims = cosine_table.shape[-1]
    first_half = block[..., :half_dims]
    second_half = block[..., half_dims : 2 * half_dims]
    return jnp.concatenate(
        [
            first_half * cosine_table - second_half * sine_table,
            second_half * cosine_table + first_half * sine_table,
            block[..., 2 * half_dims :],
        ],
        axis=-1,
    )


def contract(left_side, right_side, left_dim, right_dim):
    return lax.dot_general(
        left_side,
        right_side,
        (((left_dim,), (right_dim,)), ((), ())),
        preferred_element_type=F32,
    )


def exact_gelu(pre_act):
    below = 0.5 + 0.5 * lax.erf(pre_act * 0.5**0.5)
    density = jnp.exp(-0.5 * pre_act * pre_act) * (2.0 * jnp.pi) ** -0.5
    return pre_act * below, below + pre_act * density


def after(value, *earlier):
    return lax.optimization_barrier((value,) + earlier)[0]


def on_device(
    hidden,
    teacher,
    valid_mask,
    prefix_len,
    ln1_gain,
    ln1_bias,
    ln2_gain,
    ln2_bias,
    qkv_weight,
    qkv_bias,
    out_weight,
    out_bias,
    fc1_weight,
    fc1_bias,
    fc2_weight,
    fc2_bias,
):
    rows = hidden.shape[0]
    dp = lax.axis_size("dp")
    tp = lax.axis_size("tensor")
    ways = tp // 2
    squares = dp // 4
    total_tokens = dp * tp * rows
    heads = qkv_weight.shape[1] // (3 * HD)
    dp_index = lax.axis_index("dp")
    tp_index = lax.axis_index("tensor")
    core, y = tp_index % 2, tp_index // 2
    quarter = dp_index % 4

    def to_core(v):
        return lax.ppermute(v, "tensor", [(t, t ^ 1) for t in range(tp)])

    def from_y(v, step):
        pairs = [(t, ((t // 2 - step) % ways) * 2 + t % 2) for t in range(tp)]
        return lax.ppermute(v, "tensor", pairs)

    def to_y(v, step):
        pairs = [(t, ((t // 2 + step) % ways) * 2 + t % 2) for t in range(tp)]
        return lax.ppermute(v, "tensor", pairs)

    def flip(v, mask):
        return lax.ppermute(v, "dp", [(d, d ^ mask) for d in range(dp)])

    def tensor_sum(v):
        v = v + to_core(v)
        bit = 2
        while bit < tp:
            v = v + lax.ppermute(v, "tensor", [(t, t ^ bit) for t in range(tp)])
            bit *= 2
        return v

    def dp_sum(v):
        bit = 1
        while bit < dp:
            v = v + flip(v, bit)
            bit *= 2
        return v

    block_ids = [
        ((y + step) % ways) * 2 + (core if mate == 0 else 1 - core)
        for step in range(ways)
        for mate in (0, 1)
    ]

    def gather_near(own):
        parts, over_y = [own, to_core(own)], []
        for step in range(1, ways):
            over_y.append(from_y(own, step))
            parts += [over_y[-1], to_core(over_y[-1])]
        return jnp.concatenate(parts, axis=0), over_y

    def gather_far(own, over_y):
        first = [flip(own, 1), flip(own, 2)]
        first.append(flip(first[1], 1))
        rounds_y = [first]
        for step in range(1, ways):
            rounds_y.append(
                [from_y(first[0], step), flip(over_y[step - 1], 2), from_y(first[2], step)]
            )
        parts = [[], [], []]
        for blocks in rounds_y:
            mates = to_core(jnp.concatenate(blocks, axis=0))
            for i in range(3):
                parts[i] += [blocks[i], lax.slice_in_dim(mates, i * rows, (i + 1) * rows, axis=0)]
        return jnp.concatenate(parts[0] + parts[1] + parts[2], axis=0)

    def quarter_of(v, axis, index):
        size = v.shape[axis] // 4
        return lax.dynamic_slice_in_dim(v, index * size, size, axis)

    def swap_quarters(v):
        return [flip(quarter_of(v, 1, quarter ^ mask), mask) for mask in (1, 2, 3)]

    gain_attn = ln1_gain.astype(F32)
    shift_attn = ln1_bias.astype(F32)
    gain_mlp = ln2_gain.astype(F32)
    shift_mlp = ln2_bias.astype(F32)
    mask_f = valid_mask.astype(F32)
    count_all = dp_sum(tensor_sum(jnp.full((8, 128), jnp.sum(mask_f), F32)))[0, 0]

    def normalize(features):
        average = jnp.mean(features, axis=-1, keepdims=True)
        centered = features - average
        spread = jnp.mean(centered * centered, axis=-1, keepdims=True)
        inverse = lax.rsqrt(spread + EPSILON)
        return centered * inverse, inverse

    hidden_near, hidden_y = gather_near(hidden)
    hidden_far = gather_far(hidden, hidden_y)
    xhat, inverse = normalize(hidden_near.astype(F32))
    norm_attn = (xhat * gain_attn + shift_attn).astype(BF)
    norm_mlp = (xhat * gain_mlp + shift_mlp).astype(BF)
    qkv_all = jnp.dot(norm_attn, qkv_weight, preferred_element_type=F32) + qkv_bias.astype(F32)

    cosine_all, sine_all = rotary_tables(LEN, ROT)

    def in_order(table):
        return jnp.concatenate(
            [lax.dynamic_slice_in_dim(table, b * rows, rows, 0) for b in block_ids], axis=0
        )

    cosine_table = in_order(cosine_all)[:, None, :]
    sine_table = in_order(sine_all)[:, None, :]
    spots = jnp.concatenate([b * rows + jnp.arange(rows, dtype=jnp.int32) for b in block_ids])
    scale_factor = HD ** (-0.5)
    visible = (spots[None, :] <= spots[:, None]) | (spots[None, :] < prefix_len[0])

    split_qkv = qkv_all.reshape(LEN, heads, 3, HD)
    queries = rotate_block(split_qkv[:, :, 0], cosine_table, sine_table).astype(BF)
    keys_rot = rotate_block(split_qkv[:, :, 1], cosine_table, sine_table).astype(BF)
    values = split_qkv[:, :, 2].astype(BF)

    def masked_scores(rotated):
        scores = (
            jnp.einsum("qhd,khd->hqk", rotated, keys_rot, preferred_element_type=F32)
            * scale_factor
        )
        return jnp.where(visible[None], scores, -jnp.inf)

    scores = masked_scores(queries)
    top_score = jnp.max(scores, axis=-1, keepdims=True)
    log_total = top_score + jnp.log(jnp.sum(jnp.exp(scores - top_score), axis=-1, keepdims=True))
    attention_low = jnp.exp(scores - log_total).astype(BF)
    context = (
        jnp.einsum("hqk,khd->qhd", attention_low, values, preferred_element_type=F32)
        .astype(BF)
        .reshape(LEN, heads * HD)
    )
    hidden_pre = jnp.dot(norm_mlp, fc1_weight, preferred_element_type=F32) + fc1_bias.astype(F32)
    active, slope = exact_gelu(hidden_pre)
    active = active.astype(BF)
    branch_part = jnp.dot(context, out_weight, preferred_element_type=F32) + jnp.dot(
        active, fc2_weight, preferred_element_type=F32
    )

    def scatter_rows(part):
        blocks = part.reshape(ways, 2, rows, D)
        mine = blocks[:, 0] + to_core(blocks[:, 1].astype(BF)).astype(F32)
        total = mine[0]
        for step in range(1, ways):
            total = total + to_y(mine[step].astype(BF), step).astype(F32)
        return total

    branch = scatter_rows(branch_part)
    output_f = hidden.astype(F32) + branch + out_bias.astype(F32) + fc2_bias.astype(F32)
    mismatch = output_f - teacher.astype(F32)
    error_part = jnp.sum(mask_f[:, None] * mismatch * mismatch)
    grad_out = mask_f[:, None] * mismatch * (2.0 * total_tokens / count_all)
    bias_part = jnp.sum(grad_out, axis=0)
    grad_low = grad_out.astype(BF)
    grad_near, grad_y = gather_near(grad_low)
    grad_far = gather_far(grad_low, grad_y)

    xhat_far, _ = normalize(after(hidden_far, branch_part).astype(F32))
    norm_attn_far = (xhat_far * gain_attn + shift_attn).astype(BF)
    norm_mlp_far = (xhat_far * gain_mlp + shift_mlp).astype(BF)
    fc1_quarter = quarter_of(fc1_weight, 1, quarter)
    fc2_quarter = quarter_of(fc2_weight, 0, quarter)
    pre_far = jnp.dot(
        after(norm_mlp_far, grad_low), fc1_quarter, preferred_element_type=F32
    ) + quarter_of(fc1_bias, 0, quarter).astype(F32)
    active_far, slope_far = exact_gelu(pre_far)
    active_far = active_far.astype(BF)
    context_far = jnp.concatenate(swap_quarters(context), axis=0)

    queue = []
    due = {}
    clock = [0]
    results = {}
    token = [grad_near]

    def gate(v):
        return after(v, token[0])

    def travel(name, low):
        mask = 4
        while mask < dp:
            (got,) = yield [(low, mask)], 2
            low = (low.astype(F32) + got.astype(F32)).astype(BF)
            mask *= 2
        beside, across = yield [(low, 1), (low, 2)], 1
        (corner,) = yield [(across, 1)], 1
        results.setdefault(name, []).append((low, beside, across, corner))

    def enqueue(name, part, count):
        size = part.shape[0] // count
        for i in range(count):
            queue.append((name, lax.slice_in_dim(part, i * size, (i + 1) * size, axis=0)))

    def turn(*others):
        now = clock[0]
        clock[0] = now + 1
        arrived = due.pop(now, [])
        values = [got for _, gots in arrived for got in gots]
        if queue:
            name, held = queue.pop(0)
            values.append(held.astype(BF))
        tied = list(lax.optimization_barrier(tuple(values) + others))
        token[0] = tied[0]
        asked = []
        for walker, gots in arrived:
            gots = [tied.pop(0) for _ in gots]
            try:
                asked.append((walker, walker.send(gots)))
            except StopIteration:
                pass
        if len(values) > sum(len(gots) for _, gots in arrived):
            walker = travel(name, tied.pop(0))
            asked.append((walker, next(walker)))
        for walker, (sends, wait) in asked:
            due.setdefault(now + wait, []).append((walker, [flip(v, mask) for v, mask in sends]))
        return tied

    def joined(name, axis):
        pieces = [jnp.concatenate(piece, axis=0) for piece in zip(*results[name])]
        odd, high = quarter % 2 == 1, quarter >= 2
        a, b = jnp.where(odd, pieces[1], pieces[0]), jnp.where(odd, pieces[0], pieces[1])
        c, d = jnp.where(odd, pieces[3], pieces[2]), jnp.where(odd, pieces[2], pieces[3])
        order = [
            jnp.where(high, c, a),
            jnp.where(high, d, b),
            jnp.where(high, a, c),
            jnp.where(high, b, d),
        ]
        return jnp.concatenate([v.astype(F32) for v in order], axis=axis)

    grad_context = contract(grad_near, out_weight, 1, 1).astype(BF).reshape(LEN, heads, HD)
    grad_inner = (contract(grad_near, fc2_weight, 1, 1) * slope).astype(BF)
    attention = jnp.exp(masked_scores(queries) - log_total)
    grad_attention = jnp.einsum("qhd,khd->hqk", grad_context, values, preferred_element_type=F32)
    row_dots = jnp.sum(attention * grad_attention, axis=-1, keepdims=True)
    grad_scores = (attention * (grad_attention - row_dots)).astype(BF)
    attention_low = attention.astype(BF)
    fc2_part = contract(quarter_of(active, 1, quarter), grad_near, 0, 0) + contract(
        active_far, grad_far, 0, 0
    )
    enqueue("fc2", fc2_part, 4)
    grad_inner, grad_scores, attention_low = turn(grad_inner, grad_scores, attention_low)

    out_part = contract(quarter_of(context, 1, quarter), gate(grad_near), 0, 0) + contract(
        context_far, grad_far, 0, 0
    )
    enqueue("out", out_part, 1)
    grad_queries = (
        jnp.einsum("hqk,khd->qhd", grad_scores, keys_rot, preferred_element_type=F32)
        * scale_factor
    )
    grad_keys = (
        jnp.einsum("hqk,qhd->khd", grad_scores, queries, preferred_element_type=F32)
        * scale_factor
    )
    grad_values = jnp.einsum(
        "hqk,qhd->khd", attention_low, grad_context, preferred_element_type=F32
    )
    grad_qkv = (
        jnp.stack(
            [
                rotate_block(grad_queries, cosine_table, -sine_table),
                rotate_block(grad_keys, cosine_table, -sine_table),
                grad_values,
            ],
            axis=2,
        )
        .reshape(LEN, heads * 3 * HD)
        .astype(BF)
    )
    (grad_qkv,) = turn(grad_qkv)
    grad_qkv_far = jnp.concatenate(swap_quarters(grad_qkv), axis=0)
    grad_inner_far = (contract(gate(grad_far), fc2_quarter, 1, 1) * slope_far).astype(BF)
    (grad_inner_far,) = turn(grad_inner_far)
    fc1_part = contract(norm_mlp, gate(quarter_of(grad_inner, 1, quarter)), 0, 0) + contract(
        norm_mlp_far, grad_inner_far, 0, 0
    )
    enqueue("fc1", fc1_part, 4)
    (grad_qkv_far,) = turn(grad_qkv_far)
    qkv_part = contract(norm_attn, gate(quarter_of(grad_qkv, 1, quarter)), 0, 0) + contract(
        norm_attn_far, grad_qkv_far, 0, 0
    )
    (qkv_part,) = turn(qkv_part)
    enqueue("qkv", qkv_part, 4)
    grad_norm_mlp = contract(gate(grad_inner), fc1_weight, 1, 1)
    (grad_norm_mlp,) = turn(grad_norm_mlp)
    grad_norm_attn = contract(gate(grad_qkv), qkv_weight, 1, 1)
    (grad_norm_attn,) = turn(grad_norm_attn)

    def norm_back(gained):
        return inverse * (
            gained
            - jnp.mean(gained, axis=-1, keepdims=True)
            - xhat * jnp.mean(gained * xhat, axis=-1, keepdims=True)
        )

    xhat = gate(xhat)
    grad_hidden = norm_back(grad_norm_attn * gain_attn + grad_norm_mlp * gain_mlp)
    tensor_parts = jnp.stack(
        [
            jnp.sum(grad_norm_attn * xhat, axis=0),
            jnp.sum(grad_norm_attn, axis=0),
            jnp.sum(grad_norm_mlp * xhat, axis=0),
            jnp.sum(grad_norm_mlp, axis=0),
            bias_part,
            jnp.full((D,), error_part, F32),
        ]
    ).reshape(-1)
    fc1_bias_part = jnp.sum(grad_inner, axis=0, dtype=F32)
    qkv_bias_part = jnp.sum(grad_qkv, axis=0, dtype=F32)
    grad_hidden, tensor_parts = turn(grad_hidden, tensor_parts)
    input_grad = grad_out + scatter_rows(grad_hidden)
    (input_grad,) = turn(input_grad)
    small = jnp.concatenate([tensor_sum(tensor_parts), fc1_bias_part, qkv_bias_part])
    small = dp_sum(small)
    (small,) = turn(small)
    vectors = small[: 6 * D].reshape(6, D)
    fc1_bias_grad = small[6 * D : 6 * D + fc1_bias_part.shape[0]]
    qkv_bias_grad = small[6 * D + fc1_bias_part.shape[0] :]
    loss_value = vectors[5, 0] / (count_all * D)
    turn()
    turn()
    fc2_weight_grad = joined("fc2", 0)
    out_weight_grad = joined("out", 0)
    fc2_weight_grad, out_weight_grad = turn(fc2_weight_grad, out_weight_grad)
    while queue or due:
        turn()
    fc1_weight_grad = joined("fc1", 1)
    qkv_weight_grad = joined("qkv", 1)
    return (
        output_f.astype(BF),
        loss_value,
        input_grad,
        vectors[0],
        vectors[1],
        vectors[2],
        vectors[3],
        qkv_weight_grad,
        qkv_bias_grad,
        out_weight_grad,
        vectors[4],
        fc1_weight_grad,
        fc1_bias_grad,
        fc2_weight_grad,
        vectors[4],
    )


def solution(mesh):
    tokens = P(("dp", "tensor"), None)
    columns, lanes, down, whole = P(None, "tensor"), P("tensor"), P("tensor", None), P()
    in_specs = (
        tokens,
        tokens,
        P(("dp", "tensor")),
        P("dp"),
        whole,
        whole,
        whole,
        whole,
        columns,
        lanes,
        down,
        whole,
        columns,
        lanes,
        down,
        whole,
    )
    out_specs = (
        tokens,
        whole,
        tokens,
        whole,
        whole,
        whole,
        whole,
        columns,
        lanes,
        down,
        whole,
        columns,
        lanes,
        down,
        whole,
    )
    return jax.shard_map(
        on_device, mesh=mesh, in_specs=in_specs, out_specs=out_specs, check_vma=False
    )
```

```python
import functools

import jax
import jax.numpy as jnp
from jax import lax
from jax.experimental import pallas as pl
from jax.experimental.pallas import tpu as pltpu
from jax.sharding import PartitionSpec as P

D = 2048
HD = 256
ROT = 64
LEN = 1024
EPSILON = 1e-05
BF = jnp.bfloat16
F32 = jnp.float32


def rotary_tables(length, rot_dims):
    half_dims = rot_dims // 2
    frequency = 10000.0 ** (-2.0 * jnp.arange(half_dims, dtype=F32) / rot_dims)
    angles = jnp.arange(length, dtype=F32)[:, None] * frequency[None, :]
    return jnp.cos(angles), jnp.sin(angles)


def contract(left_side, right_side, left_dim, right_dim):
    return lax.dot_general(
        left_side,
        right_side,
        (((left_dim,), (right_dim,)), ((), ())),
        preferred_element_type=F32,
    )


def exact_gelu(pre_act):
    below = 0.5 + 0.5 * lax.erf(pre_act * 0.5**0.5)
    density = jnp.exp(-0.5 * pre_act * pre_act) * (2.0 * jnp.pi) ** -0.5
    return pre_act * below, below + pre_act * density


def after(value, *earlier):
    return lax.optimization_barrier((value,) + earlier)[0]


def rotary_lanes(cosine, sine):
    ones = jnp.ones((cosine.shape[0], 128 - ROT), F32)
    none = jnp.zeros_like(sine)
    rest = jnp.zeros_like(ones)
    keep = jnp.concatenate([cosine, cosine, ones], axis=1)
    up = jnp.concatenate([-sine, none, rest], axis=1)
    down = jnp.concatenate([none, sine, rest], axis=1)
    return keep, up, down


def turned(block, keep, up, down, sign):
    head = block[:, :128]
    half = ROT // 2
    moved = head * keep + sign * (
        pltpu.roll(head, 128 - half, 1) * up + pltpu.roll(head, half, 1) * down
    )
    return jnp.concatenate([moved, block[:, 128:]], axis=1)


def qkv_kernel(x_ref, w_ref, b_ref, keep_ref, up_ref, down_ref, o_ref):
    kind = pl.program_id(0) % 3
    tile = o_ref.shape[0] // 4

    def rows_at(i):
        return pl.ds(pl.multiple_of(i * tile, tile), tile)

    def project(i):
        return (
            jnp.dot(x_ref[rows_at(i), :], w_ref[...], preferred_element_type=F32) + b_ref[...]
        )

    @pl.when(kind == 2)
    def _():
        @pl.loop(0, 4)
        def _(i):
            o_ref[rows_at(i), :] = project(i).astype(BF)

    @pl.when(kind != 2)
    def _():
        @pl.loop(0, 4)
        def _(i):
            at = rows_at(i)
            o_ref[at, :] = turned(
                project(i), keep_ref[at, :], up_ref[at, :], down_ref[at, :], 1.0
            ).astype(BF)


def project_qkv(normed, weight, bias, tables):
    length, width = normed.shape
    columns = weight.shape[1]
    table = pl.BlockSpec((length, 128), lambda j: (0, 0))
    return pl.pallas_call(
        qkv_kernel,
        grid=(columns // HD,),
        in_specs=[
            pl.BlockSpec((length, width), lambda j: (0, 0)),
            pl.BlockSpec((width, HD), lambda j: (0, j)),
            pl.BlockSpec((1, HD), lambda j: (0, j)),
            table,
            table,
            table,
        ],
        out_specs=pl.BlockSpec((length, HD), lambda j: (0, j)),
        out_shape=jax.ShapeDtypeStruct((length, columns), BF),
        compiler_params=pltpu.CompilerParams(vmem_limit_bytes=40 << 20),
        cost_estimate=pl.CostEstimate(
            flops=2 * length * width * columns,
            bytes_accessed=2 * (length * width + width * columns + length * columns),
            transcendentals=0,
        ),
        name="qkv_rotary",
    )(normed, weight, bias.astype(F32)[None, :], *tables)


def visible_scores(queries, keys, row_spots, key_spots, prefix):
    scores = lax.dot_general(
        queries, keys, (((1,), (1,)), ((), ())), preferred_element_type=F32
    ) * (HD**-0.5)
    allowed = (key_spots <= row_spots) | (key_spots < prefix)
    return jnp.where(allowed, scores, -jnp.inf)


def attend_kernel(prefix_ref, q_ref, k_ref, v_ref, rows_ref, keys_ref, o_ref, log_ref):
    scores = visible_scores(
        q_ref[...], k_ref[...], rows_ref[...], keys_ref[...], prefix_ref[0]
    )
    top = jnp.max(scores, axis=-1, keepdims=True)
    weights = jnp.exp(scores - top)
    total = jnp.sum(weights, axis=-1, keepdims=True)
    probs = (weights * (1.0 / total)).astype(BF)
    o_ref[...] = jnp.dot(probs, v_ref[...], preferred_element_type=F32).astype(BF)
    log_ref[0] = top + jnp.log(total)


def attend(qkv, prefix, spots):
    length = qkv.shape[0]
    heads = qkv.shape[1] // (3 * HD)
    tile = length // 4
    whole = lambda part: pl.BlockSpec((length, HD), lambda h, i, p: (0, 3 * h + part))
    return pl.pallas_call(
        attend_kernel,
        grid_spec=pltpu.PrefetchScalarGridSpec(
            num_scalar_prefetch=1,
            grid=(heads, 4),
            in_specs=[
                pl.BlockSpec((tile, HD), lambda h, i, p: (i, 3 * h)),
                whole(1),
                whole(2),
                pl.BlockSpec((tile, 1), lambda h, i, p: (i, 0)),
                pl.BlockSpec((1, length), lambda h, i, p: (0, 0)),
            ],
            out_specs=[
                pl.BlockSpec((tile, HD), lambda h, i, p: (i, h)),
                pl.BlockSpec((1, tile, 1), lambda h, i, p: (h, i, 0)),
            ],
        ),
        out_shape=[
            jax.ShapeDtypeStruct((length, heads * HD), BF),
            jax.ShapeDtypeStruct((heads, length, 1), F32),
        ],
        compiler_params=pltpu.CompilerParams(vmem_limit_bytes=32 << 20),
        cost_estimate=pl.CostEstimate(
            flops=4 * heads * length * length * HD,
            bytes_accessed=8 * length * heads * HD,
            transcendentals=heads * length * length,
        ),
        name="attend",
    )(prefix, qkv, qkv, qkv, spots[:, None], spots[None, :])


def attend_back_kernel(
    prefix_ref, q_ref, k_ref, v_ref, g_ref, log_ref, rows_ref, keys_ref, keep_ref, up_ref,
    down_ref, o_ref, dk_ref, dv_ref,
):
    length = q_ref.shape[0]
    tile = length // 4
    scale = HD**-0.5
    for i in range(4):
        at = pl.ds(i * tile, tile)
        q, g = q_ref[at, :], g_ref[at, :]
        scores = visible_scores(q, k_ref[...], rows_ref[at, :], keys_ref[...], prefix_ref[0])
        probs = jnp.exp(scores - log_ref[0, at, :])
        grad_probs = lax.dot_general(
            g, v_ref[...], (((1,), (1,)), ((), ())), preferred_element_type=F32
        )
        dots = jnp.sum(probs * grad_probs, axis=-1, keepdims=True)
        grad_scores = (probs * (grad_probs - dots)).astype(BF)
        dq = jnp.dot(grad_scores, k_ref[...], preferred_element_type=F32) * scale
        o_ref[at, :HD] = turned(
            dq, keep_ref[at, :], up_ref[at, :], down_ref[at, :], -1.0
        ).astype(BF)
        dk = contract(grad_scores, q, 0, 0)
        dv = contract(probs.astype(BF), g, 0, 0)
        if i == 0:
            dk_ref[...] = dk
            dv_ref[...] = dv
        else:
            dk_ref[...] += dk
            dv_ref[...] += dv
    o_ref[:, HD : 2 * HD] = turned(
        dk_ref[...] * scale, keep_ref[...], up_ref[...], down_ref[...], -1.0
    ).astype(BF)
    o_ref[:, 2 * HD :] = dv_ref[...].astype(BF)


def attend_back(qkv, grad_context, log_total, prefix, spots, tables):
    length = qkv.shape[0]
    heads = qkv.shape[1] // (3 * HD)
    part = lambda n: pl.BlockSpec((length, HD), lambda h, p: (0, 3 * h + n))
    table = pl.BlockSpec((length, 128), lambda h, p: (0, 0))
    return pl.pallas_call(
        attend_back_kernel,
        grid_spec=pltpu.PrefetchScalarGridSpec(
            num_scalar_prefetch=1,
            grid=(heads,),
            in_specs=[
                part(0),
                part(1),
                part(2),
                pl.BlockSpec((length, HD), lambda h, p: (0, h)),
                pl.BlockSpec((1, length, 1), lambda h, p: (h, 0, 0)),
                pl.BlockSpec((length, 1), lambda h, p: (0, 0)),
                pl.BlockSpec((1, length), lambda h, p: (0, 0)),
                table,
                table,
                table,
            ],
            out_specs=pl.BlockSpec((length, 3 * HD), lambda h, p: (0, h)),
            scratch_shapes=[pltpu.VMEM((length, HD), F32), pltpu.VMEM((length, HD), F32)],
        ),
        out_shape=jax.ShapeDtypeStruct((length, heads * 3 * HD), BF),
        compiler_params=pltpu.CompilerParams(vmem_limit_bytes=48 << 20),
        cost_estimate=pl.CostEstimate(
            flops=10 * heads * length * length * HD,
            bytes_accessed=14 * length * heads * HD,
            transcendentals=heads * length * length,
        ),
        name="attend_back",
    )(prefix, qkv, qkv, qkv, grad_context, log_total, spots[:, None], spots[None, :], *tables)


def place_kernel(quarter_ref, *refs):
    pieces, out_ref = refs[-5:-1], refs[-1]
    for index, piece in enumerate(pieces):

        @pl.when(pl.program_id(0) == index)
        def _(piece=piece):
            out_ref[...] = piece[...].astype(F32)


def place_quarters(whole, pieces, shape, axis, chunk, chunks, quarter):
    rows, columns = pieces[0].shape
    if axis == 0:
        spot = lambda k, q: ((q[0] ^ k) * chunks + chunk, 0)
    else:
        spot = lambda k, q: (chunk, q[0] ^ k)
    first = whole is None
    operands = ([] if first else [whole]) + list(pieces)
    return pl.pallas_call(
        place_kernel,
        grid_spec=pltpu.PrefetchScalarGridSpec(
            num_scalar_prefetch=1,
            grid=(4,),
            in_specs=([] if first else [pl.BlockSpec(memory_space=pl.ANY)])
            + [pl.BlockSpec((rows, columns), lambda k, q: (0, 0))] * 4,
            out_specs=pl.BlockSpec((rows, columns), spot),
        ),
        out_shape=jax.ShapeDtypeStruct(shape, F32),
        input_output_aliases={} if first else {1: 0},
        compiler_params=pltpu.CompilerParams(vmem_limit_bytes=24 << 20),
        cost_estimate=pl.CostEstimate(
            flops=0, bytes_accessed=24 * rows * columns, transcendentals=0
        ),
        name="place_quarters",
    )(quarter.reshape(1), *operands)


def norms_kernel(count, gains_ref, *refs):
    blocks, (attn_ref, mlp_ref) = refs[:count], refs[count:]
    for index, block in enumerate(blocks):

        @pl.when(pl.program_id(0) == index)
        def _(block=block):
            features = block[...].astype(F32)
            average = jnp.mean(features, axis=-1, keepdims=True)
            centered = features - average
            spread = jnp.mean(centered * centered, axis=-1, keepdims=True)
            xhat = centered * lax.rsqrt(spread + EPSILON)
            attn_ref[...] = (xhat * gains_ref[0:1, :] + gains_ref[1:2, :]).astype(BF)
            mlp_ref[...] = (xhat * gains_ref[2:3, :] + gains_ref[3:4, :]).astype(BF)


def both_norms(blocks, gains):
    count = len(blocks)
    rows, width = blocks[0].shape
    shape = jax.ShapeDtypeStruct((count * rows, width), BF)
    return pl.pallas_call(
        functools.partial(norms_kernel, count),
        grid=(count,),
        in_specs=[pl.BlockSpec((8, width), lambda i: (0, 0))]
        + [pl.BlockSpec((rows, width), lambda i: (0, 0))] * count,
        out_specs=[pl.BlockSpec((rows, width), lambda i: (i, 0))] * 2,
        out_shape=[shape, shape],
        compiler_params=pltpu.CompilerParams(vmem_limit_bytes=48 << 20),
        cost_estimate=pl.CostEstimate(
            flops=12 * count * rows * width,
            bytes_accessed=6 * count * rows * width,
            transcendentals=0,
        ),
        name="both_norms",
    )(gains, *blocks)


def outer_kernel(near_ref, far_ref, right_ref, *refs):
    rights, o_ref = refs[:-1], refs[-1]
    total = contract(near_ref[...], right_ref[...], 0, 0)
    rows = rights[0].shape[0]
    for index, right in enumerate(rights):
        total += contract(far_ref[pl.ds(index * rows, rows), :], right[...], 0, 0)
    o_ref[...] = total.astype(BF)


def outer_blocks(near, far, near_right, far_blocks):
    length, left = near.shape
    width = near_right.shape[1]
    rows = far_blocks[0].shape[0]
    tile = 512
    return pl.pallas_call(
        outer_kernel,
        grid=(width // tile,),
        in_specs=[
            pl.BlockSpec((length, left), lambda j: (0, 0)),
            pl.BlockSpec(far.shape, lambda j: (0, 0)),
            pl.BlockSpec((length, tile), lambda j: (0, j)),
        ]
        + [pl.BlockSpec((rows, tile), lambda j: (0, j))] * len(far_blocks),
        out_specs=pl.BlockSpec((left, tile), lambda j: (0, j)),
        out_shape=jax.ShapeDtypeStruct((left, width), BF),
        compiler_params=pltpu.CompilerParams(vmem_limit_bytes=56 << 20),
        cost_estimate=pl.CostEstimate(
            flops=2 * (length + far.shape[0]) * left * width,
            bytes_accessed=2 * (length + far.shape[0]) * (left + width),
            transcendentals=0,
        ),
        name="outer_blocks",
    )(near, far, near_right, *far_blocks)


def back_kernel(weight_ref, slope_ref, *refs):
    blocks, o_ref = refs[:-1], refs[-1]
    for index, block in enumerate(blocks):

        @pl.when(pl.program_id(0) == index)
        def _(block=block):
            o_ref[...] = (contract(block[...], weight_ref[...], 1, 1) * slope_ref[...]).astype(BF)


def back_blocks(blocks, weight, slope):
    rows, width = blocks[0].shape
    units = weight.shape[0]
    count = len(blocks)
    return pl.pallas_call(
        back_kernel,
        grid=(count,),
        in_specs=[
            pl.BlockSpec((units, width), lambda i: (0, 0)),
            pl.BlockSpec((rows, units), lambda i: (i, 0)),
        ]
        + [pl.BlockSpec((rows, width), lambda i: (0, 0))] * count,
        out_specs=pl.BlockSpec((rows, units), lambda i: (i, 0)),
        out_shape=jax.ShapeDtypeStruct((count * rows, units), BF),
        compiler_params=pltpu.CompilerParams(vmem_limit_bytes=56 << 20),
        cost_estimate=pl.CostEstimate(
            flops=2 * count * rows * units * width,
            bytes_accessed=2 * count * rows * (width + 3 * units),
            transcendentals=0,
        ),
        name="back_blocks",
    )(weight, slope, *blocks)


def on_device(
    hidden,
    teacher,
    valid_mask,
    prefix_len,
    ln1_gain,
    ln1_bias,
    ln2_gain,
    ln2_bias,
    qkv_weight,
    qkv_bias,
    out_weight,
    out_bias,
    fc1_weight,
    fc1_bias,
    fc2_weight,
    fc2_bias,
):
    rows = hidden.shape[0]
    dp = lax.axis_size("dp")
    tp = lax.axis_size("tensor")
    ways = tp // 2
    squares = dp // 4
    total_tokens = dp * tp * rows
    heads = qkv_weight.shape[1] // (3 * HD)
    dp_index = lax.axis_index("dp")
    tp_index = lax.axis_index("tensor")
    core, y = tp_index % 2, tp_index // 2
    quarter = dp_index % 4

    def to_core(v):
        return lax.ppermute(v, "tensor", [(t, t ^ 1) for t in range(tp)])

    def from_y(v, step):
        pairs = [(t, ((t // 2 - step) % ways) * 2 + t % 2) for t in range(tp)]
        return lax.ppermute(v, "tensor", pairs)

    def to_y(v, step):
        pairs = [(t, ((t // 2 + step) % ways) * 2 + t % 2) for t in range(tp)]
        return lax.ppermute(v, "tensor", pairs)

    def flip(v, mask):
        return lax.ppermute(v, "dp", [(d, d ^ mask) for d in range(dp)])

    def tensor_sum(v):
        v = v + to_core(v)
        bit = 2
        while bit < tp:
            v = v + lax.ppermute(v, "tensor", [(t, t ^ bit) for t in range(tp)])
            bit *= 2
        return v

    def dp_sum(v):
        bit = 1
        while bit < dp:
            v = v + flip(v, bit)
            bit *= 2
        return v

    block_ids = [
        ((y + step) % ways) * 2 + (core if mate == 0 else 1 - core)
        for step in range(ways)
        for mate in (0, 1)
    ]

    def gather_near(own):
        parts, over_y = [own, to_core(own)], []
        for step in range(1, ways):
            over_y.append(from_y(own, step))
            parts += [over_y[-1], to_core(over_y[-1])]
        return parts, over_y

    def gather_far(own, over_y):
        first = [flip(own, 1), flip(own, 2)]
        first.append(flip(first[1], 1))
        rounds_y = [first]
        for step in range(1, ways):
            rounds_y.append(
                [from_y(first[0], step), flip(over_y[step - 1], 2), from_y(first[2], step)]
            )
        parts = [[], [], []]
        for blocks in rounds_y:
            for i in range(3):
                parts[i] += [blocks[i], to_core(blocks[i])]
        return parts[0] + parts[1] + parts[2]

    def quarter_of(v, axis, index):
        size = v.shape[axis] // 4
        return lax.dynamic_slice_in_dim(v, index * size, size, axis)

    def swap_quarters(v):
        return [flip(quarter_of(v, 1, quarter ^ mask), mask) for mask in (1, 2, 3)]

    gain_attn = ln1_gain.astype(F32)
    shift_attn = ln1_bias.astype(F32)
    gain_mlp = ln2_gain.astype(F32)
    shift_mlp = ln2_bias.astype(F32)
    mask_f = valid_mask.astype(F32)
    count_all = dp_sum(tensor_sum(jnp.full((8, 128), jnp.sum(mask_f), F32)))[0, 0]

    gains = jnp.pad(
        jnp.stack([gain_attn, shift_attn, gain_mlp, shift_mlp]), ((0, 4), (0, 0))
    )
    near_blocks, hidden_y = gather_near(hidden)
    far_blocks = gather_far(hidden, hidden_y)
    norm_attn, norm_mlp = both_norms(near_blocks, gains)

    cosine_all, sine_all = rotary_tables(LEN, ROT)

    def in_order(table):
        return jnp.concatenate(
            [lax.dynamic_slice_in_dim(table, b * rows, rows, 0) for b in block_ids], axis=0
        )

    tables = rotary_lanes(in_order(cosine_all), in_order(sine_all))
    spots = jnp.concatenate([b * rows + jnp.arange(rows, dtype=jnp.int32) for b in block_ids])
    qkv_low = project_qkv(norm_attn, qkv_weight, qkv_bias, tables)
    context, log_total = attend(qkv_low, prefix_len, spots)
    hidden_pre = jnp.dot(norm_mlp, fc1_weight, preferred_element_type=F32) + fc1_bias.astype(F32)
    active, slope = exact_gelu(hidden_pre)
    active = active.astype(BF)
    active, *far_blocks = lax.optimization_barrier((active, *far_blocks))
    branch_part = jnp.dot(context, out_weight, preferred_element_type=F32) + jnp.dot(
        active, fc2_weight, preferred_element_type=F32
    )

    def scatter_rows(part, meanwhile=None):
        blocks = part.reshape(ways, 2, rows, D)
        mine = blocks[:, 0] + to_core(blocks[:, 1].astype(BF)).astype(F32)
        total = mine[0]
        side_work = None
        for step in range(1, ways):
            low = mine[step].astype(BF)
            got = to_y(low, step)
            if meanwhile is not None and step == 1:
                side_work = meanwhile(low)
                got = after(got, *side_work)
            total = total + got.astype(F32)
        return total, side_work

    branch, (norm_attn_far, norm_mlp_far) = scatter_rows(
        branch_part,
        lambda sent: both_norms([after(far_blocks[0], sent)] + far_blocks[1:], gains),
    )
    output_f = hidden.astype(F32) + branch + out_bias.astype(F32) + fc2_bias.astype(F32)
    mismatch = output_f - teacher.astype(F32)
    error_part = jnp.sum(mask_f[:, None] * mismatch * mismatch)
    grad_out = mask_f[:, None] * mismatch * (2.0 * total_tokens / count_all)
    bias_part = jnp.sum(grad_out, axis=0)
    grad_low = grad_out.astype(BF)
    grad_blocks, grad_y = gather_near(grad_low)
    grad_near = jnp.concatenate(grad_blocks, axis=0)
    grad_far = gather_far(grad_low, grad_y)

    fc1_quarter = quarter_of(fc1_weight, 1, quarter)
    fc2_quarter = quarter_of(fc2_weight, 0, quarter)
    pre_far = jnp.dot(
        after(norm_mlp_far, grad_low), fc1_quarter, preferred_element_type=F32
    ) + quarter_of(fc1_bias, 0, quarter).astype(F32)
    active_far, slope_far = exact_gelu(pre_far)
    active_far = active_far.astype(BF)
    context_far = jnp.concatenate(swap_quarters(context), axis=0)

    queue = []
    due = {}
    clock = [0]
    results = {}
    token = [grad_near]

    def gate(v):
        return after(v, token[0])

    def travel(name, low):
        mask = 4
        while mask < dp:
            (got,) = yield [(low, mask)], 2
            low = (low.astype(F32) + got.astype(F32)).astype(BF)
            mask *= 2
        beside, across = yield [(low, 1), (low, 2)], 1
        (corner,) = yield [(across, 1)], 1
        results.setdefault(name, []).append((low, beside, across, corner))

    def enqueue(name, part, count):
        size = part.shape[0] // count
        for i in range(count):
            queue.append((name, lax.slice_in_dim(part, i * size, (i + 1) * size, axis=0)))

    def turn(*others):
        now = clock[0]
        clock[0] = now + 1
        arrived = due.pop(now, [])
        values = [got for _, gots in arrived for got in gots]
        if queue:
            name, held = queue.pop(0)
            values.append(held)
        tied = list(lax.optimization_barrier(tuple(values) + others))
        token[0] = tied[0]
        asked = []
        for walker, gots in arrived:
            gots = [tied.pop(0) for _ in gots]
            try:
                asked.append((walker, walker.send(gots)))
            except StopIteration:
                pass
        if len(values) > sum(len(gots) for _, gots in arrived):
            walker = travel(name, tied.pop(0))
            asked.append((walker, next(walker)))
        for walker, (sends, wait) in asked:
            due.setdefault(now + wait, []).append((walker, [flip(v, mask) for v, mask in sends]))
        return tied

    placed = {}

    def place(name, axis, chunks):
        whole, done = placed.get(name, (None, 0))
        pieces = results.get(name, [])
        while done < len(pieces):
            whole = place_one(whole, pieces[done], axis, done, chunks)
            done += 1
        placed[name] = (whole, done)
        return whole

    def place_one(whole, pieces, axis, chunk, chunks):
        rows_here, columns = pieces[0].shape
        shape = (
            (4 * rows_here * chunks, columns) if axis == 0 else (rows_here * chunks, 4 * columns)
        )
        if columns % 128 == 0:
            return place_quarters(whole, pieces, shape, axis, chunk, chunks, quarter)
        if whole is None:
            whole = jnp.zeros(shape, F32)
        for index, piece in enumerate(pieces):
            spot = quarter ^ index
            start = (
                ((spot * chunks + chunk) * rows_here, 0)
                if axis == 0
                else (chunk * rows_here, spot * columns)
            )
            whole = lax.dynamic_update_slice(whole, piece.astype(F32), start)
        return whole

    grad_inner = (contract(grad_near, fc2_weight, 1, 1) * slope).astype(BF)
    grad_context = contract(grad_near, out_weight, 1, 1).astype(BF)
    grad_qkv = attend_back(qkv_low, grad_context, log_total, prefix_len, spots, tables)
    grad_qkv_far = swap_quarters(grad_qkv)
    left_near = jnp.concatenate(
        [quarter_of(active, 1, quarter), quarter_of(context, 1, quarter)], axis=1
    )
    left_far = jnp.concatenate([active_far, context_far], axis=1)
    part = outer_blocks(left_near, left_far, grad_near, grad_far)
    units = active_far.shape[1]
    enqueue("fc2", part[:units], 4)
    enqueue("out", part[units:], 1)
    grad_inner, *grad_qkv_far = turn(grad_inner, *grad_qkv_far)

    grad_inner_far = back_blocks([gate(grad_far[0])] + grad_far[1:], fc2_quarter, slope_far)
    fc1_part = contract(norm_mlp, quarter_of(grad_inner, 1, quarter), 0, 0) + contract(
        norm_mlp_far, grad_inner_far, 0, 0
    )
    (fc1_part,) = turn(fc1_part.astype(BF))
    enqueue("fc1", fc1_part, 4)
    qkv_part = contract(norm_attn, gate(quarter_of(grad_qkv, 1, quarter)), 0, 0) + contract(
        norm_attn_far, jnp.concatenate(grad_qkv_far, axis=0), 0, 0
    )
    (qkv_part,) = turn(qkv_part.astype(BF))
    enqueue("qkv", qkv_part, 8)
    grad_norm_mlp = contract(gate(grad_inner), fc1_weight, 1, 1)
    (grad_norm_mlp,) = turn(grad_norm_mlp)
    grad_norm_attn = contract(gate(grad_qkv), qkv_weight, 1, 1)
    (grad_norm_attn,) = turn(grad_norm_attn)

    features = jnp.concatenate(near_blocks, axis=0)
    features = gate(features).astype(F32)
    centered = features - jnp.mean(features, axis=-1, keepdims=True)
    inverse = lax.rsqrt(jnp.mean(centered * centered, axis=-1, keepdims=True) + EPSILON)
    xhat = centered * inverse

    def norm_back(gained):
        return inverse * (
            gained
            - jnp.mean(gained, axis=-1, keepdims=True)
            - xhat * jnp.mean(gained * xhat, axis=-1, keepdims=True)
        )

    grad_hidden = norm_back(grad_norm_attn * gain_attn + grad_norm_mlp * gain_mlp)
    tensor_parts = jnp.stack(
        [
            jnp.sum(grad_norm_attn * xhat, axis=0),
            jnp.sum(grad_norm_attn, axis=0),
            jnp.sum(grad_norm_mlp * xhat, axis=0),
            jnp.sum(grad_norm_mlp, axis=0),
            bias_part,
            jnp.full((D,), error_part, F32),
        ]
    ).reshape(-1)
    fc1_bias_part = jnp.sum(grad_inner, axis=0, dtype=F32)
    qkv_bias_part = jnp.sum(grad_qkv, axis=0, dtype=F32)
    grad_hidden, tensor_parts = turn(grad_hidden, tensor_parts)
    input_grad = grad_out + scatter_rows(grad_hidden)[0]
    (input_grad,) = turn(input_grad)
    small = jnp.concatenate([tensor_sum(tensor_parts), fc1_bias_part, qkv_bias_part])
    small = dp_sum(small)
    (small,) = turn(small)
    vectors = small[: 6 * D].reshape(6, D)
    fc1_bias_grad = small[6 * D : 6 * D + fc1_bias_part.shape[0]]
    qkv_bias_grad = small[6 * D + fc1_bias_part.shape[0] :]
    loss_value = vectors[5, 0] / (count_all * D)
    layout = {"fc2": (0, 4), "out": (0, 1), "fc1": (1, 4), "qkv": (1, 8)}
    while queue or due:
        for name, (axis, chunks) in layout.items():
            if len(results.get(name, [])) > placed.get(name, (None, 0))[1]:
                whole, done = placed.get(name, (None, 0))
                whole = place_one(whole, results[name][done], axis, done, chunks)
                placed[name] = (whole, done + 1)
                (whole,) = turn(whole)
                placed[name] = (whole, done + 1)
                break
        else:
            turn()
    fc2_weight_grad = place("fc2", 0, 4)
    out_weight_grad = place("out", 0, 1)
    fc1_weight_grad = place("fc1", 1, 4)
    qkv_weight_grad = place("qkv", 1, 8)
    return (
        output_f.astype(BF),
        loss_value,
        input_grad,
        vectors[0],
        vectors[1],
        vectors[2],
        vectors[3],
        qkv_weight_grad,
        qkv_bias_grad,
        out_weight_grad,
        vectors[4],
        fc1_weight_grad,
        fc1_bias_grad,
        fc2_weight_grad,
        vectors[4],
    )


def solution(mesh):
    tokens = P(("dp", "tensor"), None)
    columns, lanes, down, whole = P(None, "tensor"), P("tensor"), P("tensor", None), P()
    in_specs = (
        tokens,
        tokens,
        P(("dp", "tensor")),
        P("dp"),
        whole,
        whole,
        whole,
        whole,
        columns,
        lanes,
        down,
        whole,
        columns,
        lanes,
        down,
        whole,
    )
    out_specs = (
        tokens,
        whole,
        tokens,
        whole,
        whole,
        whole,
        whole,
        columns,
        lanes,
        down,
        whole,
        columns,
        lanes,
        down,
        whole,
    )
    return jax.shard_map(
        on_device, mesh=mesh, in_specs=in_specs, out_specs=out_specs, check_vma=False
    )
```

```python
import functools

import jax
import jax.numpy as jnp
from jax import lax
from jax.experimental import pallas as pl
from jax.experimental.pallas import tpu as pltpu
from jax.sharding import PartitionSpec as P

D = 2048
HD = 256
ROT = 64
LEN = 1024
EPSILON = 1e-05
BF = jnp.bfloat16
F32 = jnp.float32


def rotary_tables(length, rot_dims):
    half_dims = rot_dims // 2
    frequency = 10000.0 ** (-2.0 * jnp.arange(half_dims, dtype=F32) / rot_dims)
    angles = jnp.arange(length, dtype=F32)[:, None] * frequency[None, :]
    return jnp.cos(angles), jnp.sin(angles)


def contract(left_side, right_side, left_dim, right_dim):
    return lax.dot_general(
        left_side,
        right_side,
        (((left_dim,), (right_dim,)), ((), ())),
        preferred_element_type=F32,
    )


def exact_gelu(pre_act):
    below = 0.5 + 0.5 * lax.erf(pre_act * 0.5**0.5)
    density = jnp.exp(-0.5 * pre_act * pre_act) * (2.0 * jnp.pi) ** -0.5
    return pre_act * below, below + pre_act * density


def after(value, *earlier):
    return lax.optimization_barrier((value,) + earlier)[0]


def rotary_lanes(cosine, sine):
    ones = jnp.ones((cosine.shape[0], 128 - ROT), F32)
    none = jnp.zeros_like(sine)
    rest = jnp.zeros_like(ones)
    keep = jnp.concatenate([cosine, cosine, ones], axis=1)
    up = jnp.concatenate([-sine, none, rest], axis=1)
    down = jnp.concatenate([none, sine, rest], axis=1)
    return keep, up, down


def turned(block, keep, up, down, sign):
    head = block[:, :128]
    half = ROT // 2
    moved = head * keep + sign * (
        pltpu.roll(head, 128 - half, 1) * up + pltpu.roll(head, half, 1) * down
    )
    return jnp.concatenate([moved, block[:, 128:]], axis=1)


def qkv_kernel(x_ref, w_ref, b_ref, keep_ref, up_ref, down_ref, *refs):
    o_ref = refs[-1]
    kind = pl.program_id(0) % 3
    rows = x_ref.shape[0]
    tile = min(rows, 512)

    def project(at):
        return (
            jnp.dot(x_ref[at, :], w_ref[...], preferred_element_type=F32) + b_ref[...]
        )

    for start in range(0, rows, tile):
        at = pl.ds(start, min(tile, rows - start))

        @pl.when(kind == 2)
        def _(at=at):
            o_ref[at, :] = project(at).astype(BF)

        @pl.when(kind != 2)
        def _(at=at):
            o_ref[at, :] = turned(
                project(at), keep_ref[at, :], up_ref[at, :], down_ref[at, :], 1.0
            ).astype(BF)


def project_qkv(normed, weight, bias, tables, length, whole=None):
    rows, width = normed.shape
    columns = weight.shape[1]
    part = 0 if whole is None else 1
    if part and rows * 2 != length:
        rest = project_qkv(normed, weight, bias, tables, rows)
        return jnp.concatenate([whole[: length - rows], rest], axis=0)
    table = pl.BlockSpec((rows, 128), lambda j: (0, 0))
    return pl.pallas_call(
        qkv_kernel,
        grid=(columns // HD,),
        in_specs=[
            pl.BlockSpec((rows, width), lambda j: (0, 0)),
            pl.BlockSpec((width, HD), lambda j: (0, j)),
            pl.BlockSpec((1, HD), lambda j: (0, j)),
            table,
            table,
            table,
        ]
        + [pl.BlockSpec(memory_space=pl.ANY)] * part,
        out_specs=pl.BlockSpec((rows, HD), lambda j: (part, j)),
        out_shape=jax.ShapeDtypeStruct((length, columns), BF),
        input_output_aliases={6: 0} if part else {},
        compiler_params=pltpu.CompilerParams(vmem_limit_bytes=40 << 20),
        cost_estimate=pl.CostEstimate(
            flops=2 * rows * width * columns,
            bytes_accessed=2 * (rows * width + width * columns + rows * columns),
            transcendentals=0,
        ),
        name="qkv_rotary",
    )(normed, weight, bias.astype(F32)[None, :], *tables, *([whole] if part else []))


def visible_scores(queries, keys, row_spots, key_spots, prefix):
    scores = lax.dot_general(
        queries, keys, (((1,), (1,)), ((), ())), preferred_element_type=F32
    ) * (HD**-0.5)
    allowed = (key_spots <= row_spots) | (key_spots < prefix)
    return jnp.where(allowed, scores, -jnp.inf)


def attend_kernel(prefix_ref, q_ref, k_ref, v_ref, rows_ref, keys_ref, o_ref, log_ref):
    scores = visible_scores(
        q_ref[...], k_ref[...], rows_ref[...], keys_ref[...], prefix_ref[0]
    )
    top = jnp.max(scores, axis=-1, keepdims=True)
    weights = jnp.exp(scores - top)
    total = jnp.sum(weights, axis=-1, keepdims=True)
    probs = (weights * (1.0 / total)).astype(BF)
    o_ref[...] = jnp.dot(probs, v_ref[...], preferred_element_type=F32).astype(BF)
    log_ref[0] = top + jnp.log(total)


def attend(qkv, prefix, spots):
    length = qkv.shape[0]
    heads = qkv.shape[1] // (3 * HD)
    tile = length // 4
    whole = lambda part: pl.BlockSpec((length, HD), lambda h, i, p: (0, 3 * h + part))
    return pl.pallas_call(
        attend_kernel,
        grid_spec=pltpu.PrefetchScalarGridSpec(
            num_scalar_prefetch=1,
            grid=(heads, 4),
            in_specs=[
                pl.BlockSpec((tile, HD), lambda h, i, p: (i, 3 * h)),
                whole(1),
                whole(2),
                pl.BlockSpec((tile, 1), lambda h, i, p: (i, 0)),
                pl.BlockSpec((1, length), lambda h, i, p: (0, 0)),
            ],
            out_specs=[
                pl.BlockSpec((tile, HD), lambda h, i, p: (i, h)),
                pl.BlockSpec((1, tile, 1), lambda h, i, p: (h, i, 0)),
            ],
        ),
        out_shape=[
            jax.ShapeDtypeStruct((length, heads * HD), BF),
            jax.ShapeDtypeStruct((heads, length, 1), F32),
        ],
        compiler_params=pltpu.CompilerParams(vmem_limit_bytes=32 << 20),
        cost_estimate=pl.CostEstimate(
            flops=4 * heads * length * length * HD,
            bytes_accessed=8 * length * heads * HD,
            transcendentals=heads * length * length,
        ),
        name="attend",
    )(prefix, qkv, qkv, qkv, spots[:, None], spots[None, :])


def attend_back_kernel(
    prefix_ref, q_ref, k_ref, v_ref, g_ref, log_ref, rows_ref, keys_ref, keep_ref, up_ref,
    down_ref, o_ref, dk_ref, dv_ref,
):
    length = q_ref.shape[0]
    tile = length // 4
    scale = HD**-0.5
    for i in range(4):
        at = pl.ds(i * tile, tile)
        q, g = q_ref[at, :], g_ref[at, :]
        scores = visible_scores(q, k_ref[...], rows_ref[at, :], keys_ref[...], prefix_ref[0])
        probs = jnp.exp(scores - log_ref[0, at, :])
        grad_probs = lax.dot_general(
            g, v_ref[...], (((1,), (1,)), ((), ())), preferred_element_type=F32
        )
        dots = jnp.sum(probs * grad_probs, axis=-1, keepdims=True)
        grad_scores = (probs * (grad_probs - dots)).astype(BF)
        dq = jnp.dot(grad_scores, k_ref[...], preferred_element_type=F32) * scale
        o_ref[at, :HD] = turned(
            dq, keep_ref[at, :], up_ref[at, :], down_ref[at, :], -1.0
        ).astype(BF)
        dk = contract(grad_scores, q, 0, 0)
        dv = contract(probs.astype(BF), g, 0, 0)
        if i == 0:
            dk_ref[...] = dk
            dv_ref[...] = dv
        else:
            dk_ref[...] += dk
            dv_ref[...] += dv
    o_ref[:, HD : 2 * HD] = turned(
        dk_ref[...] * scale, keep_ref[...], up_ref[...], down_ref[...], -1.0
    ).astype(BF)
    o_ref[:, 2 * HD :] = dv_ref[...].astype(BF)


def attend_back(qkv, grad_context, log_total, prefix, spots, tables):
    length = qkv.shape[0]
    heads = qkv.shape[1] // (3 * HD)
    part = lambda n: pl.BlockSpec((length, HD), lambda h, p: (0, 3 * h + n))
    table = pl.BlockSpec((length, 128), lambda h, p: (0, 0))
    return pl.pallas_call(
        attend_back_kernel,
        grid_spec=pltpu.PrefetchScalarGridSpec(
            num_scalar_prefetch=1,
            grid=(heads,),
            in_specs=[
                part(0),
                part(1),
                part(2),
                pl.BlockSpec((length, HD), lambda h, p: (0, h)),
                pl.BlockSpec((1, length, 1), lambda h, p: (h, 0, 0)),
                pl.BlockSpec((length, 1), lambda h, p: (0, 0)),
                pl.BlockSpec((1, length), lambda h, p: (0, 0)),
                table,
                table,
                table,
            ],
            out_specs=pl.BlockSpec((length, 3 * HD), lambda h, p: (0, h)),
            scratch_shapes=[pltpu.VMEM((length, HD), F32), pltpu.VMEM((length, HD), F32)],
        ),
        out_shape=jax.ShapeDtypeStruct((length, heads * 3 * HD), BF),
        compiler_params=pltpu.CompilerParams(vmem_limit_bytes=48 << 20),
        cost_estimate=pl.CostEstimate(
            flops=10 * heads * length * length * HD,
            bytes_accessed=14 * length * heads * HD,
            transcendentals=heads * length * length,
        ),
        name="attend_back",
    )(prefix, qkv, qkv, qkv, grad_context, log_total, spots[:, None], spots[None, :], *tables)


def place_kernel(quarter_ref, *refs):
    pieces, out_ref = refs[-5:-1], refs[-1]
    for index, piece in enumerate(pieces):

        @pl.when(pl.program_id(0) == index)
        def _(piece=piece):
            out_ref[...] = piece[...].astype(F32)


def place_quarters(whole, pieces, shape, axis, chunk, chunks, quarter):
    rows, columns = pieces[0].shape
    if axis == 0:
        spot = lambda k, q: ((q[0] ^ k) * chunks + chunk, 0)
    else:
        spot = lambda k, q: (chunk, q[0] ^ k)
    first = whole is None
    operands = ([] if first else [whole]) + list(pieces)
    return pl.pallas_call(
        place_kernel,
        grid_spec=pltpu.PrefetchScalarGridSpec(
            num_scalar_prefetch=1,
            grid=(4,),
            in_specs=([] if first else [pl.BlockSpec(memory_space=pl.ANY)])
            + [pl.BlockSpec((rows, columns), lambda k, q: (0, 0))] * 4,
            out_specs=pl.BlockSpec((rows, columns), spot),
        ),
        out_shape=jax.ShapeDtypeStruct(shape, F32),
        input_output_aliases={} if first else {1: 0},
        compiler_params=pltpu.CompilerParams(vmem_limit_bytes=24 << 20),
        cost_estimate=pl.CostEstimate(
            flops=0, bytes_accessed=24 * rows * columns, transcendentals=0
        ),
        name="place_quarters",
    )(quarter.reshape(1), *operands)


def norms_kernel(count, gains_ref, *refs):
    blocks, (attn_ref, mlp_ref) = refs[:count], refs[count:]
    for index, block in enumerate(blocks):

        @pl.when(pl.program_id(0) == index)
        def _(block=block):
            features = block[...].astype(F32)
            average = jnp.mean(features, axis=-1, keepdims=True)
            centered = features - average
            spread = jnp.mean(centered * centered, axis=-1, keepdims=True)
            xhat = centered * lax.rsqrt(spread + EPSILON)
            attn_ref[...] = (xhat * gains_ref[0:1, :] + gains_ref[1:2, :]).astype(BF)
            mlp_ref[...] = (xhat * gains_ref[2:3, :] + gains_ref[3:4, :]).astype(BF)


def both_norms(blocks, gains):
    count = len(blocks)
    rows, width = blocks[0].shape
    shape = jax.ShapeDtypeStruct((count * rows, width), BF)
    return pl.pallas_call(
        functools.partial(norms_kernel, count),
        grid=(count,),
        in_specs=[pl.BlockSpec((8, width), lambda i: (0, 0))]
        + [pl.BlockSpec((rows, width), lambda i: (0, 0))] * count,
        out_specs=[pl.BlockSpec((rows, width), lambda i: (i, 0))] * 2,
        out_shape=[shape, shape],
        compiler_params=pltpu.CompilerParams(vmem_limit_bytes=48 << 20),
        cost_estimate=pl.CostEstimate(
            flops=12 * count * rows * width,
            bytes_accessed=6 * count * rows * width,
            transcendentals=0,
        ),
        name="both_norms",
    )(gains, *blocks)


def outer_kernel(near_ref, far_ref, right_ref, *refs):
    rights, (o_ref, left_ref, joined_ref) = refs[:-3], refs[-3:]
    near = near_ref.shape[0]
    rows = rights[0].shape[0]

    @pl.when(pl.program_id(0) == 0)
    def _():
        for start in range(0, near, rows):
            left_ref[:, pl.ds(start, rows)] = near_ref[pl.ds(start, rows), :].T
        for start in range(0, far_ref.shape[0], rows):
            left_ref[:, pl.ds(near + start, rows)] = far_ref[pl.ds(start, rows), :].T

    joined_ref[:near, :] = right_ref[...]
    for index, right in enumerate(rights):
        joined_ref[pl.ds(near + index * rows, rows), :] = right[...]
    o_ref[...] = jnp.dot(left_ref[...], joined_ref[...], preferred_element_type=F32).astype(BF)


def outer_blocks(near, far, near_right, far_blocks):
    length, left = near.shape
    width = near_right.shape[1]
    rows = far_blocks[0].shape[0]
    tokens = length + far.shape[0]
    tile = 512
    return pl.pallas_call(
        outer_kernel,
        grid=(width // tile,),
        in_specs=[
            pl.BlockSpec((length, left), lambda j: (0, 0)),
            pl.BlockSpec(far.shape, lambda j: (0, 0)),
            pl.BlockSpec((length, tile), lambda j: (0, j)),
        ]
        + [pl.BlockSpec((rows, tile), lambda j: (0, j))] * len(far_blocks),
        out_specs=pl.BlockSpec((left, tile), lambda j: (0, j)),
        out_shape=jax.ShapeDtypeStruct((left, width), BF),
        scratch_shapes=[pltpu.VMEM((left, tokens), BF), pltpu.VMEM((tokens, tile), BF)],
        compiler_params=pltpu.CompilerParams(vmem_limit_bytes=56 << 20),
        cost_estimate=pl.CostEstimate(
            flops=2 * tokens * left * width,
            bytes_accessed=2 * tokens * (left + width),
            transcendentals=0,
        ),
        name="outer_blocks",
    )(near, far, near_right, *far_blocks)


def back_kernel(weight_ref, slope_ref, *refs):
    blocks, o_ref = refs[:-1], refs[-1]
    for index, block in enumerate(blocks):

        @pl.when(pl.program_id(0) == index)
        def _(block=block):
            o_ref[...] = (contract(block[...], weight_ref[...], 1, 1) * slope_ref[...]).astype(BF)


def back_blocks(blocks, weight, slope):
    rows, width = blocks[0].shape
    units = weight.shape[0]
    count = len(blocks)
    return pl.pallas_call(
        back_kernel,
        grid=(count,),
        in_specs=[
            pl.BlockSpec((units, width), lambda i: (0, 0)),
            pl.BlockSpec((rows, units), lambda i: (i, 0)),
        ]
        + [pl.BlockSpec((rows, width), lambda i: (0, 0))] * count,
        out_specs=pl.BlockSpec((rows, units), lambda i: (i, 0)),
        out_shape=jax.ShapeDtypeStruct((count * rows, units), BF),
        compiler_params=pltpu.CompilerParams(vmem_limit_bytes=56 << 20),
        cost_estimate=pl.CostEstimate(
            flops=2 * count * rows * units * width,
            bytes_accessed=2 * count * rows * (width + 3 * units),
            transcendentals=0,
        ),
        name="back_blocks",
    )(weight, slope, *blocks)


def on_device(
    hidden,
    teacher,
    valid_mask,
    prefix_len,
    ln1_gain,
    ln1_bias,
    ln2_gain,
    ln2_bias,
    qkv_weight,
    qkv_bias,
    out_weight,
    out_bias,
    fc1_weight,
    fc1_bias,
    fc2_weight,
    fc2_bias,
):
    rows = hidden.shape[0]
    dp = lax.axis_size("dp")
    tp = lax.axis_size("tensor")
    ways = tp // 2
    squares = dp // 4
    total_tokens = dp * tp * rows
    heads = qkv_weight.shape[1] // (3 * HD)
    dp_index = lax.axis_index("dp")
    tp_index = lax.axis_index("tensor")
    core, y = tp_index % 2, tp_index // 2
    quarter = dp_index % 4

    def to_core(v):
        return lax.ppermute(v, "tensor", [(t, t ^ 1) for t in range(tp)])

    def from_y(v, step):
        pairs = [(t, ((t // 2 - step) % ways) * 2 + t % 2) for t in range(tp)]
        return lax.ppermute(v, "tensor", pairs)

    def to_y(v, step):
        pairs = [(t, ((t // 2 + step) % ways) * 2 + t % 2) for t in range(tp)]
        return lax.ppermute(v, "tensor", pairs)

    def flip(v, mask):
        return lax.ppermute(v, "dp", [(d, d ^ mask) for d in range(dp)])

    block_ids = [
        ((y + step) % ways) * 2 + (core if mate == 0 else 1 - core)
        for step in range(ways)
        for mate in (0, 1)
    ]

    def gather_near(own):
        over_y = [from_y(own, step) for step in range(1, ways)]
        parts = []
        for block in [own] + over_y:
            parts += [block, to_core(block)]
        return parts, over_y

    def first_far(own):
        return [flip(own, 1), flip(own, 2)]

    def second_far(first, over_y):
        corner = flip(first[1], 1)
        beside = [from_y(first[0], step) for step in range(1, ways)]
        across = [flip(block, 2) for block in over_y]
        return corner, beside, across

    def far_parts(first, second, last):
        corner, beside, across = second
        parts = []
        for blocks in ([first[0]] + beside, [first[1]] + across, [corner] + last):
            for block in blocks:
                parts += [block, to_core(block)]
        return parts

    def quarter_of(v, axis, index):
        size = v.shape[axis] // 4
        return lax.dynamic_slice_in_dim(v, index * size, size, axis)

    def swap_quarters(v):
        return [flip(quarter_of(v, 1, quarter ^ mask), mask) for mask in (1, 2, 3)]

    gain_attn = ln1_gain.astype(F32)
    shift_attn = ln1_bias.astype(F32)
    gain_mlp = ln2_gain.astype(F32)
    shift_mlp = ln2_bias.astype(F32)
    mask_f = valid_mask.astype(F32)
    gains = jnp.pad(
        jnp.stack([gain_attn, shift_attn, gain_mlp, shift_mlp]), ((0, 4), (0, 0))
    )
    count = jnp.full((8, 128), jnp.sum(mask_f), F32)
    near_blocks, hidden_y = gather_near(hidden)
    first = first_far(hidden)
    count = count + to_core(count)

    cosine_all, sine_all = rotary_tables(LEN, ROT)

    def in_order(table):
        return jnp.concatenate(
            [lax.dynamic_slice_in_dim(table, b * rows, rows, 0) for b in block_ids], axis=0
        )

    tables = rotary_lanes(in_order(cosine_all), in_order(sine_all))
    spots = jnp.concatenate([b * rows + jnp.arange(rows, dtype=jnp.int32) for b in block_ids])
    close = 2 * rows

    def units(normed):
        return jnp.dot(normed, fc1_weight, preferred_element_type=F32) + fc1_bias.astype(F32)

    norm_attn_own, norm_mlp_own = both_norms(near_blocks[:2], gains)
    pre_own = units(norm_mlp_own)
    active_own = exact_gelu(pre_own)[0].astype(BF)
    qkv_own = project_qkv(norm_attn_own, qkv_weight, qkv_bias, [t[:close] for t in tables], LEN)

    arrived = lax.optimization_barrier(
        (active_own, qkv_own, count, *first, *near_blocks[2:])
    )
    active_own, qkv_own, count, *rest = arrived
    first, rest_blocks = rest[:2], rest[2:]
    count = count + flip(count, 1)
    norm_attn_rest, norm_mlp_rest = both_norms(rest_blocks, gains)
    count, norm_attn_rest = lax.optimization_barrier((count, norm_attn_rest))
    count = count + flip(count, 2)
    qkv_low = project_qkv(
        norm_attn_rest, qkv_weight, qkv_bias, [t[close:] for t in tables], LEN, qkv_own
    )
    count, qkv_low = lax.optimization_barrier((count, qkv_low))
    mask = 4
    while mask < dp:
        count = count + flip(count, mask)
        mask *= 2
    context, log_total = attend(qkv_low, prefix_len, spots)
    count, context, *first = lax.optimization_barrier((count, context, *first))
    second = second_far(first, hidden_y)
    context_far = swap_quarters(context)
    bit = 2
    while bit < tp:
        count = count + lax.ppermute(count, "tensor", [(t, t ^ bit) for t in range(tp)])
        bit *= 2
    pre_rest = units(norm_mlp_rest)
    active_rest = exact_gelu(pre_rest)[0].astype(BF)
    active_rest, count, *corner = lax.optimization_barrier((active_rest, count, second[0]))
    count_all = count[0, 0]
    last = [from_y(corner[0], step) for step in range(1, ways)]
    far_blocks = far_parts(first, (corner[0], second[1], second[2]), last)

    def branch_rows(context_rows, active_rows):
        return jnp.dot(context_rows, out_weight, preferred_element_type=F32) + jnp.dot(
            active_rows, fc2_weight, preferred_element_type=F32
        )

    def core_total(part):
        blocks = part.reshape(-1, 2, rows, D)
        return blocks[:, 0] + to_core(blocks[:, 1].astype(BF)).astype(F32)

    sums = core_total(branch_rows(context[close:], active_rest))
    leaving = [sums[step - 1].astype(BF) for step in range(1, ways)]
    came = [to_y(low, step) for step, low in enumerate(leaving, 1)]
    active_now, context_now, *far_blocks = lax.optimization_barrier(
        (active_own, context[:close], *far_blocks, leaving[0])
    )[:-1]
    branch = core_total(branch_rows(context_now, active_now))[0]
    far_blocks[0] = after(far_blocks[0], branch)
    norm_attn_far, norm_mlp_far = both_norms(far_blocks, gains)
    fc1_quarter = quarter_of(fc1_weight, 1, quarter)
    fc2_quarter = quarter_of(fc2_weight, 0, quarter)
    pre_far = jnp.dot(norm_mlp_far, fc1_quarter, preferred_element_type=F32) + quarter_of(
        fc1_bias, 0, quarter
    ).astype(F32)
    active_far, slope_far = exact_gelu(pre_far)
    active_far = active_far.astype(BF)
    left_far = jnp.concatenate([active_far, jnp.concatenate(context_far, axis=0)], axis=1)
    left_near = jnp.concatenate(
        [
            jnp.concatenate(
                [quarter_of(active_own, 1, quarter), quarter_of(active_rest, 1, quarter)], axis=0
            ),
            quarter_of(context, 1, quarter),
        ],
        axis=1,
    )
    came = lax.optimization_barrier((*came, left_far, left_near))
    (*came, left_far, left_near) = came
    for got in came:
        branch = branch + got.astype(F32)

    output_f = hidden.astype(F32) + branch + out_bias.astype(F32) + fc2_bias.astype(F32)
    mismatch = output_f - teacher.astype(F32)
    error_part = jnp.sum(mask_f[:, None] * mismatch * mismatch)
    grad_out = mask_f[:, None] * mismatch * (2.0 * total_tokens / count_all)
    grad_low = grad_out.astype(BF)
    grad_blocks, grad_y = gather_near(grad_low)
    grad_first = first_far(grad_low)
    tied = lax.optimization_barrier((*grad_first, *grad_blocks, *grad_y))
    grad_first, tied = list(tied[:2]), tied[2:]
    grad_blocks, grad_y = list(tied[: 2 * ways]), list(tied[2 * ways :])
    grad_second = second_far(grad_first, grad_y)
    grad_near = jnp.concatenate(grad_blocks, axis=0)
    hidden_pre = jnp.concatenate([pre_own, pre_rest], axis=0)
    grad_inner = (contract(grad_near, fc2_weight, 1, 1) * exact_gelu(hidden_pre)[1]).astype(BF)
    grad_context = contract(grad_near, out_weight, 1, 1).astype(BF)
    grad_inner, grad_context, corner, *tied = lax.optimization_barrier(
        (grad_inner, grad_context, grad_second[0], *grad_second[1], *grad_second[2])
    )
    grad_second = (corner, list(tied[: ways - 1]), list(tied[ways - 1 :]))
    grad_last = [from_y(corner, step) for step in range(1, ways)]
    grad_far = far_parts(grad_first, grad_second, grad_last)
    grad_qkv = attend_back(qkv_low, grad_context, log_total, prefix_len, spots, tables)
    grad_qkv, *grad_far = lax.optimization_barrier((grad_qkv, *grad_far))
    bias_part = jnp.sum(grad_out, axis=0)

    queue = []
    due = {}
    clock = [0]
    results = {}
    token = [grad_near]

    def gate(v):
        return after(v, token[0])

    def flipped(v, mask):
        return v, lambda value: flip(value, mask)

    def travel(name, low):
        mask = 4
        while mask < dp:
            (got,) = yield [flipped(low, mask)], 2
            low = (low.astype(F32) + got.astype(F32)).astype(BF)
            mask *= 2
        beside, across = yield [flipped(low, 1), flipped(low, 2)], 1
        (corner,) = yield [flipped(across, 1)], 1
        results.setdefault(name, []).append((low, beside, across, corner))

    def swap_walk(v, into):
        got = yield [flipped(quarter_of(v, 1, quarter ^ m), m) for m in (1, 2, 3)], 3
        into.extend(got)

    def scatter_walk(kept, mates, into):
        (got,) = yield [(mates, to_core)], 1
        sums = kept + got.astype(F32)
        total = sums[0]
        for step in range(1, ways):
            (got,) = yield [(sums[step].astype(BF), lambda v, s=step: to_y(v, s))], 2
            total = total + got.astype(F32)
        into["input"] = grad_out + total

    def small_walk(parts, others, into):
        bit = 1
        while bit < tp:
            pairs = [(t, t ^ bit) for t in range(tp)]
            (got,) = yield [(parts, lambda v, p=pairs: lax.ppermute(v, "tensor", p))], 1
            parts = parts + got
            bit *= 2
        parts = jnp.concatenate([parts, others])
        bit = 1
        while bit < dp:
            (got,) = yield [flipped(parts, bit)], 1
            parts = parts + got
            bit *= 2
        into["small"] = parts

    def walk(walker):
        asked = next(walker)
        start(walker, asked, clock[0] - 1)

    def start(walker, asked, now):
        sends, wait = asked
        due.setdefault(now + wait, []).append((walker, [move(v) for v, move in sends]))

    def enqueue(name, part, count):
        size = part.shape[0] // count
        for i in range(count):
            queue.append((name, lax.slice_in_dim(part, i * size, (i + 1) * size, axis=0)))

    def turn(*others):
        now = clock[0]
        clock[0] = now + 1
        arrived = due.pop(now, [])
        values = [got for _, gots in arrived for got in gots]
        if queue:
            name, held = queue.pop(0)
            values.append(held)
        tied = list(lax.optimization_barrier(tuple(values) + others))
        token[0] = tied[0]
        asked = []
        for walker, gots in arrived:
            gots = [tied.pop(0) for _ in gots]
            try:
                asked.append((walker, walker.send(gots)))
            except StopIteration:
                pass
        if len(values) > sum(len(gots) for _, gots in arrived):
            walker = travel(name, tied.pop(0))
            asked.append((walker, next(walker)))
        for walker, request in asked:
            start(walker, request, now)
        return tied

    placed = {}

    def place(name, axis, chunks):
        whole, done = placed.get(name, (None, 0))
        pieces = results.get(name, [])
        while done < len(pieces):
            whole = place_one(whole, pieces[done], axis, done, chunks)
            done += 1
        placed[name] = (whole, done)
        return whole

    def place_one(whole, pieces, axis, chunk, chunks):
        rows_here, columns = pieces[0].shape
        shape = (
            (4 * rows_here * chunks, columns) if axis == 0 else (rows_here * chunks, 4 * columns)
        )
        if columns % 128 == 0:
            return place_quarters(whole, pieces, shape, axis, chunk, chunks, quarter)
        if whole is None:
            whole = jnp.zeros(shape, F32)
        for index, piece in enumerate(pieces):
            spot = quarter ^ index
            start = (
                ((spot * chunks + chunk) * rows_here, 0)
                if axis == 0
                else (chunk * rows_here, spot * columns)
            )
            whole = lax.dynamic_update_slice(whole, piece.astype(F32), start)
        return whole

    part = outer_blocks(left_near, left_far, grad_near, grad_far)
    mine = active_far.shape[1]
    enqueue("fc2", part[:mine], 4)
    enqueue("out", part[mine:], 1)
    turn()
    grad_qkv_far = []
    walk(swap_walk(grad_qkv, grad_qkv_far))
    grad_inner_far = back_blocks([gate(grad_far[0])] + grad_far[1:], fc2_quarter, slope_far)
    (grad_inner_far,) = turn(grad_inner_far)
    inner_quarter = gate(quarter_of(grad_inner, 1, quarter))
    fc1_part = (
        contract(norm_mlp_own, inner_quarter[:close], 0, 0)
        + contract(norm_mlp_rest, inner_quarter[close:], 0, 0)
        + contract(norm_mlp_far, grad_inner_far, 0, 0)
    )
    (fc1_part,) = turn(fc1_part.astype(BF))
    enqueue("fc1", fc1_part, 4)
    grad_norm_attn = contract(gate(grad_qkv), qkv_weight, 1, 1)
    (grad_norm_attn,) = turn(grad_norm_attn)
    qkv_quarter = gate(quarter_of(grad_qkv, 1, quarter))
    qkv_part = (
        contract(norm_attn_own, qkv_quarter[:close], 0, 0)
        + contract(norm_attn_rest, qkv_quarter[close:], 0, 0)
        + contract(norm_attn_far, jnp.concatenate(grad_qkv_far, axis=0), 0, 0)
    )
    (qkv_part,) = turn(qkv_part.astype(BF))
    enqueue("qkv", qkv_part, 8)
    grad_norm_mlp = contract(gate(grad_inner), fc1_weight, 1, 1)
    (grad_norm_mlp,) = turn(grad_norm_mlp)

    features = gate(jnp.concatenate(near_blocks, axis=0)).astype(F32)
    centered = features - jnp.mean(features, axis=-1, keepdims=True)
    inverse = lax.rsqrt(jnp.mean(centered * centered, axis=-1, keepdims=True) + EPSILON)
    xhat = centered * inverse
    gained = grad_norm_attn * gain_attn + grad_norm_mlp * gain_mlp
    grad_hidden = inverse * (
        gained
        - jnp.mean(gained, axis=-1, keepdims=True)
        - xhat * jnp.mean(gained * xhat, axis=-1, keepdims=True)
    )
    blocks = grad_hidden.reshape(ways, 2, rows, D)
    mates = blocks[:, 1].astype(BF)
    kept, mates = turn(blocks[:, 0], mates)
    outcome = {}
    walk(scatter_walk(kept, mates, outcome))
    tensor_parts = jnp.stack(
        [
            jnp.sum(grad_norm_attn * xhat, axis=0),
            jnp.sum(grad_norm_attn, axis=0),
            jnp.sum(grad_norm_mlp * xhat, axis=0),
            jnp.sum(grad_norm_mlp, axis=0),
            bias_part,
            jnp.full((D,), error_part, F32),
        ]
    ).reshape(-1)
    fc1_bias_part = jnp.sum(grad_inner, axis=0, dtype=F32)
    qkv_bias_part = jnp.sum(grad_qkv, axis=0, dtype=F32)
    tensor_parts, fc1_bias_part, qkv_bias_part = turn(tensor_parts, fc1_bias_part, qkv_bias_part)
    walk(small_walk(tensor_parts, jnp.concatenate([fc1_bias_part, qkv_bias_part]), outcome))
    layout = {"fc2": (0, 4), "out": (0, 1), "fc1": (1, 4), "qkv": (1, 8)}
    while queue or due:
        for name, (axis, chunks) in layout.items():
            if len(results.get(name, [])) > placed.get(name, (None, 0))[1]:
                whole, done = placed.get(name, (None, 0))
                whole = place_one(whole, results[name][done], axis, done, chunks)
                placed[name] = (whole, done + 1)
                (whole,) = turn(whole)
                placed[name] = (whole, done + 1)
                break
        else:
            turn()
    input_grad = outcome["input"]
    small = outcome["small"]
    vectors = small[: 6 * D].reshape(6, D)
    fc1_bias_grad = small[6 * D : 6 * D + fc1_bias_part.shape[0]]
    qkv_bias_grad = small[6 * D + fc1_bias_part.shape[0] :]
    loss_value = vectors[5, 0] / (count_all * D)
    fc2_weight_grad = place("fc2", 0, 4)
    out_weight_grad = place("out", 0, 1)
    fc1_weight_grad = place("fc1", 1, 4)
    qkv_weight_grad = place("qkv", 1, 8)
    return (
        output_f.astype(BF),
        loss_value,
        input_grad,
        vectors[0],
        vectors[1],
        vectors[2],
        vectors[3],
        qkv_weight_grad,
        qkv_bias_grad,
        out_weight_grad,
        vectors[4],
        fc1_weight_grad,
        fc1_bias_grad,
        fc2_weight_grad,
        vectors[4],
    )


def solution(mesh):
    tokens = P(("dp", "tensor"), None)
    columns, lanes, down, whole = P(None, "tensor"), P("tensor"), P("tensor", None), P()
    in_specs = (
        tokens,
        tokens,
        P(("dp", "tensor")),
        P("dp"),
        whole,
        whole,
        whole,
        whole,
        columns,
        lanes,
        down,
        whole,
        columns,
        lanes,
        down,
        whole,
    )
    out_specs = (
        tokens,
        whole,
        tokens,
        whole,
        whole,
        whole,
        whole,
        columns,
        lanes,
        down,
        whole,
        columns,
        lanes,
        down,
        whole,
    )
    return jax.shard_map(
        on_device, mesh=mesh, in_specs=in_specs, out_specs=out_specs, check_vma=False
    )
```

```python
import functools

import jax
import jax.numpy as jnp
import numpy as np
from jax import lax
from jax.experimental import pallas as pl
from jax.experimental.pallas import tpu as pltpu
from jax.sharding import PartitionSpec as P

D = 2048
HD = 256
ROT = 64
LEN = 1024
EPSILON = 1e-05
BF = jnp.bfloat16
F32 = jnp.float32


def rotary_table(length):
    half = ROT // 2
    frequency = (10000.0 ** (-2.0 * np.arange(half, dtype=np.float32) / ROT)).astype(np.float32)
    angles = np.arange(length, dtype=np.float32)[:, None] * frequency[None, :]
    cosine, sine = np.cos(angles), np.sin(angles)
    table = np.zeros((length, 3 * 128), np.float32)
    table[:, ROT:128] = 1.0
    table[:, :half] = table[:, half:ROT] = cosine
    table[:, 128 : 128 + half] = -sine
    table[:, 256 + half : 256 + ROT] = sine
    return table


def contract(left_side, right_side, left_dim, right_dim):
    return lax.dot_general(
        left_side,
        right_side,
        (((left_dim,), (right_dim,)), ((), ())),
        preferred_element_type=F32,
    )


def exact_gelu(pre_act):
    below = 0.5 + 0.5 * lax.erf(pre_act * 0.5**0.5)
    density = jnp.exp(-0.5 * pre_act * pre_act) * (2.0 * jnp.pi) ** -0.5
    return pre_act * below, below + pre_act * density


def after(value, *earlier):
    return lax.optimization_barrier((value,) + earlier)[0]


def turned(block, keep, up, down, sign):
    head = block[:, :128]
    half = ROT // 2
    moved = head * keep + sign * (
        pltpu.roll(head, 128 - half, 1) * up + pltpu.roll(head, half, 1) * down
    )
    return jnp.concatenate([moved, block[:, 128:]], axis=1)


def qkv_kernel(x_ref, w_ref, b_ref, keep_ref, up_ref, down_ref, *refs):
    o_ref = refs[-1]
    kind = pl.program_id(0) % 3
    rows = x_ref.shape[0]
    tile = min(rows, 512)

    def project(at):
        return (
            jnp.dot(x_ref[at, :], w_ref[...], preferred_element_type=F32)
            + b_ref[...].astype(F32)
        )

    for start in range(0, rows, tile):
        at = pl.ds(start, min(tile, rows - start))

        @pl.when(kind == 2)
        def _(at=at):
            o_ref[at, :] = project(at).astype(BF)

        @pl.when(kind != 2)
        def _(at=at):
            o_ref[at, :] = turned(
                project(at), keep_ref[at, :], up_ref[at, :], down_ref[at, :], 1.0
            ).astype(BF)


def project_qkv(normed, weight, bias, table, length, whole=None):
    rows, width = normed.shape
    columns = weight.shape[1]
    part = 0 if whole is None else 1
    if part and rows * 2 != length:
        rest = project_qkv(normed, weight, bias, table[length - rows :], rows)
        return jnp.concatenate([whole[: length - rows], rest], axis=0)
    return pl.pallas_call(
        qkv_kernel,
        grid=(columns // HD,),
        in_specs=[
            pl.BlockSpec((rows, width), lambda j: (0, 0)),
            pl.BlockSpec((width, HD), lambda j: (0, j)),
            pl.BlockSpec((1, HD), lambda j: (0, j)),
        ]
        + [pl.BlockSpec((rows, 128), lambda j, k=k: (part, k)) for k in range(3)]
        + [pl.BlockSpec(memory_space=pl.ANY)] * part,
        out_specs=pl.BlockSpec((rows, HD), lambda j: (part, j)),
        out_shape=jax.ShapeDtypeStruct((length, columns), BF),
        input_output_aliases={6: 0} if part else {},
        compiler_params=pltpu.CompilerParams(vmem_limit_bytes=40 << 20),
        cost_estimate=pl.CostEstimate(
            flops=2 * rows * width * columns,
            bytes_accessed=2 * (rows * width + width * columns + rows * columns),
            transcendentals=0,
        ),
        name="qkv_rotary",
    )(normed, weight, bias[None, :], table, table, table, *([whole] if part else []))


def visible_scores(queries, keys, row_spots, key_spots, prefix):
    scores = lax.dot_general(
        queries, keys, (((1,), (1,)), ((), ())), preferred_element_type=F32
    ) * (HD**-0.5)
    allowed = (key_spots <= row_spots) | (key_spots < prefix)
    return jnp.where(allowed, scores, -jnp.inf)


def attend_kernel(prefix_ref, q_ref, k_ref, v_ref, rows_ref, keys_ref, o_ref, log_ref):
    scores = visible_scores(
        q_ref[...], k_ref[...], rows_ref[...], keys_ref[...], prefix_ref[0]
    )
    top = jnp.max(scores, axis=-1, keepdims=True)
    weights = jnp.exp(scores - top)
    total = jnp.sum(weights, axis=-1, keepdims=True)
    probs = (weights * (1.0 / total)).astype(BF)
    o_ref[...] = jnp.dot(probs, v_ref[...], preferred_element_type=F32).astype(BF)
    log_ref[0] = top + jnp.log(total)


def attend(qkv, prefix, spots):
    length = qkv.shape[0]
    heads = qkv.shape[1] // (3 * HD)
    tile = length // 4
    whole = lambda part: pl.BlockSpec((length, HD), lambda h, i, p: (0, 3 * h + part))
    return pl.pallas_call(
        attend_kernel,
        grid_spec=pltpu.PrefetchScalarGridSpec(
            num_scalar_prefetch=1,
            grid=(heads, 4),
            in_specs=[
                pl.BlockSpec((tile, HD), lambda h, i, p: (i, 3 * h)),
                whole(1),
                whole(2),
                pl.BlockSpec((tile, 1), lambda h, i, p: (i, 0)),
                pl.BlockSpec((1, length), lambda h, i, p: (0, 0)),
            ],
            out_specs=[
                pl.BlockSpec((tile, HD), lambda h, i, p: (i, h)),
                pl.BlockSpec((1, tile, 1), lambda h, i, p: (h, i, 0)),
            ],
        ),
        out_shape=[
            jax.ShapeDtypeStruct((length, heads * HD), BF),
            jax.ShapeDtypeStruct((heads, length, 1), F32),
        ],
        compiler_params=pltpu.CompilerParams(vmem_limit_bytes=32 << 20),
        cost_estimate=pl.CostEstimate(
            flops=4 * heads * length * length * HD,
            bytes_accessed=8 * length * heads * HD,
            transcendentals=heads * length * length,
        ),
        name="attend",
    )(prefix, qkv, qkv, qkv, spots[:, None], spots[None, :])


def attend_back_kernel(
    prefix_ref, q_ref, k_ref, v_ref, g_ref, log_ref, rows_ref, keys_ref, keep_ref, up_ref,
    down_ref, o_ref, dk_ref, dv_ref,
):
    length = q_ref.shape[0]
    tile = length // 4
    scale = HD**-0.5
    for i in range(4):
        at = pl.ds(i * tile, tile)
        q, g = q_ref[at, :], g_ref[at, :]
        scores = visible_scores(q, k_ref[...], rows_ref[at, :], keys_ref[...], prefix_ref[0])
        probs = jnp.exp(scores - log_ref[0, at, :])
        grad_probs = lax.dot_general(
            g, v_ref[...], (((1,), (1,)), ((), ())), preferred_element_type=F32
        )
        dots = jnp.sum(probs * grad_probs, axis=-1, keepdims=True)
        grad_scores = (probs * (grad_probs - dots)).astype(BF)
        dq = jnp.dot(grad_scores, k_ref[...], preferred_element_type=F32) * scale
        o_ref[at, :HD] = turned(
            dq, keep_ref[at, :], up_ref[at, :], down_ref[at, :], -1.0
        ).astype(BF)
        dk = contract(grad_scores, q, 0, 0)
        dv = contract(probs.astype(BF), g, 0, 0)
        if i == 0:
            dk_ref[...] = dk
            dv_ref[...] = dv
        else:
            dk_ref[...] += dk
            dv_ref[...] += dv
    o_ref[:, HD : 2 * HD] = turned(
        dk_ref[...] * scale, keep_ref[...], up_ref[...], down_ref[...], -1.0
    ).astype(BF)
    o_ref[:, 2 * HD :] = dv_ref[...].astype(BF)


def attend_back(qkv, grad_context, log_total, prefix, spots, table):
    length = qkv.shape[0]
    heads = qkv.shape[1] // (3 * HD)
    part = lambda n: pl.BlockSpec((length, HD), lambda h, p: (0, 3 * h + n))
    return pl.pallas_call(
        attend_back_kernel,
        grid_spec=pltpu.PrefetchScalarGridSpec(
            num_scalar_prefetch=1,
            grid=(heads,),
            in_specs=[
                part(0),
                part(1),
                part(2),
                pl.BlockSpec((length, HD), lambda h, p: (0, h)),
                pl.BlockSpec((1, length, 1), lambda h, p: (h, 0, 0)),
                pl.BlockSpec((length, 1), lambda h, p: (0, 0)),
                pl.BlockSpec((1, length), lambda h, p: (0, 0)),
            ]
            + [pl.BlockSpec((length, 128), lambda h, p, k=k: (0, k)) for k in range(3)],
            out_specs=pl.BlockSpec((length, 3 * HD), lambda h, p: (0, h)),
            scratch_shapes=[pltpu.VMEM((length, HD), F32), pltpu.VMEM((length, HD), F32)],
        ),
        out_shape=jax.ShapeDtypeStruct((length, heads * 3 * HD), BF),
        compiler_params=pltpu.CompilerParams(vmem_limit_bytes=48 << 20),
        cost_estimate=pl.CostEstimate(
            flops=10 * heads * length * length * HD,
            bytes_accessed=14 * length * heads * HD,
            transcendentals=heads * length * length,
        ),
        name="attend_back",
    )(prefix, qkv, qkv, qkv, grad_context, log_total, spots[:, None], spots[None, :], table, table, table)


def place_kernel(quarter_ref, *refs):
    pieces, out_ref = refs[-5:-1], refs[-1]
    for index, piece in enumerate(pieces):

        @pl.when(pl.program_id(0) == index)
        def _(piece=piece):
            out_ref[...] = piece[...].astype(F32)


def place_quarters(whole, pieces, shape, axis, chunk, chunks, quarter):
    rows, columns = pieces[0].shape
    if axis == 0:
        spot = lambda k, q: ((q[0] ^ k) * chunks + chunk, 0)
    else:
        spot = lambda k, q: (chunk, q[0] ^ k)
    first = whole is None
    operands = ([] if first else [whole]) + list(pieces)
    return pl.pallas_call(
        place_kernel,
        grid_spec=pltpu.PrefetchScalarGridSpec(
            num_scalar_prefetch=1,
            grid=(4,),
            in_specs=([] if first else [pl.BlockSpec(memory_space=pl.ANY)])
            + [pl.BlockSpec((rows, columns), lambda k, q: (0, 0))] * 4,
            out_specs=pl.BlockSpec((rows, columns), spot),
        ),
        out_shape=jax.ShapeDtypeStruct(shape, F32),
        input_output_aliases={} if first else {1: 0},
        compiler_params=pltpu.CompilerParams(vmem_limit_bytes=24 << 20),
        cost_estimate=pl.CostEstimate(
            flops=0, bytes_accessed=24 * rows * columns, transcendentals=0
        ),
        name="place_quarters",
    )(quarter.reshape(1), *operands)


def norms_kernel(count, *refs):
    gains, blocks, (attn_ref, mlp_ref) = refs[:4], refs[4 : 4 + count], refs[4 + count :]
    for index, block in enumerate(blocks):

        @pl.when(pl.program_id(0) == index)
        def _(block=block):
            features = block[...].astype(F32)
            average = jnp.mean(features, axis=-1, keepdims=True)
            centered = features - average
            spread = jnp.mean(centered * centered, axis=-1, keepdims=True)
            xhat = centered * lax.rsqrt(spread + EPSILON)
            gain_a, shift_a, gain_m, shift_m = (ref[...].astype(F32) for ref in gains)
            attn_ref[...] = (xhat * gain_a + shift_a).astype(BF)
            mlp_ref[...] = (xhat * gain_m + shift_m).astype(BF)


def both_norms(blocks, gains):
    count = len(blocks)
    rows, width = blocks[0].shape
    shape = jax.ShapeDtypeStruct((count * rows, width), BF)
    return pl.pallas_call(
        functools.partial(norms_kernel, count),
        grid=(count,),
        in_specs=[pl.BlockSpec((1, width), lambda i: (0, 0))] * 4
        + [pl.BlockSpec((rows, width), lambda i: (0, 0))] * count,
        out_specs=[pl.BlockSpec((rows, width), lambda i: (i, 0))] * 2,
        out_shape=[shape, shape],
        compiler_params=pltpu.CompilerParams(vmem_limit_bytes=48 << 20),
        cost_estimate=pl.CostEstimate(
            flops=12 * count * rows * width,
            bytes_accessed=6 * count * rows * width,
            transcendentals=0,
        ),
        name="both_norms",
    )(*gains, *blocks)


def outer_kernel(lefts, pieces, _, *refs):
    left_refs, rights, (o_ref, left_ref, joined_ref) = refs[:lefts], refs[lefts:-3], refs[-3:]

    @pl.when(pl.program_id(0) == 0)
    def _():
        for ref, (row, column) in zip(left_refs, pieces):
            count, width = ref.shape
            step = min(count, 256)
            for start in range(0, count, step):
                left_ref[pl.ds(row, width), pl.ds(column + start, step)] = ref[
                    pl.ds(start, step), :
                ].T

    column = 0
    for ref in rights:
        joined_ref[pl.ds(column, ref.shape[0]), :] = ref[...]
        column += ref.shape[0]
    o_ref[...] = jnp.dot(left_ref[...], joined_ref[...], preferred_element_type=F32).astype(BF)


def outer_blocks(lefts, rights, quarter):
    width = rights[0].shape[1]
    tokens = sum(r.shape[0] for r in rights)
    left = max(row + taken for _, taken, row, _ in lefts)
    tile = 512
    specs = [
        pl.BlockSpec((a.shape[0], taken), lambda j, q: (0, q[0]))
        if taken < a.shape[1]
        else pl.BlockSpec(a.shape, lambda j, q: (0, 0))
        for a, taken, _, _ in lefts
    ]
    return pl.pallas_call(
        functools.partial(outer_kernel, len(lefts), [(r, t) for _, _, r, t in lefts]),
        grid_spec=pltpu.PrefetchScalarGridSpec(
            num_scalar_prefetch=1,
            grid=(width // tile,),
            in_specs=specs
            + [pl.BlockSpec((r.shape[0], tile), lambda j, q: (0, j)) for r in rights],
            out_specs=pl.BlockSpec((left, tile), lambda j, q: (0, j)),
            scratch_shapes=[pltpu.VMEM((left, tokens), BF), pltpu.VMEM((tokens, tile), BF)],
        ),
        out_shape=jax.ShapeDtypeStruct((left, width), BF),
        compiler_params=pltpu.CompilerParams(vmem_limit_bytes=56 << 20),
        cost_estimate=pl.CostEstimate(
            flops=2 * tokens * left * width,
            bytes_accessed=2 * tokens * (left + width),
            transcendentals=0,
        ),
        name="outer_blocks",
    )(quarter.reshape(1), *[a for a, _, _, _ in lefts], *rights)


def back_kernel(weight_ref, slope_ref, *refs):
    blocks, o_ref = refs[:-1], refs[-1]
    for index, block in enumerate(blocks):

        @pl.when(pl.program_id(0) == index)
        def _(block=block):
            o_ref[...] = (contract(block[...], weight_ref[...], 1, 1) * slope_ref[...]).astype(BF)


def back_blocks(blocks, weight, slope):
    rows, width = blocks[0].shape
    units = weight.shape[0]
    count = len(blocks)
    return pl.pallas_call(
        back_kernel,
        grid=(count,),
        in_specs=[
            pl.BlockSpec((units, width), lambda i: (0, 0)),
            pl.BlockSpec((rows, units), lambda i: (i, 0)),
        ]
        + [pl.BlockSpec((rows, width), lambda i: (0, 0))] * count,
        out_specs=pl.BlockSpec((rows, units), lambda i: (i, 0)),
        out_shape=jax.ShapeDtypeStruct((count * rows, units), BF),
        compiler_params=pltpu.CompilerParams(vmem_limit_bytes=56 << 20),
        cost_estimate=pl.CostEstimate(
            flops=2 * count * rows * units * width,
            bytes_accessed=2 * count * rows * (width + 3 * units),
            transcendentals=0,
        ),
        name="back_blocks",
    )(weight, slope, *blocks)


def on_device(
    hidden,
    teacher,
    valid_mask,
    prefix_len,
    ln1_gain,
    ln1_bias,
    ln2_gain,
    ln2_bias,
    qkv_weight,
    qkv_bias,
    out_weight,
    out_bias,
    fc1_weight,
    fc1_bias,
    fc2_weight,
    fc2_bias,
):
    rows = hidden.shape[0]
    dp = lax.axis_size("dp")
    tp = lax.axis_size("tensor")
    ways = tp // 2
    squares = dp // 4
    total_tokens = dp * tp * rows
    heads = qkv_weight.shape[1] // (3 * HD)
    dp_index = lax.axis_index("dp")
    tp_index = lax.axis_index("tensor")
    core, y = tp_index % 2, tp_index // 2
    quarter = dp_index % 4

    def to_core(v):
        return lax.ppermute(v, "tensor", [(t, t ^ 1) for t in range(tp)])

    def from_y(v, step):
        pairs = [(t, ((t // 2 - step) % ways) * 2 + t % 2) for t in range(tp)]
        return lax.ppermute(v, "tensor", pairs)

    def to_y(v, step):
        pairs = [(t, ((t // 2 + step) % ways) * 2 + t % 2) for t in range(tp)]
        return lax.ppermute(v, "tensor", pairs)

    def flip(v, mask):
        return lax.ppermute(v, "dp", [(d, d ^ mask) for d in range(dp)])

    block_ids = [
        ((y + step) % ways) * 2 + (core if mate == 0 else 1 - core)
        for step in range(ways)
        for mate in (0, 1)
    ]

    def gather_near(own):
        over_y = [from_y(own, step) for step in range(1, ways)]
        parts = []
        for block in [own] + over_y:
            parts += [block, to_core(block)]
        return parts, over_y

    def first_far(own):
        return [flip(own, 1), flip(own, 2)]

    def second_far(first, over_y):
        corner = flip(first[1], 1)
        beside = [from_y(first[0], step) for step in range(1, ways)]
        across = [flip(block, 2) for block in over_y]
        return corner, beside, across

    def last_far(second):
        half = rows // 2
        return [(flip(v[:half], 1), flip(u[half:], 2)) for u, v in zip(second[1], second[2])]

    def far_parts(first, second, last):
        corner, beside, across = second
        parts = []
        for blocks in ([first[0]] + beside, [first[1]] + across, [corner] + last):
            for block in blocks:
                parts += [block, to_core(block)]
        return parts

    def meet(*trees):
        leaves, shape = jax.tree.flatten(trees)
        return jax.tree.unflatten(shape, lax.optimization_barrier(tuple(leaves)))

    def quarter_of(v, axis, index):
        size = v.shape[axis] // 4
        return lax.dynamic_slice_in_dim(v, index * size, size, axis)

    def swap_quarters(v):
        return [flip(quarter_of(v, 1, quarter ^ mask), mask) for mask in (1, 2, 3)]

    gain_attn = ln1_gain.astype(F32)
    shift_attn = ln1_bias.astype(F32)
    gain_mlp = ln2_gain.astype(F32)
    shift_mlp = ln2_bias.astype(F32)
    mask_f = valid_mask.astype(F32)
    gains = [v[None, :] for v in (ln1_gain, ln1_bias, ln2_gain, ln2_bias)]
    close = 2 * rows

    def units(normed):
        return jnp.dot(normed, fc1_weight, preferred_element_type=F32) + fc1_bias.astype(F32)

    count = jnp.full((8, 128), jnp.sum(mask_f), F32)
    count = count + to_core(count)
    counted = flip(count, 1)
    near_blocks, hidden_y = gather_near(hidden)
    first = first_far(hidden)
    norm_attn_own, norm_mlp_own = both_norms(near_blocks[:2], gains)
    pre_own = units(norm_mlp_own)
    active_own = exact_gelu(pre_own)[0].astype(BF)
    table = jnp.concatenate(
        [
            lax.dynamic_slice_in_dim(jnp.asarray(rotary_table(LEN)), b * rows, rows, 0)
            for b in block_ids
        ],
        axis=0,
    )
    spots = jnp.concatenate([b * rows + jnp.arange(rows, dtype=jnp.int32) for b in block_ids])
    active_own, table = after(active_own, table), after(table, active_own)
    qkv_own = project_qkv(norm_attn_own, qkv_weight, qkv_bias, table, LEN)
    active_own, qkv_own, counted, first, hidden_y = meet(
        active_own, qkv_own, counted, first, hidden_y
    )
    count = count + counted

    near_blocks = near_blocks[:2]
    for block in hidden_y:
        near_blocks += [block, to_core(block)]
    second = second_far(first, hidden_y)
    counted = flip(count, 2)
    norm_attn_rest, norm_mlp_rest = both_norms(near_blocks[2:], gains)
    qkv_low = project_qkv(norm_attn_rest, qkv_weight, qkv_bias, table, LEN, qkv_own)
    context, log_total = attend(qkv_low, prefix_len, spots)
    norm_mlp_rest = after(norm_mlp_rest, context)
    context_far = swap_quarters(context)
    pre_rest = units(norm_mlp_rest)
    active_rest = exact_gelu(pre_rest)[0].astype(BF)
    active_rest, context, counted, second, context_far = meet(
        active_rest, context, counted, second, context_far
    )
    count = count + counted

    def branch_rows(context_rows, active_rows):
        return jnp.dot(context_rows, out_weight, preferred_element_type=F32) + jnp.dot(
            active_rows, fc2_weight, preferred_element_type=F32
        )

    def core_total(part):
        blocks = part.reshape(-1, 2, rows, D)
        return blocks[:, 0] + to_core(blocks[:, 1].astype(BF)).astype(F32)

    last = last_far(second)
    counted = jnp.zeros_like(count)
    bit = 2
    while bit < tp:
        counted = lax.ppermute(count, "tensor", [(t, t ^ bit) for t in range(tp)])
        bit *= 2
        if bit < tp:
            count = count + counted
    part_rest = branch_rows(context[close:], active_rest).reshape(-1, 2, rows, D)
    mates_rest = to_core(part_rest[:, 1].astype(BF))
    part_own = branch_rows(context[:close], after(active_own, part_rest)).reshape(2, rows, D)
    part_own, mates_rest, last, counted = meet(part_own, mates_rest, last, counted)
    count = count + counted

    sums = part_rest[:, 0] + mates_rest.astype(F32)
    came = [to_y(sums[step - 1].astype(BF), step) for step in range(1, ways)]
    mates_own = to_core(part_own[1].astype(BF))
    counted = flip(count, 4) if dp > 4 else jnp.zeros_like(count)
    last = [jnp.concatenate(pair, axis=0) for pair in last]
    far_blocks = far_parts(first, second, last)
    norm_attn_far, norm_mlp_far = both_norms(far_blocks, gains)
    came, mates_own, counted, norm_mlp_far = meet(came, mates_own, counted, norm_mlp_far)
    count = count + counted
    mask = 8
    while mask < dp:
        count = count + flip(count, mask)
        mask *= 2
    branch = part_own[0] + mates_own.astype(F32)
    for got in came:
        branch = branch + got.astype(F32)
    output_f = hidden.astype(F32) + branch + out_bias.astype(F32) + fc2_bias.astype(F32)
    mismatch = output_f - teacher.astype(F32)
    error_part = jnp.sum(mask_f[:, None] * mismatch * mismatch)
    grad_out = mask_f[:, None] * mismatch * (2.0 * total_tokens / count[0, 0])
    grad_low = grad_out.astype(BF)
    grad_out, grad_low, norm_mlp_far = meet(grad_out, grad_low, norm_mlp_far)

    grad_y = [from_y(grad_low, step) for step in range(1, ways)]
    grad_first = first_far(grad_low)
    grad_mate = to_core(grad_low)
    fc1_quarter = quarter_of(fc1_weight, 1, quarter)
    fc2_quarter = quarter_of(fc2_weight, 0, quarter)
    pre_far = jnp.dot(norm_mlp_far, fc1_quarter, preferred_element_type=F32) + quarter_of(
        fc1_bias, 0, quarter
    ).astype(F32)
    active_far, slope_far = exact_gelu(pre_far)
    active_far = active_far.astype(BF)
    grad_y, grad_first, active_far, grad_mate = meet(grad_y, grad_first, active_far, grad_mate)

    grad_second = second_far(grad_first, grad_y)
    grad_blocks = [grad_low, grad_mate]
    for block in grad_y:
        grad_blocks += [block, to_core(block)]
    grad_near = jnp.concatenate(grad_blocks, axis=0)
    hidden_pre = jnp.concatenate([pre_own, pre_rest], axis=0)
    grad_inner = (contract(grad_near, fc2_weight, 1, 1) * exact_gelu(hidden_pre)[1]).astype(BF)
    grad_context = contract(grad_near, out_weight, 1, 1).astype(BF)
    grad_inner, grad_context, grad_near, grad_second = meet(
        grad_inner, grad_context, grad_near, grad_second
    )

    grad_last = last_far(grad_second)
    corner, beside, across = grad_second
    ahead = [grad_first[0]] + beside + [grad_first[1]] + across + [corner]
    mates = [to_core(block) for block in ahead]
    grad_qkv = attend_back(qkv_low, grad_context, log_total, prefix_len, spots, table)
    grad_qkv, grad_last, mates = meet(grad_qkv, grad_last, mates)

    grad_last = [jnp.concatenate(pair, axis=0) for pair in grad_last]
    ahead += grad_last
    mates += [to_core(block) for block in grad_last]
    grad_far = [block for pair in zip(ahead, mates) for block in pair]
    bias_part = jnp.sum(grad_out, axis=0)

    queue = []
    due = {}
    clock = [0]
    results = {}
    token = [grad_near]

    def gate(v):
        return after(v, token[0])

    def flipped(v, mask):
        return v, lambda value: flip(value, mask)

    def travel(name, low):
        mask = 4
        while mask < dp:
            (got,) = yield [flipped(low, mask)], 2
            low = (low.astype(F32) + got.astype(F32)).astype(BF)
            mask *= 2
        beside, across = yield [flipped(low, 1), flipped(low, 2)], 1
        (corner,) = yield [flipped(across, 1)], 1
        results.setdefault(name, []).append((low, beside, across, corner))

    def swap_walk(v, into):
        got = yield [flipped(quarter_of(v, 1, quarter ^ m), m) for m in (1, 2, 3)], 3
        into.extend(got)

    def scatter_walk(kept, mates, into):
        (got,) = yield [(mates, to_core)], 1
        sums = kept + got.astype(F32)
        total = sums[0]
        for step in range(1, ways):
            (got,) = yield [(sums[step].astype(BF), lambda v, s=step: to_y(v, s))], 2
            total = total + got.astype(F32)
        into["input"] = grad_out + total

    def small_walk(parts, others, into):
        bit = 1
        while bit < tp:
            pairs = [(t, t ^ bit) for t in range(tp)]
            (got,) = yield [(parts, lambda v, p=pairs: lax.ppermute(v, "tensor", p))], 1
            parts = parts + got
            bit *= 2
        parts = jnp.concatenate([parts, others])
        bit = 1
        while bit < dp:
            (got,) = yield [flipped(parts, bit)], 1
            parts = parts + got
            bit *= 2
        into["small"] = parts

    def walk(walker):
        asked = next(walker)
        start(walker, asked, clock[0] - 1)

    def start(walker, asked, now):
        sends, wait = asked
        due.setdefault(now + wait, []).append((walker, [move(v) for v, move in sends]))

    def enqueue(name, part, count):
        size = part.shape[0] // count
        for i in range(count):
            queue.append((name, lax.slice_in_dim(part, i * size, (i + 1) * size, axis=0)))

    def turn(*others):
        now = clock[0]
        clock[0] = now + 1
        arrived = due.pop(now, [])
        values = [got for _, gots in arrived for got in gots]
        if queue:
            name, held = queue.pop(0)
            values.append(held)
        tied = list(lax.optimization_barrier(tuple(values) + others))
        token[0] = tied[0]
        asked = []
        for walker, gots in arrived:
            gots = [tied.pop(0) for _ in gots]
            try:
                asked.append((walker, walker.send(gots)))
            except StopIteration:
                pass
        if len(values) > sum(len(gots) for _, gots in arrived):
            walker = travel(name, tied.pop(0))
            asked.append((walker, next(walker)))
        for walker, request in asked:
            start(walker, request, now)
        return tied

    placed = {}

    def place(name, axis, chunks):
        whole, done = placed.get(name, (None, 0))
        pieces = results.get(name, [])
        while done < len(pieces):
            whole = place_one(whole, pieces[done], axis, done, chunks)
            done += 1
        placed[name] = (whole, done)
        return whole

    def place_one(whole, pieces, axis, chunk, chunks):
        rows_here, columns = pieces[0].shape
        shape = (
            (4 * rows_here * chunks, columns) if axis == 0 else (rows_here * chunks, 4 * columns)
        )
        if columns % 128 == 0:
            return place_quarters(whole, pieces, shape, axis, chunk, chunks, quarter)
        if whole is None:
            whole = jnp.zeros(shape, F32)
        for index, piece in enumerate(pieces):
            spot = quarter ^ index
            start = (
                ((spot * chunks + chunk) * rows_here, 0)
                if axis == 0
                else (chunk * rows_here, spot * columns)
            )
            whole = lax.dynamic_update_slice(whole, piece.astype(F32), start)
        return whole

    mine = active_far.shape[1]
    lefts = [
        (active_own, mine, 0, 0),
        (active_rest, mine, 0, close),
        (active_far, mine, 0, LEN),
    ]
    kept_columns = context.shape[1] // 4
    context_parts = [quarter_of(context, 1, quarter)] + context_far
    for index, piece in enumerate(context_parts):
        lefts.append((piece, kept_columns, mine, index * LEN))
    part = outer_blocks(lefts, [grad_near] + grad_far, quarter)
    enqueue("fc2", part[:mine], 4)
    enqueue("out", part[mine:], 1)
    turn()
    grad_qkv_far = []
    walk(swap_walk(grad_qkv, grad_qkv_far))
    grad_inner_far = back_blocks([gate(grad_far[0])] + grad_far[1:], fc2_quarter, slope_far)
    (grad_inner_far,) = turn(grad_inner_far)
    inner_quarter = gate(quarter_of(grad_inner, 1, quarter))
    fc1_part = (
        contract(norm_mlp_own, inner_quarter[:close], 0, 0)
        + contract(norm_mlp_rest, inner_quarter[close:], 0, 0)
        + contract(norm_mlp_far, grad_inner_far, 0, 0)
    )
    (fc1_part,) = turn(fc1_part.astype(BF))
    enqueue("fc1", fc1_part, 4)
    grad_norm_attn = contract(gate(grad_qkv), qkv_weight, 1, 1)
    (grad_norm_attn,) = turn(grad_norm_attn)
    qkv_quarter = gate(quarter_of(grad_qkv, 1, quarter))
    qkv_part = (
        contract(norm_attn_own, qkv_quarter[:close], 0, 0)
        + contract(norm_attn_rest, qkv_quarter[close:], 0, 0)
        + contract(norm_attn_far, jnp.concatenate(grad_qkv_far, axis=0), 0, 0)
    )
    (qkv_part,) = turn(qkv_part.astype(BF))
    enqueue("qkv", qkv_part, 8)
    grad_norm_mlp = contract(gate(grad_inner), fc1_weight, 1, 1)
    (grad_norm_mlp,) = turn(grad_norm_mlp)

    near_blocks = lax.optimization_barrier((token[0], *near_blocks))[1:]
    features = jnp.concatenate(near_blocks, axis=0).astype(F32)
    centered = features - jnp.mean(features, axis=-1, keepdims=True)
    inverse = lax.rsqrt(jnp.mean(centered * centered, axis=-1, keepdims=True) + EPSILON)
    xhat = centered * inverse
    gained = grad_norm_attn * gain_attn + grad_norm_mlp * gain_mlp
    grad_hidden = inverse * (
        gained
        - jnp.mean(gained, axis=-1, keepdims=True)
        - xhat * jnp.mean(gained * xhat, axis=-1, keepdims=True)
    )
    blocks = grad_hidden.reshape(ways, 2, rows, D)
    mates = blocks[:, 1].astype(BF)
    kept, mates = turn(blocks[:, 0], mates)
    outcome = {}
    walk(scatter_walk(kept, mates, outcome))
    tensor_parts = jnp.stack(
        [
            jnp.sum(grad_norm_attn * xhat, axis=0),
            jnp.sum(grad_norm_attn, axis=0),
            jnp.sum(grad_norm_mlp * xhat, axis=0),
            jnp.sum(grad_norm_mlp, axis=0),
            bias_part,
            jnp.full((D,), error_part, F32),
        ]
    ).reshape(-1)
    fc1_bias_part = jnp.sum(grad_inner, axis=0, dtype=F32)
    qkv_bias_part = jnp.sum(grad_qkv, axis=0, dtype=F32)
    tensor_parts, fc1_bias_part, qkv_bias_part = turn(tensor_parts, fc1_bias_part, qkv_bias_part)
    walk(small_walk(tensor_parts, jnp.concatenate([fc1_bias_part, qkv_bias_part]), outcome))
    layout = {"fc2": (0, 4), "out": (0, 1), "fc1": (1, 4), "qkv": (1, 8)}
    while queue or due:
        for name, (axis, chunks) in layout.items():
            if len(results.get(name, [])) > placed.get(name, (None, 0))[1]:
                whole, done = placed.get(name, (None, 0))
                whole = place_one(whole, results[name][done], axis, done, chunks)
                placed[name] = (whole, done + 1)
                (whole,) = turn(whole)
                placed[name] = (whole, done + 1)
                break
        else:
            turn()
    input_grad = outcome["input"]
    small = outcome["small"]
    vectors = small[: 6 * D].reshape(6, D)
    fc1_bias_grad = small[6 * D : 6 * D + fc1_bias_part.shape[0]]
    qkv_bias_grad = small[6 * D + fc1_bias_part.shape[0] :]
    loss_value = vectors[5, 0] / (count[0, 0] * D)
    fc2_weight_grad = place("fc2", 0, 4)
    out_weight_grad = place("out", 0, 1)
    fc1_weight_grad = place("fc1", 1, 4)
    qkv_weight_grad = place("qkv", 1, 8)
    return (
        output_f.astype(BF),
        loss_value,
        input_grad,
        vectors[0],
        vectors[1],
        vectors[2],
        vectors[3],
        qkv_weight_grad,
        qkv_bias_grad,
        out_weight_grad,
        vectors[4],
        fc1_weight_grad,
        fc1_bias_grad,
        fc2_weight_grad,
        vectors[4],
    )


def solution(mesh):
    tokens = P(("dp", "tensor"), None)
    columns, lanes, down, whole = P(None, "tensor"), P("tensor"), P("tensor", None), P()
    in_specs = (
        tokens,
        tokens,
        P(("dp", "tensor")),
        P("dp"),
        whole,
        whole,
        whole,
        whole,
        columns,
        lanes,
        down,
        whole,
        columns,
        lanes,
        down,
        whole,
    )
    out_specs = (
        tokens,
        whole,
        tokens,
        whole,
        whole,
        whole,
        whole,
        columns,
        lanes,
        down,
        whole,
        columns,
        lanes,
        down,
        whole,
    )
    return jax.shard_map(
        on_device, mesh=mesh, in_specs=in_specs, out_specs=out_specs, check_vma=False
    )
```

```python
import functools

import jax
import jax.numpy as jnp
import numpy as np
from jax import lax
from jax.experimental import pallas as pl
from jax.experimental.pallas import tpu as pltpu
from jax.sharding import PartitionSpec as P

D = 2048
HD = 256
ROT = 64
LEN = 1024
EPSILON = 1e-05
BF = jnp.bfloat16
F32 = jnp.float32


def rotary_table(length):
    half = ROT // 2
    frequency = (10000.0 ** (-2.0 * np.arange(half, dtype=np.float32) / ROT)).astype(np.float32)
    angles = np.arange(length, dtype=np.float32)[:, None] * frequency[None, :]
    cosine, sine = np.cos(angles), np.sin(angles)
    table = np.zeros((length, 3 * 128), np.float32)
    table[:, ROT:128] = 1.0
    table[:, :half] = table[:, half:ROT] = cosine
    table[:, 128 : 128 + half] = -sine
    table[:, 256 + half : 256 + ROT] = sine
    return table


def contract(left_side, right_side, left_dim, right_dim):
    return lax.dot_general(
        left_side,
        right_side,
        (((left_dim,), (right_dim,)), ((), ())),
        preferred_element_type=F32,
    )


def exact_gelu(pre_act):
    below = 0.5 + 0.5 * lax.erf(pre_act * 0.5**0.5)
    density = jnp.exp(-0.5 * pre_act * pre_act) * (2.0 * jnp.pi) ** -0.5
    return pre_act * below, below + pre_act * density


def after(value, *earlier):
    return lax.optimization_barrier((value,) + earlier)[0]


def turned(block, keep, up, down, sign):
    head = block[:, :128]
    half = ROT // 2
    moved = head * keep + sign * (
        pltpu.roll(head, 128 - half, 1) * up + pltpu.roll(head, half, 1) * down
    )
    return jnp.concatenate([moved, block[:, 128:]], axis=1)


def qkv_kernel(x_ref, w_ref, b_ref, keep_ref, up_ref, down_ref, *refs):
    o_ref = refs[-1]
    kind = pl.program_id(0) % 3
    rows = x_ref.shape[0]
    tile = min(rows, 512)

    def project(at):
        return (
            jnp.dot(x_ref[at, :], w_ref[...], preferred_element_type=F32)
            + b_ref[...].astype(F32)
        )

    for start in range(0, rows, tile):
        at = pl.ds(start, min(tile, rows - start))

        @pl.when(kind == 2)
        def _(at=at):
            o_ref[at, :] = project(at).astype(BF)

        @pl.when(kind != 2)
        def _(at=at):
            o_ref[at, :] = turned(
                project(at), keep_ref[at, :], up_ref[at, :], down_ref[at, :], 1.0
            ).astype(BF)


def project_qkv(normed, weight, bias, table, length, whole=None):
    rows, width = normed.shape
    columns = weight.shape[1]
    part = 0 if whole is None else 1
    if part and rows * 2 != length:
        rest = project_qkv(normed, weight, bias, table[length - rows :], rows)
        return jnp.concatenate([whole[: length - rows], rest], axis=0)
    return pl.pallas_call(
        qkv_kernel,
        grid=(columns // HD,),
        in_specs=[
            pl.BlockSpec((rows, width), lambda j: (0, 0)),
            pl.BlockSpec((width, HD), lambda j: (0, j)),
            pl.BlockSpec((1, HD), lambda j: (0, j)),
        ]
        + [pl.BlockSpec((rows, 128), lambda j, k=k: (part, k)) for k in range(3)]
        + [pl.BlockSpec(memory_space=pl.ANY)] * part,
        out_specs=pl.BlockSpec((rows, HD), lambda j: (part, j)),
        out_shape=jax.ShapeDtypeStruct((length, columns), BF),
        input_output_aliases={6: 0} if part else {},
        compiler_params=pltpu.CompilerParams(vmem_limit_bytes=40 << 20),
        cost_estimate=pl.CostEstimate(
            flops=2 * rows * width * columns,
            bytes_accessed=2 * (rows * width + width * columns + rows * columns),
            transcendentals=0,
        ),
        name="qkv_rotary",
    )(normed, weight, bias[None, :], table, table, table, *([whole] if part else []))


def visible_scores(queries, keys, row_spots, key_spots, prefix):
    scores = lax.dot_general(
        queries, keys, (((1,), (1,)), ((), ())), preferred_element_type=F32
    ) * (HD**-0.5)
    allowed = (key_spots <= row_spots) | (key_spots < prefix)
    return jnp.where(allowed, scores, -jnp.inf)


def attend_kernel(prefix_ref, q_ref, k_ref, v_ref, rows_ref, keys_ref, o_ref, log_ref):
    scores = visible_scores(
        q_ref[...], k_ref[...], rows_ref[...], keys_ref[...], prefix_ref[0]
    )
    top = jnp.max(scores, axis=-1, keepdims=True)
    weights = jnp.exp(scores - top)
    total = jnp.sum(weights, axis=-1, keepdims=True)
    probs = (weights * (1.0 / total)).astype(BF)
    o_ref[...] = jnp.dot(probs, v_ref[...], preferred_element_type=F32).astype(BF)
    log_ref[0] = top + jnp.log(total)


def attend(qkv, prefix, spots):
    length = qkv.shape[0]
    heads = qkv.shape[1] // (3 * HD)
    tile = length // 4
    whole = lambda part: pl.BlockSpec((length, HD), lambda h, i, p: (0, 3 * h + part))
    return pl.pallas_call(
        attend_kernel,
        grid_spec=pltpu.PrefetchScalarGridSpec(
            num_scalar_prefetch=1,
            grid=(heads, 4),
            in_specs=[
                pl.BlockSpec((tile, HD), lambda h, i, p: (i, 3 * h)),
                whole(1),
                whole(2),
                pl.BlockSpec((tile, 1), lambda h, i, p: (i, 0)),
                pl.BlockSpec((1, length), lambda h, i, p: (0, 0)),
            ],
            out_specs=[
                pl.BlockSpec((tile, HD), lambda h, i, p: (i, h)),
                pl.BlockSpec((1, tile, 1), lambda h, i, p: (h, i, 0)),
            ],
        ),
        out_shape=[
            jax.ShapeDtypeStruct((length, heads * HD), BF),
            jax.ShapeDtypeStruct((heads, length, 1), F32),
        ],
        compiler_params=pltpu.CompilerParams(vmem_limit_bytes=32 << 20),
        cost_estimate=pl.CostEstimate(
            flops=4 * heads * length * length * HD,
            bytes_accessed=8 * length * heads * HD,
            transcendentals=heads * length * length,
        ),
        name="attend",
    )(prefix, qkv, qkv, qkv, spots[:, None], spots[None, :])


def attend_back_kernel(
    prefix_ref, q_ref, k_ref, v_ref, g_ref, log_ref, rows_ref, keys_ref, keep_ref, up_ref,
    down_ref, o_ref, dk_ref, dv_ref,
):
    length = q_ref.shape[0]
    tile = length // 4
    scale = HD**-0.5
    for i in range(4):
        at = pl.ds(i * tile, tile)
        q, g = q_ref[at, :], g_ref[at, :]
        scores = visible_scores(q, k_ref[...], rows_ref[at, :], keys_ref[...], prefix_ref[0])
        probs = jnp.exp(scores - log_ref[0, at, :])
        grad_probs = lax.dot_general(
            g, v_ref[...], (((1,), (1,)), ((), ())), preferred_element_type=F32
        )
        dots = jnp.sum(probs * grad_probs, axis=-1, keepdims=True)
        grad_scores = (probs * (grad_probs - dots)).astype(BF)
        dq = jnp.dot(grad_scores, k_ref[...], preferred_element_type=F32) * scale
        o_ref[at, :HD] = turned(
            dq, keep_ref[at, :], up_ref[at, :], down_ref[at, :], -1.0
        ).astype(BF)
        dk = contract(grad_scores, q, 0, 0)
        dv = contract(probs.astype(BF), g, 0, 0)
        if i == 0:
            dk_ref[...] = dk
            dv_ref[...] = dv
        else:
            dk_ref[...] += dk
            dv_ref[...] += dv
    o_ref[:, HD : 2 * HD] = turned(
        dk_ref[...] * scale, keep_ref[...], up_ref[...], down_ref[...], -1.0
    ).astype(BF)
    o_ref[:, 2 * HD :] = dv_ref[...].astype(BF)


def attend_back(qkv, grad_context, log_total, prefix, spots, table):
    length = qkv.shape[0]
    heads = qkv.shape[1] // (3 * HD)
    part = lambda n: pl.BlockSpec((length, HD), lambda h, p: (0, 3 * h + n))
    return pl.pallas_call(
        attend_back_kernel,
        grid_spec=pltpu.PrefetchScalarGridSpec(
            num_scalar_prefetch=1,
            grid=(heads,),
            in_specs=[
                part(0),
                part(1),
                part(2),
                pl.BlockSpec((length, HD), lambda h, p: (0, h)),
                pl.BlockSpec((1, length, 1), lambda h, p: (h, 0, 0)),
                pl.BlockSpec((length, 1), lambda h, p: (0, 0)),
                pl.BlockSpec((1, length), lambda h, p: (0, 0)),
            ]
            + [pl.BlockSpec((length, 128), lambda h, p, k=k: (0, k)) for k in range(3)],
            out_specs=pl.BlockSpec((length, 3 * HD), lambda h, p: (0, h)),
            scratch_shapes=[pltpu.VMEM((length, HD), F32), pltpu.VMEM((length, HD), F32)],
        ),
        out_shape=jax.ShapeDtypeStruct((length, heads * 3 * HD), BF),
        compiler_params=pltpu.CompilerParams(vmem_limit_bytes=48 << 20),
        cost_estimate=pl.CostEstimate(
            flops=10 * heads * length * length * HD,
            bytes_accessed=14 * length * heads * HD,
            transcendentals=heads * length * length,
        ),
        name="attend_back",
    )(prefix, qkv, qkv, qkv, grad_context, log_total, spots[:, None], spots[None, :], table, table, table)


def place_kernel(quarter_ref, *refs):
    pieces, out_ref = refs[-5:-1], refs[-1]
    for index, piece in enumerate(pieces):

        @pl.when(pl.program_id(0) == index)
        def _(piece=piece):
            out_ref[...] = piece[...].astype(F32)


def place_quarters(whole, pieces, shape, axis, offset, quarter):
    rows, columns = pieces[0].shape
    if axis == 0:
        each, first_row = shape[0] // 4 // rows, offset // rows
        spot = lambda k, q: ((q[0] ^ k) * each + first_row, 0)
    else:
        spot = lambda k, q: (offset // rows, q[0] ^ k)
    first = whole is None
    operands = ([] if first else [whole]) + list(pieces)
    return pl.pallas_call(
        place_kernel,
        grid_spec=pltpu.PrefetchScalarGridSpec(
            num_scalar_prefetch=1,
            grid=(4,),
            in_specs=([] if first else [pl.BlockSpec(memory_space=pl.ANY)])
            + [pl.BlockSpec((rows, columns), lambda k, q: (0, 0))] * 4,
            out_specs=pl.BlockSpec((rows, columns), spot),
        ),
        out_shape=jax.ShapeDtypeStruct(shape, F32),
        input_output_aliases={} if first else {1: 0},
        compiler_params=pltpu.CompilerParams(vmem_limit_bytes=24 << 20),
        cost_estimate=pl.CostEstimate(
            flops=0, bytes_accessed=24 * rows * columns, transcendentals=0
        ),
        name="place_quarters",
    )(quarter.reshape(1), *operands)


def norms_kernel(count, *refs):
    gains, blocks, (attn_ref, mlp_ref) = refs[:4], refs[4 : 4 + count], refs[4 + count :]
    for index, block in enumerate(blocks):

        @pl.when(pl.program_id(0) == index)
        def _(block=block):
            features = block[...].astype(F32)
            average = jnp.mean(features, axis=-1, keepdims=True)
            centered = features - average
            spread = jnp.mean(centered * centered, axis=-1, keepdims=True)
            xhat = centered * lax.rsqrt(spread + EPSILON)
            gain_a, shift_a, gain_m, shift_m = (ref[...].astype(F32) for ref in gains)
            attn_ref[...] = (xhat * gain_a + shift_a).astype(BF)
            mlp_ref[...] = (xhat * gain_m + shift_m).astype(BF)


def both_norms(blocks, gains):
    count = len(blocks)
    rows, width = blocks[0].shape
    shape = jax.ShapeDtypeStruct((count * rows, width), BF)
    return pl.pallas_call(
        functools.partial(norms_kernel, count),
        grid=(count,),
        in_specs=[pl.BlockSpec((1, width), lambda i: (0, 0))] * 4
        + [pl.BlockSpec((rows, width), lambda i: (0, 0))] * count,
        out_specs=[pl.BlockSpec((rows, width), lambda i: (i, 0))] * 2,
        out_shape=[shape, shape],
        compiler_params=pltpu.CompilerParams(vmem_limit_bytes=48 << 20),
        cost_estimate=pl.CostEstimate(
            flops=12 * count * rows * width,
            bytes_accessed=6 * count * rows * width,
            transcendentals=0,
        ),
        name="both_norms",
    )(*gains, *blocks)


def outer_kernel(lefts, pieces, outs, _, *refs):
    left_refs, rights = refs[:lefts], refs[lefts : -2 - outs]
    out_refs, (left_ref, joined_ref) = refs[-2 - outs : -2], refs[-2:]

    @pl.when(pl.program_id(0) == 0)
    def _():
        for ref, (row, column) in zip(left_refs, pieces):
            count, width = ref.shape
            step = min(count, 256)
            for start in range(0, count, step):
                left_ref[pl.ds(row, width), pl.ds(column + start, step)] = ref[
                    pl.ds(start, step), :
                ].T

    column = 0
    for ref in rights:
        joined_ref[pl.ds(column, ref.shape[0]), :] = ref[...]
        column += ref.shape[0]
    total = jnp.dot(left_ref[...], joined_ref[...], preferred_element_type=F32).astype(BF)
    row = 0
    for ref in out_refs:
        ref[...] = total[row : row + ref.shape[0], :]
        row += ref.shape[0]


def outer_blocks(lefts, rights, sizes, quarter):
    width = rights[0].shape[1]
    tokens = sum(r.shape[0] for r in rights)
    left = sum(sizes)
    tile = 512
    specs = [
        pl.BlockSpec((a.shape[0], taken), lambda j, q, m=times, o=offset: (0, q[0] * m + o))
        for a, taken, times, offset, _, _ in lefts
    ]
    pieces = [(row, token) for *_, row, token in lefts]
    return pl.pallas_call(
        functools.partial(outer_kernel, len(lefts), pieces, len(sizes)),
        grid_spec=pltpu.PrefetchScalarGridSpec(
            num_scalar_prefetch=1,
            grid=(width // tile,),
            in_specs=specs
            + [pl.BlockSpec((r.shape[0], tile), lambda j, q: (0, j)) for r in rights],
            out_specs=[pl.BlockSpec((size, tile), lambda j, q: (0, j)) for size in sizes],
            scratch_shapes=[pltpu.VMEM((left, tokens), BF), pltpu.VMEM((tokens, tile), BF)],
        ),
        out_shape=[jax.ShapeDtypeStruct((size, width), BF) for size in sizes],
        compiler_params=pltpu.CompilerParams(vmem_limit_bytes=56 << 20),
        cost_estimate=pl.CostEstimate(
            flops=2 * tokens * left * width,
            bytes_accessed=2 * tokens * (left + width),
            transcendentals=0,
        ),
        name="outer_blocks",
    )(quarter.reshape(1), *[a for a, *_ in lefts], *rights)


def back_kernel(weight_ref, slope_ref, *refs):
    blocks, o_ref = refs[:-1], refs[-1]
    for index, block in enumerate(blocks):

        @pl.when(pl.program_id(0) == index)
        def _(block=block):
            o_ref[...] = (contract(block[...], weight_ref[...], 1, 1) * slope_ref[...]).astype(BF)


def back_blocks(blocks, weight, slope):
    rows, width = blocks[0].shape
    units = weight.shape[0]
    count = len(blocks)
    return pl.pallas_call(
        back_kernel,
        grid=(count,),
        in_specs=[
            pl.BlockSpec((units, width), lambda i: (0, 0)),
            pl.BlockSpec((rows, units), lambda i: (i, 0)),
        ]
        + [pl.BlockSpec((rows, width), lambda i: (0, 0))] * count,
        out_specs=pl.BlockSpec((rows, units), lambda i: (i, 0)),
        out_shape=jax.ShapeDtypeStruct((count * rows, units), BF),
        compiler_params=pltpu.CompilerParams(vmem_limit_bytes=56 << 20),
        cost_estimate=pl.CostEstimate(
            flops=2 * count * rows * units * width,
            bytes_accessed=2 * count * rows * (width + 3 * units),
            transcendentals=0,
        ),
        name="back_blocks",
    )(weight, slope, *blocks)


def on_device(
    hidden,
    teacher,
    valid_mask,
    prefix_len,
    ln1_gain,
    ln1_bias,
    ln2_gain,
    ln2_bias,
    qkv_weight,
    qkv_bias,
    out_weight,
    out_bias,
    fc1_weight,
    fc1_bias,
    fc2_weight,
    fc2_bias,
):
    rows = hidden.shape[0]
    dp = lax.axis_size("dp")
    tp = lax.axis_size("tensor")
    ways = tp // 2
    squares = dp // 4
    total_tokens = dp * tp * rows
    heads = qkv_weight.shape[1] // (3 * HD)
    dp_index = lax.axis_index("dp")
    tp_index = lax.axis_index("tensor")
    core, y = tp_index % 2, tp_index // 2
    quarter = dp_index % 4

    def to_core(v):
        return lax.ppermute(v, "tensor", [(t, t ^ 1) for t in range(tp)])

    def from_y(v, step):
        pairs = [(t, ((t // 2 - step) % ways) * 2 + t % 2) for t in range(tp)]
        return lax.ppermute(v, "tensor", pairs)

    def to_y(v, step):
        pairs = [(t, ((t // 2 + step) % ways) * 2 + t % 2) for t in range(tp)]
        return lax.ppermute(v, "tensor", pairs)

    def flip(v, mask):
        return lax.ppermute(v, "dp", [(d, d ^ mask) for d in range(dp)])

    block_ids = [
        ((y + step) % ways) * 2 + (core if mate == 0 else 1 - core)
        for step in range(ways)
        for mate in (0, 1)
    ]

    def gather_near(own):
        over_y = [from_y(own, step) for step in range(1, ways)]
        parts = []
        for block in [own] + over_y:
            parts += [block, to_core(block)]
        return parts, over_y

    def first_far(own):
        return [flip(own, 1), flip(own, 2)]

    def second_far(first, over_y):
        corner = flip(first[1], 1)
        beside = [from_y(first[0], step) for step in range(1, ways)]
        across = [flip(block, 2) for block in over_y]
        return corner, beside, across

    def last_far(second):
        half = rows // 2
        return [(flip(v[:half], 1), flip(u[half:], 2)) for u, v in zip(second[1], second[2])]

    def far_parts(first, second, last):
        corner, beside, across = second
        parts = []
        for blocks in ([first[0]] + beside, [first[1]] + across, [corner] + last):
            for block in blocks:
                parts += [block, to_core(block)]
        return parts

    def meet(*trees):
        leaves, shape = jax.tree.flatten(trees)
        return jax.tree.unflatten(shape, lax.optimization_barrier(tuple(leaves)))

    def quarter_of(v, axis, index):
        size = v.shape[axis] // 4
        return lax.dynamic_slice_in_dim(v, index * size, size, axis)

    def swap_quarters(v):
        return [flip(quarter_of(v, 1, quarter ^ mask), mask) for mask in (1, 2, 3)]

    gain_attn = ln1_gain.astype(F32)
    shift_attn = ln1_bias.astype(F32)
    gain_mlp = ln2_gain.astype(F32)
    shift_mlp = ln2_bias.astype(F32)
    gains = [v[None, :] for v in (ln1_gain, ln1_bias, ln2_gain, ln2_bias)]
    close = 2 * rows

    def units(normed):
        return jnp.dot(normed, fc1_weight, preferred_element_type=F32) + fc1_bias.astype(F32)

    near_blocks, hidden_y = gather_near(hidden)
    first = first_far(hidden)
    norm_attn_own, norm_mlp_own = both_norms(near_blocks[:2], gains)
    mask_f = after(valid_mask, norm_mlp_own).astype(F32)
    count = jnp.full((8, 128), jnp.sum(mask_f), F32)
    count = count + to_core(count)
    counted = flip(count, 1)
    pre_own = units(norm_mlp_own)
    active_own = exact_gelu(pre_own)[0].astype(BF)
    start = after(jnp.asarray(block_ids) * rows, norm_mlp_own)
    table = jnp.concatenate(
        [
            lax.dynamic_slice_in_dim(jnp.asarray(rotary_table(LEN)), start[i], rows, 0)
            for i in range(tp)
        ],
        axis=0,
    )
    spots = jnp.concatenate([b * rows + jnp.arange(rows, dtype=jnp.int32) for b in block_ids])
    active_own, table = after(active_own, table), after(table, active_own)
    qkv_own = project_qkv(norm_attn_own, qkv_weight, qkv_bias, table, LEN)
    active_own, qkv_own, counted, first, hidden_y = meet(
        active_own, qkv_own, counted, first, hidden_y
    )
    count = count + counted

    near_blocks = near_blocks[:2]
    for block in hidden_y:
        near_blocks += [block, to_core(block)]
    second = second_far(first, hidden_y)
    counted = flip(count, 2)
    norm_attn_rest, norm_mlp_rest = both_norms(near_blocks[2:], gains)
    qkv_low = project_qkv(norm_attn_rest, qkv_weight, qkv_bias, table, LEN, qkv_own)
    context, log_total = attend(qkv_low, prefix_len, spots)
    norm_mlp_rest = after(norm_mlp_rest, context)
    context_far = swap_quarters(context)
    pre_rest = units(norm_mlp_rest)
    active_rest = exact_gelu(pre_rest)[0].astype(BF)
    active_rest, context, counted, second, context_far = meet(
        active_rest, context, counted, second, context_far
    )
    count = count + counted

    def branch_rows(context_rows, active_rows):
        return jnp.dot(context_rows, out_weight, preferred_element_type=F32) + jnp.dot(
            active_rows, fc2_weight, preferred_element_type=F32
        )

    def core_total(part):
        blocks = part.reshape(-1, 2, rows, D)
        return blocks[:, 0] + to_core(blocks[:, 1].astype(BF)).astype(F32)

    last = last_far(second)
    counted = jnp.zeros_like(count)
    bit = 2
    while bit < tp:
        counted = lax.ppermute(count, "tensor", [(t, t ^ bit) for t in range(tp)])
        bit *= 2
        if bit < tp:
            count = count + counted
    part_rest = branch_rows(context[close:], active_rest).reshape(-1, 2, rows, D)
    mates_rest = to_core(part_rest[:, 1].astype(BF))
    part_own = branch_rows(context[:close], after(active_own, part_rest)).reshape(2, rows, D)
    part_own, mates_rest, counted = meet(part_own, mates_rest, counted)
    count = count + counted

    sums = part_rest[:, 0] + mates_rest.astype(F32)
    came = [to_y(sums[step - 1].astype(BF), step) for step in range(1, ways)]
    mates_own = to_core(part_own[1].astype(BF))
    counted = flip(count, 4) if dp > 4 else jnp.zeros_like(count)
    last = [jnp.concatenate(pair, axis=0) for pair in last]
    far_blocks = far_parts(first, second, last)
    norm_attn_far, norm_mlp_far = both_norms(far_blocks, gains)
    came, mates_own, counted, norm_mlp_far = meet(came, mates_own, counted, norm_mlp_far)
    count = count + counted
    mask = 8
    while mask < dp:
        count = count + flip(count, mask)
        mask *= 2
    branch = part_own[0] + mates_own.astype(F32)
    for got in came:
        branch = branch + got.astype(F32)
    output_f = hidden.astype(F32) + branch + out_bias.astype(F32) + fc2_bias.astype(F32)
    mismatch = output_f - teacher.astype(F32)
    error_part = jnp.sum(mask_f[:, None] * mismatch * mismatch)
    grad_out = mask_f[:, None] * mismatch * (2.0 * total_tokens / count[0, 0])
    grad_low = grad_out.astype(BF)
    grad_out, grad_low, norm_mlp_far = meet(grad_out, grad_low, norm_mlp_far)

    grad_y = [from_y(grad_low, step) for step in range(1, ways)]
    grad_first = first_far(grad_low)
    grad_mate = to_core(grad_low)
    fc1_quarter = quarter_of(fc1_weight, 1, quarter)
    fc2_quarter = quarter_of(after(fc2_weight, norm_mlp_far), 0, quarter)
    context_quarter = quarter_of(after(context, norm_mlp_far), 1, quarter)
    pre_far = jnp.dot(norm_mlp_far, fc1_quarter, preferred_element_type=F32) + quarter_of(
        fc1_bias, 0, quarter
    ).astype(F32)
    active_far, slope_far = exact_gelu(pre_far)
    active_far = active_far.astype(BF)
    grad_y, grad_first, active_far, grad_mate, fc2_quarter, context_quarter = meet(
        grad_y, grad_first, active_far, grad_mate, fc2_quarter, context_quarter
    )

    grad_second = second_far(grad_first, grad_y)
    grad_blocks = [grad_low, grad_mate]
    for block in grad_y:
        grad_blocks += [block, to_core(block)]
    grad_near = jnp.concatenate(grad_blocks, axis=0)
    hidden_pre = jnp.concatenate([pre_own, pre_rest], axis=0)
    grad_inner = (contract(grad_near, fc2_weight, 1, 1) * exact_gelu(hidden_pre)[1]).astype(BF)
    grad_context = contract(grad_near, out_weight, 1, 1).astype(BF)
    grad_inner, grad_context, grad_near, grad_second = meet(
        grad_inner, grad_context, grad_near, grad_second
    )

    grad_last = last_far(grad_second)
    corner, beside, across = grad_second
    ahead = [grad_first[0]] + beside + [grad_first[1]] + across + [corner]
    mates = [to_core(block) for block in ahead]
    grad_qkv = attend_back(qkv_low, grad_context, log_total, prefix_len, spots, table)
    grad_qkv, grad_last, mates = meet(grad_qkv, grad_last, mates)

    grad_last = [jnp.concatenate(pair, axis=0) for pair in grad_last]
    ahead += grad_last
    mates += [to_core(block) for block in grad_last]
    grad_far = [block for pair in zip(ahead, mates) for block in pair]
    bias_part = jnp.sum(grad_out, axis=0)

    queue = []
    due = {}
    clock = [0]
    results = {}
    token = [grad_near]

    def gate(v):
        return after(v, token[0])

    def flipped(v, mask):
        return v, lambda value: flip(value, mask)

    def travel(name, low):
        mask = 4
        while mask < dp:
            (got,) = yield [flipped(low, mask)], 2
            low = (low.astype(F32) + got.astype(F32)).astype(BF)
            mask *= 2
        beside, across = yield [flipped(low, 1), flipped(low, 2)], 1
        (corner,) = yield [flipped(across, 1)], 1
        results.setdefault(name, []).append((low, beside, across, corner))

    def swap_walk(v, into):
        got = yield [flipped(quarter_of(v, 1, quarter ^ m), m) for m in (1, 2, 3)], 3
        into.extend(got)

    def scatter_walk(kept, mates, into):
        (got,) = yield [(mates, to_core)], 1
        sums = kept + got.astype(F32)
        total = sums[0]
        for step in range(1, ways):
            (got,) = yield [(sums[step].astype(BF), lambda v, s=step: to_y(v, s))], 2
            total = total + got.astype(F32)
        into["input"] = grad_out + total

    def small_walk(parts, others, into):
        bit = 1
        while bit < tp:
            pairs = [(t, t ^ bit) for t in range(tp)]
            (got,) = yield [(parts, lambda v, p=pairs: lax.ppermute(v, "tensor", p))], 1
            parts = parts + got
            bit *= 2
        parts = jnp.concatenate([parts, others])
        bit = 1
        while bit < dp:
            (got,) = yield [flipped(parts, bit)], 1
            parts = parts + got
            bit *= 2
        into["small"] = parts

    def walk(walker):
        asked = next(walker)
        start(walker, asked, clock[0] - 1)

    def start(walker, asked, now):
        sends, wait = asked
        due.setdefault(now + wait, []).append((walker, [move(v) for v, move in sends]))

    parts_of = {}

    def cut(part, shares):
        unit = part.shape[0] // 16
        edges = [unit * sum(shares[:i]) for i in range(len(shares) + 1)]
        return [lax.slice_in_dim(part, a, b, axis=0) for a, b in zip(edges, edges[1:])]

    def enqueue(name, chunks):
        rows_before, _ = parts_of.get(name, (0, 0))
        for piece in chunks:
            queue.append((name, piece))
            rows_before += piece.shape[0]
        parts_of[name] = (rows_before, chunks[0].shape[1])

    def turn(*others):
        now = clock[0]
        clock[0] = now + 1
        arrived = due.pop(now, [])
        values = [got for _, gots in arrived for got in gots]
        if queue:
            name, held = queue.pop(0)
            values.append(held)
        tied = list(lax.optimization_barrier(tuple(values) + others))
        token[0] = tied[0]
        asked = []
        for walker, gots in arrived:
            gots = [tied.pop(0) for _ in gots]
            try:
                asked.append((walker, walker.send(gots)))
            except StopIteration:
                pass
        if len(values) > sum(len(gots) for _, gots in arrived):
            walker = travel(name, tied.pop(0))
            asked.append((walker, next(walker)))
        for walker, request in asked:
            start(walker, request, now)
        return tied

    def place_one(whole, pieces, shape, axis, offset):
        rows_here, columns = pieces[0].shape
        if columns % 128 == 0:
            return place_quarters(whole, pieces, shape, axis, offset, quarter)
        if whole is None:
            whole = jnp.zeros(shape, F32)
        for index, piece in enumerate(pieces):
            spot = quarter ^ index
            start = (
                (spot * (shape[0] // 4) + offset, 0) if axis == 0 else (offset, spot * columns)
            )
            whole = lax.dynamic_update_slice(whole, piece.astype(F32), start)
        return whole

    half = active_far.shape[1] // 2
    rights = [grad_near] + grad_far

    def hidden_lefts(part):
        return [
            (active_own, half, 2, part, 0, 0),
            (active_rest, half, 2, part, 0, close),
            (active_far, half, 0, part, 0, LEN),
        ]

    chunk = half // 2
    kept_columns = context.shape[1] // 4
    enqueue("fc2", outer_blocks(hidden_lefts(0), rights, [chunk] * 2, quarter))
    turn()
    lefts = hidden_lefts(1)
    for index, piece in enumerate([context_quarter] + context_far):
        lefts.append((piece, kept_columns, 0, 0, half, index * LEN))
    *parts, out_part = outer_blocks(
        lefts, [gate(grad_near)] + grad_far, [chunk] * 2 + [kept_columns], quarter
    )
    enqueue("fc2", parts)
    enqueue("out", [out_part])
    grad_qkv_far = []
    walk(swap_walk(gate(grad_qkv), grad_qkv_far))
    (out_part,) = turn(out_part)
    grad_inner_far = back_blocks([gate(grad_far[0])] + grad_far[1:], fc2_quarter, slope_far)
    (grad_inner_far,) = turn(grad_inner_far)
    inner_quarter = gate(quarter_of(grad_inner, 1, quarter))
    fc1_part = (
        contract(norm_mlp_own, inner_quarter[:close], 0, 0)
        + contract(norm_mlp_rest, inner_quarter[close:], 0, 0)
        + contract(norm_mlp_far, grad_inner_far, 0, 0)
    )
    (fc1_part,) = turn(fc1_part.astype(BF))
    enqueue("fc1", cut(fc1_part, [4, 4, 4, 4]))
    qkv_quarter = gate(quarter_of(grad_qkv, 1, quarter))
    qkv_part = (
        contract(norm_attn_own, qkv_quarter[:close], 0, 0)
        + contract(norm_attn_rest, qkv_quarter[close:], 0, 0)
        + contract(norm_attn_far, jnp.concatenate(grad_qkv_far, axis=0), 0, 0)
    )
    (qkv_part,) = turn(qkv_part.astype(BF))
    enqueue("qkv", cut(qkv_part, [4, 4, 4, 2, 1, 1]))
    grad_norm_attn = contract(gate(grad_qkv), qkv_weight, 1, 1)
    (grad_norm_attn,) = turn(grad_norm_attn)
    grad_norm_mlp = contract(gate(grad_inner), fc1_weight, 1, 1)
    (grad_norm_mlp,) = turn(grad_norm_mlp)

    near_blocks = lax.optimization_barrier((token[0], *near_blocks))[1:]
    features = jnp.concatenate(near_blocks, axis=0).astype(F32)
    centered = features - jnp.mean(features, axis=-1, keepdims=True)
    inverse = lax.rsqrt(jnp.mean(centered * centered, axis=-1, keepdims=True) + EPSILON)
    xhat = centered * inverse
    gained = grad_norm_attn * gain_attn + grad_norm_mlp * gain_mlp
    lift = jnp.mean(gained, axis=-1, keepdims=True)
    pull = jnp.mean(gained * xhat, axis=-1, keepdims=True)
    tensor_parts = jnp.stack(
        [
            jnp.sum(grad_norm_attn * xhat, axis=0),
            jnp.sum(grad_norm_attn, axis=0),
            jnp.sum(grad_norm_mlp * xhat, axis=0),
            jnp.sum(grad_norm_mlp, axis=0),
            bias_part,
            jnp.full((D,), error_part, F32),
        ]
    ).reshape(-1)
    tensor_parts, lift, pull = turn(tensor_parts, lift, pull)
    grad_hidden = inverse * (gained - lift - xhat * pull)
    blocks = grad_hidden.reshape(ways, 2, rows, D)
    kept, mates = turn(blocks[:, 0], blocks[:, 1].astype(BF))
    outcome = {}
    walk(scatter_walk(kept, mates, outcome))
    fc1_bias_part = jnp.sum(gate(grad_inner), axis=0, dtype=F32)
    qkv_bias_part = jnp.sum(gate(grad_qkv), axis=0, dtype=F32)
    fc1_bias_part, qkv_bias_part = turn(fc1_bias_part, qkv_bias_part)
    walk(small_walk(tensor_parts, jnp.concatenate([fc1_bias_part, qkv_bias_part]), outcome))
    axes = {"fc2": 0, "out": 0, "fc1": 1, "qkv": 1}
    placed = {name: (None, 0, 0) for name in axes}

    def place(name):
        whole, done, offset = placed[name]
        pieces = results[name][done]
        lengths, columns = parts_of[name]
        shape = (4 * lengths, columns) if axes[name] == 0 else (lengths, 4 * columns)
        whole = place_one(whole, pieces, shape, axes[name], offset)
        placed[name] = (whole, done + 1, offset + pieces[0].shape[0])

    while queue or due:
        ready = []
        for name in axes:
            if len(ready) < 2 and len(results.get(name, [])) > placed[name][1]:
                place(name)
                ready.append(name)
        wholes = turn(*[placed[name][0] for name in ready])
        for name, whole in zip(ready, wholes):
            placed[name] = (whole,) + placed[name][1:]
    for name in axes:
        while len(results[name]) > placed[name][1]:
            place(name)
    input_grad = outcome["input"]
    small = outcome["small"]
    vectors = small[: 6 * D].reshape(6, D)
    fc1_bias_grad = small[6 * D : 6 * D + fc1_bias_part.shape[0]]
    qkv_bias_grad = small[6 * D + fc1_bias_part.shape[0] :]
    loss_value = vectors[5, 0] / (count[0, 0] * D)
    fc2_weight_grad, out_weight_grad = placed["fc2"][0], placed["out"][0]
    fc1_weight_grad, qkv_weight_grad = placed["fc1"][0], placed["qkv"][0]
    return (
        output_f.astype(BF),
        loss_value,
        input_grad,
        vectors[0],
        vectors[1],
        vectors[2],
        vectors[3],
        qkv_weight_grad,
        qkv_bias_grad,
        out_weight_grad,
        vectors[4],
        fc1_weight_grad,
        fc1_bias_grad,
        fc2_weight_grad,
        vectors[4],
    )


def solution(mesh):
    tokens = P(("dp", "tensor"), None)
    columns, lanes, down, whole = P(None, "tensor"), P("tensor"), P("tensor", None), P()
    in_specs = (
        tokens,
        tokens,
        P(("dp", "tensor")),
        P("dp"),
        whole,
        whole,
        whole,
        whole,
        columns,
        lanes,
        down,
        whole,
        columns,
        lanes,
        down,
        whole,
    )
    out_specs = (
        tokens,
        whole,
        tokens,
        whole,
        whole,
        whole,
        whole,
        columns,
        lanes,
        down,
        whole,
        columns,
        lanes,
        down,
        whole,
    )
    return jax.shard_map(
        on_device, mesh=mesh, in_specs=in_specs, out_specs=out_specs, check_vma=False
    )
```

```python
import functools

import jax
import jax.numpy as jnp
import numpy as np
from jax import lax
from jax.experimental import pallas as pl
from jax.experimental.pallas import tpu as pltpu
from jax.sharding import PartitionSpec as P

D = 2048
HD = 256
ROT = 64
LEN = 1024
EPSILON = 1e-05
BF = jnp.bfloat16
F32 = jnp.float32
SMALL = pl.CostEstimate(flops=1 << 20, bytes_accessed=1 << 16, transcendentals=0)


def rotary_table(length):
    half = ROT // 2
    frequency = (10000.0 ** (-2.0 * np.arange(half, dtype=np.float32) / ROT)).astype(np.float32)
    angles = np.arange(length, dtype=np.float32)[:, None] * frequency[None, :]
    cosine, sine = np.cos(angles), np.sin(angles)
    table = np.zeros((length, 3 * 128), np.float32)
    table[:, ROT:128] = 1.0
    table[:, :half] = table[:, half:ROT] = cosine
    table[:, 128 : 128 + half] = -sine
    table[:, 256 + half : 256 + ROT] = sine
    return table


def contract(left_side, right_side, left_dim, right_dim):
    return lax.dot_general(
        left_side,
        right_side,
        (((left_dim,), (right_dim,)), ((), ())),
        preferred_element_type=F32,
    )


def exact_gelu(pre_act):
    below = 0.5 + 0.5 * lax.erf(pre_act * 0.5**0.5)
    density = jnp.exp(-0.5 * pre_act * pre_act) * (2.0 * jnp.pi) ** -0.5
    return pre_act * below, below + pre_act * density


def after(value, *earlier):
    return lax.optimization_barrier((value,) + earlier)[0]


def turned(block, keep, up, down, sign):
    head = block[:, :128]
    half = ROT // 2
    moved = head * keep + sign * (
        pltpu.roll(head, 128 - half, 1) * up + pltpu.roll(head, half, 1) * down
    )
    return jnp.concatenate([moved, block[:, 128:]], axis=1)


def qkv_kernel(x_ref, w_ref, b_ref, keep_ref, up_ref, down_ref, *refs):
    o_ref = refs[-1]
    kind = pl.program_id(0) % 3
    rows = x_ref.shape[0]
    tile = min(rows, 512)

    def project(at):
        return (
            jnp.dot(x_ref[at, :], w_ref[...], preferred_element_type=F32)
            + b_ref[...].astype(F32)
        )

    for start in range(0, rows, tile):
        at = pl.ds(start, min(tile, rows - start))

        @pl.when(kind == 2)
        def _(at=at):
            o_ref[at, :] = project(at).astype(BF)

        @pl.when(kind != 2)
        def _(at=at):
            o_ref[at, :] = turned(
                project(at), keep_ref[at, :], up_ref[at, :], down_ref[at, :], 1.0
            ).astype(BF)


def project_qkv(normed, weight, bias, table, length, whole=None):
    rows, width = normed.shape
    columns = weight.shape[1]
    part = 0 if whole is None else 1
    if part and rows * 2 != length:
        rest = project_qkv(normed, weight, bias, table[length - rows :], rows)
        return jnp.concatenate([whole[: length - rows], rest], axis=0)
    return pl.pallas_call(
        qkv_kernel,
        grid=(columns // HD,),
        in_specs=[
            pl.BlockSpec((rows, width), lambda j: (0, 0)),
            pl.BlockSpec((width, HD), lambda j: (0, j)),
            pl.BlockSpec((1, HD), lambda j: (0, j)),
        ]
        + [pl.BlockSpec((rows, 128), lambda j, k=k: (part, k)) for k in range(3)]
        + [pl.BlockSpec(memory_space=pl.ANY)] * part,
        out_specs=pl.BlockSpec((rows, HD), lambda j: (part, j)),
        out_shape=jax.ShapeDtypeStruct((length, columns), BF),
        input_output_aliases={6: 0} if part else {},
        compiler_params=pltpu.CompilerParams(vmem_limit_bytes=40 << 20),
        cost_estimate=SMALL,
        name="qkv_rotary",
    )(normed, weight, bias[None, :], table, table, table, *([whole] if part else []))


def visible_scores(queries, keys, row_spots, key_spots, prefix):
    scores = lax.dot_general(
        queries, keys, (((1,), (1,)), ((), ())), preferred_element_type=F32
    ) * (HD**-0.5)
    allowed = (key_spots <= row_spots) | (key_spots < prefix)
    return jnp.where(allowed, scores, -jnp.inf)


def attend_kernel(prefix_ref, q_ref, k_ref, v_ref, rows_ref, keys_ref, o_ref, log_ref):
    scores = visible_scores(
        q_ref[...], k_ref[...], rows_ref[...], keys_ref[...], prefix_ref[0]
    )
    top = jnp.max(scores, axis=-1, keepdims=True)
    weights = jnp.exp(scores - top)
    total = jnp.sum(weights, axis=-1, keepdims=True)
    probs = (weights * (1.0 / total)).astype(BF)
    o_ref[...] = jnp.dot(probs, v_ref[...], preferred_element_type=F32).astype(BF)
    log_ref[0] = top + jnp.log(total)


def attend(qkv, prefix, spots):
    length = qkv.shape[0]
    heads = qkv.shape[1] // (3 * HD)
    tile = length // 4
    whole = lambda part: pl.BlockSpec((length, HD), lambda h, i, p: (0, 3 * h + part))
    return pl.pallas_call(
        attend_kernel,
        grid_spec=pltpu.PrefetchScalarGridSpec(
            num_scalar_prefetch=1,
            grid=(heads, 4),
            in_specs=[
                pl.BlockSpec((tile, HD), lambda h, i, p: (i, 3 * h)),
                whole(1),
                whole(2),
                pl.BlockSpec((tile, 1), lambda h, i, p: (i, 0)),
                pl.BlockSpec((1, length), lambda h, i, p: (0, 0)),
            ],
            out_specs=[
                pl.BlockSpec((tile, HD), lambda h, i, p: (i, h)),
                pl.BlockSpec((1, tile, 1), lambda h, i, p: (h, i, 0)),
            ],
        ),
        out_shape=[
            jax.ShapeDtypeStruct((length, heads * HD), BF),
            jax.ShapeDtypeStruct((heads, length, 1), F32),
        ],
        compiler_params=pltpu.CompilerParams(vmem_limit_bytes=32 << 20),
        cost_estimate=SMALL,
        name="attend",
    )(prefix, qkv, qkv, qkv, spots[:, None], spots[None, :])


def attend_back_kernel(
    prefix_ref, q_ref, k_ref, v_ref, g_ref, log_ref, rows_ref, keys_ref, keep_ref, up_ref,
    down_ref, o_ref, dk_ref, dv_ref,
):
    length = q_ref.shape[0]
    tile = length // 4
    scale = HD**-0.5
    for i in range(4):
        at = pl.ds(i * tile, tile)
        q, g = q_ref[at, :], g_ref[at, :]
        scores = visible_scores(q, k_ref[...], rows_ref[at, :], keys_ref[...], prefix_ref[0])
        probs = jnp.exp(scores - log_ref[0, at, :])
        grad_probs = lax.dot_general(
            g, v_ref[...], (((1,), (1,)), ((), ())), preferred_element_type=F32
        )
        dots = jnp.sum(probs * grad_probs, axis=-1, keepdims=True)
        grad_scores = (probs * (grad_probs - dots)).astype(BF)
        dq = jnp.dot(grad_scores, k_ref[...], preferred_element_type=F32) * scale
        o_ref[at, :HD] = turned(
            dq, keep_ref[at, :], up_ref[at, :], down_ref[at, :], -1.0
        ).astype(BF)
        dk = contract(grad_scores, q, 0, 0)
        dv = contract(probs.astype(BF), g, 0, 0)
        if i == 0:
            dk_ref[...] = dk
            dv_ref[...] = dv
        else:
            dk_ref[...] += dk
            dv_ref[...] += dv
    o_ref[:, HD : 2 * HD] = turned(
        dk_ref[...] * scale, keep_ref[...], up_ref[...], down_ref[...], -1.0
    ).astype(BF)
    o_ref[:, 2 * HD :] = dv_ref[...].astype(BF)


def attend_back(qkv, grad_context, log_total, prefix, spots, table):
    length = qkv.shape[0]
    heads = qkv.shape[1] // (3 * HD)
    part = lambda n: pl.BlockSpec((length, HD), lambda h, p: (0, 3 * h + n))
    return pl.pallas_call(
        attend_back_kernel,
        grid_spec=pltpu.PrefetchScalarGridSpec(
            num_scalar_prefetch=1,
            grid=(heads,),
            in_specs=[
                part(0),
                part(1),
                part(2),
                pl.BlockSpec((length, HD), lambda h, p: (0, h)),
                pl.BlockSpec((1, length, 1), lambda h, p: (h, 0, 0)),
                pl.BlockSpec((length, 1), lambda h, p: (0, 0)),
                pl.BlockSpec((1, length), lambda h, p: (0, 0)),
            ]
            + [pl.BlockSpec((length, 128), lambda h, p, k=k: (0, k)) for k in range(3)],
            out_specs=pl.BlockSpec((length, 3 * HD), lambda h, p: (0, h)),
            scratch_shapes=[pltpu.VMEM((length, HD), F32), pltpu.VMEM((length, HD), F32)],
        ),
        out_shape=jax.ShapeDtypeStruct((length, heads * 3 * HD), BF),
        compiler_params=pltpu.CompilerParams(vmem_limit_bytes=48 << 20),
        cost_estimate=SMALL,
        name="attend_back",
    )(prefix, qkv, qkv, qkv, grad_context, log_total, spots[:, None], spots[None, :], table, table, table)


def place_kernel(quarter_ref, *refs):
    pieces, out_ref = refs[-5:-1], refs[-1]
    for index, piece in enumerate(pieces):

        @pl.when(pl.program_id(0) == index)
        def _(piece=piece):
            out_ref[...] = piece[...].astype(F32)


def place_quarters(whole, near, far, shape, axis, offset, quarter):
    rows, columns = near.shape[0] // 2, near.shape[1]
    if axis == 0:
        each, first_row = shape[0] // 4 // rows, offset // rows
        spot = lambda k, q: ((q[0] ^ k) * each + first_row, 0)
    else:
        spot = lambda k, q: (offset // rows, q[0] ^ k)
    first = whole is None
    operands = ([] if first else [whole]) + [near, far, near, far]
    return pl.pallas_call(
        place_kernel,
        grid_spec=pltpu.PrefetchScalarGridSpec(
            num_scalar_prefetch=1,
            grid=(4,),
            in_specs=([] if first else [pl.BlockSpec(memory_space=pl.ANY)])
            + [pl.BlockSpec((rows, columns), lambda k, q, h=h: (h, 0)) for h in (0, 0, 1, 1)],
            out_specs=pl.BlockSpec((rows, columns), spot),
        ),
        out_shape=jax.ShapeDtypeStruct(shape, F32),
        input_output_aliases={} if first else {1: 0},
        compiler_params=pltpu.CompilerParams(vmem_limit_bytes=24 << 20),
        cost_estimate=SMALL,
        name="place_quarters",
    )(quarter.reshape(1), *operands)


def norms_kernel(count, *refs):
    gains, blocks, (attn_ref, mlp_ref) = refs[:4], refs[4 : 4 + count], refs[-2:]
    for index, block in enumerate(blocks):

        @pl.when(pl.program_id(0) == index)
        def _(block=block):
            features = block[...].astype(F32)
            average = jnp.mean(features, axis=-1, keepdims=True)
            centered = features - average
            spread = jnp.mean(centered * centered, axis=-1, keepdims=True)
            xhat = centered * lax.rsqrt(spread + EPSILON)
            gain_a, shift_a, gain_m, shift_m = (ref[...].astype(F32) for ref in gains)
            attn_ref[...] = (xhat * gain_a + shift_a).astype(BF)
            mlp_ref[...] = (xhat * gain_m + shift_m).astype(BF)


def both_norms(blocks, gains, total=None, into=()):
    count = len(blocks)
    total = total or count
    skip = total - count if into else 0
    rows, width = blocks[0].shape
    shape = jax.ShapeDtypeStruct((total * rows, width), BF)
    return pl.pallas_call(
        functools.partial(norms_kernel, count),
        grid=(count,),
        in_specs=[pl.BlockSpec((1, width), lambda i: (0, 0))] * 4
        + [pl.BlockSpec((rows, width), lambda i: (0, 0))] * count
        + [pl.BlockSpec(memory_space=pl.ANY)] * len(into),
        out_specs=[pl.BlockSpec((rows, width), lambda i: (i + skip, 0))] * 2,
        out_shape=[shape, shape],
        input_output_aliases={4 + count: 0, 5 + count: 1} if into else {},
        compiler_params=pltpu.CompilerParams(vmem_limit_bytes=48 << 20),
        cost_estimate=SMALL,
        name="both_norms",
    )(*gains, *blocks, *into)


def outer_kernel(lefts, pieces, outs, _, *refs):
    left_refs, rights = refs[:lefts], refs[lefts : -2 - outs]
    out_refs, (left_ref, joined_ref) = refs[-2 - outs : -2], refs[-2:]

    @pl.when(pl.program_id(0) == 0)
    def _():
        for ref, (row, column) in zip(left_refs, pieces):
            count, width = ref.shape
            step = min(count, 256)
            for start in range(0, count, step):
                left_ref[pl.ds(row, width), pl.ds(column + start, step)] = ref[
                    pl.ds(start, step), :
                ].T

    column = 0
    for ref in rights:
        joined_ref[pl.ds(column, ref.shape[0]), :] = ref[...]
        column += ref.shape[0]
    total = jnp.dot(left_ref[...], joined_ref[...], preferred_element_type=F32).astype(BF)
    row = 0
    for ref in out_refs:
        ref[...] = total[row : row + ref.shape[0], :]
        row += ref.shape[0]


def outer_blocks(lefts, rights, sizes, quarter):
    width = rights[0].shape[1]
    tokens = sum(r.shape[0] for r in rights)
    left = sum(sizes)
    tile = 512
    specs = [
        pl.BlockSpec((a.shape[0], taken), lambda j, q, m=times, o=offset: (0, q[0] * m + o))
        for a, taken, times, offset, _, _ in lefts
    ]
    pieces = [(row, token) for *_, row, token in lefts]
    return pl.pallas_call(
        functools.partial(outer_kernel, len(lefts), pieces, len(sizes)),
        grid_spec=pltpu.PrefetchScalarGridSpec(
            num_scalar_prefetch=1,
            grid=(width // tile,),
            in_specs=specs
            + [pl.BlockSpec((r.shape[0], tile), lambda j, q: (0, j)) for r in rights],
            out_specs=[pl.BlockSpec((size, tile), lambda j, q: (0, j)) for size in sizes],
            scratch_shapes=[pltpu.VMEM((left, tokens), BF), pltpu.VMEM((tokens, tile), BF)],
        ),
        out_shape=[jax.ShapeDtypeStruct((size, width), BF) for size in sizes],
        compiler_params=pltpu.CompilerParams(vmem_limit_bytes=56 << 20),
        cost_estimate=SMALL,
        name="outer_blocks",
    )(quarter.reshape(1), *[a for a, *_ in lefts], *rights)


def back_kernel(weight_ref, slope_ref, *refs):
    blocks, o_ref = refs[:-1], refs[-1]
    for index, block in enumerate(blocks):

        @pl.when(pl.program_id(0) == index)
        def _(block=block):
            o_ref[...] = (contract(block[...], weight_ref[...], 1, 1) * slope_ref[...]).astype(BF)


def back_blocks(blocks, weight, slope):
    rows, width = blocks[0].shape
    units = weight.shape[0]
    count = len(blocks)
    return pl.pallas_call(
        back_kernel,
        grid=(count,),
        in_specs=[
            pl.BlockSpec((units, width), lambda i: (0, 0)),
            pl.BlockSpec((rows, units), lambda i: (i, 0)),
        ]
        + [pl.BlockSpec((rows, width), lambda i: (0, 0))] * count,
        out_specs=pl.BlockSpec((rows, units), lambda i: (i, 0)),
        out_shape=jax.ShapeDtypeStruct((count * rows, units), BF),
        compiler_params=pltpu.CompilerParams(vmem_limit_bytes=56 << 20),
        cost_estimate=SMALL,
        name="back_blocks",
    )(weight, slope, *blocks)


def on_device(
    hidden,
    teacher,
    valid_mask,
    prefix_len,
    ln1_gain,
    ln1_bias,
    ln2_gain,
    ln2_bias,
    qkv_weight,
    qkv_bias,
    out_weight,
    out_bias,
    fc1_weight,
    fc1_bias,
    fc2_weight,
    fc2_bias,
):
    rows = hidden.shape[0]
    dp = lax.axis_size("dp")
    tp = lax.axis_size("tensor")
    ways = tp // 2
    squares = dp // 4
    total_tokens = dp * tp * rows
    heads = qkv_weight.shape[1] // (3 * HD)
    dp_index = lax.axis_index("dp")
    tp_index = lax.axis_index("tensor")
    core, y = tp_index % 2, tp_index // 2
    quarter = dp_index % 4

    def to_core(v):
        return lax.ppermute(v, "tensor", [(t, t ^ 1) for t in range(tp)])

    def from_y(v, step):
        pairs = [(t, ((t // 2 - step) % ways) * 2 + t % 2) for t in range(tp)]
        return lax.ppermute(v, "tensor", pairs)

    def to_y(v, step):
        pairs = [(t, ((t // 2 + step) % ways) * 2 + t % 2) for t in range(tp)]
        return lax.ppermute(v, "tensor", pairs)

    def flip(v, mask):
        return lax.ppermute(v, "dp", [(d, d ^ mask) for d in range(dp)])

    block_ids = [
        ((y + step) % ways) * 2 + (core if mate == 0 else 1 - core)
        for step in range(ways)
        for mate in (0, 1)
    ]

    def gather_near(own):
        over_y = [from_y(own, step) for step in range(1, ways)]
        parts = []
        for block in [own] + over_y:
            parts += [block, to_core(block)]
        return parts, over_y

    def first_far(own):
        return [flip(own, 1), flip(own, 2)]

    def second_far(first, over_y):
        corner = flip(first[1], 1)
        beside = [from_y(first[0], step) for step in range(1, ways)]
        across = [flip(block, 2) for block in over_y]
        return corner, beside, across

    def last_far(second):
        half = rows // 2
        return [(flip(v[:half], 1), flip(u[half:], 2)) for u, v in zip(second[1], second[2])]

    def meet(*trees):
        leaves, shape = jax.tree.flatten(trees)
        return jax.tree.unflatten(shape, lax.optimization_barrier(tuple(leaves)))

    def quarter_of(v, axis, index):
        size = v.shape[axis] // 4
        return lax.dynamic_slice_in_dim(v, index * size, size, axis)

    def swap_quarters(v):
        return [flip(quarter_of(v, 1, quarter ^ mask), mask) for mask in (1, 2, 3)]

    gain_attn = ln1_gain.astype(F32)
    shift_attn = ln1_bias.astype(F32)
    gain_mlp = ln2_gain.astype(F32)
    shift_mlp = ln2_bias.astype(F32)
    gains = [v[None, :] for v in (ln1_gain, ln1_bias, ln2_gain, ln2_bias)]
    close = 2 * rows

    def units(normed):
        return jnp.dot(normed, fc1_weight, preferred_element_type=F32) + fc1_bias.astype(F32)

    near_blocks, hidden_y = gather_near(hidden)
    first = first_far(hidden)
    norm_attn_own, norm_mlp_own = both_norms(near_blocks[:2], gains)
    mask_f = after(valid_mask, norm_mlp_own).astype(F32)
    count = jnp.full((8, 128), jnp.sum(mask_f), F32)
    count = count + to_core(count)
    counted = flip(count, 1)
    pre_own = units(norm_mlp_own)
    active_own = exact_gelu(pre_own)[0].astype(BF)
    table = jnp.concatenate(
        [
            lax.dynamic_slice_in_dim(jnp.asarray(rotary_table(LEN)), b * rows, rows, 0)
            for b in block_ids
        ],
        axis=0,
    )
    spots = jnp.concatenate([b * rows + jnp.arange(rows, dtype=jnp.int32) for b in block_ids])
    active_own, table = after(active_own, table), after(table, active_own)
    qkv_own = project_qkv(norm_attn_own, qkv_weight, qkv_bias, table, LEN)
    active_own, qkv_own, counted, first, hidden_y = meet(
        active_own, qkv_own, counted, first, hidden_y
    )
    count = count + counted

    near_blocks = near_blocks[:2]
    for block in hidden_y:
        near_blocks += [block, to_core(block)]
    second = second_far(first, hidden_y)
    first_mates = [to_core(block) for block in first]
    counted = flip(count, 2)
    norm_attn_rest, norm_mlp_rest = both_norms(near_blocks[2:], gains)
    qkv_low = project_qkv(norm_attn_rest, qkv_weight, qkv_bias, table, LEN, qkv_own)
    context, log_total = attend(qkv_low, prefix_len, spots)
    norm_mlp_rest = after(norm_mlp_rest, context)
    context_far = swap_quarters(context)
    pre_rest = units(norm_mlp_rest)
    active_rest = exact_gelu(pre_rest)[0].astype(BF)
    active_rest, context, counted, second, context_far, first_mates = meet(
        active_rest, context, counted, second, context_far, first_mates
    )
    count = count + counted

    def branch_rows(context_rows, active_rows):
        return jnp.dot(context_rows, out_weight, preferred_element_type=F32) + jnp.dot(
            active_rows, fc2_weight, preferred_element_type=F32
        )

    def core_total(part):
        blocks = part.reshape(-1, 2, rows, D)
        return blocks[:, 0] + to_core(blocks[:, 1].astype(BF)).astype(F32)

    corner, beside, across = second
    second_mates = [to_core(block) for block in [corner] + beside + across]
    counted = jnp.zeros_like(count)
    bit = 2
    while bit < tp:
        counted = lax.ppermute(count, "tensor", [(t, t ^ bit) for t in range(tp)])
        bit *= 2
        if bit < tp:
            count = count + counted
    part_rest = branch_rows(context[close:], active_rest).reshape(-1, 2, rows, D)
    mates_rest = to_core(part_rest[:, 1].astype(BF))
    part_own = branch_rows(context[:close], after(active_own, part_rest)).reshape(2, rows, D)
    part_own, mates_rest, counted, second_mates = meet(
        part_own, mates_rest, counted, second_mates
    )
    count = count + counted

    sums = part_rest[:, 0] + mates_rest.astype(F32)
    came = [to_y(sums[step - 1].astype(BF), step) for step in range(1, ways)]
    mates_own = to_core(part_own[1].astype(BF))
    counted = flip(count, 4) if dp > 4 else jnp.zeros_like(count)
    last = last_far(second)
    ahead = [first[0]] + beside + [first[1]] + across + [corner]
    mates = (
        [first_mates[0]]
        + second_mates[1:ways]
        + [first_mates[1]]
        + second_mates[ways:]
        + [second_mates[0]]
    )
    far_blocks = [block for pair in zip(ahead, mates) for block in pair]
    norms_far = both_norms(far_blocks, gains, 6 * ways)
    last, norms_far = meet(last, norms_far)
    last = [jnp.concatenate(pair, axis=0) for pair in last]
    far_blocks = [block for v in last for block in (v, to_core(v))]
    norm_attn_far, norm_mlp_far = both_norms(far_blocks, gains, 6 * ways, norms_far)
    came, mates_own, counted, norm_mlp_far = meet(came, mates_own, counted, norm_mlp_far)
    count = count + counted
    mask = 8
    while mask < dp:
        count = count + flip(count, mask)
        mask *= 2
    branch = part_own[0] + mates_own.astype(F32)
    for got in came:
        branch = branch + got.astype(F32)
    output_f = hidden.astype(F32) + branch + out_bias.astype(F32) + fc2_bias.astype(F32)
    mismatch = output_f - teacher.astype(F32)
    error_part = jnp.sum(mask_f[:, None] * mismatch * mismatch)
    grad_out = mask_f[:, None] * mismatch * (2.0 * total_tokens / count[0, 0])
    grad_low = grad_out.astype(BF)
    grad_out, grad_low, norm_mlp_far = meet(grad_out, grad_low, norm_mlp_far)

    grad_y = [from_y(grad_low, step) for step in range(1, ways)]
    grad_first = first_far(grad_low)
    grad_mate = to_core(grad_low)
    fc1_quarter = quarter_of(fc1_weight, 1, quarter)
    fc2_quarter = quarter_of(after(fc2_weight, norm_mlp_far), 0, quarter)
    context_quarter = quarter_of(after(context, norm_mlp_far), 1, quarter)
    pre_far = jnp.dot(norm_mlp_far, fc1_quarter, preferred_element_type=F32) + quarter_of(
        fc1_bias, 0, quarter
    ).astype(F32)
    active_far, slope_far = exact_gelu(pre_far)
    active_far = active_far.astype(BF)
    grad_y, grad_first, active_far, grad_mate, fc2_quarter, context_quarter = meet(
        grad_y, grad_first, active_far, grad_mate, fc2_quarter, context_quarter
    )

    grad_second = second_far(grad_first, grad_y)
    grad_blocks = [grad_low, grad_mate]
    for block in grad_y:
        grad_blocks += [block, to_core(block)]
    grad_near = jnp.concatenate(grad_blocks, axis=0)
    hidden_pre = jnp.concatenate([pre_own, pre_rest], axis=0)
    grad_inner = (contract(grad_near, fc2_weight, 1, 1) * exact_gelu(hidden_pre)[1]).astype(BF)
    grad_context = contract(grad_near, out_weight, 1, 1).astype(BF)
    grad_inner, grad_context, grad_near, grad_second = meet(
        grad_inner, grad_context, grad_near, grad_second
    )

    grad_last = last_far(grad_second)
    corner, beside, across = grad_second
    ahead = [grad_first[0]] + beside + [grad_first[1]] + across + [corner]
    mates = [to_core(block) for block in ahead]
    grad_qkv = attend_back(qkv_low, grad_context, log_total, prefix_len, spots, table)
    grad_qkv, grad_last, mates = meet(grad_qkv, grad_last, mates)

    grad_last = [jnp.concatenate(pair, axis=0) for pair in grad_last]
    ahead += grad_last
    mates += [to_core(block) for block in grad_last]
    grad_far = [block for pair in zip(ahead, mates) for block in pair]
    bias_part = jnp.sum(grad_out, axis=0)

    queue = []
    due = {}
    clock, launched = [0], [0]
    results = {}
    token = [grad_near]

    def gate(v):
        return after(v, token[0])

    def flipped(v, mask):
        return v, lambda value: flip(value, mask)

    def travel(low, name, wait):
        mask = 4
        while mask < dp:
            (got,) = yield [flipped(low, mask)], wait
            low = (low.astype(F32) + got.astype(F32)).astype(BF)
            mask, wait = mask * 2, 1
        (across,) = yield [flipped(low, 2)], 1
        near = jnp.concatenate([low, across], axis=0)
        (far,) = yield [flipped(near, 1)], 1
        results.setdefault(name, []).append((near, far))

    def swap_walk(v, into):
        got = yield [flipped(quarter_of(v, 1, quarter ^ m), m) for m in (1, 2)], 1
        into.extend(got)
        got = yield [flipped(quarter_of(v, 1, quarter ^ 3), 3)], 1
        into.extend(got)

    def last_walk(kept, mates, parts, others, into):
        (got,) = yield [(mates, to_core)], 1
        sums = kept + got.astype(F32)
        total = sums[0]
        for step in range(1, ways):
            (got,) = yield [(sums[step].astype(BF), lambda v, s=step: to_y(v, s))], 1
            total = total + got.astype(F32)
        into["input"] = grad_out + total
        bit = 1
        while bit < tp:
            pairs = [(t, t ^ bit) for t in range(tp)]
            (got,) = yield [(parts, lambda v, p=pairs: lax.ppermute(v, "tensor", p))], 1
            parts = parts + got
            bit *= 2
        parts = jnp.concatenate([parts, others])
        bit = 1
        while bit < dp:
            (got,) = yield [flipped(parts, bit)], 1
            parts = parts + got
            bit *= 2
        into["small"] = parts

    def walk(walker):
        asked = next(walker)
        start(walker, asked, clock[0] - 1)

    def start(walker, asked, now):
        sends, wait = asked
        due.setdefault(now + wait, []).append((walker, [move(v) for v, move in sends]))

    parts_of = {}

    def cut(part, shares):
        unit = part.shape[0] // 16
        edges = [unit * sum(shares[:i]) for i in range(len(shares) + 1)]
        return [lax.slice_in_dim(part, a, b, axis=0) for a, b in zip(edges, edges[1:])]

    def enqueue(name, *units):
        before, _ = parts_of.get(name, (0, 0))
        parts_of[name] = (before + sum(u.shape[0] for u in units), units[0].shape[1])
        queue.extend((unit, name) for unit in units)

    def turn(*others):
        now = clock[0]
        clock[0] = now + 1
        arrived = due.pop(now, [])
        values = [got for _, gots in arrived for got in gots]
        fresh = []
        while queue and launched[0] <= now + 1:
            fresh.append(queue.pop(0) + (max(launched[0] - now, 0) + 1,))
            launched[0] += 1
        tied = list(
            lax.optimization_barrier(tuple(values) + tuple(f[0] for f in fresh) + others)
        )
        token[0] = tied[0]
        asked = []
        for walker, gots in arrived:
            gots = [tied.pop(0) for _ in gots]
            try:
                asked.append((walker, walker.send(gots)))
            except StopIteration:
                pass
        for _, name, wait in fresh:
            walker = travel(tied.pop(0), name, wait)
            asked.append((walker, next(walker)))
        for walker, request in asked:
            start(walker, request, now)
        return tied

    def place_one(whole, near, far, shape, axis, offset):
        rows_here, columns = near.shape[0] // 2, near.shape[1]
        if columns % 128 == 0:
            return place_quarters(whole, near, far, shape, axis, offset, quarter)
        if whole is None:
            whole = jnp.zeros(shape, F32)
        pieces = (near[:rows_here], far[:rows_here], near[rows_here:], far[rows_here:])
        for index, piece in enumerate(pieces):
            spot = quarter ^ index
            start = (
                (spot * (shape[0] // 4) + offset, 0) if axis == 0 else (offset, spot * columns)
            )
            whole = lax.dynamic_update_slice(whole, piece.astype(F32), start)
        return whole

    half = active_far.shape[1] // 2
    rights = [grad_near] + grad_far

    def hidden_lefts(part):
        return [
            (active_own, half, 2, part, 0, 0),
            (active_rest, half, 2, part, 0, close),
            (active_far, half, 0, part, 0, LEN),
        ]

    chunk = half // 2
    kept_columns = context.shape[1] // 4
    enqueue("fc2", *outer_blocks(hidden_lefts(0), rights, [chunk] * 2, quarter))
    turn()
    grad_qkv_far = []
    walk(swap_walk(gate(grad_qkv), grad_qkv_far))
    lefts = hidden_lefts(1)
    for index, piece in enumerate([context_quarter] + context_far):
        lefts.append((piece, kept_columns, 0, 0, half, index * LEN))
    *parts, out_part = outer_blocks(
        lefts, [gate(grad_near)] + grad_far, [chunk] * 2 + [kept_columns], quarter
    )
    enqueue("fc2", *parts)
    enqueue("out", out_part)
    turn()
    grad_inner_far = back_blocks([gate(grad_far[0])] + grad_far[1:], fc2_quarter, slope_far)
    (grad_inner_far,) = turn(grad_inner_far)
    inner_quarter = gate(quarter_of(grad_inner, 1, quarter))
    fc1_part = (
        contract(norm_mlp_own, inner_quarter[:close], 0, 0)
        + contract(norm_mlp_rest, inner_quarter[close:], 0, 0)
        + contract(norm_mlp_far, grad_inner_far, 0, 0)
    )
    (fc1_part,) = turn(fc1_part.astype(BF))
    enqueue("fc1", *cut(fc1_part, [4, 4, 4, 4]))
    grad_norm_attn = contract(gate(grad_qkv), qkv_weight, 1, 1)
    (grad_norm_attn,) = turn(grad_norm_attn)
    grad_norm_mlp = contract(gate(grad_inner), fc1_weight, 1, 1)
    (grad_norm_mlp,) = turn(grad_norm_mlp)

    near_blocks = lax.optimization_barrier((token[0], *near_blocks))[1:]
    features = jnp.concatenate(near_blocks, axis=0).astype(F32)
    centered = features - jnp.mean(features, axis=-1, keepdims=True)
    inverse = lax.rsqrt(jnp.mean(centered * centered, axis=-1, keepdims=True) + EPSILON)
    xhat = centered * inverse
    gained = grad_norm_attn * gain_attn + grad_norm_mlp * gain_mlp
    lift = jnp.mean(gained, axis=-1, keepdims=True)
    pull = jnp.mean(gained * xhat, axis=-1, keepdims=True)
    tensor_parts = jnp.stack(
        [
            jnp.sum(grad_norm_attn * xhat, axis=0),
            jnp.sum(grad_norm_attn, axis=0),
            jnp.sum(grad_norm_mlp * xhat, axis=0),
            jnp.sum(grad_norm_mlp, axis=0),
            bias_part,
            jnp.full((D,), error_part, F32),
        ]
    ).reshape(-1)
    tensor_parts, lift, pull = turn(tensor_parts, lift, pull)
    grad_hidden = inverse * (gained - lift - xhat * pull)
    blocks = grad_hidden.reshape(ways, 2, rows, D)
    fc1_bias_part = jnp.sum(gate(grad_inner), axis=0, dtype=F32)
    qkv_bias_part = jnp.sum(gate(grad_qkv), axis=0, dtype=F32)
    kept, mates, fc1_bias_part, qkv_bias_part = turn(
        blocks[:, 0], blocks[:, 1].astype(BF), fc1_bias_part, qkv_bias_part
    )
    outcome = {}
    others = jnp.concatenate([fc1_bias_part, qkv_bias_part])
    walk(last_walk(kept, mates, tensor_parts, others, outcome))
    qkv_quarter = gate(quarter_of(grad_qkv, 1, quarter))
    qkv_part = (
        contract(norm_attn_own, qkv_quarter[:close], 0, 0)
        + contract(norm_attn_rest, qkv_quarter[close:], 0, 0)
        + contract(norm_attn_far, jnp.concatenate(grad_qkv_far, axis=0), 0, 0)
    )
    (qkv_part,) = turn(qkv_part.astype(BF))
    enqueue("qkv", *cut(qkv_part, [4, 4, 4, 2, 1, 1]))
    axes = {"fc2": 0, "out": 0, "fc1": 1, "qkv": 1}
    placed = {name: (None, 0, 0) for name in axes}

    def place(name):
        whole, done, offset = placed[name]
        pieces = results[name][done]
        lengths, columns = parts_of[name]
        shape = (4 * lengths, columns) if axes[name] == 0 else (lengths, 4 * columns)
        whole = place_one(whole, *pieces, shape, axes[name], offset)
        placed[name] = (whole, done + 1, offset + pieces[0].shape[0] // 2)

    while queue or due:
        ready = []
        for name in axes:
            if len(ready) < 2 and len(results.get(name, [])) > placed[name][1]:
                place(name)
                ready.append(name)
        wholes = turn(*[placed[name][0] for name in ready])
        for name, whole in zip(ready, wholes):
            placed[name] = (whole,) + placed[name][1:]
    for name in axes:
        while len(results[name]) > placed[name][1]:
            place(name)
    input_grad = outcome["input"]
    small = outcome["small"]
    vectors = small[: 6 * D].reshape(6, D)
    fc1_bias_grad = small[6 * D : 6 * D + fc1_bias_part.shape[0]]
    qkv_bias_grad = small[6 * D + fc1_bias_part.shape[0] :]
    loss_value = vectors[5, 0] / (count[0, 0] * D)
    fc2_weight_grad, out_weight_grad = placed["fc2"][0], placed["out"][0]
    fc1_weight_grad, qkv_weight_grad = placed["fc1"][0], placed["qkv"][0]
    return (
        output_f.astype(BF),
        loss_value,
        input_grad,
        vectors[0],
        vectors[1],
        vectors[2],
        vectors[3],
        qkv_weight_grad,
        qkv_bias_grad,
        out_weight_grad,
        vectors[4],
        fc1_weight_grad,
        fc1_bias_grad,
        fc2_weight_grad,
        vectors[4],
    )


def solution(mesh):
    tokens = P(("dp", "tensor"), None)
    columns, lanes, down, whole = P(None, "tensor"), P("tensor"), P("tensor", None), P()
    in_specs = (
        tokens,
        tokens,
        P(("dp", "tensor")),
        P("dp"),
        whole,
        whole,
        whole,
        whole,
        columns,
        lanes,
        down,
        whole,
        columns,
        lanes,
        down,
        whole,
    )
    out_specs = (
        tokens,
        whole,
        tokens,
        whole,
        whole,
        whole,
        whole,
        columns,
        lanes,
        down,
        whole,
        columns,
        lanes,
        down,
        whole,
    )
    return jax.shard_map(
        on_device, mesh=mesh, in_specs=in_specs, out_specs=out_specs, check_vma=False
    )
```

```python
import functools

import jax
import jax.numpy as jnp
import numpy as np
from jax import lax
from jax.experimental import pallas as pl
from jax.experimental.pallas import tpu as pltpu
from jax.sharding import PartitionSpec as P

D = 2048
HD = 256
ROT = 64
LEN = 1024
EPSILON = 1e-05
BF = jnp.bfloat16
F32 = jnp.float32
VMEM = 60 << 20
SMALL = pl.CostEstimate(flops=1 << 20, bytes_accessed=1 << 16, transcendentals=0)


def rotary_table(length):
    half = ROT // 2
    frequency = (10000.0 ** (-2.0 * np.arange(half, dtype=np.float32) / ROT)).astype(np.float32)
    angles = np.arange(length, dtype=np.float32)[:, None] * frequency[None, :]
    cosine, sine = np.cos(angles), np.sin(angles)
    table = np.zeros((length, 3 * 128), np.float32)
    table[:, ROT:128] = 1.0
    table[:, :half] = table[:, half:ROT] = cosine
    table[:, 128 : 128 + half] = -sine
    table[:, 256 + half : 256 + ROT] = sine
    return table


def contract(left_side, right_side, left_dim, right_dim):
    return lax.dot_general(
        left_side,
        right_side,
        (((left_dim,), (right_dim,)), ((), ())),
        preferred_element_type=F32,
    )


def exact_gelu(pre_act):
    below = 0.5 + 0.5 * lax.erf(pre_act * 0.5**0.5)
    density = jnp.exp(-0.5 * pre_act * pre_act) * (2.0 * jnp.pi) ** -0.5
    return pre_act * below, below + pre_act * density


def after(value, *earlier):
    return lax.optimization_barrier((value,) + earlier)[0]


def turned(block, keep, up, down, sign):
    head = block[:, :128]
    half = ROT // 2
    moved = head * keep + sign * (
        pltpu.roll(head, 128 - half, 1) * up + pltpu.roll(head, half, 1) * down
    )
    return jnp.concatenate([moved, block[:, 128:]], axis=1)


def qkv_kernel(x_ref, w_ref, b_ref, keep_ref, up_ref, down_ref, *refs):
    o_ref = refs[-1]
    kind = pl.program_id(0) % 3
    rows = x_ref.shape[0]
    tile = min(rows, 512)

    def project(at):
        return (
            jnp.dot(x_ref[at, :], w_ref[...], preferred_element_type=F32)
            + b_ref[...].astype(F32)
        )

    for start in range(0, rows, tile):
        at = pl.ds(start, min(tile, rows - start))

        @pl.when(kind == 2)
        def _(at=at):
            o_ref[at, :] = project(at).astype(BF)

        @pl.when(kind != 2)
        def _(at=at):
            o_ref[at, :] = turned(
                project(at), keep_ref[at, :], up_ref[at, :], down_ref[at, :], 1.0
            ).astype(BF)


def project_qkv(normed, weight, bias, table, length, whole=None):
    rows, width = normed.shape
    columns = weight.shape[1]
    part = 0 if whole is None else 1
    if part and rows * 2 != length:
        rest = project_qkv(normed, weight, bias, table[length - rows :], rows)
        return jnp.concatenate([whole[: length - rows], rest], axis=0)
    return pl.pallas_call(
        qkv_kernel,
        grid=(columns // HD,),
        in_specs=[
            pl.BlockSpec((rows, width), lambda j: (0, 0)),
            pl.BlockSpec((width, HD), lambda j: (0, j)),
            pl.BlockSpec((1, HD), lambda j: (0, j)),
        ]
        + [pl.BlockSpec((rows, 128), lambda j, k=k: (part, k)) for k in range(3)]
        + [pl.BlockSpec(memory_space=pl.ANY)] * part,
        out_specs=pl.BlockSpec((rows, HD), lambda j: (part, j)),
        out_shape=jax.ShapeDtypeStruct((length, columns), BF),
        input_output_aliases={6: 0} if part else {},
        compiler_params=pltpu.CompilerParams(vmem_limit_bytes=VMEM),
        cost_estimate=SMALL,
        name="qkv_rotary",
    )(normed, weight, bias[None, :], table, table, table, *([whole] if part else []))


def visible_scores(queries, keys, row_spots, key_spots, prefix):
    scores = lax.dot_general(
        queries, keys, (((1,), (1,)), ((), ())), preferred_element_type=F32
    ) * (HD**-0.5)
    allowed = (key_spots <= row_spots) | (key_spots < prefix)
    return jnp.where(allowed, scores, -jnp.inf)


def attend_kernel(prefix_ref, q_ref, k_ref, v_ref, rows_ref, keys_ref, o_ref, log_ref):
    scores = visible_scores(
        q_ref[...], k_ref[...], rows_ref[...], keys_ref[...], prefix_ref[0]
    )
    top = jnp.max(scores, axis=-1, keepdims=True)
    weights = jnp.exp(scores - top)
    total = jnp.sum(weights, axis=-1, keepdims=True)
    probs = (weights * (1.0 / total)).astype(BF)
    o_ref[...] = jnp.dot(probs, v_ref[...], preferred_element_type=F32).astype(BF)
    log_ref[0] = top + jnp.log(total)


def attend(qkv, prefix, spots):
    length = qkv.shape[0]
    heads = qkv.shape[1] // (3 * HD)
    tile = length // 4
    whole = lambda part: pl.BlockSpec((length, HD), lambda h, i, p: (0, 3 * h + part))
    return pl.pallas_call(
        attend_kernel,
        grid_spec=pltpu.PrefetchScalarGridSpec(
            num_scalar_prefetch=1,
            grid=(heads, 4),
            in_specs=[
                pl.BlockSpec((tile, HD), lambda h, i, p: (i, 3 * h)),
                whole(1),
                whole(2),
                pl.BlockSpec((tile, 1), lambda h, i, p: (i, 0)),
                pl.BlockSpec((1, length), lambda h, i, p: (0, 0)),
            ],
            out_specs=[
                pl.BlockSpec((tile, HD), lambda h, i, p: (i, h)),
                pl.BlockSpec((1, tile, 1), lambda h, i, p: (h, i, 0)),
            ],
        ),
        out_shape=[
            jax.ShapeDtypeStruct((length, heads * HD), BF),
            jax.ShapeDtypeStruct((heads, length, 1), F32),
        ],
        compiler_params=pltpu.CompilerParams(vmem_limit_bytes=VMEM),
        cost_estimate=SMALL,
        name="attend",
    )(prefix, qkv, qkv, qkv, spots[:, None], spots[None, :])


def attend_back_kernel(
    prefix_ref, q_ref, k_ref, v_ref, g_ref, log_ref, rows_ref, keys_ref, keep_ref, up_ref,
    down_ref, o_ref, dk_ref, dv_ref,
):
    length = q_ref.shape[0]
    tile = length // 4
    scale = HD**-0.5
    for i in range(4):
        at = pl.ds(i * tile, tile)
        q, g = q_ref[at, :], g_ref[at, :]
        scores = visible_scores(q, k_ref[...], rows_ref[at, :], keys_ref[...], prefix_ref[0])
        probs = jnp.exp(scores - log_ref[0, at, :])
        grad_probs = lax.dot_general(
            g, v_ref[...], (((1,), (1,)), ((), ())), preferred_element_type=F32
        )
        dots = jnp.sum(probs * grad_probs, axis=-1, keepdims=True)
        grad_scores = (probs * (grad_probs - dots)).astype(BF)
        dq = jnp.dot(grad_scores, k_ref[...], preferred_element_type=F32) * scale
        o_ref[at, :HD] = turned(
            dq, keep_ref[at, :], up_ref[at, :], down_ref[at, :], -1.0
        ).astype(BF)
        dk = contract(grad_scores, q, 0, 0)
        dv = contract(probs.astype(BF), g, 0, 0)
        if i == 0:
            dk_ref[...] = dk
            dv_ref[...] = dv
        else:
            dk_ref[...] += dk
            dv_ref[...] += dv
    o_ref[:, HD : 2 * HD] = turned(
        dk_ref[...] * scale, keep_ref[...], up_ref[...], down_ref[...], -1.0
    ).astype(BF)
    o_ref[:, 2 * HD :] = dv_ref[...].astype(BF)


def attend_back(qkv, grad_context, log_total, prefix, spots, table):
    length = qkv.shape[0]
    heads = qkv.shape[1] // (3 * HD)
    part = lambda n: pl.BlockSpec((length, HD), lambda h, p: (0, 3 * h + n))
    return pl.pallas_call(
        attend_back_kernel,
        grid_spec=pltpu.PrefetchScalarGridSpec(
            num_scalar_prefetch=1,
            grid=(heads,),
            in_specs=[
                part(0),
                part(1),
                part(2),
                pl.BlockSpec((length, HD), lambda h, p: (0, h)),
                pl.BlockSpec((1, length, 1), lambda h, p: (h, 0, 0)),
                pl.BlockSpec((length, 1), lambda h, p: (0, 0)),
                pl.BlockSpec((1, length), lambda h, p: (0, 0)),
            ]
            + [pl.BlockSpec((length, 128), lambda h, p, k=k: (0, k)) for k in range(3)],
            out_specs=pl.BlockSpec((length, 3 * HD), lambda h, p: (0, h)),
            scratch_shapes=[pltpu.VMEM((length, HD), F32), pltpu.VMEM((length, HD), F32)],
        ),
        out_shape=jax.ShapeDtypeStruct((length, heads * 3 * HD), BF),
        compiler_params=pltpu.CompilerParams(vmem_limit_bytes=VMEM),
        cost_estimate=SMALL,
        name="attend_back",
    )(prefix, qkv, qkv, qkv, grad_context, log_total, spots[:, None], spots[None, :], table, table, table)


def place_kernel(quarter_ref, *refs):
    pieces, out_ref = refs[-5:-1], refs[-1]
    for index, piece in enumerate(pieces):

        @pl.when(pl.program_id(0) == index)
        def _(piece=piece):
            out_ref[...] = piece[...].astype(F32)


def place_quarters(whole, near, far, shape, axis, offset, quarter):
    rows, columns = near.shape[0] // 2, near.shape[1]
    if axis == 0:
        each, first_row = shape[0] // 4 // rows, offset // rows
        spot = lambda k, q: ((q[0] ^ k) * each + first_row, 0)
    else:
        spot = lambda k, q: (offset // rows, q[0] ^ k)
    first = whole is None
    operands = ([] if first else [whole]) + [near, far, near, far]
    return pl.pallas_call(
        place_kernel,
        grid_spec=pltpu.PrefetchScalarGridSpec(
            num_scalar_prefetch=1,
            grid=(4,),
            in_specs=([] if first else [pl.BlockSpec(memory_space=pl.ANY)])
            + [pl.BlockSpec((rows, columns), lambda k, q, h=h: (h, 0)) for h in (0, 0, 1, 1)],
            out_specs=pl.BlockSpec((rows, columns), spot),
        ),
        out_shape=jax.ShapeDtypeStruct(shape, F32),
        input_output_aliases={} if first else {1: 0},
        compiler_params=pltpu.CompilerParams(vmem_limit_bytes=VMEM),
        cost_estimate=SMALL,
        name="place_quarters",
    )(quarter.reshape(1), *operands)


def norms_kernel(count, *refs):
    gains, blocks, (attn_ref, mlp_ref) = refs[:4], refs[4 : 4 + count], refs[-2:]
    for index, block in enumerate(blocks):

        @pl.when(pl.program_id(0) == index)
        def _(block=block):
            features = block[...].astype(F32)
            average = jnp.mean(features, axis=-1, keepdims=True)
            centered = features - average
            spread = jnp.mean(centered * centered, axis=-1, keepdims=True)
            xhat = centered * lax.rsqrt(spread + EPSILON)
            gain_a, shift_a, gain_m, shift_m = (ref[...].astype(F32) for ref in gains)
            attn_ref[...] = (xhat * gain_a + shift_a).astype(BF)
            mlp_ref[...] = (xhat * gain_m + shift_m).astype(BF)


def both_norms(blocks, gains, total=None, into=()):
    count = len(blocks)
    total = total or count
    skip = total - count if into else 0
    rows, width = blocks[0].shape
    shape = jax.ShapeDtypeStruct((total * rows, width), BF)
    return pl.pallas_call(
        functools.partial(norms_kernel, count),
        grid=(count,),
        in_specs=[pl.BlockSpec((1, width), lambda i: (0, 0))] * 4
        + [pl.BlockSpec((rows, width), lambda i: (0, 0))] * count
        + [pl.BlockSpec(memory_space=pl.ANY)] * len(into),
        out_specs=[pl.BlockSpec((rows, width), lambda i: (i + skip, 0))] * 2,
        out_shape=[shape, shape],
        input_output_aliases={4 + count: 0, 5 + count: 1} if into else {},
        compiler_params=pltpu.CompilerParams(vmem_limit_bytes=VMEM),
        cost_estimate=SMALL,
        name="both_norms",
    )(*gains, *blocks, *into)


def outer_kernel(lefts, pieces, outs, _, *refs):
    left_refs, rights = refs[:lefts], refs[lefts : -2 - outs]
    out_refs, (left_ref, joined_ref) = refs[-2 - outs : -2], refs[-2:]

    @pl.when(pl.program_id(0) == 0)
    def _():
        for ref, (row, column) in zip(left_refs, pieces):
            count, width = ref.shape
            step = min(count, 256)
            for start in range(0, count, step):
                left_ref[pl.ds(row, width), pl.ds(column + start, step)] = ref[
                    pl.ds(start, step), :
                ].T

    column = 0
    for ref in rights:
        joined_ref[pl.ds(column, ref.shape[0]), :] = ref[...]
        column += ref.shape[0]
    total = jnp.dot(left_ref[...], joined_ref[...], preferred_element_type=F32).astype(BF)
    row = 0
    for ref in out_refs:
        ref[...] = total[row : row + ref.shape[0], :]
        row += ref.shape[0]


def outer_blocks(lefts, rights, sizes, quarter):
    width = rights[0].shape[1]
    tokens = sum(r.shape[0] for r in rights)
    left = sum(sizes)
    tile = 512
    specs = [
        pl.BlockSpec((a.shape[0], taken), lambda j, q, m=times, o=offset: (0, q[0] * m + o))
        for a, taken, times, offset, _, _ in lefts
    ]
    pieces = [(row, token) for *_, row, token in lefts]
    return pl.pallas_call(
        functools.partial(outer_kernel, len(lefts), pieces, len(sizes)),
        grid_spec=pltpu.PrefetchScalarGridSpec(
            num_scalar_prefetch=1,
            grid=(width // tile,),
            in_specs=specs
            + [pl.BlockSpec((r.shape[0], tile), lambda j, q: (0, j)) for r in rights],
            out_specs=[pl.BlockSpec((size, tile), lambda j, q: (0, j)) for size in sizes],
            scratch_shapes=[pltpu.VMEM((left, tokens), BF), pltpu.VMEM((tokens, tile), BF)],
        ),
        out_shape=[jax.ShapeDtypeStruct((size, width), BF) for size in sizes],
        compiler_params=pltpu.CompilerParams(vmem_limit_bytes=VMEM),
        cost_estimate=SMALL,
        name="outer_blocks",
    )(quarter.reshape(1), *[a for a, *_ in lefts], *rights)


def back_kernel(weight_ref, slope_ref, *refs):
    blocks, o_ref = refs[:-1], refs[-1]
    for index, block in enumerate(blocks):

        @pl.when(pl.program_id(0) == index)
        def _(block=block):
            o_ref[...] = (contract(block[...], weight_ref[...], 1, 1) * slope_ref[...]).astype(BF)


def back_blocks(blocks, weight, slope):
    rows, width = blocks[0].shape
    units = weight.shape[0]
    count = len(blocks)
    return pl.pallas_call(
        back_kernel,
        grid=(count,),
        in_specs=[
            pl.BlockSpec((units, width), lambda i: (0, 0)),
            pl.BlockSpec((rows, units), lambda i: (i, 0)),
        ]
        + [pl.BlockSpec((rows, width), lambda i: (0, 0))] * count,
        out_specs=pl.BlockSpec((rows, units), lambda i: (i, 0)),
        out_shape=jax.ShapeDtypeStruct((count * rows, units), BF),
        compiler_params=pltpu.CompilerParams(vmem_limit_bytes=VMEM),
        cost_estimate=SMALL,
        name="back_blocks",
    )(weight, slope, *blocks)


def on_device(
    hidden,
    teacher,
    valid_mask,
    prefix_len,
    ln1_gain,
    ln1_bias,
    ln2_gain,
    ln2_bias,
    qkv_weight,
    qkv_bias,
    out_weight,
    out_bias,
    fc1_weight,
    fc1_bias,
    fc2_weight,
    fc2_bias,
):
    rows = hidden.shape[0]
    dp = lax.axis_size("dp")
    tp = lax.axis_size("tensor")
    ways = tp // 2
    squares = dp // 4
    total_tokens = dp * tp * rows
    heads = qkv_weight.shape[1] // (3 * HD)
    dp_index = lax.axis_index("dp")
    tp_index = lax.axis_index("tensor")
    core, y = tp_index % 2, tp_index // 2
    quarter = dp_index % 4

    def to_core(v):
        return lax.ppermute(v, "tensor", [(t, t ^ 1) for t in range(tp)])

    def from_y(v, step):
        pairs = [(t, ((t // 2 - step) % ways) * 2 + t % 2) for t in range(tp)]
        return lax.ppermute(v, "tensor", pairs)

    def to_y(v, step):
        pairs = [(t, ((t // 2 + step) % ways) * 2 + t % 2) for t in range(tp)]
        return lax.ppermute(v, "tensor", pairs)

    def flip(v, mask):
        return lax.ppermute(v, "dp", [(d, d ^ mask) for d in range(dp)])

    block_ids = [
        ((y + step) % ways) * 2 + (core if mate == 0 else 1 - core)
        for step in range(ways)
        for mate in (0, 1)
    ]

    def gather_near(own):
        over_y = [from_y(own, step) for step in range(1, ways)]
        parts = []
        for block in [own] + over_y:
            parts += [block, to_core(block)]
        return parts, over_y

    def first_far(own):
        return [flip(own, 1), flip(own, 2)]

    def second_far(first, over_y):
        corner = flip(first[1], 1)
        beside = [from_y(first[0], step) for step in range(1, ways)]
        across = [flip(block, 2) for block in over_y]
        return corner, beside, across

    def last_far(second):
        half = rows // 2
        return [(flip(v[:half], 1), flip(u[half:], 2)) for u, v in zip(second[1], second[2])]

    def meet(*trees):
        leaves, shape = jax.tree.flatten(trees)
        return jax.tree.unflatten(shape, lax.optimization_barrier(tuple(leaves)))

    def quarter_of(v, axis, index):
        size = v.shape[axis] // 4
        return lax.dynamic_slice_in_dim(v, index * size, size, axis)

    def swap_quarters(v):
        return [flip(quarter_of(v, 1, quarter ^ mask), mask) for mask in (1, 2, 3)]

    gain_attn = ln1_gain.astype(F32)
    shift_attn = ln1_bias.astype(F32)
    gain_mlp = ln2_gain.astype(F32)
    shift_mlp = ln2_bias.astype(F32)
    gains = [v[None, :] for v in (ln1_gain, ln1_bias, ln2_gain, ln2_bias)]
    close = 2 * rows

    def units(normed):
        return jnp.dot(normed, fc1_weight, preferred_element_type=F32) + fc1_bias.astype(F32)

    near_blocks, hidden_y = gather_near(hidden)
    first = first_far(hidden)
    norm_attn_own, norm_mlp_own = both_norms(near_blocks[:2], gains)
    mask_f = after(valid_mask, norm_mlp_own).astype(F32)
    count = jnp.full((8, 128), jnp.sum(mask_f), F32)
    count = count + to_core(count)
    counted = flip(count, 1)
    pre_own = units(norm_mlp_own)
    active_own = exact_gelu(pre_own)[0].astype(BF)
    table = jnp.concatenate(
        [
            lax.dynamic_slice_in_dim(jnp.asarray(rotary_table(LEN)), b * rows, rows, 0)
            for b in block_ids
        ],
        axis=0,
    )
    spots = jnp.concatenate([b * rows + jnp.arange(rows, dtype=jnp.int32) for b in block_ids])
    active_own, table = after(active_own, table), after(table, active_own)
    qkv_own = project_qkv(norm_attn_own, qkv_weight, qkv_bias, table, LEN)
    active_own, qkv_own, counted, first, hidden_y = meet(
        active_own, qkv_own, counted, first, hidden_y
    )
    count = count + counted

    near_blocks = near_blocks[:2]
    for block in hidden_y:
        near_blocks += [block, to_core(block)]
    second = second_far(first, hidden_y)
    first_mates = [to_core(block) for block in first]
    counted = flip(count, 2)
    norm_attn_rest, norm_mlp_rest = both_norms(near_blocks[2:], gains)
    qkv_low = project_qkv(norm_attn_rest, qkv_weight, qkv_bias, table, LEN, qkv_own)
    context, log_total = attend(qkv_low, prefix_len, spots)
    norm_mlp_rest = after(norm_mlp_rest, context)
    context_far = swap_quarters(context)
    pre_rest = units(norm_mlp_rest)
    active_rest = exact_gelu(pre_rest)[0].astype(BF)
    active_rest, context, counted, second, context_far, first_mates = meet(
        active_rest, context, counted, second, context_far, first_mates
    )
    count = count + counted

    def branch_rows(context_rows, active_rows):
        return jnp.dot(context_rows, out_weight, preferred_element_type=F32) + jnp.dot(
            active_rows, fc2_weight, preferred_element_type=F32
        )

    def core_total(part):
        blocks = part.reshape(-1, 2, rows, D)
        return blocks[:, 0] + to_core(blocks[:, 1].astype(BF)).astype(F32)

    corner, beside, across = second
    second_mates = [to_core(block) for block in [corner] + beside + across]
    counted = jnp.zeros_like(count)
    bit = 2
    while bit < tp:
        counted = lax.ppermute(count, "tensor", [(t, t ^ bit) for t in range(tp)])
        bit *= 2
        if bit < tp:
            count = count + counted
    part_rest = branch_rows(context[close:], active_rest).reshape(-1, 2, rows, D)
    mates_rest = to_core(part_rest[:, 1].astype(BF))
    part_own = branch_rows(context[:close], after(active_own, part_rest)).reshape(2, rows, D)
    part_own, mates_rest, counted, second_mates = meet(
        part_own, mates_rest, counted, second_mates
    )
    count = count + counted

    sums = part_rest[:, 0] + mates_rest.astype(F32)
    came = [to_y(sums[step - 1].astype(BF), step) for step in range(1, ways)]
    mates_own = to_core(part_own[1].astype(BF))
    counted = flip(count, 4) if dp > 4 else jnp.zeros_like(count)
    last = last_far(second)
    ahead = [first[0]] + beside + [first[1]] + across + [corner]
    mates = (
        [first_mates[0]]
        + second_mates[1:ways]
        + [first_mates[1]]
        + second_mates[ways:]
        + [second_mates[0]]
    )
    far_blocks = [block for pair in zip(ahead, mates) for block in pair]
    norms_far = both_norms(far_blocks, gains, 6 * ways)
    last, norms_far = meet(last, norms_far)
    last = [jnp.concatenate(pair, axis=0) for pair in last]
    far_blocks = [block for v in last for block in (v, to_core(v))]
    norm_attn_far, norm_mlp_far = both_norms(far_blocks, gains, 6 * ways, norms_far)
    came, mates_own, counted, norm_mlp_far = meet(came, mates_own, counted, norm_mlp_far)
    count = count + counted
    mask = 8
    while mask < dp:
        count = count + flip(count, mask)
        mask *= 2
    branch = part_own[0] + mates_own.astype(F32)
    for got in came:
        branch = branch + got.astype(F32)
    output_f = hidden.astype(F32) + branch + out_bias.astype(F32) + fc2_bias.astype(F32)
    mismatch = output_f - teacher.astype(F32)
    error_part = jnp.sum(mask_f[:, None] * mismatch * mismatch)
    grad_out = mask_f[:, None] * mismatch * (2.0 * total_tokens / count[0, 0])
    grad_low = grad_out.astype(BF)
    grad_out, grad_low, norm_mlp_far = meet(grad_out, grad_low, norm_mlp_far)

    grad_y = [from_y(grad_low, step) for step in range(1, ways)]
    grad_first = first_far(grad_low)
    grad_mate = to_core(grad_low)
    fc1_quarter = quarter_of(fc1_weight, 1, quarter)
    fc2_quarter = quarter_of(after(fc2_weight, norm_mlp_far), 0, quarter)
    context_quarter = quarter_of(after(context, norm_mlp_far), 1, quarter)
    pre_far = jnp.dot(norm_mlp_far, fc1_quarter, preferred_element_type=F32) + quarter_of(
        fc1_bias, 0, quarter
    ).astype(F32)
    active_far, slope_far = exact_gelu(pre_far)
    active_far = active_far.astype(BF)
    grad_y, grad_first, active_far, grad_mate, fc2_quarter, context_quarter = meet(
        grad_y, grad_first, active_far, grad_mate, fc2_quarter, context_quarter
    )

    grad_second = second_far(grad_first, grad_y)
    grad_blocks = [grad_low, grad_mate]
    for block in grad_y:
        grad_blocks += [block, to_core(block)]
    grad_near = jnp.concatenate(grad_blocks, axis=0)
    grad_context = contract(grad_near, out_weight, 1, 1).astype(BF)
    grad_qkv = attend_back(qkv_low, grad_context, log_total, prefix_len, spots, table)
    grad_qkv, grad_near, grad_second = meet(grad_qkv, grad_near, grad_second)

    grad_last = last_far(grad_second)
    corner, beside, across = grad_second
    ahead = [grad_first[0]] + beside + [grad_first[1]] + across + [corner]
    mates = [to_core(block) for block in ahead]
    swapped = [flip(quarter_of(grad_qkv, 1, quarter ^ m), m) for m in (1, 2)]
    hidden_pre = jnp.concatenate([pre_own, pre_rest], axis=0)
    grad_inner = (contract(grad_near, fc2_weight, 1, 1) * exact_gelu(hidden_pre)[1]).astype(BF)
    grad_inner, grad_last, mates = meet(grad_inner, grad_last, mates)

    grad_last = [jnp.concatenate(pair, axis=0) for pair in grad_last]
    ahead += grad_last
    mates += [to_core(block) for block in grad_last]
    grad_far = [block for pair in zip(ahead, mates) for block in pair]
    bias_part = jnp.sum(grad_out, axis=0)

    queue = []
    due = {}
    clock, launched = [0], [0]
    results = {}
    token = [grad_near]

    def gate(v):
        return after(v, token[0])

    def flipped(v, mask):
        return v, lambda value: flip(value, mask)

    def travel(low, name, wait):
        mask = 4
        while mask < dp:
            (got,) = yield [flipped(low, mask)], wait
            low = (low.astype(F32) + got.astype(F32)).astype(BF)
            mask, wait = mask * 2, 1
        (across,) = yield [flipped(low, 2)], 1
        near = jnp.concatenate([low, across], axis=0)
        (far,) = yield [flipped(near, 1)], 1
        results.setdefault(name, []).append((near, far))

    def swap_walk(v, into):
        got = yield [flipped(quarter_of(v, 1, quarter ^ 3), 3)], 2
        into.extend(got)

    def last_walk(kept, mates, parts, others, into):
        (got,) = yield [(mates, to_core)], 1
        sums = kept + got.astype(F32)
        total = sums[0]
        for step in range(1, ways):
            (got,) = yield [(sums[step].astype(BF), lambda v, s=step: to_y(v, s))], 1
            total = total + got.astype(F32)
        into["input"] = grad_out + total
        bit = 1
        while bit < tp:
            pairs = [(t, t ^ bit) for t in range(tp)]
            (got,) = yield [(parts, lambda v, p=pairs: lax.ppermute(v, "tensor", p))], 1
            parts = parts + got
            bit *= 2
        parts = jnp.concatenate([parts, others])
        bit = 1
        while bit < dp:
            (got,) = yield [flipped(parts, bit)], 1
            parts = parts + got
            bit *= 2
        into["small"] = parts

    def walk(walker):
        asked = next(walker)
        start(walker, asked, clock[0] - 1)

    def start(walker, asked, now):
        sends, wait = asked
        due.setdefault(now + wait, []).append((walker, [move(v) for v, move in sends]))

    parts_of = {}

    def cut(part, shares):
        unit = part.shape[0] // 16
        edges = [unit * sum(shares[:i]) for i in range(len(shares) + 1)]
        return [lax.slice_in_dim(part, a, b, axis=0) for a, b in zip(edges, edges[1:])]

    def enqueue(name, *units):
        before, _ = parts_of.get(name, (0, 0))
        parts_of[name] = (before + sum(u.shape[0] for u in units), units[0].shape[1])
        queue.extend((unit, name) for unit in units)

    def turn(*others):
        now = clock[0]
        clock[0] = now + 1
        arrived = due.pop(now, [])
        values = [got for _, gots in arrived for got in gots]
        fresh = []
        while queue and launched[0] <= now + 1:
            fresh.append(queue.pop(0) + (max(launched[0] - now, 0) + 1,))
            launched[0] += 1
        tied = list(
            lax.optimization_barrier(tuple(values) + tuple(f[0] for f in fresh) + others)
        )
        token[0] = tied[0]
        asked = []
        for walker, gots in arrived:
            gots = [tied.pop(0) for _ in gots]
            try:
                asked.append((walker, walker.send(gots)))
            except StopIteration:
                pass
        for _, name, wait in fresh:
            walker = travel(tied.pop(0), name, wait)
            asked.append((walker, next(walker)))
        for walker, request in asked:
            start(walker, request, now)
        return tied

    def place_one(whole, near, far, shape, axis, offset):
        rows_here, columns = near.shape[0] // 2, near.shape[1]
        if columns % 128 == 0:
            return place_quarters(whole, near, far, shape, axis, offset, quarter)
        if whole is None:
            whole = jnp.zeros(shape, F32)
        pieces = (near[:rows_here], far[:rows_here], near[rows_here:], far[rows_here:])
        for index, piece in enumerate(pieces):
            spot = quarter ^ index
            start = (
                (spot * (shape[0] // 4) + offset, 0) if axis == 0 else (offset, spot * columns)
            )
            whole = lax.dynamic_update_slice(whole, piece.astype(F32), start)
        return whole

    half = active_far.shape[1] // 2
    rights = [grad_near] + grad_far

    def hidden_lefts(part):
        return [
            (active_own, half, 2, part, 0, 0),
            (active_rest, half, 2, part, 0, close),
            (active_far, half, 0, part, 0, LEN),
        ]

    chunk = half // 2
    kept_columns = context.shape[1] // 4
    enqueue("fc2", *outer_blocks(hidden_lefts(0), rights, [chunk] * 2, quarter))
    grad_qkv_far = list(turn(*swapped))
    walk(swap_walk(gate(grad_qkv), grad_qkv_far))
    lefts = hidden_lefts(1)
    for index, piece in enumerate([context_quarter] + context_far):
        lefts.append((piece, kept_columns, 0, 0, half, index * LEN))
    *parts, out_part = outer_blocks(
        lefts, [gate(grad_near)] + grad_far, [chunk] * 2 + [kept_columns], quarter
    )
    enqueue("fc2", *parts)
    enqueue("out", out_part)
    turn()
    grad_inner_far = back_blocks([gate(grad_far[0])] + grad_far[1:], fc2_quarter, slope_far)
    (grad_inner_far,) = turn(grad_inner_far)
    inner_quarter = gate(quarter_of(grad_inner, 1, quarter))
    fc1_part = (
        contract(norm_mlp_own, inner_quarter[:close], 0, 0)
        + contract(norm_mlp_rest, inner_quarter[close:], 0, 0)
        + contract(norm_mlp_far, grad_inner_far, 0, 0)
    )
    (fc1_part,) = turn(fc1_part.astype(BF))
    enqueue("fc1", *cut(fc1_part, [4, 4, 4, 4]))
    grad_norm_attn = contract(gate(grad_qkv), qkv_weight, 1, 1)
    (grad_norm_attn,) = turn(grad_norm_attn)
    grad_norm_mlp = contract(gate(grad_inner), fc1_weight, 1, 1)
    (grad_norm_mlp,) = turn(grad_norm_mlp)

    near_blocks = lax.optimization_barrier((token[0], *near_blocks))[1:]
    features = jnp.concatenate(near_blocks, axis=0).astype(F32)
    centered = features - jnp.mean(features, axis=-1, keepdims=True)
    inverse = lax.rsqrt(jnp.mean(centered * centered, axis=-1, keepdims=True) + EPSILON)
    xhat = centered * inverse
    gained = grad_norm_attn * gain_attn + grad_norm_mlp * gain_mlp
    lift = jnp.mean(gained, axis=-1, keepdims=True)
    pull = jnp.mean(gained * xhat, axis=-1, keepdims=True)
    tensor_parts = jnp.stack(
        [
            jnp.sum(grad_norm_attn * xhat, axis=0),
            jnp.sum(grad_norm_attn, axis=0),
            jnp.sum(grad_norm_mlp * xhat, axis=0),
            jnp.sum(grad_norm_mlp, axis=0),
            bias_part,
            jnp.full((D,), error_part, F32),
        ]
    ).reshape(-1)
    tensor_parts, lift, pull = turn(tensor_parts, lift, pull)
    grad_hidden = inverse * (gained - lift - xhat * pull)
    blocks = grad_hidden.reshape(ways, 2, rows, D)
    fc1_bias_part = jnp.sum(gate(grad_inner), axis=0, dtype=F32)
    qkv_bias_part = jnp.sum(gate(grad_qkv), axis=0, dtype=F32)
    kept, mates, fc1_bias_part, qkv_bias_part = turn(
        blocks[:, 0], blocks[:, 1].astype(BF), fc1_bias_part, qkv_bias_part
    )
    outcome = {}
    others = jnp.concatenate([fc1_bias_part, qkv_bias_part])
    walk(last_walk(kept, mates, tensor_parts, others, outcome))
    qkv_quarter = gate(quarter_of(grad_qkv, 1, quarter))
    qkv_part = (
        contract(norm_attn_own, qkv_quarter[:close], 0, 0)
        + contract(norm_attn_rest, qkv_quarter[close:], 0, 0)
        + contract(norm_attn_far, jnp.concatenate(grad_qkv_far, axis=0), 0, 0)
    )
    (qkv_part,) = turn(qkv_part.astype(BF))
    enqueue("qkv", *cut(qkv_part, [4, 4, 4, 2, 1, 1]))
    axes = {"fc2": 0, "out": 0, "fc1": 1, "qkv": 1}
    placed = {name: (None, 0, 0) for name in axes}

    def place(name):
        whole, done, offset = placed[name]
        pieces = results[name][done]
        lengths, columns = parts_of[name]
        shape = (4 * lengths, columns) if axes[name] == 0 else (lengths, 4 * columns)
        whole = place_one(whole, *pieces, shape, axes[name], offset)
        placed[name] = (whole, done + 1, offset + pieces[0].shape[0] // 2)

    while queue or due:
        ready = []
        for name in axes:
            if len(ready) < 2 and len(results.get(name, [])) > placed[name][1]:
                place(name)
                ready.append(name)
        wholes = turn(*[placed[name][0] for name in ready])
        for name, whole in zip(ready, wholes):
            placed[name] = (whole,) + placed[name][1:]
    for name in axes:
        while len(results[name]) > placed[name][1]:
            place(name)
    input_grad = outcome["input"]
    small = outcome["small"]
    vectors = small[: 6 * D].reshape(6, D)
    fc1_bias_grad = small[6 * D : 6 * D + fc1_bias_part.shape[0]]
    qkv_bias_grad = small[6 * D + fc1_bias_part.shape[0] :]
    loss_value = vectors[5, 0] / (count[0, 0] * D)
    fc2_weight_grad, out_weight_grad = placed["fc2"][0], placed["out"][0]
    fc1_weight_grad, qkv_weight_grad = placed["fc1"][0], placed["qkv"][0]
    return (
        output_f.astype(BF),
        loss_value,
        input_grad,
        vectors[0],
        vectors[1],
        vectors[2],
        vectors[3],
        qkv_weight_grad,
        qkv_bias_grad,
        out_weight_grad,
        vectors[4],
        fc1_weight_grad,
        fc1_bias_grad,
        fc2_weight_grad,
        vectors[4],
    )


def solution(mesh):
    tokens = P(("dp", "tensor"), None)
    columns, lanes, down, whole = P(None, "tensor"), P("tensor"), P("tensor", None), P()
    in_specs = (
        tokens,
        tokens,
        P(("dp", "tensor")),
        P("dp"),
        whole,
        whole,
        whole,
        whole,
        columns,
        lanes,
        down,
        whole,
        columns,
        lanes,
        down,
        whole,
    )
    out_specs = (
        tokens,
        whole,
        tokens,
        whole,
        whole,
        whole,
        whole,
        columns,
        lanes,
        down,
        whole,
        columns,
        lanes,
        down,
        whole,
    )
    return jax.shard_map(
        on_device, mesh=mesh, in_specs=in_specs, out_specs=out_specs, check_vma=False
    )
```

```python
import functools

import jax
import jax.numpy as jnp
import numpy as np
from jax import lax
from jax.experimental import pallas as pl
from jax.experimental.pallas import tpu as pltpu
from jax.sharding import PartitionSpec as P

D = 2048
HD = 256
ROT = 64
LEN = 1024
EPSILON = 1e-05
BF = jnp.bfloat16
F32 = jnp.float32
SMALL = pl.CostEstimate(flops=1 << 20, bytes_accessed=1 << 16, transcendentals=0)


def rotary_table(length):
    half = ROT // 2
    frequency = (10000.0 ** (-2.0 * np.arange(half, dtype=np.float32) / ROT)).astype(np.float32)
    angles = np.arange(length, dtype=np.float32)[:, None] * frequency[None, :]
    cosine, sine = np.cos(angles), np.sin(angles)
    table = np.zeros((length, 3 * 128), np.float32)
    table[:, ROT:128] = 1.0
    table[:, :half] = table[:, half:ROT] = cosine
    table[:, 128 : 128 + half] = -sine
    table[:, 256 + half : 256 + ROT] = sine
    return table


def contract(left_side, right_side, left_dim, right_dim):
    return lax.dot_general(
        left_side,
        right_side,
        (((left_dim,), (right_dim,)), ((), ())),
        preferred_element_type=F32,
    )


def exact_gelu(pre_act):
    below = 0.5 + 0.5 * lax.erf(pre_act * 0.5**0.5)
    density = jnp.exp(-0.5 * pre_act * pre_act) * (2.0 * jnp.pi) ** -0.5
    return pre_act * below, below + pre_act * density


def after(value, *earlier):
    return lax.optimization_barrier((value,) + earlier)[0]


def turned(block, keep, up, down, sign):
    head = block[:, :128]
    half = ROT // 2
    moved = head * keep + sign * (
        pltpu.roll(head, 128 - half, 1) * up + pltpu.roll(head, half, 1) * down
    )
    return jnp.concatenate([moved, block[:, 128:]], axis=1)


def qkv_kernel(x_ref, w_ref, b_ref, keep_ref, up_ref, down_ref, *refs):
    o_ref = refs[-1]
    kind = pl.program_id(0) % 3
    rows = x_ref.shape[0]
    tile = min(rows, 512)

    def project(at):
        return (
            jnp.dot(x_ref[at, :], w_ref[...], preferred_element_type=F32)
            + b_ref[...].astype(F32)
        )

    for start in range(0, rows, tile):
        at = pl.ds(start, min(tile, rows - start))

        @pl.when(kind == 2)
        def _(at=at):
            o_ref[at, :] = project(at).astype(BF)

        @pl.when(kind != 2)
        def _(at=at):
            o_ref[at, :] = turned(
                project(at), keep_ref[at, :], up_ref[at, :], down_ref[at, :], 1.0
            ).astype(BF)


def project_qkv(normed, weight, bias, table, length, whole=None):
    rows, width = normed.shape
    columns = weight.shape[1]
    part = 0 if whole is None else 1
    if part and rows * 2 != length:
        rest = project_qkv(normed, weight, bias, table[length - rows :], rows)
        return jnp.concatenate([whole[: length - rows], rest], axis=0)
    return pl.pallas_call(
        qkv_kernel,
        grid=(columns // HD,),
        in_specs=[
            pl.BlockSpec((rows, width), lambda j: (0, 0)),
            pl.BlockSpec((width, HD), lambda j: (0, j)),
            pl.BlockSpec((1, HD), lambda j: (0, j)),
        ]
        + [pl.BlockSpec((rows, 128), lambda j, k=k: (part, k)) for k in range(3)]
        + [pl.BlockSpec(memory_space=pl.ANY)] * part,
        out_specs=pl.BlockSpec((rows, HD), lambda j: (part, j)),
        out_shape=jax.ShapeDtypeStruct((length, columns), BF),
        input_output_aliases={6: 0} if part else {},
        compiler_params=pltpu.CompilerParams(vmem_limit_bytes=24 << 20),
        cost_estimate=SMALL,
        name="qkv_rotary",
    )(normed, weight, bias[None, :], table, table, table, *([whole] if part else []))


def visible_scores(queries, keys, row_spots, key_spots, prefix):
    scores = lax.dot_general(
        queries, keys, (((1,), (1,)), ((), ())), preferred_element_type=F32
    ) * (HD**-0.5)
    allowed = (key_spots <= row_spots) | (key_spots < prefix)
    return jnp.where(allowed, scores, -jnp.inf)


def attend_kernel(prefix_ref, q_ref, k_ref, v_ref, rows_ref, keys_ref, o_ref, log_ref):
    scores = visible_scores(
        q_ref[...], k_ref[...], rows_ref[...], keys_ref[...], prefix_ref[0]
    )
    top = jnp.max(scores, axis=-1, keepdims=True)
    weights = jnp.exp(scores - top)
    total = jnp.sum(weights, axis=-1, keepdims=True)
    probs = (weights * (1.0 / total)).astype(BF)
    o_ref[...] = jnp.dot(probs, v_ref[...], preferred_element_type=F32).astype(BF)
    log_ref[0] = top + jnp.log(total)


def attend(qkv, prefix, spots):
    length = qkv.shape[0]
    heads = qkv.shape[1] // (3 * HD)
    tile = length // 4
    whole = lambda part: pl.BlockSpec((length, HD), lambda h, i, p: (0, 3 * h + part))
    return pl.pallas_call(
        attend_kernel,
        grid_spec=pltpu.PrefetchScalarGridSpec(
            num_scalar_prefetch=1,
            grid=(heads, 4),
            in_specs=[
                pl.BlockSpec((tile, HD), lambda h, i, p: (i, 3 * h)),
                whole(1),
                whole(2),
                pl.BlockSpec((tile, 1), lambda h, i, p: (i, 0)),
                pl.BlockSpec((1, length), lambda h, i, p: (0, 0)),
            ],
            out_specs=[
                pl.BlockSpec((tile, HD), lambda h, i, p: (i, h)),
                pl.BlockSpec((1, tile, 1), lambda h, i, p: (h, i, 0)),
            ],
        ),
        out_shape=[
            jax.ShapeDtypeStruct((length, heads * HD), BF),
            jax.ShapeDtypeStruct((heads, length, 1), F32),
        ],
        compiler_params=pltpu.CompilerParams(vmem_limit_bytes=20 << 20),
        cost_estimate=SMALL,
        name="attend",
    )(prefix, qkv, qkv, qkv, spots[:, None], spots[None, :])


def attend_back_kernel(
    prefix_ref, q_ref, k_ref, v_ref, g_ref, log_ref, rows_ref, keys_ref, keep_ref, up_ref,
    down_ref, o_ref, dk_ref, dv_ref,
):
    length = q_ref.shape[0]
    tile = length // 4
    scale = HD**-0.5
    for i in range(4):
        at = pl.ds(i * tile, tile)
        q, g = q_ref[at, :], g_ref[at, :]
        scores = visible_scores(q, k_ref[...], rows_ref[at, :], keys_ref[...], prefix_ref[0])
        probs = jnp.exp(scores - log_ref[0, at, :])
        grad_probs = lax.dot_general(
            g, v_ref[...], (((1,), (1,)), ((), ())), preferred_element_type=F32
        )
        dots = jnp.sum(probs * grad_probs, axis=-1, keepdims=True)
        grad_scores = (probs * (grad_probs - dots)).astype(BF)
        dq = jnp.dot(grad_scores, k_ref[...], preferred_element_type=F32) * scale
        o_ref[at, :HD] = turned(
            dq, keep_ref[at, :], up_ref[at, :], down_ref[at, :], -1.0
        ).astype(BF)
        dk = contract(grad_scores, q, 0, 0)
        dv = contract(probs.astype(BF), g, 0, 0)
        if i == 0:
            dk_ref[...] = dk
            dv_ref[...] = dv
        else:
            dk_ref[...] += dk
            dv_ref[...] += dv
    o_ref[:, HD : 2 * HD] = turned(
        dk_ref[...] * scale, keep_ref[...], up_ref[...], down_ref[...], -1.0
    ).astype(BF)
    o_ref[:, 2 * HD :] = dv_ref[...].astype(BF)


def attend_back(qkv, grad_context, log_total, prefix, spots, table):
    length = qkv.shape[0]
    heads = qkv.shape[1] // (3 * HD)
    part = lambda n: pl.BlockSpec((length, HD), lambda h, p: (0, 3 * h + n))
    return pl.pallas_call(
        attend_back_kernel,
        grid_spec=pltpu.PrefetchScalarGridSpec(
            num_scalar_prefetch=1,
            grid=(heads,),
            in_specs=[
                part(0),
                part(1),
                part(2),
                pl.BlockSpec((length, HD), lambda h, p: (0, h)),
                pl.BlockSpec((1, length, 1), lambda h, p: (h, 0, 0)),
                pl.BlockSpec((length, 1), lambda h, p: (0, 0)),
                pl.BlockSpec((1, length), lambda h, p: (0, 0)),
            ]
            + [pl.BlockSpec((length, 128), lambda h, p, k=k: (0, k)) for k in range(3)],
            out_specs=pl.BlockSpec((length, 3 * HD), lambda h, p: (0, h)),
            scratch_shapes=[pltpu.VMEM((length, HD), F32), pltpu.VMEM((length, HD), F32)],
        ),
        out_shape=jax.ShapeDtypeStruct((length, heads * 3 * HD), BF),
        compiler_params=pltpu.CompilerParams(vmem_limit_bytes=32 << 20),
        cost_estimate=SMALL,
        name="attend_back",
    )(prefix, qkv, qkv, qkv, grad_context, log_total, spots[:, None], spots[None, :], table, table, table)


def back_rows_kernel(now_ref, grad_ref, weight_ref, *refs):
    o_ref = refs[-1]

    @pl.when(now_ref[0] == 1)
    def _():
        o_ref[...] = contract(grad_ref[...], weight_ref[...], 1, 1)

    if len(refs) == 2:

        @pl.when(now_ref[0] == 0)
        def _():
            o_ref[...] = refs[0][...]


def back_rows(grad, weight, now, before=None):
    length, units = grad.shape
    width = weight.shape[0]
    tile = 256
    kept = [] if before is None else [before]
    return pl.pallas_call(
        back_rows_kernel,
        grid_spec=pltpu.PrefetchScalarGridSpec(
            num_scalar_prefetch=1,
            grid=(width // tile,),
            in_specs=[
                pl.BlockSpec((length, units), lambda j, n: (0, 0)),
                pl.BlockSpec((tile, units), lambda j, n: (j * n[0], 0)),
            ]
            + [pl.BlockSpec((length, tile), lambda j, n: (0, 0))] * len(kept),
            out_specs=pl.BlockSpec((length, tile), lambda j, n: (0, j * n[0])),
        ),
        out_shape=jax.ShapeDtypeStruct((length, width), F32),
        input_output_aliases={3: 0} if kept else {},
        compiler_params=pltpu.CompilerParams(vmem_limit_bytes=24 << 20),
        cost_estimate=SMALL,
        name="back_rows",
    )(now.astype(jnp.int32).reshape(1), grad, weight, *kept)


def place_kernel(quarter_ref, *refs):
    pieces, out_ref = refs[-5:-1], refs[-1]
    for index, piece in enumerate(pieces):

        @pl.when(pl.program_id(0) == index)
        def _(piece=piece):
            out_ref[...] = piece[...].astype(F32)


def place_quarters(whole, near, far, shape, axis, offset, quarter):
    rows, columns = near.shape[0] // 2, near.shape[1]
    if axis == 0:
        each, first_row = shape[0] // 4 // rows, offset // rows
        spot = lambda k, q: ((q[0] ^ k) * each + first_row, 0)
    else:
        spot = lambda k, q: (offset // rows, q[0] ^ k)
    first = whole is None
    operands = ([] if first else [whole]) + [near, far, near, far]
    return pl.pallas_call(
        place_kernel,
        grid_spec=pltpu.PrefetchScalarGridSpec(
            num_scalar_prefetch=1,
            grid=(4,),
            in_specs=([] if first else [pl.BlockSpec(memory_space=pl.ANY)])
            + [pl.BlockSpec((rows, columns), lambda k, q, h=h: (h, 0)) for h in (0, 0, 1, 1)],
            out_specs=pl.BlockSpec((rows, columns), spot),
        ),
        out_shape=jax.ShapeDtypeStruct(shape, F32),
        input_output_aliases={} if first else {1: 0},
        compiler_params=pltpu.CompilerParams(vmem_limit_bytes=12 << 20),
        cost_estimate=SMALL,
        name="place_quarters",
    )(quarter.reshape(1), *operands)


def norms_kernel(count, *refs):
    gains, blocks, (attn_ref, mlp_ref) = refs[:4], refs[4 : 4 + count], refs[-2:]
    for index, block in enumerate(blocks):

        @pl.when(pl.program_id(0) == index)
        def _(block=block):
            features = block[...].astype(F32)
            average = jnp.mean(features, axis=-1, keepdims=True)
            centered = features - average
            spread = jnp.mean(centered * centered, axis=-1, keepdims=True)
            xhat = centered * lax.rsqrt(spread + EPSILON)
            gain_a, shift_a, gain_m, shift_m = (ref[...].astype(F32) for ref in gains)
            attn_ref[...] = (xhat * gain_a + shift_a).astype(BF)
            mlp_ref[...] = (xhat * gain_m + shift_m).astype(BF)


def both_norms(blocks, gains, total=None, into=()):
    count = len(blocks)
    total = total or count
    skip = total - count if into else 0
    rows, width = blocks[0].shape
    shape = jax.ShapeDtypeStruct((total * rows, width), BF)
    return pl.pallas_call(
        functools.partial(norms_kernel, count),
        grid=(count,),
        in_specs=[pl.BlockSpec((1, width), lambda i: (0, 0))] * 4
        + [pl.BlockSpec((rows, width), lambda i: (0, 0))] * count
        + [pl.BlockSpec(memory_space=pl.ANY)] * len(into),
        out_specs=[pl.BlockSpec((rows, width), lambda i: (i + skip, 0))] * 2,
        out_shape=[shape, shape],
        input_output_aliases={4 + count: 0, 5 + count: 1} if into else {},
        compiler_params=pltpu.CompilerParams(vmem_limit_bytes=32 << 20),
        cost_estimate=SMALL,
        name="both_norms",
    )(*gains, *blocks, *into)


def outer_kernel(lefts, pieces, outs, _, *refs):
    left_refs, rights = refs[:lefts], refs[lefts : -2 - outs]
    out_refs, (left_ref, joined_ref) = refs[-2 - outs : -2], refs[-2:]

    @pl.when(pl.program_id(0) == 0)
    def _():
        for ref, (row, column) in zip(left_refs, pieces):
            count, width = ref.shape
            step = min(count, 256)
            for start in range(0, count, step):
                left_ref[pl.ds(row, width), pl.ds(column + start, step)] = ref[
                    pl.ds(start, step), :
                ].T

    column = 0
    for ref in rights:
        joined_ref[pl.ds(column, ref.shape[0]), :] = ref[...]
        column += ref.shape[0]
    total = jnp.dot(left_ref[...], joined_ref[...], preferred_element_type=F32).astype(BF)
    row = 0
    for ref in out_refs:
        ref[...] = total[row : row + ref.shape[0], :]
        row += ref.shape[0]


def outer_blocks(lefts, rights, sizes, quarter):
    width = rights[0].shape[1]
    tokens = sum(r.shape[0] for r in rights)
    left = sum(sizes)
    tile = 512
    specs = [
        pl.BlockSpec((a.shape[0], taken), lambda j, q, m=times, o=offset: (0, q[0] * m + o))
        for a, taken, times, offset, _, _ in lefts
    ]
    pieces = [(row, token) for *_, row, token in lefts]
    return pl.pallas_call(
        functools.partial(outer_kernel, len(lefts), pieces, len(sizes)),
        grid_spec=pltpu.PrefetchScalarGridSpec(
            num_scalar_prefetch=1,
            grid=(width // tile,),
            in_specs=specs
            + [pl.BlockSpec((r.shape[0], tile), lambda j, q: (0, j)) for r in rights],
            out_specs=[pl.BlockSpec((size, tile), lambda j, q: (0, j)) for size in sizes],
            scratch_shapes=[pltpu.VMEM((left, tokens), BF), pltpu.VMEM((tokens, tile), BF)],
        ),
        out_shape=[jax.ShapeDtypeStruct((size, width), BF) for size in sizes],
        compiler_params=pltpu.CompilerParams(vmem_limit_bytes=40 << 20),
        cost_estimate=SMALL,
        name="outer_blocks",
    )(quarter.reshape(1), *[a for a, *_ in lefts], *rights)


def back_kernel(weight_ref, slope_ref, *refs):
    blocks, o_ref = refs[:-1], refs[-1]
    for index, block in enumerate(blocks):

        @pl.when(pl.program_id(0) == index)
        def _(block=block):
            o_ref[...] = (contract(block[...], weight_ref[...], 1, 1) * slope_ref[...]).astype(BF)


def back_blocks(blocks, weight, slope):
    rows, width = blocks[0].shape
    units = weight.shape[0]
    count = len(blocks)
    return pl.pallas_call(
        back_kernel,
        grid=(count,),
        in_specs=[
            pl.BlockSpec((units, width), lambda i: (0, 0)),
            pl.BlockSpec((rows, units), lambda i: (i, 0)),
        ]
        + [pl.BlockSpec((rows, width), lambda i: (0, 0))] * count,
        out_specs=pl.BlockSpec((rows, units), lambda i: (i, 0)),
        out_shape=jax.ShapeDtypeStruct((count * rows, units), BF),
        compiler_params=pltpu.CompilerParams(vmem_limit_bytes=36 << 20),
        cost_estimate=SMALL,
        name="back_blocks",
    )(weight, slope, *blocks)


def on_device(
    hidden,
    teacher,
    valid_mask,
    prefix_len,
    ln1_gain,
    ln1_bias,
    ln2_gain,
    ln2_bias,
    qkv_weight,
    qkv_bias,
    out_weight,
    out_bias,
    fc1_weight,
    fc1_bias,
    fc2_weight,
    fc2_bias,
):
    rows = hidden.shape[0]
    dp = lax.axis_size("dp")
    tp = lax.axis_size("tensor")
    ways = tp // 2
    squares = dp // 4
    total_tokens = dp * tp * rows
    heads = qkv_weight.shape[1] // (3 * HD)
    dp_index = lax.axis_index("dp")
    tp_index = lax.axis_index("tensor")
    core, y = tp_index % 2, tp_index // 2
    quarter = dp_index % 4

    def to_core(v):
        return lax.ppermute(v, "tensor", [(t, t ^ 1) for t in range(tp)])

    def from_y(v, step):
        pairs = [(t, ((t // 2 - step) % ways) * 2 + t % 2) for t in range(tp)]
        return lax.ppermute(v, "tensor", pairs)

    def to_y(v, step):
        pairs = [(t, ((t // 2 + step) % ways) * 2 + t % 2) for t in range(tp)]
        return lax.ppermute(v, "tensor", pairs)

    def flip(v, mask):
        return lax.ppermute(v, "dp", [(d, d ^ mask) for d in range(dp)])

    block_ids = [
        ((y + step) % ways) * 2 + (core if mate == 0 else 1 - core)
        for step in range(ways)
        for mate in (0, 1)
    ]

    def gather_near(own):
        over_y = [from_y(own, step) for step in range(1, ways)]
        parts = []
        for block in [own] + over_y:
            parts += [block, to_core(block)]
        return parts, over_y

    def first_far(own):
        return [flip(own, 1), flip(own, 2)]

    def second_far(first, over_y):
        corner = flip(first[1], 1)
        beside = [from_y(first[0], step) for step in range(1, ways)]
        across = [flip(block, 2) for block in over_y]
        return corner, beside, across

    def last_far(second):
        half = rows // 2
        return [(flip(v[:half], 1), flip(u[half:], 2)) for u, v in zip(second[1], second[2])]

    def meet(*trees):
        leaves, shape = jax.tree.flatten(trees)
        return jax.tree.unflatten(shape, lax.optimization_barrier(tuple(leaves)))

    def quarter_of(v, axis, index):
        size = v.shape[axis] // 4
        return lax.dynamic_slice_in_dim(v, index * size, size, axis)

    def swap_quarters(v):
        return [flip(quarter_of(v, 1, quarter ^ mask), mask) for mask in (1, 2, 3)]

    gain_attn = ln1_gain.astype(F32)
    shift_attn = ln1_bias.astype(F32)
    gain_mlp = ln2_gain.astype(F32)
    shift_mlp = ln2_bias.astype(F32)
    gains = [v[None, :] for v in (ln1_gain, ln1_bias, ln2_gain, ln2_bias)]
    close = 2 * rows

    def units(normed):
        return jnp.dot(normed, fc1_weight, preferred_element_type=F32) + fc1_bias.astype(F32)

    near_blocks, hidden_y = gather_near(hidden)
    first = first_far(hidden)
    norm_attn_own, norm_mlp_own = both_norms(near_blocks[:2], gains)
    mask_f = after(valid_mask, norm_mlp_own).astype(F32)
    count = jnp.full((8, 128), jnp.sum(mask_f), F32)
    count = count + to_core(count)
    counted = flip(count, 1)
    pre_own = units(norm_mlp_own)
    active_own = exact_gelu(pre_own)[0].astype(BF)
    table = jnp.concatenate(
        [
            lax.dynamic_slice_in_dim(jnp.asarray(rotary_table(LEN)), b * rows, rows, 0)
            for b in block_ids
        ],
        axis=0,
    )
    spots = jnp.concatenate([b * rows + jnp.arange(rows, dtype=jnp.int32) for b in block_ids])
    active_own, table = after(active_own, table), after(table, active_own)
    qkv_own = project_qkv(norm_attn_own, qkv_weight, qkv_bias, table, LEN)
    active_own, qkv_own, counted, first, hidden_y = meet(
        active_own, qkv_own, counted, first, hidden_y
    )
    count = count + counted

    near_blocks = near_blocks[:2]
    for block in hidden_y:
        near_blocks += [block, to_core(block)]
    second = second_far(first, hidden_y)
    first_mates = [to_core(block) for block in first]
    counted = flip(count, 2)
    norm_attn_rest, norm_mlp_rest = both_norms(near_blocks[2:], gains)
    qkv_low = project_qkv(norm_attn_rest, qkv_weight, qkv_bias, table, LEN, qkv_own)
    context, log_total = attend(qkv_low, prefix_len, spots)
    norm_mlp_rest = after(norm_mlp_rest, context)
    context_far = swap_quarters(context)
    pre_rest = units(norm_mlp_rest)
    active_rest = exact_gelu(pre_rest)[0].astype(BF)
    active_rest, context, counted, second, context_far, first_mates = meet(
        active_rest, context, counted, second, context_far, first_mates
    )
    count = count + counted

    def branch_rows(context_rows, active_rows):
        return jnp.dot(context_rows, out_weight, preferred_element_type=F32) + jnp.dot(
            active_rows, fc2_weight, preferred_element_type=F32
        )

    def core_total(part):
        blocks = part.reshape(-1, 2, rows, D)
        return blocks[:, 0] + to_core(blocks[:, 1].astype(BF)).astype(F32)

    corner, beside, across = second
    second_mates = [to_core(block) for block in [corner] + beside + across]
    counted = jnp.zeros_like(count)
    bit = 2
    while bit < tp:
        counted = lax.ppermute(count, "tensor", [(t, t ^ bit) for t in range(tp)])
        bit *= 2
        if bit < tp:
            count = count + counted
    part_rest = branch_rows(context[close:], active_rest).reshape(-1, 2, rows, D)
    mates_rest = to_core(part_rest[:, 1].astype(BF))
    part_own = branch_rows(context[:close], after(active_own, part_rest)).reshape(2, rows, D)
    part_own, mates_rest, counted, second_mates = meet(
        part_own, mates_rest, counted, second_mates
    )
    count = count + counted

    sums = part_rest[:, 0] + mates_rest.astype(F32)
    came = [to_y(sums[step - 1].astype(BF), step) for step in range(1, ways)]
    mates_own = to_core(part_own[1].astype(BF))
    counted = flip(count, 4) if dp > 4 else jnp.zeros_like(count)
    last = last_far(second)
    ahead = [first[0]] + beside + [first[1]] + across + [corner]
    mates = (
        [first_mates[0]]
        + second_mates[1:ways]
        + [first_mates[1]]
        + second_mates[ways:]
        + [second_mates[0]]
    )
    far_blocks = [block for pair in zip(ahead, mates) for block in pair]
    norms_far = both_norms(far_blocks, gains, 6 * ways)
    last, norms_far = meet(last, norms_far)
    last = [jnp.concatenate(pair, axis=0) for pair in last]
    far_blocks = [block for v in last for block in (v, to_core(v))]
    norm_attn_far, norm_mlp_far = both_norms(far_blocks, gains, 6 * ways, norms_far)
    came, mates_own, counted, norm_mlp_far = meet(came, mates_own, counted, norm_mlp_far)
    count = count + counted
    mask = 8
    while mask < dp:
        count = count + flip(count, mask)
        mask *= 2
    branch = part_own[0] + mates_own.astype(F32)
    for got in came:
        branch = branch + got.astype(F32)
    output_f = hidden.astype(F32) + branch + out_bias.astype(F32) + fc2_bias.astype(F32)
    mismatch = output_f - teacher.astype(F32)
    error_part = jnp.sum(mask_f[:, None] * mismatch * mismatch)
    grad_out = mask_f[:, None] * mismatch * (2.0 * total_tokens / count[0, 0])
    grad_low = grad_out.astype(BF)
    grad_out, grad_low, norm_mlp_far = meet(grad_out, grad_low, norm_mlp_far)

    grad_y = [from_y(grad_low, step) for step in range(1, ways)]
    grad_first = first_far(grad_low)
    grad_mate = to_core(grad_low)
    fc1_quarter = quarter_of(fc1_weight, 1, quarter)
    fc2_quarter = quarter_of(after(fc2_weight, norm_mlp_far), 0, quarter)
    context_quarter = quarter_of(after(context, norm_mlp_far), 1, quarter)
    pre_far = jnp.dot(norm_mlp_far, fc1_quarter, preferred_element_type=F32) + quarter_of(
        fc1_bias, 0, quarter
    ).astype(F32)
    active_far, slope_far = exact_gelu(pre_far)
    active_far = active_far.astype(BF)
    grad_y, grad_first, active_far, grad_mate, fc2_quarter, context_quarter = meet(
        grad_y, grad_first, active_far, grad_mate, fc2_quarter, context_quarter
    )

    grad_second = second_far(grad_first, grad_y)
    grad_blocks = [grad_low, grad_mate]
    for block in grad_y:
        grad_blocks += [block, to_core(block)]
    grad_near = jnp.concatenate(grad_blocks, axis=0)
    grad_context = contract(grad_near, out_weight, 1, 1).astype(BF)
    grad_qkv = attend_back(qkv_low, grad_context, log_total, prefix_len, spots, table)
    grad_qkv, grad_near, grad_second = meet(grad_qkv, grad_near, grad_second)

    grad_last = last_far(grad_second)
    corner, beside, across = grad_second
    ahead = [grad_first[0]] + beside + [grad_first[1]] + across + [corner]
    mates = [to_core(block) for block in ahead]
    swapped = [flip(quarter_of(grad_qkv, 1, quarter ^ m), m) for m in (1, 2)]
    hidden_pre = jnp.concatenate([pre_own, pre_rest], axis=0)
    grad_inner = (contract(grad_near, fc2_weight, 1, 1) * exact_gelu(hidden_pre)[1]).astype(BF)
    grad_inner, grad_last, mates = meet(grad_inner, grad_last, mates)

    grad_last = [jnp.concatenate(pair, axis=0) for pair in grad_last]
    ahead += grad_last
    mates += [to_core(block) for block in grad_last]
    grad_far = [block for pair in zip(ahead, mates) for block in pair]
    bias_part = jnp.sum(grad_out, axis=0)

    queue = []
    due = {}
    clock, launched = [0], [0]
    results = {}
    token = [grad_near]

    def gate(v):
        return after(v, token[0])

    def flipped(v, mask):
        return v, lambda value: flip(value, mask)

    def travel(low, name, wait):
        mask = 4
        while mask < dp:
            (got,) = yield [flipped(low, mask)], wait
            low = (low.astype(F32) + got.astype(F32)).astype(BF)
            mask, wait = mask * 2, 1
        (across,) = yield [flipped(low, 2)], 1
        near = jnp.concatenate([low, across], axis=0)
        (far,) = yield [flipped(near, 1)], 1
        results.setdefault(name, []).append((near, far))

    def swap_walk(v, into):
        got = yield [flipped(quarter_of(v, 1, quarter ^ 3), 3)], 2
        into.extend(got)

    def last_walk(kept, mates, parts, others, into):
        (got,) = yield [(mates, to_core)], 1
        sums = kept + got.astype(F32)
        total = sums[0]
        for step in range(1, ways):
            (got,) = yield [(sums[step].astype(BF), lambda v, s=step: to_y(v, s))], 1
            total = total + got.astype(F32)
        into["input"] = grad_out + total
        bit = 1
        while bit < tp:
            pairs = [(t, t ^ bit) for t in range(tp)]
            (got,) = yield [(parts, lambda v, p=pairs: lax.ppermute(v, "tensor", p))], 1
            parts = parts + got
            bit *= 2
        parts = jnp.concatenate([parts, others])
        bit = 1
        while bit < dp:
            (got,) = yield [flipped(parts, bit)], 1
            parts = parts + got
            bit *= 2
        into["small"] = parts

    def walk(walker):
        asked = next(walker)
        start(walker, asked, clock[0] - 1)

    def start(walker, asked, now):
        sends, wait = asked
        due.setdefault(now + wait, []).append((walker, [move(v) for v, move in sends]))

    parts_of = {}

    def cut(part, shares):
        unit = part.shape[0] // 16
        edges = [unit * sum(shares[:i]) for i in range(len(shares) + 1)]
        return [lax.slice_in_dim(part, a, b, axis=0) for a, b in zip(edges, edges[1:])]

    def enqueue(name, *units):
        before, _ = parts_of.get(name, (0, 0))
        parts_of[name] = (before + sum(u.shape[0] for u in units), units[0].shape[1])
        queue.extend((unit, name) for unit in units)

    def turn(*others):
        now = clock[0]
        clock[0] = now + 1
        arrived = due.pop(now, [])
        values = [got for _, gots in arrived for got in gots]
        fresh = []
        while queue and launched[0] <= now + 1:
            fresh.append(queue.pop(0) + (max(launched[0] - now, 0) + 1,))
            launched[0] += 1
        tied = list(
            lax.optimization_barrier(tuple(values) + tuple(f[0] for f in fresh) + others)
        )
        token[0] = tied[0]
        asked = []
        for walker, gots in arrived:
            gots = [tied.pop(0) for _ in gots]
            try:
                asked.append((walker, walker.send(gots)))
            except StopIteration:
                pass
        for _, name, wait in fresh:
            walker = travel(tied.pop(0), name, wait)
            asked.append((walker, next(walker)))
        for walker, request in asked:
            start(walker, request, now)
        return tied

    def place_one(whole, near, far, shape, axis, offset):
        rows_here, columns = near.shape[0] // 2, near.shape[1]
        if columns % 128 == 0:
            return place_quarters(whole, near, far, shape, axis, offset, quarter)
        if whole is None:
            whole = jnp.zeros(shape, F32)
        pieces = (near[:rows_here], far[:rows_here], near[rows_here:], far[rows_here:])
        for index, piece in enumerate(pieces):
            spot = quarter ^ index
            start = (
                (spot * (shape[0] // 4) + offset, 0) if axis == 0 else (offset, spot * columns)
            )
            whole = lax.dynamic_update_slice(whole, piece.astype(F32), start)
        return whole

    half = active_far.shape[1] // 2
    rights = [grad_near] + grad_far

    def hidden_lefts(part):
        return [
            (active_own, half, 2, part, 0, 0),
            (active_rest, half, 2, part, 0, close),
            (active_far, half, 0, part, 0, LEN),
        ]

    chunk = half // 2
    kept_columns = context.shape[1] // 4
    enqueue("fc2", *outer_blocks(hidden_lefts(0), rights, [chunk] * 2, quarter))
    grad_norm_attn = back_rows(after(grad_qkv, *queue[0][:1]), qkv_weight, core)
    (grad_norm_attn,) = turn(grad_norm_attn)
    grad_qkv_far = []
    walk(swap_walk(gate(grad_qkv), grad_qkv_far))
    lefts = hidden_lefts(1)
    for index, piece in enumerate([context_quarter] + context_far):
        lefts.append((piece, kept_columns, 0, 0, half, index * LEN))
    *parts, out_part = outer_blocks(
        lefts, [gate(grad_near)] + grad_far, [chunk] * 2 + [kept_columns], quarter
    )
    enqueue("fc2", *parts)
    enqueue("out", out_part)
    swapped = turn(*swapped)
    grad_inner_far = back_blocks([gate(grad_far[0])] + grad_far[1:], fc2_quarter, slope_far)
    (grad_inner_far,) = turn(grad_inner_far)
    inner_quarter = gate(quarter_of(grad_inner, 1, quarter))
    fc1_part = (
        contract(norm_mlp_own, inner_quarter[:close], 0, 0)
        + contract(norm_mlp_rest, inner_quarter[close:], 0, 0)
        + contract(norm_mlp_far, grad_inner_far, 0, 0)
    )
    (fc1_part,) = turn(fc1_part.astype(BF))
    enqueue("fc1", *cut(fc1_part, [4, 4, 4, 4]))
    grad_norm_attn = back_rows(gate(grad_qkv), qkv_weight, 1 - core, grad_norm_attn)
    (grad_norm_attn,) = turn(grad_norm_attn)
    grad_norm_mlp = contract(gate(grad_inner), fc1_weight, 1, 1)
    (grad_norm_mlp,) = turn(grad_norm_mlp)

    near_blocks = lax.optimization_barrier((token[0], *near_blocks))[1:]
    features = jnp.concatenate(near_blocks, axis=0).astype(F32)
    centered = features - jnp.mean(features, axis=-1, keepdims=True)
    inverse = lax.rsqrt(jnp.mean(centered * centered, axis=-1, keepdims=True) + EPSILON)
    xhat = centered * inverse
    gained = grad_norm_attn * gain_attn + grad_norm_mlp * gain_mlp
    lift = jnp.mean(gained, axis=-1, keepdims=True)
    pull = jnp.mean(gained * xhat, axis=-1, keepdims=True)
    tensor_parts = jnp.stack(
        [
            jnp.sum(grad_norm_attn * xhat, axis=0),
            jnp.sum(grad_norm_attn, axis=0),
            jnp.sum(grad_norm_mlp * xhat, axis=0),
            jnp.sum(grad_norm_mlp, axis=0),
            bias_part,
            jnp.full((D,), error_part, F32),
        ]
    ).reshape(-1)
    tensor_parts, lift, pull = turn(tensor_parts, lift, pull)
    grad_hidden = inverse * (gained - lift - xhat * pull)
    blocks = grad_hidden.reshape(ways, 2, rows, D)
    fc1_bias_part = jnp.sum(gate(grad_inner), axis=0, dtype=F32)
    qkv_bias_part = jnp.sum(gate(grad_qkv), axis=0, dtype=F32)
    kept, mates, fc1_bias_part, qkv_bias_part = turn(
        blocks[:, 0], blocks[:, 1].astype(BF), fc1_bias_part, qkv_bias_part
    )
    outcome = {}
    others = jnp.concatenate([fc1_bias_part, qkv_bias_part])
    walk(last_walk(kept, mates, tensor_parts, others, outcome))
    qkv_quarter = gate(quarter_of(grad_qkv, 1, quarter))
    qkv_part = (
        contract(norm_attn_own, qkv_quarter[:close], 0, 0)
        + contract(norm_attn_rest, qkv_quarter[close:], 0, 0)
        + contract(norm_attn_far, jnp.concatenate([*swapped, *grad_qkv_far], axis=0), 0, 0)
    )
    (qkv_part,) = turn(qkv_part.astype(BF))
    enqueue("qkv", *cut(qkv_part, [4, 4, 4, 2, 1, 1]))
    axes = {"fc2": 0, "out": 0, "fc1": 1, "qkv": 1}
    placed = {name: (None, 0, 0) for name in axes}

    def place(name):
        whole, done, offset = placed[name]
        pieces = results[name][done]
        lengths, columns = parts_of[name]
        shape = (4 * lengths, columns) if axes[name] == 0 else (lengths, 4 * columns)
        whole = place_one(whole, *pieces, shape, axes[name], offset)
        placed[name] = (whole, done + 1, offset + pieces[0].shape[0] // 2)

    while queue or due:
        ready = []
        for name in axes:
            if len(ready) < 2 and len(results.get(name, [])) > placed[name][1]:
                place(name)
                ready.append(name)
        wholes = turn(*[placed[name][0] for name in ready])
        for name, whole in zip(ready, wholes):
            placed[name] = (whole,) + placed[name][1:]
    for name in axes:
        while len(results[name]) > placed[name][1]:
            place(name)
    input_grad = outcome["input"]
    small = outcome["small"]
    vectors = small[: 6 * D].reshape(6, D)
    fc1_bias_grad = small[6 * D : 6 * D + fc1_bias_part.shape[0]]
    qkv_bias_grad = small[6 * D + fc1_bias_part.shape[0] :]
    loss_value = vectors[5, 0] / (count[0, 0] * D)
    fc2_weight_grad, out_weight_grad = placed["fc2"][0], placed["out"][0]
    fc1_weight_grad, qkv_weight_grad = placed["fc1"][0], placed["qkv"][0]
    return (
        output_f.astype(BF),
        loss_value,
        input_grad,
        vectors[0],
        vectors[1],
        vectors[2],
        vectors[3],
        qkv_weight_grad,
        qkv_bias_grad,
        out_weight_grad,
        vectors[4],
        fc1_weight_grad,
        fc1_bias_grad,
        fc2_weight_grad,
        vectors[4],
    )


def solution(mesh):
    tokens = P(("dp", "tensor"), None)
    columns, lanes, down, whole = P(None, "tensor"), P("tensor"), P("tensor", None), P()
    in_specs = (
        tokens,
        tokens,
        P(("dp", "tensor")),
        P("dp"),
        whole,
        whole,
        whole,
        whole,
        columns,
        lanes,
        down,
        whole,
        columns,
        lanes,
        down,
        whole,
    )
    out_specs = (
        tokens,
        whole,
        tokens,
        whole,
        whole,
        whole,
        whole,
        columns,
        lanes,
        down,
        whole,
        columns,
        lanes,
        down,
        whole,
    )
    return jax.shard_map(
        on_device, mesh=mesh, in_specs=in_specs, out_specs=out_specs, check_vma=False
    )
```

```python
import functools

import jax
import jax.numpy as jnp
import numpy as np
from jax import lax
from jax.experimental import pallas as pl
from jax.experimental.pallas import tpu as pltpu
from jax.sharding import PartitionSpec as P

D = 2048
HD = 256
ROT = 64
LEN = 1024
EPSILON = 1e-05
BF = jnp.bfloat16
F32 = jnp.float32
SMALL = pl.CostEstimate(flops=1 << 20, bytes_accessed=1 << 16, transcendentals=0)


def rotary_table(length):
    half = ROT // 2
    frequency = (10000.0 ** (-2.0 * np.arange(half, dtype=np.float32) / ROT)).astype(np.float32)
    angles = np.arange(length, dtype=np.float32)[:, None] * frequency[None, :]
    cosine, sine = np.cos(angles), np.sin(angles)
    table = np.zeros((length, 3 * 128), np.float32)
    table[:, ROT:128] = 1.0
    table[:, :half] = table[:, half:ROT] = cosine
    table[:, 128 : 128 + half] = -sine
    table[:, 256 + half : 256 + ROT] = sine
    return table


def contract(left_side, right_side, left_dim, right_dim):
    return lax.dot_general(
        left_side,
        right_side,
        (((left_dim,), (right_dim,)), ((), ())),
        preferred_element_type=F32,
    )


def exact_gelu(pre_act):
    below = 0.5 + 0.5 * lax.erf(pre_act * 0.5**0.5)
    density = jnp.exp(-0.5 * pre_act * pre_act) * (2.0 * jnp.pi) ** -0.5
    return pre_act * below, below + pre_act * density


def after(value, *earlier):
    return lax.optimization_barrier((value,) + earlier)[0]


def turned(block, keep, up, down, sign):
    head = block[:, :128]
    half = ROT // 2
    moved = head * keep + sign * (
        pltpu.roll(head, 128 - half, 1) * up + pltpu.roll(head, half, 1) * down
    )
    return jnp.concatenate([moved, block[:, 128:]], axis=1)


def qkv_kernel(x_ref, w_ref, b_ref, keep_ref, up_ref, down_ref, *refs):
    o_ref = refs[-1]
    kind = pl.program_id(0) % 3
    rows = x_ref.shape[0]
    tile = min(rows, 512)

    def project(at):
        return (
            jnp.dot(x_ref[at, :], w_ref[...], preferred_element_type=F32)
            + b_ref[...].astype(F32)
        )

    for start in range(0, rows, tile):
        at = pl.ds(start, min(tile, rows - start))

        @pl.when(kind == 2)
        def _(at=at):
            o_ref[at, :] = project(at).astype(BF)

        @pl.when(kind != 2)
        def _(at=at):
            o_ref[at, :] = turned(
                project(at), keep_ref[at, :], up_ref[at, :], down_ref[at, :], 1.0
            ).astype(BF)


def project_qkv(normed, weight, bias, table, length, whole=None):
    rows, width = normed.shape
    columns = weight.shape[1]
    part = 0 if whole is None else 1
    if part and rows * 2 != length:
        rest = project_qkv(normed, weight, bias, table[length - rows :], rows)
        return jnp.concatenate([whole[: length - rows], rest], axis=0)
    return pl.pallas_call(
        qkv_kernel,
        grid=(columns // HD,),
        in_specs=[
            pl.BlockSpec((rows, width), lambda j: (0, 0)),
            pl.BlockSpec((width, HD), lambda j: (0, j)),
            pl.BlockSpec((1, HD), lambda j: (0, j)),
        ]
        + [pl.BlockSpec((rows, 128), lambda j, k=k: (part, k)) for k in range(3)]
        + [pl.BlockSpec(memory_space=pl.ANY)] * part,
        out_specs=pl.BlockSpec((rows, HD), lambda j: (part, j)),
        out_shape=jax.ShapeDtypeStruct((length, columns), BF),
        input_output_aliases={6: 0} if part else {},
        compiler_params=pltpu.CompilerParams(vmem_limit_bytes=40 << 20),
        cost_estimate=SMALL,
        name="qkv_rotary",
    )(normed, weight, bias[None, :], table, table, table, *([whole] if part else []))


def visible_scores(queries, keys, row_spots, key_spots, prefix):
    scores = lax.dot_general(
        queries, keys, (((1,), (1,)), ((), ())), preferred_element_type=F32
    ) * (HD**-0.5)
    allowed = (key_spots <= row_spots) | (key_spots < prefix)
    return jnp.where(allowed, scores, -jnp.inf)


def attend_kernel(prefix_ref, q_ref, k_ref, v_ref, rows_ref, keys_ref, o_ref, log_ref):
    scores = visible_scores(
        q_ref[...], k_ref[...], rows_ref[...], keys_ref[...], prefix_ref[0]
    )
    top = jnp.max(scores, axis=-1, keepdims=True)
    weights = jnp.exp(scores - top)
    total = jnp.sum(weights, axis=-1, keepdims=True)
    probs = (weights * (1.0 / total)).astype(BF)
    o_ref[...] = jnp.dot(probs, v_ref[...], preferred_element_type=F32).astype(BF)
    log_ref[0] = top + jnp.log(total)


def attend(qkv, prefix, spots):
    length = qkv.shape[0]
    heads = qkv.shape[1] // (3 * HD)
    tile = length // 4
    whole = lambda part: pl.BlockSpec((length, HD), lambda h, i, p: (0, 3 * h + part))
    return pl.pallas_call(
        attend_kernel,
        grid_spec=pltpu.PrefetchScalarGridSpec(
            num_scalar_prefetch=1,
            grid=(heads, 4),
            in_specs=[
                pl.BlockSpec((tile, HD), lambda h, i, p: (i, 3 * h)),
                whole(1),
                whole(2),
                pl.BlockSpec((tile, 1), lambda h, i, p: (i, 0)),
                pl.BlockSpec((1, length), lambda h, i, p: (0, 0)),
            ],
            out_specs=[
                pl.BlockSpec((tile, HD), lambda h, i, p: (i, h)),
                pl.BlockSpec((1, tile, 1), lambda h, i, p: (h, i, 0)),
            ],
        ),
        out_shape=[
            jax.ShapeDtypeStruct((length, heads * HD), BF),
            jax.ShapeDtypeStruct((heads, length, 1), F32),
        ],
        compiler_params=pltpu.CompilerParams(vmem_limit_bytes=32 << 20),
        cost_estimate=SMALL,
        name="attend",
    )(prefix, qkv, qkv, qkv, spots[:, None], spots[None, :])


def attend_back_kernel(
    prefix_ref, q_ref, k_ref, v_ref, g_ref, log_ref, rows_ref, keys_ref, keep_ref, up_ref,
    down_ref, o_ref, dk_ref, dv_ref,
):
    length = q_ref.shape[0]
    tile = length // 4
    scale = HD**-0.5
    for i in range(4):
        at = pl.ds(i * tile, tile)
        q, g = q_ref[at, :], g_ref[at, :]
        scores = visible_scores(q, k_ref[...], rows_ref[at, :], keys_ref[...], prefix_ref[0])
        probs = jnp.exp(scores - log_ref[0, at, :])
        grad_probs = lax.dot_general(
            g, v_ref[...], (((1,), (1,)), ((), ())), preferred_element_type=F32
        )
        dots = jnp.sum(probs * grad_probs, axis=-1, keepdims=True)
        grad_scores = (probs * (grad_probs - dots)).astype(BF)
        dq = jnp.dot(grad_scores, k_ref[...], preferred_element_type=F32) * scale
        o_ref[at, :HD] = turned(
            dq, keep_ref[at, :], up_ref[at, :], down_ref[at, :], -1.0
        ).astype(BF)
        dk = contract(grad_scores, q, 0, 0)
        dv = contract(probs.astype(BF), g, 0, 0)
        if i == 0:
            dk_ref[...] = dk
            dv_ref[...] = dv
        else:
            dk_ref[...] += dk
            dv_ref[...] += dv
    o_ref[:, HD : 2 * HD] = turned(
        dk_ref[...] * scale, keep_ref[...], up_ref[...], down_ref[...], -1.0
    ).astype(BF)
    o_ref[:, 2 * HD :] = dv_ref[...].astype(BF)


def attend_back(qkv, grad_context, log_total, prefix, spots, table):
    length = qkv.shape[0]
    heads = qkv.shape[1] // (3 * HD)
    part = lambda n: pl.BlockSpec((length, HD), lambda h, p: (0, 3 * h + n))
    return pl.pallas_call(
        attend_back_kernel,
        grid_spec=pltpu.PrefetchScalarGridSpec(
            num_scalar_prefetch=1,
            grid=(heads,),
            in_specs=[
                part(0),
                part(1),
                part(2),
                pl.BlockSpec((length, HD), lambda h, p: (0, h)),
                pl.BlockSpec((1, length, 1), lambda h, p: (h, 0, 0)),
                pl.BlockSpec((length, 1), lambda h, p: (0, 0)),
                pl.BlockSpec((1, length), lambda h, p: (0, 0)),
            ]
            + [pl.BlockSpec((length, 128), lambda h, p, k=k: (0, k)) for k in range(3)],
            out_specs=pl.BlockSpec((length, 3 * HD), lambda h, p: (0, h)),
            scratch_shapes=[pltpu.VMEM((length, HD), F32), pltpu.VMEM((length, HD), F32)],
        ),
        out_shape=jax.ShapeDtypeStruct((length, heads * 3 * HD), BF),
        compiler_params=pltpu.CompilerParams(vmem_limit_bytes=48 << 20),
        cost_estimate=SMALL,
        name="attend_back",
    )(prefix, qkv, qkv, qkv, grad_context, log_total, spots[:, None], spots[None, :], table, table, table)


def norm_back_kernel(
    count, grad_qkv_ref, grad_inner_ref, qkv_ref, fc1_ref, gain_a_ref, gain_m_ref, *refs
):
    blocks, (o_ref, sums_ref, qkv_sum_ref, inner_sum_ref, rows_ref) = refs[:count], refs[count:]
    step = pl.program_id(0)
    for index, block in enumerate(blocks):

        @pl.when(step == index)
        def _(block=block):
            rows_ref[...] = block[...]

    features = rows_ref[...].astype(F32)
    centered = features - jnp.mean(features, axis=-1, keepdims=True)
    inverse = lax.rsqrt(jnp.mean(centered * centered, axis=-1, keepdims=True) + EPSILON)
    xhat = centered * inverse
    grad_attn = contract(grad_qkv_ref[...], qkv_ref[...], 1, 1)
    grad_mlp = contract(grad_inner_ref[...], fc1_ref[...], 1, 1)
    gained = grad_attn * gain_a_ref[...].astype(F32) + grad_mlp * gain_m_ref[...].astype(F32)
    o_ref[...] = inverse * (
        gained
        - jnp.mean(gained, axis=-1, keepdims=True)
        - xhat * jnp.mean(gained * xhat, axis=-1, keepdims=True)
    )
    pairs = (
        (sums_ref, 0, grad_attn * xhat),
        (sums_ref, 1, grad_attn),
        (sums_ref, 2, grad_mlp * xhat),
        (sums_ref, 3, grad_mlp),
        (qkv_sum_ref, 0, grad_qkv_ref[...].astype(F32)),
        (inner_sum_ref, 0, grad_inner_ref[...].astype(F32)),
    )
    for ref, row, values in pairs:
        total = jnp.sum(values, axis=0, keepdims=True)

        @pl.when(step == 0)
        def _(ref=ref, row=row, total=total):
            ref[row : row + 1, :] = total

        @pl.when(step > 0)
        def _(ref=ref, row=row, total=total):
            ref[row : row + 1, :] += total


def norm_back(grad_qkv, grad_inner, qkv_weight, fc1_weight, gains, blocks):
    count = len(blocks)
    rows, width = blocks[0].shape
    each = lambda a: pl.BlockSpec((rows, a.shape[1]), lambda i: (i, 0))
    full = lambda a: pl.BlockSpec(a.shape, lambda i: (0, 0), pipeline_mode=pl.Buffered(1))
    sums = [(8, width), (8, grad_qkv.shape[1]), (8, grad_inner.shape[1])]
    return pl.pallas_call(
        functools.partial(norm_back_kernel, count),
        grid=(count,),
        in_specs=[each(grad_qkv), each(grad_inner), full(qkv_weight), full(fc1_weight)]
        + [full(gains[0]), full(gains[2])]
        + [full(b) for b in blocks],
        out_specs=[pl.BlockSpec((rows, width), lambda i: (i, 0))]
        + [pl.BlockSpec(shape, lambda i: (0, 0)) for shape in sums],
        out_shape=[jax.ShapeDtypeStruct((count * rows, width), F32)]
        + [jax.ShapeDtypeStruct(shape, F32) for shape in sums],
        scratch_shapes=[pltpu.VMEM((rows, width), BF)],
        compiler_params=pltpu.CompilerParams(vmem_limit_bytes=56 << 20),
        cost_estimate=SMALL,
        name="norm_back",
    )(grad_qkv, grad_inner, qkv_weight, fc1_weight, gains[0], gains[2], *blocks)


def place_kernel(quarter_ref, *refs):
    pieces, out_ref = refs[-5:-1], refs[-1]
    for index, piece in enumerate(pieces):

        @pl.when(pl.program_id(0) == index)
        def _(piece=piece):
            out_ref[...] = piece[...].astype(F32)


def place_quarters(whole, near, far, shape, axis, offset, quarter):
    rows, columns = near.shape[0] // 2, near.shape[1]
    if axis == 0:
        each, first_row = shape[0] // 4 // rows, offset // rows
        spot = lambda k, q: ((q[0] ^ k) * each + first_row, 0)
    else:
        spot = lambda k, q: (offset // rows, q[0] ^ k)
    first = whole is None
    operands = ([] if first else [whole]) + [near, far, near, far]
    return pl.pallas_call(
        place_kernel,
        grid_spec=pltpu.PrefetchScalarGridSpec(
            num_scalar_prefetch=1,
            grid=(4,),
            in_specs=([] if first else [pl.BlockSpec(memory_space=pl.ANY)])
            + [pl.BlockSpec((rows, columns), lambda k, q, h=h: (h, 0)) for h in (0, 0, 1, 1)],
            out_specs=pl.BlockSpec((rows, columns), spot),
        ),
        out_shape=jax.ShapeDtypeStruct(shape, F32),
        input_output_aliases={} if first else {1: 0},
        compiler_params=pltpu.CompilerParams(vmem_limit_bytes=24 << 20),
        cost_estimate=SMALL,
        name="place_quarters",
    )(quarter.reshape(1), *operands)


def norms_kernel(count, *refs):
    gains, blocks, (attn_ref, mlp_ref) = refs[:4], refs[4 : 4 + count], refs[-2:]
    for index, block in enumerate(blocks):

        @pl.when(pl.program_id(0) == index)
        def _(block=block):
            features = block[...].astype(F32)
            average = jnp.mean(features, axis=-1, keepdims=True)
            centered = features - average
            spread = jnp.mean(centered * centered, axis=-1, keepdims=True)
            xhat = centered * lax.rsqrt(spread + EPSILON)
            gain_a, shift_a, gain_m, shift_m = (ref[...].astype(F32) for ref in gains)
            attn_ref[...] = (xhat * gain_a + shift_a).astype(BF)
            mlp_ref[...] = (xhat * gain_m + shift_m).astype(BF)


def both_norms(blocks, gains, total=None, into=()):
    count = len(blocks)
    total = total or count
    skip = total - count if into else 0
    rows, width = blocks[0].shape
    shape = jax.ShapeDtypeStruct((total * rows, width), BF)
    return pl.pallas_call(
        functools.partial(norms_kernel, count),
        grid=(count,),
        in_specs=[pl.BlockSpec((1, width), lambda i: (0, 0))] * 4
        + [pl.BlockSpec((rows, width), lambda i: (0, 0))] * count
        + [pl.BlockSpec(memory_space=pl.ANY)] * len(into),
        out_specs=[pl.BlockSpec((rows, width), lambda i: (i + skip, 0))] * 2,
        out_shape=[shape, shape],
        input_output_aliases={4 + count: 0, 5 + count: 1} if into else {},
        compiler_params=pltpu.CompilerParams(vmem_limit_bytes=48 << 20),
        cost_estimate=SMALL,
        name="both_norms",
    )(*gains, *blocks, *into)


def outer_kernel(lefts, pieces, outs, _, *refs):
    left_refs, rights = refs[:lefts], refs[lefts : -2 - outs]
    out_refs, (left_ref, joined_ref) = refs[-2 - outs : -2], refs[-2:]

    @pl.when(pl.program_id(0) == 0)
    def _():
        for ref, (row, column) in zip(left_refs, pieces):
            count, width = ref.shape
            step = min(count, 256)
            for start in range(0, count, step):
                left_ref[pl.ds(row, width), pl.ds(column + start, step)] = ref[
                    pl.ds(start, step), :
                ].T

    column = 0
    for ref in rights:
        joined_ref[pl.ds(column, ref.shape[0]), :] = ref[...]
        column += ref.shape[0]
    total = jnp.dot(left_ref[...], joined_ref[...], preferred_element_type=F32).astype(BF)
    row = 0
    for ref in out_refs:
        ref[...] = total[row : row + ref.shape[0], :]
        row += ref.shape[0]


def outer_blocks(lefts, rights, sizes, quarter):
    width = rights[0].shape[1]
    tokens = sum(r.shape[0] for r in rights)
    left = sum(sizes)
    tile = 512
    specs = [
        pl.BlockSpec((a.shape[0], taken), lambda j, q, m=times, o=offset: (0, q[0] * m + o))
        for a, taken, times, offset, _, _ in lefts
    ]
    pieces = [(row, token) for *_, row, token in lefts]
    return pl.pallas_call(
        functools.partial(outer_kernel, len(lefts), pieces, len(sizes)),
        grid_spec=pltpu.PrefetchScalarGridSpec(
            num_scalar_prefetch=1,
            grid=(width // tile,),
            in_specs=specs
            + [pl.BlockSpec((r.shape[0], tile), lambda j, q: (0, j)) for r in rights],
            out_specs=[pl.BlockSpec((size, tile), lambda j, q: (0, j)) for size in sizes],
            scratch_shapes=[pltpu.VMEM((left, tokens), BF), pltpu.VMEM((tokens, tile), BF)],
        ),
        out_shape=[jax.ShapeDtypeStruct((size, width), BF) for size in sizes],
        compiler_params=pltpu.CompilerParams(vmem_limit_bytes=56 << 20),
        cost_estimate=SMALL,
        name="outer_blocks",
    )(quarter.reshape(1), *[a for a, *_ in lefts], *rights)


def back_kernel(weight_ref, slope_ref, *refs):
    blocks, o_ref = refs[:-1], refs[-1]
    for index, block in enumerate(blocks):

        @pl.when(pl.program_id(0) == index)
        def _(block=block):
            o_ref[...] = (contract(block[...], weight_ref[...], 1, 1) * slope_ref[...]).astype(BF)


def back_blocks(blocks, weight, slope):
    rows, width = blocks[0].shape
    units = weight.shape[0]
    count = len(blocks)
    return pl.pallas_call(
        back_kernel,
        grid=(count,),
        in_specs=[
            pl.BlockSpec((units, width), lambda i: (0, 0)),
            pl.BlockSpec((rows, units), lambda i: (i, 0)),
        ]
        + [pl.BlockSpec((rows, width), lambda i: (0, 0))] * count,
        out_specs=pl.BlockSpec((rows, units), lambda i: (i, 0)),
        out_shape=jax.ShapeDtypeStruct((count * rows, units), BF),
        compiler_params=pltpu.CompilerParams(vmem_limit_bytes=56 << 20),
        cost_estimate=SMALL,
        name="back_blocks",
    )(weight, slope, *blocks)


def on_device(
    hidden,
    teacher,
    valid_mask,
    prefix_len,
    ln1_gain,
    ln1_bias,
    ln2_gain,
    ln2_bias,
    qkv_weight,
    qkv_bias,
    out_weight,
    out_bias,
    fc1_weight,
    fc1_bias,
    fc2_weight,
    fc2_bias,
):
    rows = hidden.shape[0]
    dp = lax.axis_size("dp")
    tp = lax.axis_size("tensor")
    ways = tp // 2
    squares = dp // 4
    total_tokens = dp * tp * rows
    heads = qkv_weight.shape[1] // (3 * HD)
    dp_index = lax.axis_index("dp")
    tp_index = lax.axis_index("tensor")
    core, y = tp_index % 2, tp_index // 2
    quarter = dp_index % 4

    def to_core(v):
        return lax.ppermute(v, "tensor", [(t, t ^ 1) for t in range(tp)])

    def from_y(v, step):
        pairs = [(t, ((t // 2 - step) % ways) * 2 + t % 2) for t in range(tp)]
        return lax.ppermute(v, "tensor", pairs)

    def to_y(v, step):
        pairs = [(t, ((t // 2 + step) % ways) * 2 + t % 2) for t in range(tp)]
        return lax.ppermute(v, "tensor", pairs)

    def flip(v, mask):
        return lax.ppermute(v, "dp", [(d, d ^ mask) for d in range(dp)])

    block_ids = [
        ((y + step) % ways) * 2 + (core if mate == 0 else 1 - core)
        for step in range(ways)
        for mate in (0, 1)
    ]

    def gather_near(own):
        over_y = [from_y(own, step) for step in range(1, ways)]
        parts = []
        for block in [own] + over_y:
            parts += [block, to_core(block)]
        return parts, over_y

    def first_far(own):
        return [flip(own, 1), flip(own, 2)]

    def second_far(first, over_y):
        corner = flip(first[1], 1)
        beside = [from_y(first[0], step) for step in range(1, ways)]
        across = [flip(block, 2) for block in over_y]
        return corner, beside, across

    def last_far(second):
        half = rows // 2
        return [(flip(v[:half], 1), flip(u[half:], 2)) for u, v in zip(second[1], second[2])]

    def meet(*trees):
        leaves, shape = jax.tree.flatten(trees)
        return jax.tree.unflatten(shape, lax.optimization_barrier(tuple(leaves)))

    def quarter_of(v, axis, index):
        size = v.shape[axis] // 4
        return lax.dynamic_slice_in_dim(v, index * size, size, axis)

    def swap_quarters(v):
        return [flip(quarter_of(v, 1, quarter ^ mask), mask) for mask in (1, 2, 3)]

    gain_attn = ln1_gain.astype(F32)
    shift_attn = ln1_bias.astype(F32)
    gain_mlp = ln2_gain.astype(F32)
    shift_mlp = ln2_bias.astype(F32)
    gains = [v[None, :] for v in (ln1_gain, ln1_bias, ln2_gain, ln2_bias)]
    close = 2 * rows

    def units(normed):
        return jnp.dot(normed, fc1_weight, preferred_element_type=F32) + fc1_bias.astype(F32)

    near_blocks, hidden_y = gather_near(hidden)
    first = first_far(hidden)
    norm_attn_own, norm_mlp_own = both_norms(near_blocks[:2], gains)
    mask_f = after(valid_mask, norm_mlp_own).astype(F32)
    count = jnp.full((8, 128), jnp.sum(mask_f), F32)
    count = count + to_core(count)
    counted = flip(count, 1)
    pre_own = units(norm_mlp_own)
    active_own = exact_gelu(pre_own)[0].astype(BF)
    table = jnp.concatenate(
        [
            lax.dynamic_slice_in_dim(jnp.asarray(rotary_table(LEN)), b * rows, rows, 0)
            for b in block_ids
        ],
        axis=0,
    )
    spots = jnp.concatenate([b * rows + jnp.arange(rows, dtype=jnp.int32) for b in block_ids])
    active_own, table = after(active_own, table), after(table, active_own)
    qkv_own = project_qkv(norm_attn_own, qkv_weight, qkv_bias, table, LEN)
    active_own, qkv_own, counted, first, hidden_y = meet(
        active_own, qkv_own, counted, first, hidden_y
    )
    count = count + counted

    near_blocks = near_blocks[:2]
    for block in hidden_y:
        near_blocks += [block, to_core(block)]
    second = second_far(first, hidden_y)
    first_mates = [to_core(block) for block in first]
    counted = flip(count, 2)
    norm_attn_rest, norm_mlp_rest = both_norms(near_blocks[2:], gains)
    qkv_low = project_qkv(norm_attn_rest, qkv_weight, qkv_bias, table, LEN, qkv_own)
    context, log_total = attend(qkv_low, prefix_len, spots)
    norm_mlp_rest = after(norm_mlp_rest, context)
    context_far = swap_quarters(context)
    pre_rest = units(norm_mlp_rest)
    active_rest = exact_gelu(pre_rest)[0].astype(BF)
    active_rest, context, counted, second, context_far, first_mates = meet(
        active_rest, context, counted, second, context_far, first_mates
    )
    count = count + counted

    def branch_rows(context_rows, active_rows):
        return jnp.dot(context_rows, out_weight, preferred_element_type=F32) + jnp.dot(
            active_rows, fc2_weight, preferred_element_type=F32
        )

    def core_total(part):
        blocks = part.reshape(-1, 2, rows, D)
        return blocks[:, 0] + to_core(blocks[:, 1].astype(BF)).astype(F32)

    corner, beside, across = second
    second_mates = [to_core(block) for block in [corner] + beside + across]
    counted = jnp.zeros_like(count)
    bit = 2
    while bit < tp:
        counted = lax.ppermute(count, "tensor", [(t, t ^ bit) for t in range(tp)])
        bit *= 2
        if bit < tp:
            count = count + counted
    part_rest = branch_rows(context[close:], active_rest).reshape(-1, 2, rows, D)
    mates_rest = to_core(part_rest[:, 1].astype(BF))
    part_own = branch_rows(context[:close], after(active_own, part_rest)).reshape(2, rows, D)
    part_own, mates_rest, counted, second_mates = meet(
        part_own, mates_rest, counted, second_mates
    )
    count = count + counted

    sums = part_rest[:, 0] + mates_rest.astype(F32)
    came = [to_y(sums[step - 1].astype(BF), step) for step in range(1, ways)]
    mates_own = to_core(part_own[1].astype(BF))
    counted = flip(count, 4) if dp > 4 else jnp.zeros_like(count)
    last = last_far(second)
    ahead = [first[0]] + beside + [first[1]] + across + [corner]
    mates = (
        [first_mates[0]]
        + second_mates[1:ways]
        + [first_mates[1]]
        + second_mates[ways:]
        + [second_mates[0]]
    )
    far_blocks = [block for pair in zip(ahead, mates) for block in pair]
    norms_far = both_norms(far_blocks, gains, 6 * ways)
    came, mates_own, counted, norms_far, last = meet(came, mates_own, counted, norms_far, last)
    count = count + counted
    mask = 8
    while mask < dp:
        count = count + flip(count, mask)
        mask *= 2
    branch = part_own[0] + mates_own.astype(F32)
    for got in came:
        branch = branch + got.astype(F32)
    output_f = hidden.astype(F32) + branch + out_bias.astype(F32) + fc2_bias.astype(F32)
    mismatch = output_f - teacher.astype(F32)
    error_part = jnp.sum(mask_f[:, None] * mismatch * mismatch)
    grad_out = mask_f[:, None] * mismatch * (2.0 * total_tokens / count[0, 0])
    grad_low = grad_out.astype(BF)
    grad_out, grad_low, last = meet(grad_out, grad_low, last)

    grad_y = [from_y(grad_low, step) for step in range(1, ways)]
    grad_first = first_far(grad_low)
    grad_mate = to_core(grad_low)
    last = [jnp.concatenate([after(v, grad_mate), u], axis=0) for v, u in last]
    far_blocks = [block for v in last for block in (v, to_core(v))]
    norm_attn_far, norm_mlp_far = both_norms(far_blocks, gains, 6 * ways, norms_far)
    fc1_quarter = quarter_of(fc1_weight, 1, quarter)
    fc2_quarter = quarter_of(after(fc2_weight, norm_mlp_far), 0, quarter)
    context_quarter = quarter_of(after(context, norm_mlp_far), 1, quarter)
    pre_far = jnp.dot(norm_mlp_far, fc1_quarter, preferred_element_type=F32) + quarter_of(
        fc1_bias, 0, quarter
    ).astype(F32)
    active_far, slope_far = exact_gelu(pre_far)
    active_far = active_far.astype(BF)
    grad_y, grad_first, active_far, grad_mate, fc2_quarter, context_quarter = meet(
        grad_y, grad_first, active_far, grad_mate, fc2_quarter, context_quarter
    )

    grad_second = second_far(grad_first, grad_y)
    grad_blocks = [grad_low, grad_mate]
    for block in grad_y:
        grad_blocks += [block, to_core(block)]
    grad_near = jnp.concatenate(grad_blocks, axis=0)
    hidden_pre = jnp.concatenate([pre_own, pre_rest], axis=0)
    grad_inner = (contract(grad_near, fc2_weight, 1, 1) * exact_gelu(hidden_pre)[1]).astype(BF)
    grad_context = contract(grad_near, out_weight, 1, 1).astype(BF)
    grad_inner, grad_context, grad_near, grad_second = meet(
        grad_inner, grad_context, grad_near, grad_second
    )

    grad_last = last_far(grad_second)
    corner, beside, across = grad_second
    ahead = [grad_first[0]] + beside + [grad_first[1]] + across + [corner]
    mates = [to_core(block) for block in ahead]
    grad_qkv = attend_back(qkv_low, grad_context, log_total, prefix_len, spots, table)
    grad_qkv, grad_last, mates = meet(grad_qkv, grad_last, mates)

    last_mates = [tuple(to_core(v) for v in pair) for pair in grad_last]
    swapped = [flip(quarter_of(grad_qkv, 1, quarter ^ m), m) for m in (1, 2)]
    grad_far = [block for pair in zip(ahead, mates) for block in pair]
    halves = [v for pair, mate in zip(grad_last, last_mates) for v in pair + mate]

    queue = []
    due = {}
    clock, launched = [0], [0]
    results = {}
    token = [grad_near]

    def gate(v):
        return after(v, token[0])

    def flipped(v, mask):
        return v, lambda value: flip(value, mask)

    def travel(low, name, wait):
        mask = 4
        while mask < dp:
            (got,) = yield [flipped(low, mask)], wait
            low = (low.astype(F32) + got.astype(F32)).astype(BF)
            mask, wait = mask * 2, 1
        (across,) = yield [flipped(low, 2)], 1
        near = jnp.concatenate([low, across], axis=0)
        (far,) = yield [flipped(near, 1)], 1
        results.setdefault(name, []).append((near, far))

    def swap_walk(v, into):
        got = yield [flipped(quarter_of(v, 1, quarter ^ 3), 3)], 2
        into.extend(got)

    def last_walk(kept, mates, parts, others, into):
        (got,) = yield [(mates, to_core)], 1
        sums = kept + got.astype(F32)
        total = sums[0]
        for step in range(1, ways):
            (got,) = yield [(sums[step].astype(BF), lambda v, s=step: to_y(v, s))], 1
            total = total + got.astype(F32)
        into["input"] = grad_out + total
        bit = 1
        while bit < tp:
            pairs = [(t, t ^ bit) for t in range(tp)]
            (got,) = yield [(parts, lambda v, p=pairs: lax.ppermute(v, "tensor", p))], 1
            parts = parts + got
            bit *= 2
        parts = jnp.concatenate([parts, others])
        bit = 1
        while bit < dp:
            (got,) = yield [flipped(parts, bit)], 1
            parts = parts + got
            bit *= 2
        into["small"] = parts

    def walk(walker):
        asked = next(walker)
        start(walker, asked, clock[0] - 1)

    def start(walker, asked, now):
        sends, wait = asked
        due.setdefault(now + wait, []).append((walker, [move(v) for v, move in sends]))

    parts_of = {}

    def cut(part, shares):
        unit = part.shape[0] // 16
        edges = [unit * sum(shares[:i]) for i in range(len(shares) + 1)]
        return [lax.slice_in_dim(part, a, b, axis=0) for a, b in zip(edges, edges[1:])]

    def enqueue(name, *units):
        before, _ = parts_of.get(name, (0, 0))
        parts_of[name] = (before + sum(u.shape[0] for u in units), units[0].shape[1])
        queue.extend((unit, name) for unit in units)

    def turn(*others):
        now = clock[0]
        clock[0] = now + 1
        arrived = due.pop(now, [])
        values = [got for _, gots in arrived for got in gots]
        fresh = []
        while queue and launched[0] <= now + 1:
            fresh.append(queue.pop(0) + (max(launched[0] - now, 0) + 1,))
            launched[0] += 1
        tied = list(
            lax.optimization_barrier(tuple(values) + tuple(f[0] for f in fresh) + others)
        )
        token[0] = tied[0]
        asked = []
        for walker, gots in arrived:
            gots = [tied.pop(0) for _ in gots]
            try:
                asked.append((walker, walker.send(gots)))
            except StopIteration:
                pass
        for _, name, wait in fresh:
            walker = travel(tied.pop(0), name, wait)
            asked.append((walker, next(walker)))
        for walker, request in asked:
            start(walker, request, now)
        return tied

    def place_one(whole, near, far, shape, axis, offset):
        rows_here, columns = near.shape[0] // 2, near.shape[1]
        if columns % 128 == 0:
            return place_quarters(whole, near, far, shape, axis, offset, quarter)
        if whole is None:
            whole = jnp.zeros(shape, F32)
        pieces = (near[:rows_here], far[:rows_here], near[rows_here:], far[rows_here:])
        for index, piece in enumerate(pieces):
            spot = quarter ^ index
            start = (
                (spot * (shape[0] // 4) + offset, 0) if axis == 0 else (offset, spot * columns)
            )
            whole = lax.dynamic_update_slice(whole, piece.astype(F32), start)
        return whole

    half = active_far.shape[1] // 2
    rights = [grad_near] + grad_far + halves

    def hidden_lefts(part):
        return [
            (active_own, half, 2, part, 0, 0),
            (active_rest, half, 2, part, 0, close),
            (active_far, half, 0, part, 0, LEN),
        ]

    chunk = half // 2
    kept_columns = context.shape[1] // 4
    enqueue("fc2", *outer_blocks(hidden_lefts(0), rights, [chunk] * 2, quarter))
    turn()
    grad_qkv_far = []
    walk(swap_walk(gate(grad_qkv), grad_qkv_far))
    lefts = hidden_lefts(1)
    for index, piece in enumerate([context_quarter] + context_far):
        lefts.append((piece, kept_columns, 0, 0, half, index * LEN))
    *parts, out_part = outer_blocks(
        lefts, [gate(grad_near)] + rights[1:], [chunk] * 2 + [kept_columns], quarter
    )
    enqueue("fc2", *parts)
    enqueue("out", out_part)
    swapped = turn(*swapped)
    halves = lax.optimization_barrier((token[0], *halves))[1:]
    grad_far += [jnp.concatenate(halves[i : i + 2], axis=0) for i in range(0, len(halves), 2)]
    grad_inner_far = back_blocks([gate(grad_far[0])] + grad_far[1:], fc2_quarter, slope_far)
    (grad_inner_far,) = turn(grad_inner_far)
    inner_quarter = gate(quarter_of(grad_inner, 1, quarter))
    fc1_part = (
        contract(norm_mlp_own, inner_quarter[:close], 0, 0)
        + contract(norm_mlp_rest, inner_quarter[close:], 0, 0)
        + contract(norm_mlp_far, grad_inner_far, 0, 0)
    )
    (fc1_part,) = turn(fc1_part.astype(BF))
    enqueue("fc1", *cut(fc1_part, [4, 4, 4, 4]))
    grad_hidden, sums, qkv_sum, inner_sum = norm_back(
        gate(grad_qkv), grad_inner, qkv_weight, fc1_weight, gains, near_blocks
    )
    grad_hidden, sums = turn(grad_hidden, sums)
    blocks = grad_hidden.reshape(ways, 2, rows, D)
    kept, mates = blocks[:, 0], blocks[:, 1].astype(BF)
    bias_part = jnp.sum(gate(grad_out), axis=0)
    tensor_parts = jnp.concatenate(
        [sums[:4].reshape(-1), bias_part, jnp.full((D,), error_part, F32)]
    )
    fc1_bias_part, qkv_bias_part = inner_sum[0], qkv_sum[0]
    others = jnp.concatenate([fc1_bias_part, qkv_bias_part])
    outcome = {}
    qkv_quarter = gate(quarter_of(grad_qkv, 1, quarter))
    qkv_part = (
        contract(norm_attn_own, qkv_quarter[:close], 0, 0)
        + contract(norm_attn_rest, qkv_quarter[close:], 0, 0)
        + contract(norm_attn_far, jnp.concatenate([*swapped, *grad_qkv_far], axis=0), 0, 0)
    )
    qkv_part, mates, tensor_parts = turn(qkv_part.astype(BF), mates, tensor_parts)
    walk(last_walk(kept, mates, tensor_parts, others, outcome))
    enqueue("qkv", *cut(qkv_part, [4, 4, 4, 2, 1, 1]))
    axes = {"fc2": 0, "out": 0, "fc1": 1, "qkv": 1}
    placed = {name: (None, 0, 0) for name in axes}

    def place(name):
        whole, done, offset = placed[name]
        pieces = results[name][done]
        lengths, columns = parts_of[name]
        shape = (4 * lengths, columns) if axes[name] == 0 else (lengths, 4 * columns)
        whole = place_one(whole, *pieces, shape, axes[name], offset)
        placed[name] = (whole, done + 1, offset + pieces[0].shape[0] // 2)

    while queue or due:
        ready = []
        for name in axes:
            if len(ready) < 2 and len(results.get(name, [])) > placed[name][1]:
                place(name)
                ready.append(name)
        wholes = turn(*[placed[name][0] for name in ready])
        for name, whole in zip(ready, wholes):
            placed[name] = (whole,) + placed[name][1:]
    for name in axes:
        while len(results[name]) > placed[name][1]:
            place(name)
    input_grad = outcome["input"]
    small = outcome["small"]
    vectors = small[: 6 * D].reshape(6, D)
    fc1_bias_grad = small[6 * D : 6 * D + fc1_bias_part.shape[0]]
    qkv_bias_grad = small[6 * D + fc1_bias_part.shape[0] :]
    loss_value = vectors[5, 0] / (count[0, 0] * D)
    fc2_weight_grad, out_weight_grad = placed["fc2"][0], placed["out"][0]
    fc1_weight_grad, qkv_weight_grad = placed["fc1"][0], placed["qkv"][0]
    return (
        output_f.astype(BF),
        loss_value,
        input_grad,
        vectors[0],
        vectors[1],
        vectors[2],
        vectors[3],
        qkv_weight_grad,
        qkv_bias_grad,
        out_weight_grad,
        vectors[4],
        fc1_weight_grad,
        fc1_bias_grad,
        fc2_weight_grad,
        vectors[4],
    )


def solution(mesh):
    tokens = P(("dp", "tensor"), None)
    columns, lanes, down, whole = P(None, "tensor"), P("tensor"), P("tensor", None), P()
    in_specs = (
        tokens,
        tokens,
        P(("dp", "tensor")),
        P("dp"),
        whole,
        whole,
        whole,
        whole,
        columns,
        lanes,
        down,
        whole,
        columns,
        lanes,
        down,
        whole,
    )
    out_specs = (
        tokens,
        whole,
        tokens,
        whole,
        whole,
        whole,
        whole,
        columns,
        lanes,
        down,
        whole,
        columns,
        lanes,
        down,
        whole,
    )
    return jax.shard_map(
        on_device, mesh=mesh, in_specs=in_specs, out_specs=out_specs, check_vma=False
    )
```

```python
import functools

import jax
import jax.numpy as jnp
import numpy as np
from jax import lax
from jax.experimental import pallas as pl
from jax.experimental.pallas import tpu as pltpu
from jax.sharding import PartitionSpec as P

D = 2048
HD = 256
ROT = 64
LEN = 1024
EPSILON = 1e-05
BF = jnp.bfloat16
F32 = jnp.float32
SMALL = pl.CostEstimate(flops=1 << 20, bytes_accessed=1 << 16, transcendentals=0)


def rotary_table(length):
    half = ROT // 2
    frequency = (10000.0 ** (-2.0 * np.arange(half, dtype=np.float32) / ROT)).astype(np.float32)
    angles = np.arange(length, dtype=np.float32)[:, None] * frequency[None, :]
    cosine, sine = np.cos(angles), np.sin(angles)
    table = np.zeros((length, 3 * 128), np.float32)
    table[:, ROT:128] = 1.0
    table[:, :half] = table[:, half:ROT] = cosine
    table[:, 128 : 128 + half] = -sine
    table[:, 256 + half : 256 + ROT] = sine
    return table


def contract(left_side, right_side, left_dim, right_dim):
    return lax.dot_general(
        left_side,
        right_side,
        (((left_dim,), (right_dim,)), ((), ())),
        preferred_element_type=F32,
    )


def exact_gelu(pre_act):
    below = 0.5 + 0.5 * lax.erf(pre_act * 0.5**0.5)
    density = jnp.exp(-0.5 * pre_act * pre_act) * (2.0 * jnp.pi) ** -0.5
    return pre_act * below, below + pre_act * density


def after(value, *earlier):
    return lax.optimization_barrier((value,) + earlier)[0]


def turned(block, keep, up, down, sign):
    head = block[:, :128]
    half = ROT // 2
    moved = head * keep + sign * (
        pltpu.roll(head, 128 - half, 1) * up + pltpu.roll(head, half, 1) * down
    )
    return jnp.concatenate([moved, block[:, 128:]], axis=1)


def qkv_kernel(x_ref, w_ref, b_ref, keep_ref, up_ref, down_ref, *refs):
    o_ref = refs[-1]
    kind = pl.program_id(0) % 3
    rows = x_ref.shape[0]
    tile = min(rows, 512)

    def project(at):
        return (
            jnp.dot(x_ref[at, :], w_ref[...], preferred_element_type=F32)
            + b_ref[...].astype(F32)
        )

    for start in range(0, rows, tile):
        at = pl.ds(start, min(tile, rows - start))

        @pl.when(kind == 2)
        def _(at=at):
            o_ref[at, :] = project(at).astype(BF)

        @pl.when(kind != 2)
        def _(at=at):
            o_ref[at, :] = turned(
                project(at), keep_ref[at, :], up_ref[at, :], down_ref[at, :], 1.0
            ).astype(BF)


def project_qkv(normed, weight, bias, table, length, whole=None):
    rows, width = normed.shape
    columns = weight.shape[1]
    part = 0 if whole is None else 1
    if part and rows * 2 != length:
        rest = project_qkv(normed, weight, bias, table[length - rows :], rows)
        return jnp.concatenate([whole[: length - rows], rest], axis=0)
    return pl.pallas_call(
        qkv_kernel,
        grid=(columns // HD,),
        in_specs=[
            pl.BlockSpec((rows, width), lambda j: (0, 0)),
            pl.BlockSpec((width, HD), lambda j: (0, j)),
            pl.BlockSpec((1, HD), lambda j: (0, j)),
        ]
        + [pl.BlockSpec((rows, 128), lambda j, k=k: (part, k)) for k in range(3)]
        + [pl.BlockSpec(memory_space=pl.ANY)] * part,
        out_specs=pl.BlockSpec((rows, HD), lambda j: (part, j)),
        out_shape=jax.ShapeDtypeStruct((length, columns), BF),
        input_output_aliases={6: 0} if part else {},
        compiler_params=pltpu.CompilerParams(vmem_limit_bytes=40 << 20),
        cost_estimate=SMALL,
        name="qkv_rotary",
    )(normed, weight, bias[None, :], table, table, table, *([whole] if part else []))


def visible_scores(queries, keys, row_spots, key_spots, prefix):
    scores = lax.dot_general(
        queries, keys, (((1,), (1,)), ((), ())), preferred_element_type=F32
    ) * (HD**-0.5)
    allowed = (key_spots <= row_spots) | (key_spots < prefix)
    return jnp.where(allowed, scores, -jnp.inf)


def attend_kernel(prefix_ref, q_ref, k_ref, v_ref, rows_ref, keys_ref, o_ref, log_ref):
    scores = visible_scores(
        q_ref[...], k_ref[...], rows_ref[...], keys_ref[...], prefix_ref[0]
    )
    top = jnp.max(scores, axis=-1, keepdims=True)
    weights = jnp.exp(scores - top)
    total = jnp.sum(weights, axis=-1, keepdims=True)
    probs = (weights * (1.0 / total)).astype(BF)
    o_ref[...] = jnp.dot(probs, v_ref[...], preferred_element_type=F32).astype(BF)
    log_ref[0] = top + jnp.log(total)


def attend(qkv, prefix, spots):
    length = qkv.shape[0]
    heads = qkv.shape[1] // (3 * HD)
    tile = length // 4
    whole = lambda part: pl.BlockSpec((length, HD), lambda h, i, p: (0, 3 * h + part))
    return pl.pallas_call(
        attend_kernel,
        grid_spec=pltpu.PrefetchScalarGridSpec(
            num_scalar_prefetch=1,
            grid=(heads, 4),
            in_specs=[
                pl.BlockSpec((tile, HD), lambda h, i, p: (i, 3 * h)),
                whole(1),
                whole(2),
                pl.BlockSpec((tile, 1), lambda h, i, p: (i, 0)),
                pl.BlockSpec((1, length), lambda h, i, p: (0, 0)),
            ],
            out_specs=[
                pl.BlockSpec((tile, HD), lambda h, i, p: (i, h)),
                pl.BlockSpec((1, tile, 1), lambda h, i, p: (h, i, 0)),
            ],
        ),
        out_shape=[
            jax.ShapeDtypeStruct((length, heads * HD), BF),
            jax.ShapeDtypeStruct((heads, length, 1), F32),
        ],
        compiler_params=pltpu.CompilerParams(vmem_limit_bytes=32 << 20),
        cost_estimate=SMALL,
        name="attend",
    )(prefix, qkv, qkv, qkv, spots[:, None], spots[None, :])


def attend_back_kernel(
    prefix_ref, q_ref, k_ref, v_ref, g_ref, log_ref, rows_ref, keys_ref, keep_ref, up_ref,
    down_ref, o_ref, dk_ref, dv_ref,
):
    length = q_ref.shape[0]
    tile = length // 4
    scale = HD**-0.5
    for i in range(4):
        at = pl.ds(i * tile, tile)
        q, g = q_ref[at, :], g_ref[at, :]
        scores = visible_scores(q, k_ref[...], rows_ref[at, :], keys_ref[...], prefix_ref[0])
        probs = jnp.exp(scores - log_ref[0, at, :])
        grad_probs = lax.dot_general(
            g, v_ref[...], (((1,), (1,)), ((), ())), preferred_element_type=F32
        )
        dots = jnp.sum(probs * grad_probs, axis=-1, keepdims=True)
        grad_scores = (probs * (grad_probs - dots)).astype(BF)
        dq = jnp.dot(grad_scores, k_ref[...], preferred_element_type=F32) * scale
        o_ref[at, :HD] = turned(
            dq, keep_ref[at, :], up_ref[at, :], down_ref[at, :], -1.0
        ).astype(BF)
        dk = contract(grad_scores, q, 0, 0)
        dv = contract(probs.astype(BF), g, 0, 0)
        if i == 0:
            dk_ref[...] = dk
            dv_ref[...] = dv
        else:
            dk_ref[...] += dk
            dv_ref[...] += dv
    o_ref[:, HD : 2 * HD] = turned(
        dk_ref[...] * scale, keep_ref[...], up_ref[...], down_ref[...], -1.0
    ).astype(BF)
    o_ref[:, 2 * HD :] = dv_ref[...].astype(BF)


def attend_back(qkv, grad_context, log_total, prefix, spots, table):
    length = qkv.shape[0]
    heads = qkv.shape[1] // (3 * HD)
    part = lambda n: pl.BlockSpec((length, HD), lambda h, p: (0, 3 * h + n))
    return pl.pallas_call(
        attend_back_kernel,
        grid_spec=pltpu.PrefetchScalarGridSpec(
            num_scalar_prefetch=1,
            grid=(heads,),
            in_specs=[
                part(0),
                part(1),
                part(2),
                pl.BlockSpec((length, HD), lambda h, p: (0, h)),
                pl.BlockSpec((1, length, 1), lambda h, p: (h, 0, 0)),
                pl.BlockSpec((length, 1), lambda h, p: (0, 0)),
                pl.BlockSpec((1, length), lambda h, p: (0, 0)),
            ]
            + [pl.BlockSpec((length, 128), lambda h, p, k=k: (0, k)) for k in range(3)],
            out_specs=pl.BlockSpec((length, 3 * HD), lambda h, p: (0, h)),
            scratch_shapes=[pltpu.VMEM((length, HD), F32), pltpu.VMEM((length, HD), F32)],
        ),
        out_shape=jax.ShapeDtypeStruct((length, heads * 3 * HD), BF),
        compiler_params=pltpu.CompilerParams(vmem_limit_bytes=48 << 20),
        cost_estimate=SMALL,
        name="attend_back",
    )(prefix, qkv, qkv, qkv, grad_context, log_total, spots[:, None], spots[None, :], table, table, table)


def norm_back_kernel(
    count, grad_qkv_ref, grad_inner_ref, qkv_ref, fc1_ref, gain_a_ref, gain_m_ref, *refs
):
    blocks, (o_ref, sums_ref, qkv_sum_ref, inner_sum_ref, rows_ref) = refs[:count], refs[count:]
    step = pl.program_id(0)
    for index, block in enumerate(blocks):

        @pl.when(step == index)
        def _(block=block):
            rows_ref[...] = block[...]

    features = rows_ref[...].astype(F32)
    centered = features - jnp.mean(features, axis=-1, keepdims=True)
    inverse = lax.rsqrt(jnp.mean(centered * centered, axis=-1, keepdims=True) + EPSILON)
    xhat = centered * inverse
    grad_attn = contract(grad_qkv_ref[...], qkv_ref[...], 1, 1)
    grad_mlp = contract(grad_inner_ref[...], fc1_ref[...], 1, 1)
    gained = grad_attn * gain_a_ref[...].astype(F32) + grad_mlp * gain_m_ref[...].astype(F32)
    o_ref[...] = inverse * (
        gained
        - jnp.mean(gained, axis=-1, keepdims=True)
        - xhat * jnp.mean(gained * xhat, axis=-1, keepdims=True)
    )
    pairs = (
        (sums_ref, 0, grad_attn * xhat),
        (sums_ref, 1, grad_attn),
        (sums_ref, 2, grad_mlp * xhat),
        (sums_ref, 3, grad_mlp),
        (qkv_sum_ref, 0, grad_qkv_ref[...].astype(F32)),
        (inner_sum_ref, 0, grad_inner_ref[...].astype(F32)),
    )
    for ref, row, values in pairs:
        total = jnp.sum(values, axis=0, keepdims=True)

        @pl.when(step == 0)
        def _(ref=ref, row=row, total=total):
            ref[row : row + 1, :] = total

        @pl.when(step > 0)
        def _(ref=ref, row=row, total=total):
            ref[row : row + 1, :] += total


def norm_back(grad_qkv, grad_inner, qkv_weight, fc1_weight, gains, blocks):
    count = len(blocks)
    rows, width = blocks[0].shape
    each = lambda a: pl.BlockSpec((rows, a.shape[1]), lambda i: (i, 0))
    full = lambda a: pl.BlockSpec(a.shape, lambda i: (0, 0), pipeline_mode=pl.Buffered(1))
    sums = [(8, width), (8, grad_qkv.shape[1]), (8, grad_inner.shape[1])]
    return pl.pallas_call(
        functools.partial(norm_back_kernel, count),
        grid=(count,),
        in_specs=[each(grad_qkv), each(grad_inner), full(qkv_weight), full(fc1_weight)]
        + [full(gains[0]), full(gains[2])]
        + [full(b) for b in blocks],
        out_specs=[pl.BlockSpec((rows, width), lambda i: (i, 0))]
        + [pl.BlockSpec(shape, lambda i: (0, 0)) for shape in sums],
        out_shape=[jax.ShapeDtypeStruct((count * rows, width), F32)]
        + [jax.ShapeDtypeStruct(shape, F32) for shape in sums],
        scratch_shapes=[pltpu.VMEM((rows, width), BF)],
        compiler_params=pltpu.CompilerParams(vmem_limit_bytes=56 << 20),
        cost_estimate=SMALL,
        name="norm_back",
    )(grad_qkv, grad_inner, qkv_weight, fc1_weight, gains[0], gains[2], *blocks)


def place_kernel(axis, offsets, joins, where_ref, *refs):
    chunks = len(offsets)
    pair_refs, refs = refs[: 2 * joins], refs[2 * joins :]
    sources, (*outs, wide_ref, sems) = refs[: 2 * chunks], refs[2 * chunks :]
    out_ref = outs[-1 - joins]
    rows, columns = wide_ref.shape[1:]

    @pl.when(where_ref[1] == 1)
    def _():
        for index, offset in enumerate(offsets):
            copies = []
            for k in range(4):
                source = sources[2 * index + k % 2]
                wide_ref[k] = source[pl.ds(k // 2 * rows, rows), :].astype(F32)
                place = where_ref[0] ^ k
                if axis == 0:
                    row = place * (out_ref.shape[0] // 4) + offset
                    target = out_ref.at[pl.ds(pl.multiple_of(row, 8), rows), :]
                else:
                    column = pl.multiple_of(place * columns, 128)
                    target = out_ref.at[pl.ds(offset, rows), pl.ds(column, columns)]
                copies.append(pltpu.make_async_copy(wide_ref.at[k], target, sems.at[k]))
                copies[-1].start()
            for copy in copies:
                copy.wait()

    if joins:
        half = pair_refs[0].shape[0]
        outs[-1][:half, :] = pair_refs[0][...]
        outs[-1][half:, :] = pair_refs[1][...]


def place_quarters(whole, items, shape, axis, quarter, now, pair=()):
    rows, columns = items[0][0].shape[0] // 2, items[0][0].shape[1]
    blocks = list(pair) + [a for near, far, _ in items for a in (near, far)]
    first = whole is None
    out_specs = [pl.BlockSpec(memory_space=pl.ANY)]
    out_shape = [jax.ShapeDtypeStruct(shape, F32)]
    if pair:
        joined = (2 * pair[0].shape[0], pair[0].shape[1])
        out_specs.append(pl.BlockSpec(joined, lambda i, w: (0, 0)))
        out_shape.append(jax.ShapeDtypeStruct(joined, BF))
    out = pl.pallas_call(
        functools.partial(place_kernel, axis, [o for *_, o in items], 1 if pair else 0),
        grid_spec=pltpu.PrefetchScalarGridSpec(
            num_scalar_prefetch=1,
            grid=(1,),
            in_specs=[pl.BlockSpec(a.shape, lambda i, w: (0, 0)) for a in blocks]
            + ([] if first else [pl.BlockSpec(memory_space=pl.ANY)]),
            out_specs=out_specs,
            scratch_shapes=[
                pltpu.VMEM((4, rows, columns), F32),
                pltpu.SemaphoreType.DMA((4,)),
            ],
        ),
        out_shape=out_shape,
        input_output_aliases={} if first else {1 + len(blocks): 0},
        compiler_params=pltpu.CompilerParams(vmem_limit_bytes=32 << 20 if pair else 20 << 20),
        cost_estimate=SMALL,
        name="place_quarters",
    )(jnp.stack([quarter, now]), *blocks, *([] if first else [whole]))
    return out if pair else out[0]


def norms_kernel(count, *refs):
    gains, blocks, (attn_ref, mlp_ref) = refs[:4], refs[4 : 4 + count], refs[-2:]
    for index, block in enumerate(blocks):

        @pl.when(pl.program_id(0) == index)
        def _(block=block):
            features = block[...].astype(F32)
            average = jnp.mean(features, axis=-1, keepdims=True)
            centered = features - average
            spread = jnp.mean(centered * centered, axis=-1, keepdims=True)
            xhat = centered * lax.rsqrt(spread + EPSILON)
            gain_a, shift_a, gain_m, shift_m = (ref[...].astype(F32) for ref in gains)
            attn_ref[...] = (xhat * gain_a + shift_a).astype(BF)
            mlp_ref[...] = (xhat * gain_m + shift_m).astype(BF)


def both_norms(blocks, gains, total=None, into=()):
    count = len(blocks)
    total = total or count
    skip = total - count if into else 0
    rows, width = blocks[0].shape
    shape = jax.ShapeDtypeStruct((total * rows, width), BF)
    return pl.pallas_call(
        functools.partial(norms_kernel, count),
        grid=(count,),
        in_specs=[pl.BlockSpec((1, width), lambda i: (0, 0))] * 4
        + [pl.BlockSpec((rows, width), lambda i: (0, 0))] * count
        + [pl.BlockSpec(memory_space=pl.ANY)] * len(into),
        out_specs=[pl.BlockSpec((rows, width), lambda i: (i + skip, 0))] * 2,
        out_shape=[shape, shape],
        input_output_aliases={4 + count: 0, 5 + count: 1} if into else {},
        compiler_params=pltpu.CompilerParams(vmem_limit_bytes=48 << 20),
        cost_estimate=SMALL,
        name="both_norms",
    )(*gains, *blocks, *into)


def outer_kernel(lefts, pieces, outs, _, *refs):
    left_refs, rights = refs[:lefts], refs[lefts : -2 - outs]
    out_refs, (left_ref, joined_ref) = refs[-2 - outs : -2], refs[-2:]

    @pl.when(pl.program_id(0) == 0)
    def _():
        for ref, (row, column) in zip(left_refs, pieces):
            count, width = ref.shape
            step = min(count, 256)
            for start in range(0, count, step):
                left_ref[pl.ds(row, width), pl.ds(column + start, step)] = ref[
                    pl.ds(start, step), :
                ].T

    column = 0
    for ref in rights:
        joined_ref[pl.ds(column, ref.shape[0]), :] = ref[...]
        column += ref.shape[0]
    total = jnp.dot(left_ref[...], joined_ref[...], preferred_element_type=F32).astype(BF)
    row = 0
    for ref in out_refs:
        ref[...] = total[row : row + ref.shape[0], :]
        row += ref.shape[0]


def outer_blocks(lefts, rights, sizes, quarter):
    width = rights[0].shape[1]
    tokens = sum(r.shape[0] for r in rights)
    left = sum(sizes)
    tile = 512
    specs = [
        pl.BlockSpec((a.shape[0], taken), lambda j, q, m=times, o=offset: (0, q[0] * m + o))
        for a, taken, times, offset, _, _ in lefts
    ]
    pieces = [(row, token) for *_, row, token in lefts]
    return pl.pallas_call(
        functools.partial(outer_kernel, len(lefts), pieces, len(sizes)),
        grid_spec=pltpu.PrefetchScalarGridSpec(
            num_scalar_prefetch=1,
            grid=(width // tile,),
            in_specs=specs
            + [pl.BlockSpec((r.shape[0], tile), lambda j, q: (0, j)) for r in rights],
            out_specs=[pl.BlockSpec((size, tile), lambda j, q: (0, j)) for size in sizes],
            scratch_shapes=[pltpu.VMEM((left, tokens), BF), pltpu.VMEM((tokens, tile), BF)],
        ),
        out_shape=[jax.ShapeDtypeStruct((size, width), BF) for size in sizes],
        compiler_params=pltpu.CompilerParams(vmem_limit_bytes=56 << 20),
        cost_estimate=SMALL,
        name="outer_blocks",
    )(quarter.reshape(1), *[a for a, *_ in lefts], *rights)


def back_kernel(weight_ref, slope_ref, *refs):
    blocks, o_ref = refs[:-1], refs[-1]
    for index, block in enumerate(blocks):

        @pl.when(pl.program_id(0) == index)
        def _(block=block):
            o_ref[...] = (contract(block[...], weight_ref[...], 1, 1) * slope_ref[...]).astype(BF)


def back_blocks(blocks, weight, slope):
    rows, width = blocks[0].shape
    units = weight.shape[0]
    count = len(blocks)
    return pl.pallas_call(
        back_kernel,
        grid=(count,),
        in_specs=[
            pl.BlockSpec((units, width), lambda i: (0, 0)),
            pl.BlockSpec((rows, units), lambda i: (i, 0)),
        ]
        + [pl.BlockSpec((rows, width), lambda i: (0, 0))] * count,
        out_specs=pl.BlockSpec((rows, units), lambda i: (i, 0)),
        out_shape=jax.ShapeDtypeStruct((count * rows, units), BF),
        compiler_params=pltpu.CompilerParams(vmem_limit_bytes=56 << 20),
        cost_estimate=SMALL,
        name="back_blocks",
    )(weight, slope, *blocks)


def on_device(
    hidden,
    teacher,
    valid_mask,
    prefix_len,
    ln1_gain,
    ln1_bias,
    ln2_gain,
    ln2_bias,
    qkv_weight,
    qkv_bias,
    out_weight,
    out_bias,
    fc1_weight,
    fc1_bias,
    fc2_weight,
    fc2_bias,
):
    rows = hidden.shape[0]
    dp = lax.axis_size("dp")
    tp = lax.axis_size("tensor")
    ways = tp // 2
    squares = dp // 4
    total_tokens = dp * tp * rows
    heads = qkv_weight.shape[1] // (3 * HD)
    dp_index = lax.axis_index("dp")
    tp_index = lax.axis_index("tensor")
    core, y = tp_index % 2, tp_index // 2
    quarter = dp_index % 4

    def to_core(v):
        return lax.ppermute(v, "tensor", [(t, t ^ 1) for t in range(tp)])

    def from_y(v, step):
        pairs = [(t, ((t // 2 - step) % ways) * 2 + t % 2) for t in range(tp)]
        return lax.ppermute(v, "tensor", pairs)

    def to_y(v, step):
        pairs = [(t, ((t // 2 + step) % ways) * 2 + t % 2) for t in range(tp)]
        return lax.ppermute(v, "tensor", pairs)

    def flip(v, mask):
        return lax.ppermute(v, "dp", [(d, d ^ mask) for d in range(dp)])

    block_ids = [
        ((y + step) % ways) * 2 + (core if mate == 0 else 1 - core)
        for step in range(ways)
        for mate in (0, 1)
    ]

    def gather_near(own):
        over_y = [from_y(own, step) for step in range(1, ways)]
        parts = []
        for block in [own] + over_y:
            parts += [block, to_core(block)]
        return parts, over_y

    def first_far(own):
        return [flip(own, 1), flip(own, 2)]

    def second_far(first, over_y):
        corner = flip(first[1], 1)
        beside = [from_y(first[0], step) for step in range(1, ways)]
        across = [flip(block, 2) for block in over_y]
        return corner, beside, across

    def last_far(second):
        half = rows // 2
        return [(flip(v[:half], 1), flip(u[half:], 2)) for u, v in zip(second[1], second[2])]

    def meet(*trees):
        leaves, shape = jax.tree.flatten(trees)
        return jax.tree.unflatten(shape, lax.optimization_barrier(tuple(leaves)))

    def quarter_of(v, axis, index):
        size = v.shape[axis] // 4
        return lax.dynamic_slice_in_dim(v, index * size, size, axis)

    def swap_quarters(v):
        return [flip(quarter_of(v, 1, quarter ^ mask), mask) for mask in (1, 2, 3)]

    gain_attn = ln1_gain.astype(F32)
    shift_attn = ln1_bias.astype(F32)
    gain_mlp = ln2_gain.astype(F32)
    shift_mlp = ln2_bias.astype(F32)
    gains = [v[None, :] for v in (ln1_gain, ln1_bias, ln2_gain, ln2_bias)]
    close = 2 * rows

    def units(normed):
        return jnp.dot(normed, fc1_weight, preferred_element_type=F32) + fc1_bias.astype(F32)

    near_blocks, hidden_y = gather_near(hidden)
    first = first_far(hidden)
    norm_attn_own, norm_mlp_own = both_norms(near_blocks[:2], gains)
    mask_f = after(valid_mask, norm_mlp_own).astype(F32)
    count = jnp.full((8, 128), jnp.sum(mask_f), F32)
    count = count + to_core(count)
    counted = flip(count, 1)
    pre_own = units(norm_mlp_own)
    active_own = exact_gelu(pre_own)[0].astype(BF)
    table = jnp.concatenate(
        [
            lax.dynamic_slice_in_dim(jnp.asarray(rotary_table(LEN)), b * rows, rows, 0)
            for b in block_ids
        ],
        axis=0,
    )
    spots = jnp.concatenate([b * rows + jnp.arange(rows, dtype=jnp.int32) for b in block_ids])
    active_own, table = after(active_own, table), after(table, active_own)
    qkv_own = project_qkv(norm_attn_own, qkv_weight, qkv_bias, table, LEN)
    active_own, qkv_own, counted, first, hidden_y = meet(
        active_own, qkv_own, counted, first, hidden_y
    )
    count = count + counted

    near_blocks = near_blocks[:2]
    for block in hidden_y:
        near_blocks += [block, to_core(block)]
    second = second_far(first, hidden_y)
    first_mates = [to_core(block) for block in first]
    counted = flip(count, 2)
    norm_attn_rest, norm_mlp_rest = both_norms(near_blocks[2:], gains)
    qkv_low = project_qkv(norm_attn_rest, qkv_weight, qkv_bias, table, LEN, qkv_own)
    context, log_total = attend(qkv_low, prefix_len, spots)
    norm_mlp_rest = after(norm_mlp_rest, context)
    context_far = swap_quarters(context)
    pre_rest = units(norm_mlp_rest)
    active_rest = exact_gelu(pre_rest)[0].astype(BF)
    active_rest, context, counted, second, context_far, first_mates = meet(
        active_rest, context, counted, second, context_far, first_mates
    )
    count = count + counted

    def branch_rows(context_rows, active_rows):
        return jnp.dot(context_rows, out_weight, preferred_element_type=F32) + jnp.dot(
            active_rows, fc2_weight, preferred_element_type=F32
        )

    def core_total(part):
        blocks = part.reshape(-1, 2, rows, D)
        return blocks[:, 0] + to_core(blocks[:, 1].astype(BF)).astype(F32)

    corner, beside, across = second
    second_mates = [to_core(block) for block in [corner] + beside + across]
    counted = jnp.zeros_like(count)
    bit = 2
    while bit < tp:
        counted = lax.ppermute(count, "tensor", [(t, t ^ bit) for t in range(tp)])
        bit *= 2
        if bit < tp:
            count = count + counted
    part_rest = branch_rows(context[close:], active_rest).reshape(-1, 2, rows, D)
    mates_rest = to_core(part_rest[:, 1].astype(BF))
    part_own = branch_rows(context[:close], after(active_own, part_rest)).reshape(2, rows, D)
    part_own, mates_rest, counted, second_mates = meet(
        part_own, mates_rest, counted, second_mates
    )
    count = count + counted

    sums = part_rest[:, 0] + mates_rest.astype(F32)
    came = [to_y(sums[step - 1].astype(BF), step) for step in range(1, ways)]
    mates_own = to_core(part_own[1].astype(BF))
    counted = flip(count, 4) if dp > 4 else jnp.zeros_like(count)
    last = last_far(second)
    ahead = [first[0]] + beside + [first[1]] + across + [corner]
    mates = (
        [first_mates[0]]
        + second_mates[1:ways]
        + [first_mates[1]]
        + second_mates[ways:]
        + [second_mates[0]]
    )
    far_blocks = [block for pair in zip(ahead, mates) for block in pair]
    norms_far = both_norms(far_blocks, gains, 6 * ways)
    came, mates_own, counted, norms_far, last = meet(came, mates_own, counted, norms_far, last)
    last_mates = [tuple(to_core(v) for v in pair) for pair in last]
    count = count + counted
    mask = 8
    while mask < dp:
        count = count + flip(count, mask)
        mask *= 2
    branch = part_own[0] + mates_own.astype(F32)
    for got in came:
        branch = branch + got.astype(F32)
    output_f = hidden.astype(F32) + branch + out_bias.astype(F32) + fc2_bias.astype(F32)
    mismatch = output_f - teacher.astype(F32)
    error_part = jnp.sum(mask_f[:, None] * mismatch * mismatch)
    grad_out = mask_f[:, None] * mismatch * (2.0 * total_tokens / count[0, 0])
    grad_low = grad_out.astype(BF)
    grad_out, grad_low, last, last_mates = meet(grad_out, grad_low, last, last_mates)

    grad_y = [from_y(grad_low, step) for step in range(1, ways)]
    grad_first = first_far(grad_low)
    grad_mate = to_core(grad_low)
    far_blocks = [v for pair, mate in zip(last, last_mates) for v in pair + mate]
    norm_attn_far, norm_mlp_far = both_norms(far_blocks, gains, 12 * ways, norms_far)
    fc1_quarter = quarter_of(fc1_weight, 1, quarter)
    fc2_quarter = quarter_of(after(fc2_weight, norm_mlp_far), 0, quarter)
    context_quarter = quarter_of(after(context, norm_mlp_far), 1, quarter)
    pre_far = jnp.dot(norm_mlp_far, fc1_quarter, preferred_element_type=F32) + quarter_of(
        fc1_bias, 0, quarter
    ).astype(F32)
    active_far, slope_far = exact_gelu(pre_far)
    active_far = active_far.astype(BF)
    grad_y, grad_first, active_far, grad_mate, fc2_quarter, context_quarter = meet(
        grad_y, grad_first, active_far, grad_mate, fc2_quarter, context_quarter
    )

    grad_second = second_far(grad_first, grad_y)
    grad_blocks = [grad_low, grad_mate]
    for block in grad_y:
        grad_blocks += [block, to_core(block)]
    grad_near = jnp.concatenate(grad_blocks, axis=0)
    hidden_pre = jnp.concatenate([pre_own, pre_rest], axis=0)
    grad_inner = (contract(grad_near, fc2_weight, 1, 1) * exact_gelu(hidden_pre)[1]).astype(BF)
    grad_context = contract(grad_near, out_weight, 1, 1).astype(BF)
    grad_inner, grad_context, grad_near, grad_second = meet(
        grad_inner, grad_context, grad_near, grad_second
    )

    grad_last = last_far(grad_second)
    corner, beside, across = grad_second
    ahead = [grad_first[0]] + beside + [grad_first[1]] + across + [corner]
    mates = [to_core(block) for block in ahead]
    grad_qkv = attend_back(qkv_low, grad_context, log_total, prefix_len, spots, table)
    grad_qkv, grad_last, mates = meet(grad_qkv, grad_last, mates)

    last_mates = [tuple(to_core(v) for v in pair) for pair in grad_last]
    swapped = [flip(quarter_of(grad_qkv, 1, quarter ^ m), m) for m in (1, 2)]
    grad_far = [block for pair in zip(ahead, mates) for block in pair]
    halves = [v for pair, mate in zip(grad_last, last_mates) for v in pair + mate]

    queue = []
    due = {}
    clock, launched = [0], [0]
    join = [lambda low, across: jnp.concatenate([low, across], axis=0)]
    results = {}
    token = [grad_near]

    def gate(v):
        return after(v, token[0])

    def flipped(v, mask):
        return v, lambda value: flip(value, mask)

    def travel(low, name, wait):
        mask = 4
        while mask < dp:
            (got,) = yield [flipped(low, mask)], wait
            low = (low.astype(F32) + got.astype(F32)).astype(BF)
            mask, wait = mask * 2, 1
        (across,) = yield [flipped(low, 2)], 1
        near = join[0](low, across)
        (far,) = yield [flipped(near, 1)], 1
        results.setdefault(name, []).append((near, far))

    def swap_walk(v, into):
        got = yield [flipped(quarter_of(v, 1, quarter ^ 3), 3)], 2
        into.extend(got)

    def last_walk(kept, mates, parts, others, into):
        got, more = yield [(mates, to_core), (parts, to_core)], 1
        sums, parts = kept + got.astype(F32), parts + more
        total = sums[0]
        for step in range(1, ways):
            (got,) = yield [(sums[step].astype(BF), lambda v, s=step: to_y(v, s))], 1
            total = total + got.astype(F32)
        into["input"] = grad_out + total
        bit = 2
        while bit < tp:
            pairs = [(t, t ^ bit) for t in range(tp)]
            (got,) = yield [(parts, lambda v, p=pairs: lax.ppermute(v, "tensor", p))], 1
            parts = parts + got
            bit *= 2
        parts = jnp.concatenate([parts, others])
        bit = 1
        while bit < dp:
            (got,) = yield [flipped(parts, bit)], 1
            parts = parts + got
            bit *= 2
        into["small"] = parts

    def walk(walker):
        asked = next(walker)
        start(walker, asked, clock[0] - 1)

    def start(walker, asked, now):
        sends, wait = asked
        due.setdefault(now + wait, []).append((walker, [move(v) for v, move in sends]))

    parts_of = {}

    def cut(part, shares):
        unit = part.shape[0] // 16
        edges = [unit * sum(shares[:i]) for i in range(len(shares) + 1)]
        return [lax.slice_in_dim(part, a, b, axis=0) for a, b in zip(edges, edges[1:])]

    def enqueue(name, *units):
        before, _ = parts_of.get(name, (0, 0))
        parts_of[name] = (before + sum(u.shape[0] for u in units), units[0].shape[1])
        queue.extend((unit, name) for unit in units)

    def turn(*others):
        now = clock[0]
        clock[0] = now + 1
        arrived = due.pop(now, [])
        values = [got for _, gots in arrived for got in gots]
        fresh = []
        while queue and launched[0] <= now + 1:
            fresh.append(queue.pop(0) + (max(launched[0] - now, 0) + 1,))
            launched[0] += 1
        tied = list(
            lax.optimization_barrier(tuple(values) + tuple(f[0] for f in fresh) + others)
        )
        token[0] = tied[0]
        asked = []
        for walker, gots in arrived:
            gots = [tied.pop(0) for _ in gots]
            try:
                asked.append((walker, walker.send(gots)))
            except StopIteration:
                pass
        for _, name, wait in fresh:
            walker = travel(tied.pop(0), name, wait)
            asked.append((walker, next(walker)))
        for walker, request in asked:
            start(walker, request, now)
        return tied

    always = jnp.ones((), jnp.int32)

    def place_one(whole, near, far, shape, axis, offset, now):
        rows_here, columns = near.shape[0] // 2, near.shape[1]
        if columns % 128 == 0:
            return place_quarters(whole, [(near, far, offset)], shape, axis, quarter, now)
        if whole is None:
            whole = jnp.zeros(shape, F32)
        pieces = (near[:rows_here], far[:rows_here], near[rows_here:], far[rows_here:])
        for index, piece in enumerate(pieces):
            spot = quarter ^ index
            start = (
                (spot * (shape[0] // 4) + offset, 0) if axis == 0 else (offset, spot * columns)
            )
            whole = lax.dynamic_update_slice(whole, piece.astype(F32), start)
        return whole

    half = active_far.shape[1] // 2
    rights = [grad_near] + grad_far + halves

    def hidden_lefts(part):
        return [
            (active_own, half, 2, part, 0, 0),
            (active_rest, half, 2, part, 0, close),
            (active_far, half, 0, part, 0, LEN),
        ]

    chunk = half // 2
    kept_columns = context.shape[1] // 4
    enqueue("fc2", *outer_blocks(hidden_lefts(0), rights, [chunk] * 2, quarter))
    turn()
    grad_qkv_far = []
    walk(swap_walk(gate(grad_qkv), grad_qkv_far))
    lefts = hidden_lefts(1)
    for index, piece in enumerate([context_quarter] + context_far):
        lefts.append((piece, kept_columns, 0, 0, half, index * LEN))
    *parts, out_part = outer_blocks(
        lefts, [gate(grad_near)] + rights[1:], [chunk] * 2 + [kept_columns], quarter
    )
    enqueue("fc2", *parts)
    enqueue("out", out_part)
    swapped = turn(*swapped)
    halves = lax.optimization_barrier((token[0], *halves))[1:]
    grad_far += [jnp.concatenate(halves[i : i + 2], axis=0) for i in range(0, len(halves), 2)]
    grad_inner_far = back_blocks([gate(grad_far[0])] + grad_far[1:], fc2_quarter, slope_far)
    (grad_inner_far,) = turn(grad_inner_far)
    inner_quarter = gate(quarter_of(grad_inner, 1, quarter))
    fc1_part = (
        contract(norm_mlp_own, inner_quarter[:close], 0, 0)
        + contract(norm_mlp_rest, inner_quarter[close:], 0, 0)
        + contract(norm_mlp_far, grad_inner_far, 0, 0)
    )
    (fc1_part,) = turn(fc1_part.astype(BF))
    enqueue("fc1", *cut(fc1_part, [4, 4, 4, 4]))
    grad_hidden, sums, qkv_sum, inner_sum = norm_back(
        gate(grad_qkv), grad_inner, qkv_weight, fc1_weight, gains, near_blocks
    )
    grad_hidden, sums = turn(grad_hidden, sums)
    blocks = grad_hidden.reshape(ways, 2, rows, D)
    kept, mates = blocks[:, 0], blocks[:, 1].astype(BF)
    bias_part = jnp.sum(gate(grad_out), axis=0)
    tensor_parts = jnp.concatenate(
        [sums[:4].reshape(-1), bias_part, jnp.full((D,), error_part, F32)]
    )
    fc1_bias_part, qkv_bias_part = inner_sum[0], qkv_sum[0]
    others = jnp.concatenate([fc1_bias_part, qkv_bias_part])
    outcome = {}
    qkv_quarter = gate(quarter_of(grad_qkv, 1, quarter))
    qkv_part = (
        contract(norm_attn_own, qkv_quarter[:close], 0, 0)
        + contract(norm_attn_rest, qkv_quarter[close:], 0, 0)
        + contract(norm_attn_far, jnp.concatenate([*swapped, *grad_qkv_far], axis=0), 0, 0)
    )
    qkv_part, mates, tensor_parts = turn(qkv_part.astype(BF), mates, tensor_parts)
    walk(last_walk(kept, mates, tensor_parts, others, outcome))
    enqueue("qkv", *cut(qkv_part, [4, 4, 4, 2, 1, 1]))
    axes = {"fc2": 0, "out": 0, "fc1": 1, "qkv": 1}
    placed = {name: (None, 0) for name in axes}

    def place_at(name, index, now):
        near, far = results[name][index]
        lengths, columns = parts_of[name]
        shape = (4 * lengths, columns) if axes[name] == 0 else (lengths, 4 * columns)
        offset = sum(n.shape[0] // 2 for n, _ in results[name][:index])
        return place_one(placed[name][0], near, far, shape, axes[name], offset, now)

    def place(name):
        placed[name] = (place_at(name, placed[name][1], always), placed[name][1] + 1)

    shared = 3

    def place_and_join(low, across):
        lengths, columns = parts_of["fc2"]
        items, offset = [], 0
        for near, far in results["fc2"][:shared]:
            items.append((near, far, offset))
            offset += near.shape[0] // 2
        whole, near = place_quarters(
            None, items, (4 * lengths, columns), 0, quarter, core, (low, across)
        )
        placed["fc2"] = (whole, shared)
        return near

    simple_join = join[0]
    turns_here = 0
    while queue or due:
        ready = []
        join[0] = place_and_join if turns_here == 1 else simple_join
        for name in axes if turns_here > 1 else ():
            if len(ready) < 2 and len(results.get(name, [])) > placed[name][1]:
                place(name)
                ready.append(name)
        wholes = turn(*[placed[name][0] for name in ready])
        for name, whole in zip(ready, wholes):
            placed[name] = (whole,) + placed[name][1:]
        turns_here += 1
    for name in axes:
        while len(results[name]) > placed[name][1]:
            place(name)
    for index in range(shared):
        placed["fc2"] = (place_at("fc2", index, 1 - core), placed["fc2"][1])
    input_grad = outcome["input"]
    small = outcome["small"]
    vectors = small[: 6 * D].reshape(6, D)
    fc1_bias_grad = small[6 * D : 6 * D + fc1_bias_part.shape[0]]
    qkv_bias_grad = small[6 * D + fc1_bias_part.shape[0] :]
    loss_value = vectors[5, 0] / (count[0, 0] * D)
    fc2_weight_grad, out_weight_grad = placed["fc2"][0], placed["out"][0]
    fc1_weight_grad, qkv_weight_grad = placed["fc1"][0], placed["qkv"][0]
    return (
        output_f.astype(BF),
        loss_value,
        input_grad,
        vectors[0],
        vectors[1],
        vectors[2],
        vectors[3],
        qkv_weight_grad,
        qkv_bias_grad,
        out_weight_grad,
        vectors[4],
        fc1_weight_grad,
        fc1_bias_grad,
        fc2_weight_grad,
        vectors[4],
    )


def solution(mesh):
    tokens = P(("dp", "tensor"), None)
    columns, lanes, down, whole = P(None, "tensor"), P("tensor"), P("tensor", None), P()
    in_specs = (
        tokens,
        tokens,
        P(("dp", "tensor")),
        P("dp"),
        whole,
        whole,
        whole,
        whole,
        columns,
        lanes,
        down,
        whole,
        columns,
        lanes,
        down,
        whole,
    )
    out_specs = (
        tokens,
        whole,
        tokens,
        whole,
        whole,
        whole,
        whole,
        columns,
        lanes,
        down,
        whole,
        columns,
        lanes,
        down,
        whole,
    )
    return jax.shard_map(
        on_device, mesh=mesh, in_specs=in_specs, out_specs=out_specs, check_vma=False
    )
```

```python
import functools

import jax
import jax.numpy as jnp
import numpy as np
from jax import lax
from jax.experimental import pallas as pl
from jax.experimental.pallas import tpu as pltpu
from jax.sharding import PartitionSpec as P

D = 2048
HD = 256
ROT = 64
LEN = 1024
EPSILON = 1e-05
BF = jnp.bfloat16
F32 = jnp.float32
SMALL = pl.CostEstimate(flops=1 << 20, bytes_accessed=1 << 16, transcendentals=0)


def rotary_table(length):
    half = ROT // 2
    frequency = (10000.0 ** (-2.0 * np.arange(half, dtype=np.float32) / ROT)).astype(np.float32)
    angles = np.arange(length, dtype=np.float32)[:, None] * frequency[None, :]
    cosine, sine = np.cos(angles), np.sin(angles)
    table = np.zeros((length, 3 * 128), np.float32)
    table[:, ROT:128] = 1.0
    table[:, :half] = table[:, half:ROT] = cosine
    table[:, 128 : 128 + half] = -sine
    table[:, 256 + half : 256 + ROT] = sine
    return table


def contract(left_side, right_side, left_dim, right_dim):
    return lax.dot_general(
        left_side,
        right_side,
        (((left_dim,), (right_dim,)), ((), ())),
        preferred_element_type=F32,
    )


def exact_gelu(pre_act):
    below = 0.5 + 0.5 * lax.erf(pre_act * 0.5**0.5)
    density = jnp.exp(-0.5 * pre_act * pre_act) * (2.0 * jnp.pi) ** -0.5
    return pre_act * below, below + pre_act * density


def after(value, *earlier):
    return lax.optimization_barrier((value,) + earlier)[0]


def turned(block, keep, up, down, sign):
    head = block[:, :128]
    half = ROT // 2
    moved = head * keep + sign * (
        pltpu.roll(head, 128 - half, 1) * up + pltpu.roll(head, half, 1) * down
    )
    return jnp.concatenate([moved, block[:, 128:]], axis=1)


def qkv_kernel(own_ref, rest_ref, w_ref, b_ref, keep_ref, up_ref, down_ref, o_ref):
    kind = pl.program_id(0) % 3
    row = 0
    for x_ref in (own_ref, rest_ref):
        rows = x_ref.shape[0]
        tile = min(rows, 512)
        for start in range(0, rows, tile):
            here = pl.ds(start, min(tile, rows - start))
            at = pl.ds(row + start, min(tile, rows - start))

            def project(x_ref=x_ref, here=here):
                return (
                    jnp.dot(x_ref[here, :], w_ref[...], preferred_element_type=F32)
                    + b_ref[...].astype(F32)
                )

            @pl.when(kind == 2)
            def _(at=at, project=project):
                o_ref[at, :] = project().astype(BF)

            @pl.when(kind != 2)
            def _(at=at, project=project):
                o_ref[at, :] = turned(
                    project(), keep_ref[at, :], up_ref[at, :], down_ref[at, :], 1.0
                ).astype(BF)

        row += rows


def project_qkv(own, rest, weight, bias, table):
    length, width = own.shape[0] + rest.shape[0], own.shape[1]
    columns = weight.shape[1]
    return pl.pallas_call(
        qkv_kernel,
        grid=(columns // HD,),
        in_specs=[
            pl.BlockSpec(own.shape, lambda j: (0, 0)),
            pl.BlockSpec(rest.shape, lambda j: (0, 0)),
            pl.BlockSpec((width, HD), lambda j: (0, j)),
            pl.BlockSpec((1, HD), lambda j: (0, j)),
        ]
        + [pl.BlockSpec((length, 128), lambda j, k=k: (0, k)) for k in range(3)],
        out_specs=pl.BlockSpec((length, HD), lambda j: (0, j)),
        out_shape=jax.ShapeDtypeStruct((length, columns), BF),
        compiler_params=pltpu.CompilerParams(vmem_limit_bytes=40 << 20),
        cost_estimate=SMALL,
        name="qkv_rotary",
    )(own, rest, weight, bias[None, :], table, table, table)


def visible_scores(queries, keys, row_spots, key_spots, prefix):
    scores = lax.dot_general(
        queries, keys, (((1,), (1,)), ((), ())), preferred_element_type=F32
    ) * (HD**-0.5)
    allowed = (key_spots <= row_spots) | (key_spots < prefix)
    return jnp.where(allowed, scores, -jnp.inf)


def attend_kernel(prefix_ref, q_ref, k_ref, v_ref, rows_ref, keys_ref, o_ref, log_ref):
    scores = visible_scores(
        q_ref[...], k_ref[...], rows_ref[...], keys_ref[...], prefix_ref[0]
    )
    top = jnp.max(scores, axis=-1, keepdims=True)
    weights = jnp.exp(scores - top)
    total = jnp.sum(weights, axis=-1, keepdims=True)
    probs = (weights * (1.0 / total)).astype(BF)
    o_ref[...] = jnp.dot(probs, v_ref[...], preferred_element_type=F32).astype(BF)
    log_ref[0] = top + jnp.log(total)


def attend(qkv, prefix, spots):
    length = qkv.shape[0]
    heads = qkv.shape[1] // (3 * HD)
    tile = length // 4
    whole = lambda part: pl.BlockSpec((length, HD), lambda h, i, p: (0, 3 * h + part))
    return pl.pallas_call(
        attend_kernel,
        grid_spec=pltpu.PrefetchScalarGridSpec(
            num_scalar_prefetch=1,
            grid=(heads, 4),
            in_specs=[
                pl.BlockSpec((tile, HD), lambda h, i, p: (i, 3 * h)),
                whole(1),
                whole(2),
                pl.BlockSpec((tile, 1), lambda h, i, p: (i, 0)),
                pl.BlockSpec((1, length), lambda h, i, p: (0, 0)),
            ],
            out_specs=[
                pl.BlockSpec((tile, HD), lambda h, i, p: (i, h)),
                pl.BlockSpec((1, tile, 1), lambda h, i, p: (h, i, 0)),
            ],
        ),
        out_shape=[
            jax.ShapeDtypeStruct((length, heads * HD), BF),
            jax.ShapeDtypeStruct((heads, length, 1), F32),
        ],
        compiler_params=pltpu.CompilerParams(vmem_limit_bytes=32 << 20),
        cost_estimate=SMALL,
        name="attend",
    )(prefix, qkv, qkv, qkv, spots[:, None], spots[None, :])


def attend_back_kernel(
    prefix_ref, q_ref, k_ref, v_ref, g_ref, log_ref, rows_ref, keys_ref, keep_ref, up_ref,
    down_ref, o_ref, dk_ref, dv_ref,
):
    length = q_ref.shape[0]
    tile = length // 4
    scale = HD**-0.5
    for i in range(4):
        at = pl.ds(i * tile, tile)
        q, g = q_ref[at, :], g_ref[at, :]
        scores = visible_scores(q, k_ref[...], rows_ref[at, :], keys_ref[...], prefix_ref[0])
        probs = jnp.exp(scores - log_ref[0, at, :])
        grad_probs = lax.dot_general(
            g, v_ref[...], (((1,), (1,)), ((), ())), preferred_element_type=F32
        )
        dots = jnp.sum(probs * grad_probs, axis=-1, keepdims=True)
        grad_scores = (probs * (grad_probs - dots)).astype(BF)
        dq = jnp.dot(grad_scores, k_ref[...], preferred_element_type=F32) * scale
        o_ref[at, :HD] = turned(
            dq, keep_ref[at, :], up_ref[at, :], down_ref[at, :], -1.0
        ).astype(BF)
        dk = contract(grad_scores, q, 0, 0)
        dv = contract(probs.astype(BF), g, 0, 0)
        if i == 0:
            dk_ref[...] = dk
            dv_ref[...] = dv
        else:
            dk_ref[...] += dk
            dv_ref[...] += dv
    o_ref[:, HD : 2 * HD] = turned(
        dk_ref[...] * scale, keep_ref[...], up_ref[...], down_ref[...], -1.0
    ).astype(BF)
    o_ref[:, 2 * HD :] = dv_ref[...].astype(BF)


def attend_back(qkv, grad_context, log_total, prefix, spots, table):
    length = qkv.shape[0]
    heads = qkv.shape[1] // (3 * HD)
    part = lambda n: pl.BlockSpec((length, HD), lambda h, p: (0, 3 * h + n))
    return pl.pallas_call(
        attend_back_kernel,
        grid_spec=pltpu.PrefetchScalarGridSpec(
            num_scalar_prefetch=1,
            grid=(heads,),
            in_specs=[
                part(0),
                part(1),
                part(2),
                pl.BlockSpec((length, HD), lambda h, p: (0, h)),
                pl.BlockSpec((1, length, 1), lambda h, p: (h, 0, 0)),
                pl.BlockSpec((length, 1), lambda h, p: (0, 0)),
                pl.BlockSpec((1, length), lambda h, p: (0, 0)),
            ]
            + [pl.BlockSpec((length, 128), lambda h, p, k=k: (0, k)) for k in range(3)],
            out_specs=pl.BlockSpec((length, 3 * HD), lambda h, p: (0, h)),
            scratch_shapes=[pltpu.VMEM((length, HD), F32), pltpu.VMEM((length, HD), F32)],
        ),
        out_shape=jax.ShapeDtypeStruct((length, heads * 3 * HD), BF),
        compiler_params=pltpu.CompilerParams(vmem_limit_bytes=48 << 20),
        cost_estimate=SMALL,
        name="attend_back",
    )(prefix, qkv, qkv, qkv, grad_context, log_total, spots[:, None], spots[None, :], table, table, table)


def norm_back_kernel(
    count, grad_qkv_ref, grad_inner_ref, qkv_ref, fc1_ref, gains_ref, *refs
):
    blocks, (o_ref, sums_ref, qkv_sum_ref, inner_sum_ref, rows_ref) = refs[:count], refs[count:]
    step = pl.program_id(0)
    for index, block in enumerate(blocks):

        @pl.when(step == index)
        def _(block=block):
            rows_ref[...] = block[...]

    features = rows_ref[...].astype(F32)
    centered = features - jnp.mean(features, axis=-1, keepdims=True)
    inverse = lax.rsqrt(jnp.mean(centered * centered, axis=-1, keepdims=True) + EPSILON)
    xhat = centered * inverse
    grad_attn = contract(grad_qkv_ref[...], qkv_ref[...], 1, 1)
    grad_mlp = contract(grad_inner_ref[...], fc1_ref[...], 1, 1)
    gain_a, gain_m = gains_ref[0:1, :].astype(F32), gains_ref[2:3, :].astype(F32)
    gained = grad_attn * gain_a + grad_mlp * gain_m
    o_ref[...] = inverse * (
        gained
        - jnp.mean(gained, axis=-1, keepdims=True)
        - xhat * jnp.mean(gained * xhat, axis=-1, keepdims=True)
    )
    pairs = (
        (sums_ref, 0, grad_attn * xhat),
        (sums_ref, 1, grad_attn),
        (sums_ref, 2, grad_mlp * xhat),
        (sums_ref, 3, grad_mlp),
        (qkv_sum_ref, 0, grad_qkv_ref[...].astype(F32)),
        (inner_sum_ref, 0, grad_inner_ref[...].astype(F32)),
    )
    for ref, row, values in pairs:
        total = jnp.sum(values, axis=0, keepdims=True)

        @pl.when(step == 0)
        def _(ref=ref, row=row, total=total):
            ref[row : row + 1, :] = total

        @pl.when(step > 0)
        def _(ref=ref, row=row, total=total):
            ref[row : row + 1, :] += total


def norm_back(grad_qkv, grad_inner, qkv_weight, fc1_weight, gains, blocks):
    count = len(blocks)
    rows, width = blocks[0].shape
    each = lambda a: pl.BlockSpec((rows, a.shape[1]), lambda i: (i, 0))
    full = lambda a: pl.BlockSpec(a.shape, lambda i: (0, 0), pipeline_mode=pl.Buffered(1))
    sums = [(8, width), (8, grad_qkv.shape[1]), (8, grad_inner.shape[1])]
    return pl.pallas_call(
        functools.partial(norm_back_kernel, count),
        grid=(count,),
        in_specs=[each(grad_qkv), each(grad_inner), full(qkv_weight), full(fc1_weight)]
        + [full(gains)]
        + [full(b) for b in blocks],
        out_specs=[pl.BlockSpec((rows, width), lambda i: (i, 0))]
        + [pl.BlockSpec(shape, lambda i: (0, 0)) for shape in sums],
        out_shape=[jax.ShapeDtypeStruct((count * rows, width), F32)]
        + [jax.ShapeDtypeStruct(shape, F32) for shape in sums],
        scratch_shapes=[pltpu.VMEM((rows, width), BF)],
        compiler_params=pltpu.CompilerParams(vmem_limit_bytes=56 << 20),
        cost_estimate=SMALL,
        name="norm_back",
    )(grad_qkv, grad_inner, qkv_weight, fc1_weight, gains, *blocks)


def place_kernel(quarter_ref, *refs):
    pieces, out_ref = refs[-5:-1], refs[-1]
    for index, piece in enumerate(pieces):

        @pl.when(pl.program_id(0) == index)
        def _(piece=piece):
            out_ref[...] = piece[...].astype(F32)


def place_quarters(whole, near, far, shape, axis, offset, quarter):
    rows, columns = near.shape[0] // 2, near.shape[1]
    if axis == 0:
        each, first_row = shape[0] // 4 // rows, offset // rows
        spot = lambda k, q: ((q[0] ^ k) * each + first_row, 0)
    else:
        spot = lambda k, q: (offset // rows, q[0] ^ k)
    first = whole is None
    operands = ([] if first else [whole]) + [near, far, near, far]
    return pl.pallas_call(
        place_kernel,
        grid_spec=pltpu.PrefetchScalarGridSpec(
            num_scalar_prefetch=1,
            grid=(4,),
            in_specs=([] if first else [pl.BlockSpec(memory_space=pl.ANY)])
            + [pl.BlockSpec((rows, columns), lambda k, q, h=h: (h, 0)) for h in (0, 0, 1, 1)],
            out_specs=pl.BlockSpec((rows, columns), spot),
        ),
        out_shape=jax.ShapeDtypeStruct(shape, F32),
        input_output_aliases={} if first else {1: 0},
        compiler_params=pltpu.CompilerParams(vmem_limit_bytes=24 << 20),
        cost_estimate=SMALL,
        name="place_quarters",
    )(quarter.reshape(1), *operands)


def norms_kernel(count, *refs):
    gains_ref, blocks, (attn_ref, mlp_ref) = refs[0], refs[1 : 1 + count], refs[-2:]
    for index, block in enumerate(blocks):

        @pl.when(pl.program_id(0) == index)
        def _(block=block):
            features = block[...].astype(F32)
            average = jnp.mean(features, axis=-1, keepdims=True)
            centered = features - average
            spread = jnp.mean(centered * centered, axis=-1, keepdims=True)
            xhat = centered * lax.rsqrt(spread + EPSILON)
            gain_a, shift_a, gain_m, shift_m = (
                gains_ref[i : i + 1, :].astype(F32) for i in range(4)
            )
            attn_ref[...] = (xhat * gain_a + shift_a).astype(BF)
            mlp_ref[...] = (xhat * gain_m + shift_m).astype(BF)


def both_norms(blocks, gains, total=None, into=()):
    count = len(blocks)
    total = total or count
    skip = total - count if into else 0
    rows, width = blocks[0].shape
    shape = jax.ShapeDtypeStruct((total * rows, width), BF)
    return pl.pallas_call(
        functools.partial(norms_kernel, count),
        grid=(count,),
        in_specs=[pl.BlockSpec(gains.shape, lambda i: (0, 0))]
        + [pl.BlockSpec((rows, width), lambda i: (0, 0))] * count
        + [pl.BlockSpec(memory_space=pl.ANY)] * len(into),
        out_specs=[pl.BlockSpec((rows, width), lambda i: (i + skip, 0))] * 2,
        out_shape=[shape, shape],
        input_output_aliases={1 + count: 0, 2 + count: 1} if into else {},
        compiler_params=pltpu.CompilerParams(vmem_limit_bytes=48 << 20),
        cost_estimate=SMALL,
        name="both_norms",
    )(gains, *blocks, *into)


def outer_kernel(lefts, pieces, outs, _, *refs):
    left_refs, rights = refs[:lefts], refs[lefts : -2 - outs]
    out_refs, (left_ref, joined_ref) = refs[-2 - outs : -2], refs[-2:]

    @pl.when(pl.program_id(0) == 0)
    def _():
        for ref, (row, column) in zip(left_refs, pieces):
            count, width = ref.shape
            step = min(count, 256)
            for start in range(0, count, step):
                left_ref[pl.ds(row, width), pl.ds(column + start, step)] = ref[
                    pl.ds(start, step), :
                ].T

    column = 0
    for ref in rights:
        joined_ref[pl.ds(column, ref.shape[0]), :] = ref[...]
        column += ref.shape[0]
    total = jnp.dot(left_ref[...], joined_ref[...], preferred_element_type=F32).astype(BF)
    row = 0
    for ref in out_refs:
        ref[...] = total[row : row + ref.shape[0], :]
        row += ref.shape[0]


def outer_blocks(lefts, rights, sizes, quarter):
    width = rights[0].shape[1]
    tokens = sum(r.shape[0] for r in rights)
    left = sum(sizes)
    tile = 512
    specs = [
        pl.BlockSpec((a.shape[0], taken), lambda j, q, m=times, o=offset: (0, q[0] * m + o))
        for a, taken, times, offset, _, _ in lefts
    ]
    pieces = [(row, token) for *_, row, token in lefts]
    return pl.pallas_call(
        functools.partial(outer_kernel, len(lefts), pieces, len(sizes)),
        grid_spec=pltpu.PrefetchScalarGridSpec(
            num_scalar_prefetch=1,
            grid=(width // tile,),
            in_specs=specs
            + [pl.BlockSpec((r.shape[0], tile), lambda j, q: (0, j)) for r in rights],
            out_specs=[pl.BlockSpec((size, tile), lambda j, q: (0, j)) for size in sizes],
            scratch_shapes=[pltpu.VMEM((left, tokens), BF), pltpu.VMEM((tokens, tile), BF)],
        ),
        out_shape=[jax.ShapeDtypeStruct((size, width), BF) for size in sizes],
        compiler_params=pltpu.CompilerParams(vmem_limit_bytes=56 << 20),
        cost_estimate=SMALL,
        name="outer_blocks",
    )(quarter.reshape(1), *[a for a, *_ in lefts], *rights)


def back_kernel(weight_ref, slope_ref, *refs):
    blocks, o_ref = refs[:-1], refs[-1]
    for index, block in enumerate(blocks):

        @pl.when(pl.program_id(0) == index)
        def _(block=block):
            o_ref[...] = (contract(block[...], weight_ref[...], 1, 1) * slope_ref[...]).astype(BF)


def back_blocks(blocks, weight, slope):
    rows, width = blocks[0].shape
    units = weight.shape[0]
    count = len(blocks)
    return pl.pallas_call(
        back_kernel,
        grid=(count,),
        in_specs=[
            pl.BlockSpec((units, width), lambda i: (0, 0)),
            pl.BlockSpec((rows, units), lambda i: (i, 0)),
        ]
        + [pl.BlockSpec((rows, width), lambda i: (0, 0))] * count,
        out_specs=pl.BlockSpec((rows, units), lambda i: (i, 0)),
        out_shape=jax.ShapeDtypeStruct((count * rows, units), BF),
        compiler_params=pltpu.CompilerParams(vmem_limit_bytes=56 << 20),
        cost_estimate=SMALL,
        name="back_blocks",
    )(weight, slope, *blocks)


def on_device(
    hidden,
    teacher,
    valid_mask,
    prefix_len,
    ln1_gain,
    ln1_bias,
    ln2_gain,
    ln2_bias,
    qkv_weight,
    qkv_bias,
    out_weight,
    out_bias,
    fc1_weight,
    fc1_bias,
    fc2_weight,
    fc2_bias,
):
    rows = hidden.shape[0]
    dp = lax.axis_size("dp")
    tp = lax.axis_size("tensor")
    ways = tp // 2
    squares = dp // 4
    total_tokens = dp * tp * rows
    heads = qkv_weight.shape[1] // (3 * HD)
    dp_index = lax.axis_index("dp")
    tp_index = lax.axis_index("tensor")
    core, y = tp_index % 2, tp_index // 2
    quarter = dp_index % 4

    def to_core(v):
        return lax.ppermute(v, "tensor", [(t, t ^ 1) for t in range(tp)])

    def from_y(v, step):
        pairs = [(t, ((t // 2 - step) % ways) * 2 + t % 2) for t in range(tp)]
        return lax.ppermute(v, "tensor", pairs)

    def to_y(v, step):
        pairs = [(t, ((t // 2 + step) % ways) * 2 + t % 2) for t in range(tp)]
        return lax.ppermute(v, "tensor", pairs)

    def flip(v, mask):
        return lax.ppermute(v, "dp", [(d, d ^ mask) for d in range(dp)])

    block_ids = [
        ((y + step) % ways) * 2 + (core if mate == 0 else 1 - core)
        for step in range(ways)
        for mate in (0, 1)
    ]

    def gather_near(own):
        over_y = [from_y(own, step) for step in range(1, ways)]
        parts = []
        for block in [own] + over_y:
            parts += [block, to_core(block)]
        return parts, over_y

    def first_far(own):
        return [flip(own, 1), flip(own, 2)]

    def second_far(first, over_y):
        corner = flip(first[1], 1)
        beside = [from_y(first[0], step) for step in range(1, ways)]
        across = [flip(block, 2) for block in over_y]
        return corner, beside, across

    def last_far(second):
        half = rows // 2
        return [(flip(v[:half], 1), flip(u[half:], 2)) for u, v in zip(second[1], second[2])]

    def meet(*trees):
        leaves, shape = jax.tree.flatten(trees)
        return jax.tree.unflatten(shape, lax.optimization_barrier(tuple(leaves)))

    def quarter_of(v, axis, index):
        size = v.shape[axis] // 4
        return lax.dynamic_slice_in_dim(v, index * size, size, axis)

    def swap_quarters(v):
        return [flip(quarter_of(v, 1, quarter ^ mask), mask) for mask in (1, 2, 3)]

    gain_attn = ln1_gain.astype(F32)
    shift_attn = ln1_bias.astype(F32)
    gain_mlp = ln2_gain.astype(F32)
    shift_mlp = ln2_bias.astype(F32)
    gains = jnp.stack([ln1_gain, ln1_bias, ln2_gain, ln2_bias])
    close = 2 * rows

    def units(normed):
        return jnp.dot(normed, fc1_weight, preferred_element_type=F32) + fc1_bias.astype(F32)

    near_blocks, hidden_y = gather_near(hidden)
    first = first_far(hidden)
    norm_attn_own, norm_mlp_own = both_norms(near_blocks[:2], gains)
    pre_own = units(norm_mlp_own)
    active_own = exact_gelu(pre_own)[0].astype(BF)
    mask_f = after(valid_mask, active_own).astype(F32)
    count = jnp.full((8, 128), jnp.sum(mask_f), F32)
    counted = to_core(count)
    table = jnp.concatenate(
        [
            lax.dynamic_slice_in_dim(jnp.asarray(rotary_table(LEN)), b * rows, rows, 0)
            for b in block_ids
        ],
        axis=0,
    )
    spots = jnp.concatenate([b * rows + jnp.arange(rows, dtype=jnp.int32) for b in block_ids])
    active_own, table, spots, counted, first, hidden_y, norm_attn_own = meet(
        active_own, table, spots, counted, first, hidden_y, norm_attn_own
    )
    count = count + counted

    near_blocks = near_blocks[:2]
    for block in hidden_y:
        near_blocks += [block, to_core(block)]
    second = second_far(first, hidden_y)
    counted = flip(count, 1)
    norm_attn_rest, norm_mlp_rest = both_norms(near_blocks[2:], gains)
    qkv_low = project_qkv(norm_attn_own, norm_attn_rest, qkv_weight, qkv_bias, table)
    context, log_total = attend(qkv_low, prefix_len, spots)
    norm_mlp_rest = after(norm_mlp_rest, context)
    context_far = swap_quarters(context)
    pre_rest = units(norm_mlp_rest)
    active_rest = exact_gelu(pre_rest)[0].astype(BF)
    active_rest, context, counted, second, context_far = meet(
        active_rest, context, counted, second, context_far
    )
    count = count + counted

    def branch_rows(context_rows, active_rows):
        return jnp.dot(context_rows, out_weight, preferred_element_type=F32) + jnp.dot(
            active_rows, fc2_weight, preferred_element_type=F32
        )

    def core_total(part):
        blocks = part.reshape(-1, 2, rows, D)
        return blocks[:, 0] + to_core(blocks[:, 1].astype(BF)).astype(F32)

    corner, beside, across = second
    first_mates = [to_core(block) for block in first]
    second_mates = [to_core(block) for block in [corner] + beside + across]
    count = count + flip(count, 2)
    counted = jnp.zeros_like(count)
    bit = 2
    while bit < tp:
        counted = lax.ppermute(count, "tensor", [(t, t ^ bit) for t in range(tp)])
        bit *= 2
        if bit < tp:
            count = count + counted
    part_rest = branch_rows(context[close:], active_rest).reshape(-1, 2, rows, D)
    mates_rest = to_core(part_rest[:, 1].astype(BF))
    part_own = branch_rows(context[:close], after(active_own, part_rest)).reshape(2, rows, D)
    part_own, mates_rest, counted, first_mates, second_mates = meet(
        part_own, mates_rest, counted, first_mates, second_mates
    )
    count = count + counted

    sums = part_rest[:, 0] + mates_rest.astype(F32)
    came = [to_y(sums[step - 1].astype(BF), step) for step in range(1, ways)]
    mates_own = to_core(part_own[1].astype(BF))
    counted = flip(count, 4) if dp > 4 else jnp.zeros_like(count)
    last = [flip(block, 1) for block in across]
    ahead = [first[0]] + beside + [first[1]] + across + [corner]
    mates = (
        [first_mates[0]]
        + second_mates[1:ways]
        + [first_mates[1]]
        + second_mates[ways:]
        + [second_mates[0]]
    )
    far_blocks = [block for pair in zip(ahead, mates) for block in pair]
    norms_far = both_norms(far_blocks, gains, 6 * ways)
    came, mates_own, counted, norms_far, last = meet(came, mates_own, counted, norms_far, last)
    count = count + counted
    mask = 8
    while mask < dp:
        count = count + flip(count, mask)
        mask *= 2
    branch = part_own[0] + mates_own.astype(F32)
    for got in came:
        branch = branch + got.astype(F32)
    output_f = hidden.astype(F32) + branch + out_bias.astype(F32) + fc2_bias.astype(F32)
    mismatch = output_f - teacher.astype(F32)
    scale = 2.0 * total_tokens / count[0, 0]
    grad_out = mask_f[:, None] * mismatch * scale
    grad_low = grad_out.astype(BF)
    grad_out, grad_low, last = meet(grad_out, grad_low, last)

    grad_y = [from_y(grad_low, step) for step in range(1, ways)]
    grad_first = first_far(grad_low)
    grad_mate = to_core(grad_low)
    far_blocks = [block for v in last for block in (v, to_core(v))]
    norm_attn_far, norm_mlp_far = both_norms(far_blocks, gains, 6 * ways, norms_far)
    fc1_quarter = quarter_of(fc1_weight, 1, quarter)
    fc2_quarter = quarter_of(after(fc2_weight, norm_mlp_far), 0, quarter)
    context_quarter = quarter_of(after(context, norm_mlp_far), 1, quarter)
    pre_far = jnp.dot(norm_mlp_far, fc1_quarter, preferred_element_type=F32) + quarter_of(
        fc1_bias, 0, quarter
    ).astype(F32)
    active_far, slope_far = exact_gelu(pre_far)
    active_far = active_far.astype(BF)
    grad_y, grad_first, active_far, grad_mate, fc2_quarter, context_quarter = meet(
        grad_y, grad_first, active_far, grad_mate, fc2_quarter, context_quarter
    )

    grad_second = second_far(grad_first, grad_y)
    grad_blocks = [grad_low, grad_mate]
    for block in grad_y:
        grad_blocks += [block, to_core(block)]
    grad_near = jnp.concatenate(grad_blocks, axis=0)
    grad_context = contract(grad_near, out_weight, 1, 1).astype(BF)
    grad_qkv = attend_back(qkv_low, grad_context, log_total, prefix_len, spots, table)
    grad_qkv, grad_near, grad_second = meet(grad_qkv, grad_near, grad_second)

    grad_last = last_far(grad_second)
    corner, beside, across = grad_second
    ahead = [grad_first[0]] + beside + [grad_first[1]] + across + [corner]
    mates = [to_core(block) for block in ahead]
    swapped = [flip(quarter_of(grad_qkv, 1, quarter ^ m), m) for m in (1, 2)]
    hidden_pre = jnp.concatenate([pre_own, pre_rest], axis=0)
    grad_inner = (contract(grad_near, fc2_weight, 1, 1) * exact_gelu(hidden_pre)[1]).astype(BF)
    grad_inner, grad_last, mates = meet(grad_inner, grad_last, mates)

    last_mates = [tuple(to_core(v) for v in pair) for pair in grad_last]
    grad_far = [block for pair in zip(ahead, mates) for block in pair]
    halves = [v for pair, mate in zip(grad_last, last_mates) for v in pair + mate]

    queue = []
    due = {}
    clock, launched = [0], [0]
    results = {}
    token = [grad_near]

    def gate(v):
        return after(v, token[0])

    def flipped(v, mask):
        return v, lambda value: flip(value, mask)

    def travel(low, name, wait):
        mask = 4
        while mask < dp:
            (got,) = yield [flipped(low, mask)], wait
            low = (low.astype(F32) + got.astype(F32)).astype(BF)
            mask, wait = mask * 2, 1
        (across,) = yield [flipped(low, 2)], 1
        near = jnp.concatenate([low, across], axis=0)
        (far,) = yield [flipped(near, 1)], 1
        results.setdefault(name, []).append((near, far))

    def swap_walk(v, into):
        got = yield [flipped(quarter_of(v, 1, quarter ^ 3), 3)], 2
        into.extend(got)

    def last_walk(kept, mates, parts, others, into):
        (got,) = yield [(mates, to_core)], 1
        sums = kept + got.astype(F32)
        total = sums[0]
        for step in range(1, ways):
            (got,) = yield [(sums[step].astype(BF), lambda v, s=step: to_y(v, s))], 1
            total = total + got.astype(F32)
        into["input"] = grad_out + total
        bit = 1
        while bit < tp:
            pairs = [(t, t ^ bit) for t in range(tp)]
            (got,) = yield [(parts, lambda v, p=pairs: lax.ppermute(v, "tensor", p))], 1
            parts = parts + got
            bit *= 2
        parts = jnp.concatenate([parts, others])
        bit = 1
        while bit < dp:
            (got,) = yield [flipped(parts, bit)], 1
            parts = parts + got
            bit *= 2
        into["small"] = parts

    def walk(walker):
        asked = next(walker)
        start(walker, asked, clock[0] - 1)

    def start(walker, asked, now):
        sends, wait = asked
        due.setdefault(now + wait, []).append((walker, [move(v) for v, move in sends]))

    parts_of = {}

    def cut(part, shares):
        unit = part.shape[0] // 16
        edges = [unit * sum(shares[:i]) for i in range(len(shares) + 1)]
        return [lax.slice_in_dim(part, a, b, axis=0) for a, b in zip(edges, edges[1:])]

    def enqueue(name, *units):
        before, _ = parts_of.get(name, (0, 0))
        parts_of[name] = (before + sum(u.shape[0] for u in units), units[0].shape[1])
        queue.extend((unit, name) for unit in units)

    def turn(*others):
        now = clock[0]
        clock[0] = now + 1
        arrived = due.pop(now, [])
        values = [got for _, gots in arrived for got in gots]
        fresh = []
        while queue and launched[0] <= now + 1:
            fresh.append(queue.pop(0) + (max(launched[0] - now, 0) + 1,))
            launched[0] += 1
        tied = list(
            lax.optimization_barrier(tuple(values) + tuple(f[0] for f in fresh) + others)
        )
        token[0] = tied[0]
        asked = []
        for walker, gots in arrived:
            gots = [tied.pop(0) for _ in gots]
            try:
                asked.append((walker, walker.send(gots)))
            except StopIteration:
                pass
        for _, name, wait in fresh:
            walker = travel(tied.pop(0), name, wait)
            asked.append((walker, next(walker)))
        for walker, request in asked:
            start(walker, request, now)
        return tied

    def place_one(whole, near, far, shape, axis, offset):
        rows_here, columns = near.shape[0] // 2, near.shape[1]
        if columns % 128 == 0:
            return place_quarters(whole, near, far, shape, axis, offset, quarter)
        if whole is None:
            whole = jnp.zeros(shape, F32)
        pieces = (near[:rows_here], far[:rows_here], near[rows_here:], far[rows_here:])
        for index, piece in enumerate(pieces):
            spot = quarter ^ index
            start = (
                (spot * (shape[0] // 4) + offset, 0) if axis == 0 else (offset, spot * columns)
            )
            whole = lax.dynamic_update_slice(whole, piece.astype(F32), start)
        return whole

    half = active_far.shape[1] // 2
    rights = [grad_near] + grad_far + halves

    def hidden_lefts(part):
        return [
            (active_own, half, 2, part, 0, 0),
            (active_rest, half, 2, part, 0, close),
            (active_far, half, 0, part, 0, LEN),
        ]

    chunk = half // 2
    kept_columns = context.shape[1] // 4
    enqueue("fc2", *outer_blocks(hidden_lefts(0), rights, [chunk] * 2, quarter))
    turn()
    grad_qkv_far = []
    walk(swap_walk(gate(grad_qkv), grad_qkv_far))
    lefts = hidden_lefts(1)
    for index, piece in enumerate([context_quarter] + context_far):
        lefts.append((piece, kept_columns, 0, 0, half, index * LEN))
    *parts, out_part = outer_blocks(
        lefts, [gate(grad_near)] + rights[1:], [chunk] * 2 + [kept_columns], quarter
    )
    enqueue("fc2", *parts)
    enqueue("out", out_part)
    swapped = turn(*swapped)
    halves = lax.optimization_barrier((token[0], *halves))[1:]
    grad_far += [jnp.concatenate(halves[i : i + 2], axis=0) for i in range(0, len(halves), 2)]
    grad_inner_far = back_blocks([gate(grad_far[0])] + grad_far[1:], fc2_quarter, slope_far)
    (grad_inner_far,) = turn(grad_inner_far)
    inner_quarter = gate(quarter_of(grad_inner, 1, quarter))
    fc1_part = (
        contract(norm_mlp_own, inner_quarter[:close], 0, 0)
        + contract(norm_mlp_rest, inner_quarter[close:], 0, 0)
        + contract(norm_mlp_far, grad_inner_far, 0, 0)
    )
    (fc1_part,) = turn(fc1_part.astype(BF))
    enqueue("fc1", *cut(fc1_part, [4, 4, 4, 4]))
    grad_hidden, sums, qkv_sum, inner_sum = norm_back(
        gate(grad_qkv), grad_inner, qkv_weight, fc1_weight, gains, near_blocks
    )
    grad_hidden, sums = turn(grad_hidden, sums)
    blocks = grad_hidden.reshape(ways, 2, rows, D)
    kept, mates = blocks[:, 0], blocks[:, 1].astype(BF)
    grad_later = gate(grad_out)
    bias_part = jnp.sum(grad_later, axis=0)
    error_part = jnp.sum(grad_later * grad_later) / (scale * scale)
    tensor_parts = jnp.concatenate(
        [sums[:4].reshape(-1), bias_part, jnp.full((D,), error_part, F32)]
    )
    fc1_bias_part, qkv_bias_part = inner_sum[0], qkv_sum[0]
    others = jnp.concatenate([fc1_bias_part, qkv_bias_part])
    outcome = {}
    qkv_quarter = gate(quarter_of(grad_qkv, 1, quarter))
    qkv_part = (
        contract(norm_attn_own, qkv_quarter[:close], 0, 0)
        + contract(norm_attn_rest, qkv_quarter[close:], 0, 0)
        + contract(norm_attn_far, jnp.concatenate([*swapped, *grad_qkv_far], axis=0), 0, 0)
    )
    qkv_part, mates, tensor_parts = turn(qkv_part.astype(BF), mates, tensor_parts)
    walk(last_walk(kept, mates, tensor_parts, others, outcome))
    enqueue("qkv", *cut(qkv_part, [4, 4, 4, 2, 1, 1]))
    axes = {"fc2": 0, "out": 0, "fc1": 1, "qkv": 1}
    placed = {name: (None, 0, 0) for name in axes}

    def place(name):
        whole, done, offset = placed[name]
        pieces = results[name][done]
        lengths, columns = parts_of[name]
        shape = (4 * lengths, columns) if axes[name] == 0 else (lengths, 4 * columns)
        whole = place_one(whole, *pieces, shape, axes[name], offset)
        placed[name] = (whole, done + 1, offset + pieces[0].shape[0] // 2)

    while queue or due:
        ready = []
        for name in axes:
            if len(ready) < 2 and len(results.get(name, [])) > placed[name][1]:
                place(name)
                ready.append(name)
        wholes = turn(*[placed[name][0] for name in ready])
        for name, whole in zip(ready, wholes):
            placed[name] = (whole,) + placed[name][1:]
    for name in axes:
        while len(results[name]) > placed[name][1]:
            place(name)
    input_grad = outcome["input"]
    small = outcome["small"]
    vectors = small[: 6 * D].reshape(6, D)
    fc1_bias_grad = small[6 * D : 6 * D + fc1_bias_part.shape[0]]
    qkv_bias_grad = small[6 * D + fc1_bias_part.shape[0] :]
    loss_value = vectors[5, 0] / (count[0, 0] * D)
    fc2_weight_grad, out_weight_grad = placed["fc2"][0], placed["out"][0]
    fc1_weight_grad, qkv_weight_grad = placed["fc1"][0], placed["qkv"][0]
    return (
        output_f.astype(BF),
        loss_value,
        input_grad,
        vectors[0],
        vectors[1],
        vectors[2],
        vectors[3],
        qkv_weight_grad,
        qkv_bias_grad,
        out_weight_grad,
        vectors[4],
        fc1_weight_grad,
        fc1_bias_grad,
        fc2_weight_grad,
        vectors[4],
    )


def solution(mesh):
    tokens = P(("dp", "tensor"), None)
    columns, lanes, down, whole = P(None, "tensor"), P("tensor"), P("tensor", None), P()
    in_specs = (
        tokens,
        tokens,
        P(("dp", "tensor")),
        P("dp"),
        whole,
        whole,
        whole,
        whole,
        columns,
        lanes,
        down,
        whole,
        columns,
        lanes,
        down,
        whole,
    )
    out_specs = (
        tokens,
        whole,
        tokens,
        whole,
        whole,
        whole,
        whole,
        columns,
        lanes,
        down,
        whole,
        columns,
        lanes,
        down,
        whole,
    )
    return jax.shard_map(
        on_device, mesh=mesh, in_specs=in_specs, out_specs=out_specs, check_vma=False
    )
```

```python
import functools

import jax
import jax.numpy as jnp
import numpy as np
from jax import lax
from jax.experimental import pallas as pl
from jax.experimental.pallas import tpu as pltpu
from jax.sharding import PartitionSpec as P

D = 2048
HD = 256
ROT = 64
LEN = 1024
EPSILON = 1e-05
BF = jnp.bfloat16
F32 = jnp.float32
SMALL = pl.CostEstimate(flops=1 << 20, bytes_accessed=1 << 16, transcendentals=0)


def rotary_table(length):
    half = ROT // 2
    frequency = (10000.0 ** (-2.0 * np.arange(half, dtype=np.float32) / ROT)).astype(np.float32)
    angles = np.arange(length, dtype=np.float32)[:, None] * frequency[None, :]
    cosine, sine = np.cos(angles), np.sin(angles)
    table = np.zeros((length, 3 * 128), np.float32)
    table[:, ROT:128] = 1.0
    table[:, :half] = table[:, half:ROT] = cosine
    table[:, 128 : 128 + half] = -sine
    table[:, 256 + half : 256 + ROT] = sine
    return table


def contract(left_side, right_side, left_dim, right_dim):
    return lax.dot_general(
        left_side,
        right_side,
        (((left_dim,), (right_dim,)), ((), ())),
        preferred_element_type=F32,
    )


def exact_gelu(pre_act):
    below = 0.5 + 0.5 * lax.erf(pre_act * 0.5**0.5)
    density = jnp.exp(-0.5 * pre_act * pre_act) * (2.0 * jnp.pi) ** -0.5
    return pre_act * below, below + pre_act * density


def after(value, *earlier):
    return lax.optimization_barrier((value,) + earlier)[0]


def turned(block, keep, up, down, sign):
    head = block[:, :128]
    half = ROT // 2
    moved = head * keep + sign * (
        pltpu.roll(head, 128 - half, 1) * up + pltpu.roll(head, half, 1) * down
    )
    return jnp.concatenate([moved, block[:, 128:]], axis=1)


def qkv_kernel(own_ref, rest_ref, w_ref, b_ref, keep_ref, up_ref, down_ref, o_ref):
    kind = pl.program_id(0) % 3
    row = 0
    for x_ref in (own_ref, rest_ref):
        rows = x_ref.shape[0]
        tile = min(rows, 512)
        for start in range(0, rows, tile):
            here = pl.ds(start, min(tile, rows - start))
            at = pl.ds(row + start, min(tile, rows - start))

            def project(x_ref=x_ref, here=here):
                return (
                    jnp.dot(x_ref[here, :], w_ref[...], preferred_element_type=F32)
                    + b_ref[...].astype(F32)
                )

            @pl.when(kind == 2)
            def _(at=at, project=project):
                o_ref[at, :] = project().astype(BF)

            @pl.when(kind != 2)
            def _(at=at, project=project):
                o_ref[at, :] = turned(
                    project(), keep_ref[at, :], up_ref[at, :], down_ref[at, :], 1.0
                ).astype(BF)

        row += rows


def project_qkv(own, rest, weight, bias, table):
    length, width = own.shape[0] + rest.shape[0], own.shape[1]
    columns = weight.shape[1]
    return pl.pallas_call(
        qkv_kernel,
        grid=(columns // HD,),
        in_specs=[
            pl.BlockSpec(own.shape, lambda j: (0, 0)),
            pl.BlockSpec(rest.shape, lambda j: (0, 0)),
            pl.BlockSpec((width, HD), lambda j: (0, j)),
            pl.BlockSpec((1, HD), lambda j: (0, j)),
        ]
        + [pl.BlockSpec((length, 128), lambda j, k=k: (0, k)) for k in range(3)],
        out_specs=pl.BlockSpec((length, HD), lambda j: (0, j)),
        out_shape=jax.ShapeDtypeStruct((length, columns), BF),
        compiler_params=pltpu.CompilerParams(vmem_limit_bytes=40 << 20),
        cost_estimate=SMALL,
        name="qkv_rotary",
    )(own, rest, weight, bias[None, :], table, table, table)


def visible_scores(queries, keys, row_spots, key_spots, prefix):
    scores = lax.dot_general(
        queries, keys, (((1,), (1,)), ((), ())), preferred_element_type=F32
    ) * (HD**-0.5)
    allowed = (key_spots <= row_spots) | (key_spots < prefix)
    return jnp.where(allowed, scores, -jnp.inf)


def attend_kernel(prefix_ref, q_ref, k_ref, v_ref, rows_ref, keys_ref, o_ref, log_ref):
    scores = visible_scores(
        q_ref[...], k_ref[...], rows_ref[...], keys_ref[...], prefix_ref[0]
    )
    top = jnp.max(scores, axis=-1, keepdims=True)
    weights = jnp.exp(scores - top)
    total = jnp.sum(weights, axis=-1, keepdims=True)
    probs = (weights * (1.0 / total)).astype(BF)
    o_ref[...] = jnp.dot(probs, v_ref[...], preferred_element_type=F32).astype(BF)
    log_ref[0] = top + jnp.log(total)


def attend(qkv, prefix, spots):
    length = qkv.shape[0]
    heads = qkv.shape[1] // (3 * HD)
    tile = length // 4
    whole = lambda part: pl.BlockSpec((length, HD), lambda h, i, p: (0, 3 * h + part))
    return pl.pallas_call(
        attend_kernel,
        grid_spec=pltpu.PrefetchScalarGridSpec(
            num_scalar_prefetch=1,
            grid=(heads, 4),
            in_specs=[
                pl.BlockSpec((tile, HD), lambda h, i, p: (i, 3 * h)),
                whole(1),
                whole(2),
                pl.BlockSpec((tile, 1), lambda h, i, p: (i, 0)),
                pl.BlockSpec((1, length), lambda h, i, p: (0, 0)),
            ],
            out_specs=[
                pl.BlockSpec((tile, HD), lambda h, i, p: (i, h)),
                pl.BlockSpec((1, tile, 1), lambda h, i, p: (h, i, 0)),
            ],
        ),
        out_shape=[
            jax.ShapeDtypeStruct((length, heads * HD), BF),
            jax.ShapeDtypeStruct((heads, length, 1), F32),
        ],
        compiler_params=pltpu.CompilerParams(vmem_limit_bytes=32 << 20),
        cost_estimate=SMALL,
        name="attend",
    )(prefix, qkv, qkv, qkv, spots[:, None], spots[None, :])


def attend_back_kernel(
    prefix_ref, q_ref, k_ref, v_ref, g_ref, log_ref, rows_ref, keys_ref, keep_ref, up_ref,
    down_ref, o_ref, dk_ref, dv_ref,
):
    length = q_ref.shape[0]
    tile = length // 4
    scale = HD**-0.5
    for i in range(4):
        at = pl.ds(i * tile, tile)
        q, g = q_ref[at, :], g_ref[at, :]
        scores = visible_scores(q, k_ref[...], rows_ref[at, :], keys_ref[...], prefix_ref[0])
        probs = jnp.exp(scores - log_ref[0, at, :])
        grad_probs = lax.dot_general(
            g, v_ref[...], (((1,), (1,)), ((), ())), preferred_element_type=F32
        )
        dots = jnp.sum(probs * grad_probs, axis=-1, keepdims=True)
        grad_scores = (probs * (grad_probs - dots)).astype(BF)
        dq = jnp.dot(grad_scores, k_ref[...], preferred_element_type=F32) * scale
        o_ref[at, :HD] = turned(
            dq, keep_ref[at, :], up_ref[at, :], down_ref[at, :], -1.0
        ).astype(BF)
        dk = contract(grad_scores, q, 0, 0)
        dv = contract(probs.astype(BF), g, 0, 0)
        if i == 0:
            dk_ref[...] = dk
            dv_ref[...] = dv
        else:
            dk_ref[...] += dk
            dv_ref[...] += dv
    o_ref[:, HD : 2 * HD] = turned(
        dk_ref[...] * scale, keep_ref[...], up_ref[...], down_ref[...], -1.0
    ).astype(BF)
    o_ref[:, 2 * HD :] = dv_ref[...].astype(BF)


def attend_back(qkv, grad_context, log_total, prefix, spots, table):
    length = qkv.shape[0]
    heads = qkv.shape[1] // (3 * HD)
    part = lambda n: pl.BlockSpec((length, HD), lambda h, p: (0, 3 * h + n))
    return pl.pallas_call(
        attend_back_kernel,
        grid_spec=pltpu.PrefetchScalarGridSpec(
            num_scalar_prefetch=1,
            grid=(heads,),
            in_specs=[
                part(0),
                part(1),
                part(2),
                pl.BlockSpec((length, HD), lambda h, p: (0, h)),
                pl.BlockSpec((1, length, 1), lambda h, p: (h, 0, 0)),
                pl.BlockSpec((length, 1), lambda h, p: (0, 0)),
                pl.BlockSpec((1, length), lambda h, p: (0, 0)),
            ]
            + [pl.BlockSpec((length, 128), lambda h, p, k=k: (0, k)) for k in range(3)],
            out_specs=pl.BlockSpec((length, 3 * HD), lambda h, p: (0, h)),
            scratch_shapes=[pltpu.VMEM((length, HD), F32), pltpu.VMEM((length, HD), F32)],
        ),
        out_shape=jax.ShapeDtypeStruct((length, heads * 3 * HD), BF),
        compiler_params=pltpu.CompilerParams(vmem_limit_bytes=48 << 20),
        cost_estimate=SMALL,
        name="attend_back",
    )(prefix, qkv, qkv, qkv, grad_context, log_total, spots[:, None], spots[None, :], table, table, table)


def norm_back_kernel(
    count, grad_qkv_ref, grad_inner_ref, qkv_ref, fc1_ref, gains_ref, *refs
):
    blocks, (o_ref, sums_ref, qkv_sum_ref, inner_sum_ref, rows_ref) = refs[:count], refs[count:]
    step = pl.program_id(0)
    for index, block in enumerate(blocks):

        @pl.when(step == index)
        def _(block=block):
            rows_ref[...] = block[...]

    features = rows_ref[...].astype(F32)
    centered = features - jnp.mean(features, axis=-1, keepdims=True)
    inverse = lax.rsqrt(jnp.mean(centered * centered, axis=-1, keepdims=True) + EPSILON)
    xhat = centered * inverse
    grad_attn = contract(grad_qkv_ref[...], qkv_ref[...], 1, 1)
    grad_mlp = contract(grad_inner_ref[...], fc1_ref[...], 1, 1)
    gain_a, gain_m = gains_ref[0:1, :].astype(F32), gains_ref[2:3, :].astype(F32)
    gained = grad_attn * gain_a + grad_mlp * gain_m
    o_ref[...] = inverse * (
        gained
        - jnp.mean(gained, axis=-1, keepdims=True)
        - xhat * jnp.mean(gained * xhat, axis=-1, keepdims=True)
    )
    pairs = (
        (sums_ref, 0, grad_attn * xhat),
        (sums_ref, 1, grad_attn),
        (sums_ref, 2, grad_mlp * xhat),
        (sums_ref, 3, grad_mlp),
        (qkv_sum_ref, 0, grad_qkv_ref[...].astype(F32)),
        (inner_sum_ref, 0, grad_inner_ref[...].astype(F32)),
    )
    for ref, row, values in pairs:
        total = jnp.sum(values, axis=0, keepdims=True)

        @pl.when(step == 0)
        def _(ref=ref, row=row, total=total):
            ref[row : row + 1, :] = total

        @pl.when(step > 0)
        def _(ref=ref, row=row, total=total):
            ref[row : row + 1, :] += total


def norm_back(grad_qkv, grad_inner, qkv_weight, fc1_weight, gains, blocks, skip):
    count = len(blocks)
    rows, width = blocks[0].shape
    each = lambda a: pl.BlockSpec((rows, a.shape[1]), lambda i: (i + skip, 0))
    full = lambda a: pl.BlockSpec(a.shape, lambda i: (0, 0), pipeline_mode=pl.Buffered(1))
    sums = [(8, width), (8, grad_qkv.shape[1]), (8, grad_inner.shape[1])]
    return pl.pallas_call(
        functools.partial(norm_back_kernel, count),
        grid=(count,),
        in_specs=[each(grad_qkv), each(grad_inner), full(qkv_weight), full(fc1_weight)]
        + [full(gains)]
        + [full(b) for b in blocks],
        out_specs=[pl.BlockSpec((rows, width), lambda i: (i, 0))]
        + [pl.BlockSpec(shape, lambda i: (0, 0)) for shape in sums],
        out_shape=[jax.ShapeDtypeStruct((count * rows, width), F32)]
        + [jax.ShapeDtypeStruct(shape, F32) for shape in sums],
        scratch_shapes=[pltpu.VMEM((rows, width), BF)],
        compiler_params=pltpu.CompilerParams(vmem_limit_bytes=56 << 20),
        cost_estimate=SMALL,
        name="norm_back",
    )(grad_qkv, grad_inner, qkv_weight, fc1_weight, gains, *blocks)


def place_kernel(quarter_ref, *refs):
    pieces, out_ref = refs[-5:-1], refs[-1]
    for index, piece in enumerate(pieces):

        @pl.when(pl.program_id(0) == index)
        def _(piece=piece):
            out_ref[...] = piece[...].astype(F32)


def place_quarters(whole, near, far, shape, axis, offset, quarter):
    rows, columns = near.shape[0] // 2, near.shape[1]
    if axis == 0:
        each, first_row = shape[0] // 4 // rows, offset // rows
        spot = lambda k, q: ((q[0] ^ k) * each + first_row, 0)
    else:
        spot = lambda k, q: (offset // rows, q[0] ^ k)
    first = whole is None
    operands = ([] if first else [whole]) + [near, far, near, far]
    return pl.pallas_call(
        place_kernel,
        grid_spec=pltpu.PrefetchScalarGridSpec(
            num_scalar_prefetch=1,
            grid=(4,),
            in_specs=([] if first else [pl.BlockSpec(memory_space=pl.ANY)])
            + [pl.BlockSpec((rows, columns), lambda k, q, h=h: (h, 0)) for h in (0, 0, 1, 1)],
            out_specs=pl.BlockSpec((rows, columns), spot),
        ),
        out_shape=jax.ShapeDtypeStruct(shape, F32),
        input_output_aliases={} if first else {1: 0},
        compiler_params=pltpu.CompilerParams(vmem_limit_bytes=24 << 20),
        cost_estimate=SMALL,
        name="place_quarters",
    )(quarter.reshape(1), *operands)


def norms_kernel(count, *refs):
    gains_ref, blocks, (attn_ref, mlp_ref) = refs[0], refs[1 : 1 + count], refs[-2:]
    for index, block in enumerate(blocks):

        @pl.when(pl.program_id(0) == index)
        def _(block=block):
            features = block[...].astype(F32)
            average = jnp.mean(features, axis=-1, keepdims=True)
            centered = features - average
            spread = jnp.mean(centered * centered, axis=-1, keepdims=True)
            xhat = centered * lax.rsqrt(spread + EPSILON)
            gain_a, shift_a, gain_m, shift_m = (
                gains_ref[i : i + 1, :].astype(F32) for i in range(4)
            )
            attn_ref[...] = (xhat * gain_a + shift_a).astype(BF)
            mlp_ref[...] = (xhat * gain_m + shift_m).astype(BF)


def both_norms(blocks, gains, total=None, into=()):
    count = len(blocks)
    total = total or count
    skip = total - count if into else 0
    rows, width = blocks[0].shape
    shape = jax.ShapeDtypeStruct((total * rows, width), BF)
    return pl.pallas_call(
        functools.partial(norms_kernel, count),
        grid=(count,),
        in_specs=[pl.BlockSpec(gains.shape, lambda i: (0, 0))]
        + [pl.BlockSpec((rows, width), lambda i: (0, 0))] * count
        + [pl.BlockSpec(memory_space=pl.ANY)] * len(into),
        out_specs=[pl.BlockSpec((rows, width), lambda i: (i + skip, 0))] * 2,
        out_shape=[shape, shape],
        input_output_aliases={1 + count: 0, 2 + count: 1} if into else {},
        compiler_params=pltpu.CompilerParams(vmem_limit_bytes=48 << 20),
        cost_estimate=SMALL,
        name="both_norms",
    )(gains, *blocks, *into)


def outer_kernel(lefts, pieces, outs, _, *refs):
    left_refs, rights = refs[:lefts], refs[lefts : -2 - outs]
    out_refs, (left_ref, joined_ref) = refs[-2 - outs : -2], refs[-2:]

    @pl.when(pl.program_id(0) == 0)
    def _():
        for ref, (row, column) in zip(left_refs, pieces):
            count, width = ref.shape
            step = min(count, 256)
            for start in range(0, count, step):
                left_ref[pl.ds(row, width), pl.ds(column + start, step)] = ref[
                    pl.ds(start, step), :
                ].T

    column = 0
    for ref in rights:
        joined_ref[pl.ds(column, ref.shape[0]), :] = ref[...]
        column += ref.shape[0]
    total = jnp.dot(left_ref[...], joined_ref[...], preferred_element_type=F32).astype(BF)
    row = 0
    for ref in out_refs:
        ref[...] = total[row : row + ref.shape[0], :]
        row += ref.shape[0]


def outer_blocks(lefts, rights, sizes, quarter):
    width = rights[0].shape[1]
    tokens = sum(r.shape[0] for r in rights)
    left = sum(sizes)
    tile = 512
    specs = [
        pl.BlockSpec((a.shape[0], taken), lambda j, q, m=times, o=offset: (0, q[0] * m + o))
        for a, taken, times, offset, _, _ in lefts
    ]
    pieces = [(row, token) for *_, row, token in lefts]
    return pl.pallas_call(
        functools.partial(outer_kernel, len(lefts), pieces, len(sizes)),
        grid_spec=pltpu.PrefetchScalarGridSpec(
            num_scalar_prefetch=1,
            grid=(width // tile,),
            in_specs=specs
            + [pl.BlockSpec((r.shape[0], tile), lambda j, q: (0, j)) for r in rights],
            out_specs=[pl.BlockSpec((size, tile), lambda j, q: (0, j)) for size in sizes],
            scratch_shapes=[pltpu.VMEM((left, tokens), BF), pltpu.VMEM((tokens, tile), BF)],
        ),
        out_shape=[jax.ShapeDtypeStruct((size, width), BF) for size in sizes],
        compiler_params=pltpu.CompilerParams(vmem_limit_bytes=56 << 20),
        cost_estimate=SMALL,
        name="outer_blocks",
    )(quarter.reshape(1), *[a for a, *_ in lefts], *rights)


def back_kernel(weight_ref, slope_ref, *refs):
    blocks, o_ref = refs[:-1], refs[-1]
    for index, block in enumerate(blocks):

        @pl.when(pl.program_id(0) == index)
        def _(block=block):
            o_ref[...] = (contract(block[...], weight_ref[...], 1, 1) * slope_ref[...]).astype(BF)


def back_blocks(blocks, weight, slope):
    rows, width = blocks[0].shape
    units = weight.shape[0]
    count = len(blocks)
    return pl.pallas_call(
        back_kernel,
        grid=(count,),
        in_specs=[
            pl.BlockSpec((units, width), lambda i: (0, 0)),
            pl.BlockSpec((rows, units), lambda i: (i, 0)),
        ]
        + [pl.BlockSpec((rows, width), lambda i: (0, 0))] * count,
        out_specs=pl.BlockSpec((rows, units), lambda i: (i, 0)),
        out_shape=jax.ShapeDtypeStruct((count * rows, units), BF),
        compiler_params=pltpu.CompilerParams(vmem_limit_bytes=56 << 20),
        cost_estimate=SMALL,
        name="back_blocks",
    )(weight, slope, *blocks)


def on_device(
    hidden,
    teacher,
    valid_mask,
    prefix_len,
    ln1_gain,
    ln1_bias,
    ln2_gain,
    ln2_bias,
    qkv_weight,
    qkv_bias,
    out_weight,
    out_bias,
    fc1_weight,
    fc1_bias,
    fc2_weight,
    fc2_bias,
):
    rows = hidden.shape[0]
    dp = lax.axis_size("dp")
    tp = lax.axis_size("tensor")
    ways = tp // 2
    squares = dp // 4
    total_tokens = dp * tp * rows
    heads = qkv_weight.shape[1] // (3 * HD)
    dp_index = lax.axis_index("dp")
    tp_index = lax.axis_index("tensor")
    core, y = tp_index % 2, tp_index // 2
    quarter = dp_index % 4

    def to_core(v):
        return lax.ppermute(v, "tensor", [(t, t ^ 1) for t in range(tp)])

    def from_y(v, step):
        pairs = [(t, ((t // 2 - step) % ways) * 2 + t % 2) for t in range(tp)]
        return lax.ppermute(v, "tensor", pairs)

    def to_y(v, step):
        pairs = [(t, ((t // 2 + step) % ways) * 2 + t % 2) for t in range(tp)]
        return lax.ppermute(v, "tensor", pairs)

    def flip(v, mask):
        return lax.ppermute(v, "dp", [(d, d ^ mask) for d in range(dp)])

    block_ids = [
        ((y + step) % ways) * 2 + (core if mate == 0 else 1 - core)
        for step in range(ways)
        for mate in (0, 1)
    ]

    def gather_near(own):
        over_y = [from_y(own, step) for step in range(1, ways)]
        parts = []
        for block in [own] + over_y:
            parts += [block, to_core(block)]
        return parts, over_y

    def first_far(own):
        return [flip(own, 1), flip(own, 2)]

    def second_far(first, over_y):
        corner = flip(first[1], 1)
        beside = [from_y(first[0], step) for step in range(1, ways)]
        across = [flip(block, 2) for block in over_y]
        return corner, beside, across

    def last_far(second):
        half = rows // 2
        return [(flip(v[:half], 1), flip(u[half:], 2)) for u, v in zip(second[1], second[2])]

    def meet(*trees):
        leaves, shape = jax.tree.flatten(trees)
        return jax.tree.unflatten(shape, lax.optimization_barrier(tuple(leaves)))

    def quarter_of(v, axis, index):
        size = v.shape[axis] // 4
        return lax.dynamic_slice_in_dim(v, index * size, size, axis)

    def swap_quarters(v):
        return [flip(quarter_of(v, 1, quarter ^ mask), mask) for mask in (1, 2, 3)]

    gain_attn = ln1_gain.astype(F32)
    shift_attn = ln1_bias.astype(F32)
    gain_mlp = ln2_gain.astype(F32)
    shift_mlp = ln2_bias.astype(F32)
    gains = jnp.stack([ln1_gain, ln1_bias, ln2_gain, ln2_bias])
    close = 2 * rows

    def units(normed):
        return jnp.dot(normed, fc1_weight, preferred_element_type=F32) + fc1_bias.astype(F32)

    near_blocks, hidden_y = gather_near(hidden)
    first = first_far(hidden)
    norm_attn_own, norm_mlp_own = both_norms(near_blocks[:2], gains)
    pre_own = units(norm_mlp_own)
    active_own = exact_gelu(pre_own)[0].astype(BF)
    mask_f = after(valid_mask, active_own).astype(F32)
    count = jnp.full((8, 128), jnp.sum(mask_f), F32)
    counted = to_core(count)
    table = jnp.concatenate(
        [
            lax.dynamic_slice_in_dim(jnp.asarray(rotary_table(LEN)), b * rows, rows, 0)
            for b in block_ids
        ],
        axis=0,
    )
    spots = jnp.concatenate([b * rows + jnp.arange(rows, dtype=jnp.int32) for b in block_ids])
    active_own, table, spots, counted, first, hidden_y, norm_attn_own = meet(
        active_own, table, spots, counted, first, hidden_y, norm_attn_own
    )
    count = count + counted

    near_blocks = near_blocks[:2]
    for block in hidden_y:
        near_blocks += [block, to_core(block)]
    second = second_far(first, hidden_y)
    counted = flip(count, 1)
    norm_attn_rest, norm_mlp_rest = both_norms(near_blocks[2:], gains)
    qkv_low = project_qkv(norm_attn_own, norm_attn_rest, qkv_weight, qkv_bias, table)
    context, log_total = attend(qkv_low, prefix_len, spots)
    norm_mlp_rest = after(norm_mlp_rest, context)
    context_far = swap_quarters(context)
    pre_rest = units(norm_mlp_rest)
    active_rest = exact_gelu(pre_rest)[0].astype(BF)
    active_rest, context, counted, second, context_far = meet(
        active_rest, context, counted, second, context_far
    )
    count = count + counted

    def branch_rows(context_rows, active_rows):
        return jnp.dot(context_rows, out_weight, preferred_element_type=F32) + jnp.dot(
            active_rows, fc2_weight, preferred_element_type=F32
        )

    def core_total(part):
        blocks = part.reshape(-1, 2, rows, D)
        return blocks[:, 0] + to_core(blocks[:, 1].astype(BF)).astype(F32)

    corner, beside, across = second
    first_mates = [to_core(block) for block in first]
    second_mates = [to_core(block) for block in [corner] + beside + across]
    count = count + flip(count, 2)
    counted = jnp.zeros_like(count)
    bit = 2
    while bit < tp:
        counted = lax.ppermute(count, "tensor", [(t, t ^ bit) for t in range(tp)])
        bit *= 2
        if bit < tp:
            count = count + counted
    part_rest = branch_rows(context[close:], active_rest).reshape(-1, 2, rows, D)
    mates_rest = to_core(part_rest[:, 1].astype(BF))
    part_own = branch_rows(context[:close], after(active_own, part_rest)).reshape(2, rows, D)
    part_own, mates_rest, counted, first_mates, second_mates = meet(
        part_own, mates_rest, counted, first_mates, second_mates
    )
    count = count + counted

    sums = part_rest[:, 0] + mates_rest.astype(F32)
    came = [to_y(sums[step - 1].astype(BF), step) for step in range(1, ways)]
    mates_own = to_core(part_own[1].astype(BF))
    counted = flip(count, 4) if dp > 4 else jnp.zeros_like(count)
    last = [flip(block, 1) for block in across]
    ahead = [first[0]] + beside + [first[1]] + across + [corner]
    mates = (
        [first_mates[0]]
        + second_mates[1:ways]
        + [first_mates[1]]
        + second_mates[ways:]
        + [second_mates[0]]
    )
    far_blocks = [block for pair in zip(ahead, mates) for block in pair]
    norms_far = both_norms(far_blocks, gains, 6 * ways)
    came, mates_own, counted, norms_far, last = meet(came, mates_own, counted, norms_far, last)
    count = count + counted
    mask = 8
    while mask < dp:
        count = count + flip(count, mask)
        mask *= 2
    branch = part_own[0] + mates_own.astype(F32)
    for got in came:
        branch = branch + got.astype(F32)
    output_f = hidden.astype(F32) + branch + out_bias.astype(F32) + fc2_bias.astype(F32)
    mismatch = output_f - teacher.astype(F32)
    scale = 2.0 * total_tokens / count[0, 0]
    grad_out = mask_f[:, None] * mismatch * scale
    grad_low = grad_out.astype(BF)
    grad_out, grad_low, last = meet(grad_out, grad_low, last)

    grad_y = [from_y(grad_low, step) for step in range(1, ways)]
    grad_first = first_far(grad_low)
    grad_mate = to_core(grad_low)
    far_blocks = [block for v in last for block in (v, to_core(v))]
    norm_attn_far, norm_mlp_far = both_norms(far_blocks, gains, 6 * ways, norms_far)
    fc1_quarter = quarter_of(fc1_weight, 1, quarter)
    fc2_quarter = quarter_of(after(fc2_weight, norm_mlp_far), 0, quarter)
    context_quarter = quarter_of(after(context, norm_mlp_far), 1, quarter)
    pre_far = jnp.dot(norm_mlp_far, fc1_quarter, preferred_element_type=F32) + quarter_of(
        fc1_bias, 0, quarter
    ).astype(F32)
    active_far, slope_far = exact_gelu(pre_far)
    active_far = active_far.astype(BF)
    grad_y, grad_first, active_far, grad_mate, fc2_quarter, context_quarter = meet(
        grad_y, grad_first, active_far, grad_mate, fc2_quarter, context_quarter
    )

    grad_second = second_far(grad_first, grad_y)
    grad_blocks = [grad_low, grad_mate]
    for block in grad_y:
        grad_blocks += [block, to_core(block)]
    grad_near = jnp.concatenate(grad_blocks, axis=0)
    grad_context = contract(grad_near, out_weight, 1, 1).astype(BF)
    grad_qkv = attend_back(qkv_low, grad_context, log_total, prefix_len, spots, table)
    grad_qkv, grad_near, grad_second = meet(grad_qkv, grad_near, grad_second)

    grad_last = last_far(grad_second)
    corner, beside, across = grad_second
    ahead = [grad_first[0]] + beside + [grad_first[1]] + across + [corner]
    mates = [to_core(block) for block in ahead]
    swapped = [flip(quarter_of(grad_qkv, 1, quarter ^ m), m) for m in (1, 2)]
    hidden_pre = jnp.concatenate([pre_own, pre_rest], axis=0)
    grad_inner = (contract(grad_near, fc2_weight, 1, 1) * exact_gelu(hidden_pre)[1]).astype(BF)
    grad_inner, grad_last, mates = meet(grad_inner, grad_last, mates)

    last_mates = [tuple(to_core(v) for v in pair) for pair in grad_last]
    grad_far = [block for pair in zip(ahead, mates) for block in pair]
    halves = [v for pair, mate in zip(grad_last, last_mates) for v in pair + mate]

    queue = []
    due = {}
    clock, launched = [0], [0]
    results = {}
    token = [grad_near]

    def gate(v):
        return after(v, token[0])

    def flipped(v, mask):
        return v, lambda value: flip(value, mask)

    def travel(low, name, wait):
        mask = 4
        while mask < dp:
            (got,) = yield [flipped(low, mask)], wait
            low = (low.astype(F32) + got.astype(F32)).astype(BF)
            mask, wait = mask * 2, 1
        (across,) = yield [flipped(low, 2)], 1
        near = jnp.concatenate([low, across], axis=0)
        (far,) = yield [flipped(near, 1)], 1
        results.setdefault(name, []).append((near, far))

    def swap_walk(v, into):
        got = yield [flipped(quarter_of(v, 1, quarter ^ 3), 3)], 2
        into.extend(got)

    def last_walk(kept, mates, parts, others, into):
        (got,) = yield [(mates, to_core)], 1
        sums = kept + got.astype(F32)
        total = sums[0]
        for step in range(1, ways):
            (got,) = yield [(sums[step].astype(BF), lambda v, s=step: to_y(v, s))], 1
            total = total + got.astype(F32)
        into["input"] = grad_out + total
        bit = 1
        while bit < tp:
            pairs = [(t, t ^ bit) for t in range(tp)]
            (got,) = yield [(parts, lambda v, p=pairs: lax.ppermute(v, "tensor", p))], 1
            parts = parts + got
            bit *= 2
        parts = jnp.concatenate([parts, others])
        bit = 1
        while bit < dp:
            (got,) = yield [flipped(parts, bit)], 1
            parts = parts + got
            bit *= 2
        into["small"] = parts

    def walk(walker):
        asked = next(walker)
        start(walker, asked, clock[0] - 1)

    def start(walker, asked, now):
        sends, wait = asked
        due.setdefault(now + wait, []).append((walker, [move(v) for v, move in sends]))

    parts_of = {}

    def cut(part, shares):
        unit = part.shape[0] // 16
        edges = [unit * sum(shares[:i]) for i in range(len(shares) + 1)]
        return [lax.slice_in_dim(part, a, b, axis=0) for a, b in zip(edges, edges[1:])]

    def enqueue(name, *units):
        before, _ = parts_of.get(name, (0, 0))
        parts_of[name] = (before + sum(u.shape[0] for u in units), units[0].shape[1])
        queue.extend((unit, name) for unit in units)

    def turn(*others):
        now = clock[0]
        clock[0] = now + 1
        arrived = due.pop(now, [])
        values = [got for _, gots in arrived for got in gots]
        fresh = []
        while queue and launched[0] <= now + 1:
            fresh.append(queue.pop(0) + (max(launched[0] - now, 0) + 1,))
            launched[0] += 1
        tied = list(
            lax.optimization_barrier(tuple(values) + tuple(f[0] for f in fresh) + others)
        )
        token[0] = tied[0]
        asked = []
        for walker, gots in arrived:
            gots = [tied.pop(0) for _ in gots]
            try:
                asked.append((walker, walker.send(gots)))
            except StopIteration:
                pass
        for _, name, wait in fresh:
            walker = travel(tied.pop(0), name, wait)
            asked.append((walker, next(walker)))
        for walker, request in asked:
            start(walker, request, now)
        return tied

    def place_one(whole, near, far, shape, axis, offset):
        rows_here, columns = near.shape[0] // 2, near.shape[1]
        if columns % 128 == 0:
            return place_quarters(whole, near, far, shape, axis, offset, quarter)
        if whole is None:
            whole = jnp.zeros(shape, F32)
        pieces = (near[:rows_here], far[:rows_here], near[rows_here:], far[rows_here:])
        for index, piece in enumerate(pieces):
            spot = quarter ^ index
            start = (
                (spot * (shape[0] // 4) + offset, 0) if axis == 0 else (offset, spot * columns)
            )
            whole = lax.dynamic_update_slice(whole, piece.astype(F32), start)
        return whole

    half = active_far.shape[1] // 2
    rights = [grad_near] + grad_far + halves

    def hidden_lefts(part):
        return [
            (active_own, half, 2, part, 0, 0),
            (active_rest, half, 2, part, 0, close),
            (active_far, half, 0, part, 0, LEN),
        ]

    chunk = half // 2
    kept_columns = context.shape[1] // 4
    enqueue("fc2", *outer_blocks(hidden_lefts(0), rights, [chunk] * 2, quarter))
    turn()
    grad_qkv_far = []
    walk(swap_walk(gate(grad_qkv), grad_qkv_far))
    lefts = hidden_lefts(1)
    for index, piece in enumerate([context_quarter] + context_far):
        lefts.append((piece, kept_columns, 0, 0, half, index * LEN))
    *parts, out_part = outer_blocks(
        lefts, [gate(grad_near)] + rights[1:], [chunk] * 2 + [kept_columns], quarter
    )
    enqueue("fc2", *parts)
    enqueue("out", out_part)
    swapped = turn(*swapped)
    halves = lax.optimization_barrier((token[0], *halves))[1:]
    grad_far += [jnp.concatenate(halves[i : i + 2], axis=0) for i in range(0, len(halves), 2)]
    grad_inner_far = back_blocks([gate(grad_far[0])] + grad_far[1:], fc2_quarter, slope_far)
    (grad_inner_far,) = turn(grad_inner_far)
    inner_quarter = gate(quarter_of(grad_inner, 1, quarter))
    fc1_part = (
        contract(norm_mlp_own, inner_quarter[:close], 0, 0)
        + contract(norm_mlp_rest, inner_quarter[close:], 0, 0)
        + contract(norm_mlp_far, grad_inner_far, 0, 0)
    )
    (fc1_part,) = turn(fc1_part.astype(BF))
    enqueue("fc1", *cut(fc1_part, [4, 4, 4, 4]))
    def norm_back_part(part):
        made = norm_back(
            gate(grad_qkv),
            grad_inner,
            qkv_weight,
            fc1_weight,
            gains,
            near_blocks[part * ways : (part + 1) * ways],
            part * ways,
        )
        return turn(*made)

    first_part, second_part = norm_back_part(0), norm_back_part(1)
    sums, qkv_sum, inner_sum = (a + b for a, b in zip(first_part[1:], second_part[1:]))
    blocks = [v.reshape(-1, 2, rows, D) for v in (first_part[0], second_part[0])]
    kept = jnp.concatenate([v[:, 0] for v in blocks], axis=0)
    mates = jnp.concatenate([v[:, 1].astype(BF) for v in blocks], axis=0)
    grad_later = gate(grad_out)
    bias_part = jnp.sum(grad_later, axis=0)
    error_part = jnp.sum(grad_later * grad_later) / (scale * scale)
    tensor_parts = jnp.concatenate(
        [sums[:4].reshape(-1), bias_part, jnp.full((D,), error_part, F32)]
    )
    fc1_bias_part, qkv_bias_part = inner_sum[0], qkv_sum[0]
    others = jnp.concatenate([fc1_bias_part, qkv_bias_part])
    outcome = {}
    qkv_quarter = gate(quarter_of(grad_qkv, 1, quarter))
    qkv_part = (
        contract(norm_attn_own, qkv_quarter[:close], 0, 0)
        + contract(norm_attn_rest, qkv_quarter[close:], 0, 0)
        + contract(norm_attn_far, jnp.concatenate([*swapped, *grad_qkv_far], axis=0), 0, 0)
    )
    qkv_part, mates, tensor_parts = turn(qkv_part.astype(BF), mates, tensor_parts)
    walk(last_walk(kept, mates, tensor_parts, others, outcome))
    enqueue("qkv", *cut(qkv_part, [4, 4, 4, 2, 1, 1]))
    axes = {"fc2": 0, "out": 0, "fc1": 1, "qkv": 1}
    placed = {name: (None, 0, 0) for name in axes}

    def place(name):
        whole, done, offset = placed[name]
        pieces = results[name][done]
        lengths, columns = parts_of[name]
        shape = (4 * lengths, columns) if axes[name] == 0 else (lengths, 4 * columns)
        whole = place_one(whole, *pieces, shape, axes[name], offset)
        placed[name] = (whole, done + 1, offset + pieces[0].shape[0] // 2)

    while queue or due:
        ready = []
        for name in axes:
            if len(ready) < 2 and len(results.get(name, [])) > placed[name][1]:
                place(name)
                ready.append(name)
        wholes = turn(*[placed[name][0] for name in ready])
        for name, whole in zip(ready, wholes):
            placed[name] = (whole,) + placed[name][1:]
    for name in axes:
        while len(results[name]) > placed[name][1]:
            place(name)
    input_grad = outcome["input"]
    small = outcome["small"]
    vectors = small[: 6 * D].reshape(6, D)
    fc1_bias_grad = small[6 * D : 6 * D + fc1_bias_part.shape[0]]
    qkv_bias_grad = small[6 * D + fc1_bias_part.shape[0] :]
    loss_value = vectors[5, 0] / (count[0, 0] * D)
    fc2_weight_grad, out_weight_grad = placed["fc2"][0], placed["out"][0]
    fc1_weight_grad, qkv_weight_grad = placed["fc1"][0], placed["qkv"][0]
    return (
        output_f.astype(BF),
        loss_value,
        input_grad,
        vectors[0],
        vectors[1],
        vectors[2],
        vectors[3],
        qkv_weight_grad,
        qkv_bias_grad,
        out_weight_grad,
        vectors[4],
        fc1_weight_grad,
        fc1_bias_grad,
        fc2_weight_grad,
        vectors[4],
    )


def solution(mesh):
    tokens = P(("dp", "tensor"), None)
    columns, lanes, down, whole = P(None, "tensor"), P("tensor"), P("tensor", None), P()
    in_specs = (
        tokens,
        tokens,
        P(("dp", "tensor")),
        P("dp"),
        whole,
        whole,
        whole,
        whole,
        columns,
        lanes,
        down,
        whole,
        columns,
        lanes,
        down,
        whole,
    )
    out_specs = (
        tokens,
        whole,
        tokens,
        whole,
        whole,
        whole,
        whole,
        columns,
        lanes,
        down,
        whole,
        columns,
        lanes,
        down,
        whole,
    )
    return jax.shard_map(
        on_device, mesh=mesh, in_specs=in_specs, out_specs=out_specs, check_vma=False
    )
```

```python
import functools

import jax
import jax.numpy as jnp
import numpy as np
from jax import lax
from jax.experimental import pallas as pl
from jax.experimental.pallas import tpu as pltpu
from jax.sharding import PartitionSpec as P

D = 2048
HD = 256
ROT = 64
LEN = 1024
EPSILON = 1e-05
BF = jnp.bfloat16
F32 = jnp.float32
SMALL = pl.CostEstimate(flops=1 << 20, bytes_accessed=1 << 16, transcendentals=0)


def rotary_table(length):
    half = ROT // 2
    frequency = (10000.0 ** (-2.0 * np.arange(half, dtype=np.float32) / ROT)).astype(np.float32)
    angles = np.arange(length, dtype=np.float32)[:, None] * frequency[None, :]
    cosine, sine = np.cos(angles), np.sin(angles)
    table = np.zeros((length, 3 * 128), np.float32)
    table[:, ROT:128] = 1.0
    table[:, :half] = table[:, half:ROT] = cosine
    table[:, 128 : 128 + half] = -sine
    table[:, 256 + half : 256 + ROT] = sine
    return table


def contract(left_side, right_side, left_dim, right_dim):
    return lax.dot_general(
        left_side,
        right_side,
        (((left_dim,), (right_dim,)), ((), ())),
        preferred_element_type=F32,
    )


def exact_gelu(pre_act):
    below = 0.5 + 0.5 * lax.erf(pre_act * 0.5**0.5)
    density = jnp.exp(-0.5 * pre_act * pre_act) * (2.0 * jnp.pi) ** -0.5
    return pre_act * below, below + pre_act * density


def after(value, *earlier):
    return lax.optimization_barrier((value,) + earlier)[0]


def turned(block, keep, up, down, sign):
    head = block[:, :128]
    half = ROT // 2
    moved = head * keep + sign * (
        pltpu.roll(head, 128 - half, 1) * up + pltpu.roll(head, half, 1) * down
    )
    return jnp.concatenate([moved, block[:, 128:]], axis=1)


def qkv_kernel(own_ref, rest_ref, w_ref, b_ref, keep_ref, up_ref, down_ref, o_ref):
    kind = pl.program_id(0) % 3
    row = 0
    for x_ref in (own_ref, rest_ref):
        rows = x_ref.shape[0]
        tile = min(rows, 512)
        for start in range(0, rows, tile):
            here = pl.ds(start, min(tile, rows - start))
            at = pl.ds(row + start, min(tile, rows - start))

            def project(x_ref=x_ref, here=here):
                return (
                    jnp.dot(x_ref[here, :], w_ref[...], preferred_element_type=F32)
                    + b_ref[...].astype(F32)
                )

            @pl.when(kind == 2)
            def _(at=at, project=project):
                o_ref[at, :] = project().astype(BF)

            @pl.when(kind != 2)
            def _(at=at, project=project):
                o_ref[at, :] = turned(
                    project(), keep_ref[at, :], up_ref[at, :], down_ref[at, :], 1.0
                ).astype(BF)

        row += rows


def project_qkv(own, rest, weight, bias, table):
    length, width = own.shape[0] + rest.shape[0], own.shape[1]
    columns = weight.shape[1]
    return pl.pallas_call(
        qkv_kernel,
        grid=(columns // HD,),
        in_specs=[
            pl.BlockSpec(own.shape, lambda j: (0, 0)),
            pl.BlockSpec(rest.shape, lambda j: (0, 0)),
            pl.BlockSpec((width, HD), lambda j: (0, j)),
            pl.BlockSpec((1, HD), lambda j: (0, j)),
        ]
        + [pl.BlockSpec((length, 128), lambda j, k=k: (0, k)) for k in range(3)],
        out_specs=pl.BlockSpec((length, HD), lambda j: (0, j)),
        out_shape=jax.ShapeDtypeStruct((length, columns), BF),
        compiler_params=pltpu.CompilerParams(vmem_limit_bytes=40 << 20),
        cost_estimate=SMALL,
        name="qkv_rotary",
    )(own, rest, weight, bias[None, :], table, table, table)


def visible_scores(queries, keys, row_spots, key_spots, prefix):
    scores = lax.dot_general(
        queries, keys, (((1,), (1,)), ((), ())), preferred_element_type=F32
    ) * (HD**-0.5)
    allowed = (key_spots <= row_spots) | (key_spots < prefix)
    return jnp.where(allowed, scores, -jnp.inf)


def attend_kernel(prefix_ref, q_ref, k_ref, v_ref, rows_ref, keys_ref, o_ref, log_ref):
    scores = visible_scores(
        q_ref[...], k_ref[...], rows_ref[...], keys_ref[...], prefix_ref[0]
    )
    top = jnp.max(scores, axis=-1, keepdims=True)
    weights = jnp.exp(scores - top)
    total = jnp.sum(weights, axis=-1, keepdims=True)
    probs = (weights * (1.0 / total)).astype(BF)
    o_ref[...] = jnp.dot(probs, v_ref[...], preferred_element_type=F32).astype(BF)
    log_ref[0] = top + jnp.log(total)


def attend(qkv, prefix, spots):
    length = qkv.shape[0]
    heads = qkv.shape[1] // (3 * HD)
    tile = length // 4
    whole = lambda part: pl.BlockSpec((length, HD), lambda h, i, p: (0, 3 * h + part))
    return pl.pallas_call(
        attend_kernel,
        grid_spec=pltpu.PrefetchScalarGridSpec(
            num_scalar_prefetch=1,
            grid=(heads, 4),
            in_specs=[
                pl.BlockSpec((tile, HD), lambda h, i, p: (i, 3 * h)),
                whole(1),
                whole(2),
                pl.BlockSpec((tile, 1), lambda h, i, p: (i, 0)),
                pl.BlockSpec((1, length), lambda h, i, p: (0, 0)),
            ],
            out_specs=[
                pl.BlockSpec((tile, HD), lambda h, i, p: (i, h)),
                pl.BlockSpec((1, tile, 1), lambda h, i, p: (h, i, 0)),
            ],
        ),
        out_shape=[
            jax.ShapeDtypeStruct((length, heads * HD), BF),
            jax.ShapeDtypeStruct((heads, length, 1), F32),
        ],
        compiler_params=pltpu.CompilerParams(vmem_limit_bytes=32 << 20),
        cost_estimate=SMALL,
        name="attend",
    )(prefix, qkv, qkv, qkv, spots[:, None], spots[None, :])


def attend_back_kernel(
    prefix_ref, q_ref, k_ref, v_ref, g_ref, log_ref, rows_ref, keys_ref, keep_ref, up_ref,
    down_ref, o_ref, dk_ref, dv_ref,
):
    length = q_ref.shape[0]
    tile = length // 4
    scale = HD**-0.5
    for i in range(4):
        at = pl.ds(i * tile, tile)
        q, g = q_ref[at, :], g_ref[at, :]
        scores = visible_scores(q, k_ref[...], rows_ref[at, :], keys_ref[...], prefix_ref[0])
        probs = jnp.exp(scores - log_ref[0, at, :])
        grad_probs = lax.dot_general(
            g, v_ref[...], (((1,), (1,)), ((), ())), preferred_element_type=F32
        )
        dots = jnp.sum(probs * grad_probs, axis=-1, keepdims=True)
        grad_scores = (probs * (grad_probs - dots)).astype(BF)
        dq = jnp.dot(grad_scores, k_ref[...], preferred_element_type=F32) * scale
        o_ref[at, :HD] = turned(
            dq, keep_ref[at, :], up_ref[at, :], down_ref[at, :], -1.0
        ).astype(BF)
        dk = contract(grad_scores, q, 0, 0)
        dv = contract(probs.astype(BF), g, 0, 0)
        if i == 0:
            dk_ref[...] = dk
            dv_ref[...] = dv
        else:
            dk_ref[...] += dk
            dv_ref[...] += dv
    o_ref[:, HD : 2 * HD] = turned(
        dk_ref[...] * scale, keep_ref[...], up_ref[...], down_ref[...], -1.0
    ).astype(BF)
    o_ref[:, 2 * HD :] = dv_ref[...].astype(BF)


def attend_back(qkv, grad_context, log_total, prefix, spots, table):
    length = qkv.shape[0]
    heads = qkv.shape[1] // (3 * HD)
    part = lambda n: pl.BlockSpec((length, HD), lambda h, p: (0, 3 * h + n))
    return pl.pallas_call(
        attend_back_kernel,
        grid_spec=pltpu.PrefetchScalarGridSpec(
            num_scalar_prefetch=1,
            grid=(heads,),
            in_specs=[
                part(0),
                part(1),
                part(2),
                pl.BlockSpec((length, HD), lambda h, p: (0, h)),
                pl.BlockSpec((1, length, 1), lambda h, p: (h, 0, 0)),
                pl.BlockSpec((length, 1), lambda h, p: (0, 0)),
                pl.BlockSpec((1, length), lambda h, p: (0, 0)),
            ]
            + [pl.BlockSpec((length, 128), lambda h, p, k=k: (0, k)) for k in range(3)],
            out_specs=pl.BlockSpec((length, 3 * HD), lambda h, p: (0, h)),
            scratch_shapes=[pltpu.VMEM((length, HD), F32), pltpu.VMEM((length, HD), F32)],
        ),
        out_shape=jax.ShapeDtypeStruct((length, heads * 3 * HD), BF),
        compiler_params=pltpu.CompilerParams(vmem_limit_bytes=48 << 20),
        cost_estimate=SMALL,
        name="attend_back",
    )(prefix, qkv, qkv, qkv, grad_context, log_total, spots[:, None], spots[None, :], table, table, table)


def norm_back_kernel(
    count, grad_qkv_ref, grad_inner_ref, qkv_ref, fc1_ref, gains_ref, *refs
):
    blocks, (o_ref, sums_ref, qkv_sum_ref, inner_sum_ref, rows_ref) = refs[:count], refs[count:]
    step = pl.program_id(0)
    for index, block in enumerate(blocks):

        @pl.when(step == index)
        def _(block=block):
            rows_ref[...] = block[...]

    features = rows_ref[...].astype(F32)
    centered = features - jnp.mean(features, axis=-1, keepdims=True)
    inverse = lax.rsqrt(jnp.mean(centered * centered, axis=-1, keepdims=True) + EPSILON)
    xhat = centered * inverse
    grad_attn = contract(grad_qkv_ref[...], qkv_ref[...], 1, 1)
    grad_mlp = contract(grad_inner_ref[...], fc1_ref[...], 1, 1)
    gain_a, gain_m = gains_ref[0:1, :].astype(F32), gains_ref[2:3, :].astype(F32)
    gained = grad_attn * gain_a + grad_mlp * gain_m
    o_ref[...] = inverse * (
        gained
        - jnp.mean(gained, axis=-1, keepdims=True)
        - xhat * jnp.mean(gained * xhat, axis=-1, keepdims=True)
    )
    pairs = (
        (sums_ref, 0, grad_attn * xhat),
        (sums_ref, 1, grad_attn),
        (sums_ref, 2, grad_mlp * xhat),
        (sums_ref, 3, grad_mlp),
        (qkv_sum_ref, 0, grad_qkv_ref[...].astype(F32)),
        (inner_sum_ref, 0, grad_inner_ref[...].astype(F32)),
    )
    for ref, row, values in pairs:
        total = jnp.sum(values, axis=0, keepdims=True)

        @pl.when(step == 0)
        def _(ref=ref, row=row, total=total):
            ref[row : row + 1, :] = total

        @pl.when(step > 0)
        def _(ref=ref, row=row, total=total):
            ref[row : row + 1, :] += total


def norm_back(grad_qkv, grad_inner, qkv_weight, fc1_weight, gains, blocks, skip):
    count = len(blocks)
    rows, width = blocks[0].shape
    each = lambda a: pl.BlockSpec((rows, a.shape[1]), lambda i: (i + skip, 0))
    full = lambda a: pl.BlockSpec(a.shape, lambda i: (0, 0), pipeline_mode=pl.Buffered(1))
    sums = [(8, width), (8, grad_qkv.shape[1]), (8, grad_inner.shape[1])]
    return pl.pallas_call(
        functools.partial(norm_back_kernel, count),
        grid=(count,),
        in_specs=[each(grad_qkv), each(grad_inner), full(qkv_weight), full(fc1_weight)]
        + [full(gains)]
        + [full(b) for b in blocks],
        out_specs=[pl.BlockSpec((rows, width), lambda i: (i, 0))]
        + [pl.BlockSpec(shape, lambda i: (0, 0)) for shape in sums],
        out_shape=[jax.ShapeDtypeStruct((count * rows, width), F32)]
        + [jax.ShapeDtypeStruct(shape, F32) for shape in sums],
        scratch_shapes=[pltpu.VMEM((rows, width), BF)],
        compiler_params=pltpu.CompilerParams(vmem_limit_bytes=56 << 20),
        cost_estimate=SMALL,
        name="norm_back",
    )(grad_qkv, grad_inner, qkv_weight, fc1_weight, gains, *blocks)


def place_kernel(quarter_ref, *refs):
    pieces, out_ref = refs[-5:-1], refs[-1]
    for index, piece in enumerate(pieces):

        @pl.when(pl.program_id(0) == index)
        def _(piece=piece):
            out_ref[...] = piece[...].astype(F32)


def place_quarters(whole, near, far, shape, axis, offset, quarter):
    rows, columns = near.shape[0] // 2, near.shape[1]
    if axis == 0:
        each, first_row = shape[0] // 4 // rows, offset // rows
        spot = lambda k, q: ((q[0] ^ k) * each + first_row, 0)
    else:
        spot = lambda k, q: (offset // rows, q[0] ^ k)
    first = whole is None
    operands = ([] if first else [whole]) + [near, far, near, far]
    return pl.pallas_call(
        place_kernel,
        grid_spec=pltpu.PrefetchScalarGridSpec(
            num_scalar_prefetch=1,
            grid=(4,),
            in_specs=([] if first else [pl.BlockSpec(memory_space=pl.ANY)])
            + [pl.BlockSpec((rows, columns), lambda k, q, h=h: (h, 0)) for h in (0, 0, 1, 1)],
            out_specs=pl.BlockSpec((rows, columns), spot),
        ),
        out_shape=jax.ShapeDtypeStruct(shape, F32),
        input_output_aliases={} if first else {1: 0},
        compiler_params=pltpu.CompilerParams(vmem_limit_bytes=24 << 20),
        cost_estimate=SMALL,
        name="place_quarters",
    )(quarter.reshape(1), *operands)


def norms_kernel(count, *refs):
    gains_ref, blocks, (attn_ref, mlp_ref) = refs[0], refs[1 : 1 + count], refs[-2:]
    for index, block in enumerate(blocks):

        @pl.when(pl.program_id(0) == index)
        def _(block=block):
            features = block[...].astype(F32)
            average = jnp.mean(features, axis=-1, keepdims=True)
            centered = features - average
            spread = jnp.mean(centered * centered, axis=-1, keepdims=True)
            xhat = centered * lax.rsqrt(spread + EPSILON)
            gain_a, shift_a, gain_m, shift_m = (
                gains_ref[i : i + 1, :].astype(F32) for i in range(4)
            )
            attn_ref[...] = (xhat * gain_a + shift_a).astype(BF)
            mlp_ref[...] = (xhat * gain_m + shift_m).astype(BF)


def both_norms(blocks, gains, total=None, into=()):
    count = len(blocks)
    total = total or count
    skip = total - count if into else 0
    rows, width = blocks[0].shape
    shape = jax.ShapeDtypeStruct((total * rows, width), BF)
    return pl.pallas_call(
        functools.partial(norms_kernel, count),
        grid=(count,),
        in_specs=[pl.BlockSpec(gains.shape, lambda i: (0, 0))]
        + [pl.BlockSpec((rows, width), lambda i: (0, 0))] * count
        + [pl.BlockSpec(memory_space=pl.ANY)] * len(into),
        out_specs=[pl.BlockSpec((rows, width), lambda i: (i + skip, 0))] * 2,
        out_shape=[shape, shape],
        input_output_aliases={1 + count: 0, 2 + count: 1} if into else {},
        compiler_params=pltpu.CompilerParams(vmem_limit_bytes=48 << 20),
        cost_estimate=SMALL,
        name="both_norms",
    )(gains, *blocks, *into)


def outer_kernel(lefts, pieces, outs, _, *refs):
    left_refs, rights = refs[:lefts], refs[lefts : -2 - outs]
    out_refs, (left_ref, joined_ref) = refs[-2 - outs : -2], refs[-2:]

    @pl.when(pl.program_id(0) == 0)
    def _():
        for ref, (row, column) in zip(left_refs, pieces):
            count, width = ref.shape
            step = min(count, 256)
            for start in range(0, count, step):
                left_ref[pl.ds(row, width), pl.ds(column + start, step)] = ref[
                    pl.ds(start, step), :
                ].T

    column = 0
    for ref in rights:
        joined_ref[pl.ds(column, ref.shape[0]), :] = ref[...]
        column += ref.shape[0]
    total = jnp.dot(left_ref[...], joined_ref[...], preferred_element_type=F32).astype(BF)
    row = 0
    for ref in out_refs:
        ref[...] = total[row : row + ref.shape[0], :]
        row += ref.shape[0]


def outer_blocks(lefts, rights, sizes, quarter):
    width = rights[0].shape[1]
    tokens = sum(r.shape[0] for r in rights)
    left = sum(sizes)
    tile = 512
    specs = [
        pl.BlockSpec((a.shape[0], taken), lambda j, q, m=times, o=offset: (0, q[0] * m + o))
        for a, taken, times, offset, _, _ in lefts
    ]
    pieces = [(row, token) for *_, row, token in lefts]
    return pl.pallas_call(
        functools.partial(outer_kernel, len(lefts), pieces, len(sizes)),
        grid_spec=pltpu.PrefetchScalarGridSpec(
            num_scalar_prefetch=1,
            grid=(width // tile,),
            in_specs=specs
            + [pl.BlockSpec((r.shape[0], tile), lambda j, q: (0, j)) for r in rights],
            out_specs=[pl.BlockSpec((size, tile), lambda j, q: (0, j)) for size in sizes],
            scratch_shapes=[pltpu.VMEM((left, tokens), BF), pltpu.VMEM((tokens, tile), BF)],
        ),
        out_shape=[jax.ShapeDtypeStruct((size, width), BF) for size in sizes],
        compiler_params=pltpu.CompilerParams(vmem_limit_bytes=56 << 20),
        cost_estimate=SMALL,
        name="outer_blocks",
    )(quarter.reshape(1), *[a for a, *_ in lefts], *rights)


def back_kernel(weight_ref, slope_ref, *refs):
    blocks, o_ref = refs[:-1], refs[-1]
    for index, block in enumerate(blocks):

        @pl.when(pl.program_id(0) == index)
        def _(block=block):
            o_ref[...] = (contract(block[...], weight_ref[...], 1, 1) * slope_ref[...]).astype(BF)


def back_blocks(blocks, weight, slope):
    rows, width = blocks[0].shape
    units = weight.shape[0]
    count = len(blocks)
    return pl.pallas_call(
        back_kernel,
        grid=(count,),
        in_specs=[
            pl.BlockSpec((units, width), lambda i: (0, 0)),
            pl.BlockSpec((rows, units), lambda i: (i, 0)),
        ]
        + [pl.BlockSpec((rows, width), lambda i: (0, 0))] * count,
        out_specs=pl.BlockSpec((rows, units), lambda i: (i, 0)),
        out_shape=jax.ShapeDtypeStruct((count * rows, units), BF),
        compiler_params=pltpu.CompilerParams(vmem_limit_bytes=56 << 20),
        cost_estimate=SMALL,
        name="back_blocks",
    )(weight, slope, *blocks)


def on_device(
    hidden,
    teacher,
    valid_mask,
    prefix_len,
    ln1_gain,
    ln1_bias,
    ln2_gain,
    ln2_bias,
    qkv_weight,
    qkv_bias,
    out_weight,
    out_bias,
    fc1_weight,
    fc1_bias,
    fc2_weight,
    fc2_bias,
):
    rows = hidden.shape[0]
    dp = lax.axis_size("dp")
    tp = lax.axis_size("tensor")
    ways = tp // 2
    squares = dp // 4
    total_tokens = dp * tp * rows
    heads = qkv_weight.shape[1] // (3 * HD)
    dp_index = lax.axis_index("dp")
    tp_index = lax.axis_index("tensor")
    core, y = tp_index % 2, tp_index // 2
    quarter = dp_index % 4

    def to_core(v):
        return lax.ppermute(v, "tensor", [(t, t ^ 1) for t in range(tp)])

    def from_y(v, step):
        pairs = [(t, ((t // 2 - step) % ways) * 2 + t % 2) for t in range(tp)]
        return lax.ppermute(v, "tensor", pairs)

    def to_y(v, step):
        pairs = [(t, ((t // 2 + step) % ways) * 2 + t % 2) for t in range(tp)]
        return lax.ppermute(v, "tensor", pairs)

    def flip(v, mask):
        return lax.ppermute(v, "dp", [(d, d ^ mask) for d in range(dp)])

    block_ids = [
        ((y + step) % ways) * 2 + (core if mate == 0 else 1 - core)
        for step in range(ways)
        for mate in (0, 1)
    ]

    def gather_near(own):
        over_y = [from_y(own, step) for step in range(1, ways)]
        parts = []
        for block in [own] + over_y:
            parts += [block, to_core(block)]
        return parts, over_y

    def first_far(own):
        return [flip(own, 1), flip(own, 2)]

    def second_far(first, over_y):
        corner = flip(first[1], 1)
        beside = [from_y(first[0], step) for step in range(1, ways)]
        across = [flip(block, 2) for block in over_y]
        return corner, beside, across

    def meet(*trees):
        leaves, shape = jax.tree.flatten(trees)
        return jax.tree.unflatten(shape, lax.optimization_barrier(tuple(leaves)))

    def quarter_of(v, axis, index):
        size = v.shape[axis] // 4
        return lax.dynamic_slice_in_dim(v, index * size, size, axis)

    def swap_quarters(v):
        return [flip(quarter_of(v, 1, quarter ^ mask), mask) for mask in (1, 2, 3)]

    gain_attn = ln1_gain.astype(F32)
    shift_attn = ln1_bias.astype(F32)
    gain_mlp = ln2_gain.astype(F32)
    shift_mlp = ln2_bias.astype(F32)
    gains = jnp.stack([ln1_gain, ln1_bias, ln2_gain, ln2_bias])
    close = 2 * rows

    def units(normed):
        return jnp.dot(normed, fc1_weight, preferred_element_type=F32) + fc1_bias.astype(F32)

    near_blocks, hidden_y = gather_near(hidden)
    first = first_far(hidden)
    norm_attn_own, norm_mlp_own = both_norms(near_blocks[:2], gains)
    pre_own = units(norm_mlp_own)
    active_own = exact_gelu(pre_own)[0].astype(BF)
    mask_f = after(valid_mask, active_own).astype(F32)
    count = jnp.full((8, 128), jnp.sum(mask_f), F32)
    counted = to_core(count)
    table = jnp.concatenate(
        [
            lax.dynamic_slice_in_dim(jnp.asarray(rotary_table(LEN)), b * rows, rows, 0)
            for b in block_ids
        ],
        axis=0,
    )
    spots = jnp.concatenate([b * rows + jnp.arange(rows, dtype=jnp.int32) for b in block_ids])
    active_own, table, spots, counted, first, hidden_y, norm_attn_own = meet(
        active_own, table, spots, counted, first, hidden_y, norm_attn_own
    )
    count = count + counted

    near_blocks = near_blocks[:2]
    for block in hidden_y:
        near_blocks += [block, to_core(block)]
    second = second_far(first, hidden_y)
    counted = flip(count, 1)
    norm_attn_rest, norm_mlp_rest = both_norms(near_blocks[2:], gains)
    qkv_low = project_qkv(norm_attn_own, norm_attn_rest, qkv_weight, qkv_bias, table)
    context, log_total = attend(qkv_low, prefix_len, spots)
    norm_mlp_rest = after(norm_mlp_rest, context)
    context_far = swap_quarters(context)
    pre_rest = units(norm_mlp_rest)
    active_rest = exact_gelu(pre_rest)[0].astype(BF)
    active_rest, context, counted, second, context_far = meet(
        active_rest, context, counted, second, context_far
    )
    count = count + counted

    def branch_rows(context_rows, active_rows):
        return jnp.dot(context_rows, out_weight, preferred_element_type=F32) + jnp.dot(
            active_rows, fc2_weight, preferred_element_type=F32
        )

    def core_total(part):
        blocks = part.reshape(-1, 2, rows, D)
        return blocks[:, 0] + to_core(blocks[:, 1].astype(BF)).astype(F32)

    corner, beside, across = second
    first_mates = [to_core(block) for block in first]
    second_mates = [to_core(block) for block in [corner] + beside + across]
    count = count + flip(count, 2)
    counted = jnp.zeros_like(count)
    bit = 2
    while bit < tp:
        counted = lax.ppermute(count, "tensor", [(t, t ^ bit) for t in range(tp)])
        bit *= 2
        if bit < tp:
            count = count + counted
    part_rest = branch_rows(context[close:], active_rest).reshape(-1, 2, rows, D)
    mates_rest = to_core(part_rest[:, 1].astype(BF))
    part_own = branch_rows(context[:close], after(active_own, part_rest)).reshape(2, rows, D)
    part_own, mates_rest, counted, first_mates, second_mates = meet(
        part_own, mates_rest, counted, first_mates, second_mates
    )
    count = count + counted

    sums = part_rest[:, 0] + mates_rest.astype(F32)
    came = [to_y(sums[step - 1].astype(BF), step) for step in range(1, ways)]
    mates_own = to_core(part_own[1].astype(BF))
    counted = flip(count, 4) if dp > 4 else jnp.zeros_like(count)
    last = [flip(block, 1) for block in across]
    ahead = [first[0]] + beside + [first[1]] + across + [corner]
    mates = (
        [first_mates[0]]
        + second_mates[1:ways]
        + [first_mates[1]]
        + second_mates[ways:]
        + [second_mates[0]]
    )
    far_blocks = [block for pair in zip(ahead, mates) for block in pair]
    norms_far = both_norms(far_blocks, gains, 6 * ways)
    came, mates_own, counted, norms_far, last = meet(came, mates_own, counted, norms_far, last)
    count = count + counted
    mask = 8
    while mask < dp:
        count = count + flip(count, mask)
        mask *= 2
    branch = part_own[0] + mates_own.astype(F32)
    for got in came:
        branch = branch + got.astype(F32)
    output_f = hidden.astype(F32) + branch + out_bias.astype(F32) + fc2_bias.astype(F32)
    mismatch = output_f - teacher.astype(F32)
    scale = 2.0 * total_tokens / count[0, 0]
    grad_out = mask_f[:, None] * mismatch * scale
    grad_low = grad_out.astype(BF)
    grad_out, grad_low, last = meet(grad_out, grad_low, last)

    grad_y = [from_y(grad_low, step) for step in range(1, ways)]
    grad_first = first_far(grad_low)
    grad_mate = to_core(grad_low)
    far_blocks = [block for v in last for block in (v, to_core(v))]
    norm_attn_far, norm_mlp_far = both_norms(far_blocks, gains, 6 * ways, norms_far)
    fc1_quarter = quarter_of(fc1_weight, 1, quarter)
    fc2_quarter = quarter_of(after(fc2_weight, norm_mlp_far), 0, quarter)
    context_quarter = quarter_of(after(context, norm_mlp_far), 1, quarter)
    pre_far = jnp.dot(norm_mlp_far, fc1_quarter, preferred_element_type=F32) + quarter_of(
        fc1_bias, 0, quarter
    ).astype(F32)
    active_far, slope_far = exact_gelu(pre_far)
    active_far = active_far.astype(BF)
    grad_y, grad_first, active_far, grad_mate, fc2_quarter, context_quarter = meet(
        grad_y, grad_first, active_far, grad_mate, fc2_quarter, context_quarter
    )

    grad_second = second_far(grad_first, grad_y)
    grad_blocks = [grad_low, grad_mate]
    for block in grad_y:
        grad_blocks += [block, to_core(block)]
    grad_near = jnp.concatenate(grad_blocks, axis=0)
    grad_context = contract(grad_near, out_weight, 1, 1).astype(BF)
    grad_qkv = attend_back(qkv_low, grad_context, log_total, prefix_len, spots, table)
    grad_qkv, grad_near, grad_second = meet(grad_qkv, grad_near, grad_second)

    corner, beside, across = grad_second
    grad_last = [flip(block, 1) for block in across]
    ahead = [grad_first[0]] + beside + [grad_first[1]] + across + [corner]
    mates = [to_core(block) for block in ahead]
    swapped_z = flip(quarter_of(grad_qkv, 1, quarter ^ 2), 2)
    hidden_pre = jnp.concatenate([pre_own, pre_rest], axis=0)
    grad_inner = (contract(grad_near, fc2_weight, 1, 1) * exact_gelu(hidden_pre)[1]).astype(BF)
    grad_inner, grad_last, mates, swapped_z = meet(grad_inner, grad_last, mates, swapped_z)

    swapped_x = flip(quarter_of(grad_qkv, 1, quarter ^ 1), 1)
    ahead += grad_last
    mates += [to_core(block) for block in grad_last]
    grad_far = [block for pair in zip(ahead, mates) for block in pair]

    queue = []
    due = {}
    clock, launched = [0], [0]
    results = {}
    token = [grad_near]

    def gate(v):
        return after(v, token[0])

    def flipped(v, mask):
        return v, lambda value: flip(value, mask)

    def travel(low, name, wait):
        mask = 4
        while mask < dp:
            (got,) = yield [flipped(low, mask)], wait
            low = (low.astype(F32) + got.astype(F32)).astype(BF)
            mask, wait = mask * 2, 1
        (across,) = yield [flipped(low, 2)], 1
        near = jnp.concatenate([low, across], axis=0)
        (far,) = yield [flipped(near, 1)], 1
        results.setdefault(name, []).append((near, far))

    def swap_walk(v, into):
        got = yield [flipped(quarter_of(v, 1, quarter ^ 3), 3)], 2
        into.extend(got)

    def last_walk(kept, mates, parts, others, into):
        (got,) = yield [(mates, to_core)], 1
        sums = kept + got.astype(F32)
        total = sums[0]
        for step in range(1, ways):
            (got,) = yield [(sums[step].astype(BF), lambda v, s=step: to_y(v, s))], 1
            total = total + got.astype(F32)
        into["input"] = grad_out + total
        bit = 1
        while bit < tp:
            pairs = [(t, t ^ bit) for t in range(tp)]
            (got,) = yield [(parts, lambda v, p=pairs: lax.ppermute(v, "tensor", p))], 1
            parts = parts + got
            bit *= 2
        parts = jnp.concatenate([parts, others])
        bit = 1
        while bit < dp:
            (got,) = yield [flipped(parts, bit)], 1
            parts = parts + got
            bit *= 2
        into["small"] = parts

    def walk(walker):
        asked = next(walker)
        start(walker, asked, clock[0] - 1)

    def start(walker, asked, now):
        sends, wait = asked
        due.setdefault(now + wait, []).append((walker, [move(v) for v, move in sends]))

    parts_of = {}

    def cut(part, shares):
        unit = part.shape[0] // 16
        edges = [unit * sum(shares[:i]) for i in range(len(shares) + 1)]
        return [lax.slice_in_dim(part, a, b, axis=0) for a, b in zip(edges, edges[1:])]

    def enqueue(name, *units):
        before, _ = parts_of.get(name, (0, 0))
        parts_of[name] = (before + sum(u.shape[0] for u in units), units[0].shape[1])
        queue.extend((unit, name) for unit in units)

    def turn(*others):
        now = clock[0]
        clock[0] = now + 1
        arrived = due.pop(now, [])
        values = [got for _, gots in arrived for got in gots]
        fresh = []
        while queue and launched[0] <= now + 1:
            fresh.append(queue.pop(0) + (max(launched[0] - now, 0) + 1,))
            launched[0] += 1
        tied = list(
            lax.optimization_barrier(tuple(values) + tuple(f[0] for f in fresh) + others)
        )
        token[0] = tied[0]
        asked = []
        for walker, gots in arrived:
            gots = [tied.pop(0) for _ in gots]
            try:
                asked.append((walker, walker.send(gots)))
            except StopIteration:
                pass
        for _, name, wait in fresh:
            walker = travel(tied.pop(0), name, wait)
            asked.append((walker, next(walker)))
        for walker, request in asked:
            start(walker, request, now)
        return tied

    def place_one(whole, near, far, shape, axis, offset):
        rows_here, columns = near.shape[0] // 2, near.shape[1]
        if columns % 128 == 0:
            return place_quarters(whole, near, far, shape, axis, offset, quarter)
        if whole is None:
            whole = jnp.zeros(shape, F32)
        pieces = (near[:rows_here], far[:rows_here], near[rows_here:], far[rows_here:])
        for index, piece in enumerate(pieces):
            spot = quarter ^ index
            start = (
                (spot * (shape[0] // 4) + offset, 0) if axis == 0 else (offset, spot * columns)
            )
            whole = lax.dynamic_update_slice(whole, piece.astype(F32), start)
        return whole

    half = active_far.shape[1] // 2
    rights = [grad_near] + grad_far

    def hidden_lefts(part):
        return [
            (active_own, half, 2, part, 0, 0),
            (active_rest, half, 2, part, 0, close),
            (active_far, half, 0, part, 0, LEN),
        ]

    chunk = half // 2
    kept_columns = context.shape[1] // 4
    enqueue("fc2", *outer_blocks(hidden_lefts(0), rights, [chunk] * 2, quarter))
    turn()
    grad_qkv_far = []
    walk(swap_walk(gate(grad_qkv), grad_qkv_far))
    lefts = hidden_lefts(1)
    for index, piece in enumerate([context_quarter] + context_far):
        lefts.append((piece, kept_columns, 0, 0, half, index * LEN))
    *parts, out_part = outer_blocks(
        lefts, [gate(grad_near)] + rights[1:], [chunk] * 2 + [kept_columns], quarter
    )
    enqueue("fc2", *parts)
    enqueue("out", out_part)
    (swapped_x,) = turn(swapped_x)
    grad_inner_far = back_blocks([gate(grad_far[0])] + grad_far[1:], fc2_quarter, slope_far)
    (grad_inner_far,) = turn(grad_inner_far)
    inner_quarter = gate(quarter_of(grad_inner, 1, quarter))
    fc1_part = (
        contract(norm_mlp_own, inner_quarter[:close], 0, 0)
        + contract(norm_mlp_rest, inner_quarter[close:], 0, 0)
        + contract(norm_mlp_far, grad_inner_far, 0, 0)
    )
    (fc1_part,) = turn(fc1_part.astype(BF))
    enqueue("fc1", *cut(fc1_part, [4, 4, 4, 4]))
    def norm_back_part(part):
        made = norm_back(
            gate(grad_qkv),
            grad_inner,
            qkv_weight,
            fc1_weight,
            gains,
            near_blocks[part * ways : (part + 1) * ways],
            part * ways,
        )
        return turn(*made)

    first_part, second_part = norm_back_part(0), norm_back_part(1)
    sums, qkv_sum, inner_sum = (a + b for a, b in zip(first_part[1:], second_part[1:]))
    blocks = [v.reshape(-1, 2, rows, D) for v in (first_part[0], second_part[0])]
    kept = jnp.concatenate([v[:, 0] for v in blocks], axis=0)
    mates = jnp.concatenate([v[:, 1].astype(BF) for v in blocks], axis=0)
    grad_later = gate(grad_out)
    bias_part = jnp.sum(grad_later, axis=0)
    error_part = jnp.sum(grad_later * grad_later) / (scale * scale)
    tensor_parts = jnp.concatenate(
        [sums[:4].reshape(-1), bias_part, jnp.full((D,), error_part, F32)]
    )
    fc1_bias_part, qkv_bias_part = inner_sum[0], qkv_sum[0]
    others = jnp.concatenate([fc1_bias_part, qkv_bias_part])
    outcome = {}
    qkv_quarter = gate(quarter_of(grad_qkv, 1, quarter))
    qkv_part = (
        contract(norm_attn_own, qkv_quarter[:close], 0, 0)
        + contract(norm_attn_rest, qkv_quarter[close:], 0, 0)
        + contract(norm_attn_far, jnp.concatenate([swapped_x, swapped_z, *grad_qkv_far], axis=0), 0, 0)
    )
    qkv_part, mates, tensor_parts = turn(qkv_part.astype(BF), mates, tensor_parts)
    walk(last_walk(kept, mates, tensor_parts, others, outcome))
    enqueue("qkv", *cut(qkv_part, [4, 4, 4, 4]))
    axes = {"fc2": 0, "out": 0, "fc1": 1, "qkv": 1}
    placed = {name: (None, 0, 0) for name in axes}

    def place(name):
        whole, done, offset = placed[name]
        pieces = results[name][done]
        lengths, columns = parts_of[name]
        shape = (4 * lengths, columns) if axes[name] == 0 else (lengths, 4 * columns)
        whole = place_one(whole, *pieces, shape, axes[name], offset)
        placed[name] = (whole, done + 1, offset + pieces[0].shape[0] // 2)

    while queue or due:
        ready = []
        for name in axes:
            if len(ready) < 2 and len(results.get(name, [])) > placed[name][1]:
                place(name)
                ready.append(name)
        wholes = turn(*[placed[name][0] for name in ready])
        for name, whole in zip(ready, wholes):
            placed[name] = (whole,) + placed[name][1:]
    for name in axes:
        while len(results[name]) > placed[name][1]:
            place(name)
    input_grad = outcome["input"]
    small = outcome["small"]
    vectors = small[: 6 * D].reshape(6, D)
    fc1_bias_grad = small[6 * D : 6 * D + fc1_bias_part.shape[0]]
    qkv_bias_grad = small[6 * D + fc1_bias_part.shape[0] :]
    loss_value = vectors[5, 0] / (count[0, 0] * D)
    fc2_weight_grad, out_weight_grad = placed["fc2"][0], placed["out"][0]
    fc1_weight_grad, qkv_weight_grad = placed["fc1"][0], placed["qkv"][0]
    return (
        output_f.astype(BF),
        loss_value,
        input_grad,
        vectors[0],
        vectors[1],
        vectors[2],
        vectors[3],
        qkv_weight_grad,
        qkv_bias_grad,
        out_weight_grad,
        vectors[4],
        fc1_weight_grad,
        fc1_bias_grad,
        fc2_weight_grad,
        vectors[4],
    )


def solution(mesh):
    tokens = P(("dp", "tensor"), None)
    columns, lanes, down, whole = P(None, "tensor"), P("tensor"), P("tensor", None), P()
    in_specs = (
        tokens,
        tokens,
        P(("dp", "tensor")),
        P("dp"),
        whole,
        whole,
        whole,
        whole,
        columns,
        lanes,
        down,
        whole,
        columns,
        lanes,
        down,
        whole,
    )
    out_specs = (
        tokens,
        whole,
        tokens,
        whole,
        whole,
        whole,
        whole,
        columns,
        lanes,
        down,
        whole,
        columns,
        lanes,
        down,
        whole,
    )
    return jax.shard_map(
        on_device, mesh=mesh, in_specs=in_specs, out_specs=out_specs, check_vma=False
    )
```

```python
import functools

import jax
import jax.numpy as jnp
import numpy as np
from jax import lax
from jax.experimental import pallas as pl
from jax.experimental.pallas import tpu as pltpu
from jax.sharding import PartitionSpec as P

D = 2048
HD = 256
ROT = 64
LEN = 1024
EPSILON = 1e-05
BF = jnp.bfloat16
F32 = jnp.float32
SMALL = pl.CostEstimate(flops=1 << 20, bytes_accessed=1 << 16, transcendentals=0)


def rotary_table(length):
    half = ROT // 2
    frequency = (10000.0 ** (-2.0 * np.arange(half, dtype=np.float32) / ROT)).astype(np.float32)
    angles = np.arange(length, dtype=np.float32)[:, None] * frequency[None, :]
    cosine, sine = np.cos(angles), np.sin(angles)
    table = np.zeros((length, 3 * 128), np.float32)
    table[:, ROT:128] = 1.0
    table[:, :half] = table[:, half:ROT] = cosine
    table[:, 128 : 128 + half] = -sine
    table[:, 256 + half : 256 + ROT] = sine
    return table


def contract(left_side, right_side, left_dim, right_dim):
    return lax.dot_general(
        left_side,
        right_side,
        (((left_dim,), (right_dim,)), ((), ())),
        preferred_element_type=F32,
    )


def exact_gelu(pre_act):
    below = 0.5 + 0.5 * lax.erf(pre_act * 0.5**0.5)
    density = jnp.exp(-0.5 * pre_act * pre_act) * (2.0 * jnp.pi) ** -0.5
    return pre_act * below, below + pre_act * density


def after(value, *earlier):
    return lax.optimization_barrier((value,) + earlier)[0]


def turned(block, keep, up, down, sign):
    head = block[:, :128]
    half = ROT // 2
    moved = head * keep + sign * (
        pltpu.roll(head, 128 - half, 1) * up + pltpu.roll(head, half, 1) * down
    )
    return jnp.concatenate([moved, block[:, 128:]], axis=1)


def qkv_kernel(own_ref, rest_ref, w_ref, b_ref, keep_ref, up_ref, down_ref, o_ref):
    kind = pl.program_id(0) % 3
    row = 0
    for x_ref in (own_ref, rest_ref):
        rows = x_ref.shape[0]
        tile = min(rows, 512)
        for start in range(0, rows, tile):
            here = pl.ds(start, min(tile, rows - start))
            at = pl.ds(row + start, min(tile, rows - start))

            def project(x_ref=x_ref, here=here):
                return (
                    jnp.dot(x_ref[here, :], w_ref[...], preferred_element_type=F32)
                    + b_ref[...].astype(F32)
                )

            @pl.when(kind == 2)
            def _(at=at, project=project):
                o_ref[at, :] = project().astype(BF)

            @pl.when(kind != 2)
            def _(at=at, project=project):
                o_ref[at, :] = turned(
                    project(), keep_ref[at, :], up_ref[at, :], down_ref[at, :], 1.0
                ).astype(BF)

        row += rows


def project_qkv(own, rest, weight, bias, table):
    length, width = own.shape[0] + rest.shape[0], own.shape[1]
    columns = weight.shape[1]
    return pl.pallas_call(
        qkv_kernel,
        grid=(columns // HD,),
        in_specs=[
            pl.BlockSpec(own.shape, lambda j: (0, 0)),
            pl.BlockSpec(rest.shape, lambda j: (0, 0)),
            pl.BlockSpec((width, HD), lambda j: (0, j)),
            pl.BlockSpec((1, HD), lambda j: (0, j)),
        ]
        + [pl.BlockSpec((length, 128), lambda j, k=k: (0, k)) for k in range(3)],
        out_specs=pl.BlockSpec((length, HD), lambda j: (0, j)),
        out_shape=jax.ShapeDtypeStruct((length, columns), BF),
        compiler_params=pltpu.CompilerParams(vmem_limit_bytes=40 << 20),
        cost_estimate=SMALL,
        name="qkv_rotary",
    )(own, rest, weight, bias[None, :], table, table, table)


def visible_scores(queries, keys, row_spots, key_spots, prefix):
    scores = lax.dot_general(
        queries, keys, (((1,), (1,)), ((), ())), preferred_element_type=F32
    ) * (HD**-0.5)
    allowed = (key_spots <= row_spots) | (key_spots < prefix)
    return jnp.where(allowed, scores, -jnp.inf)


def attend_kernel(prefix_ref, q_ref, k_ref, v_ref, rows_ref, keys_ref, o_ref, log_ref):
    scores = visible_scores(
        q_ref[...], k_ref[...], rows_ref[...], keys_ref[...], prefix_ref[0]
    )
    top = jnp.max(scores, axis=-1, keepdims=True)
    weights = jnp.exp(scores - top)
    total = jnp.sum(weights, axis=-1, keepdims=True)
    probs = (weights * (1.0 / total)).astype(BF)
    o_ref[...] = jnp.dot(probs, v_ref[...], preferred_element_type=F32).astype(BF)
    log_ref[0] = top + jnp.log(total)


def attend(qkv, prefix, spots):
    length = qkv.shape[0]
    heads = qkv.shape[1] // (3 * HD)
    tile = length // 4
    whole = lambda part: pl.BlockSpec((length, HD), lambda h, i, p: (0, 3 * h + part))
    return pl.pallas_call(
        attend_kernel,
        grid_spec=pltpu.PrefetchScalarGridSpec(
            num_scalar_prefetch=1,
            grid=(heads, 4),
            in_specs=[
                pl.BlockSpec((tile, HD), lambda h, i, p: (i, 3 * h)),
                whole(1),
                whole(2),
                pl.BlockSpec((tile, 1), lambda h, i, p: (i, 0)),
                pl.BlockSpec((1, length), lambda h, i, p: (0, 0)),
            ],
            out_specs=[
                pl.BlockSpec((tile, HD), lambda h, i, p: (i, h)),
                pl.BlockSpec((1, tile, 1), lambda h, i, p: (h, i, 0)),
            ],
        ),
        out_shape=[
            jax.ShapeDtypeStruct((length, heads * HD), BF),
            jax.ShapeDtypeStruct((heads, length, 1), F32),
        ],
        compiler_params=pltpu.CompilerParams(vmem_limit_bytes=32 << 20),
        cost_estimate=SMALL,
        name="attend",
    )(prefix, qkv, qkv, qkv, spots[:, None], spots[None, :])


def attend_back_kernel(
    prefix_ref, q_ref, k_ref, v_ref, g_ref, log_ref, rows_ref, keys_ref, keep_ref, up_ref,
    down_ref, o_ref, dk_ref, dv_ref,
):
    length = q_ref.shape[0]
    tile = length // 4
    scale = HD**-0.5
    for i in range(4):
        at = pl.ds(i * tile, tile)
        q, g = q_ref[at, :], g_ref[at, :]
        scores = visible_scores(q, k_ref[...], rows_ref[at, :], keys_ref[...], prefix_ref[0])
        probs = jnp.exp(scores - log_ref[0, at, :])
        grad_probs = lax.dot_general(
            g, v_ref[...], (((1,), (1,)), ((), ())), preferred_element_type=F32
        )
        dots = jnp.sum(probs * grad_probs, axis=-1, keepdims=True)
        grad_scores = (probs * (grad_probs - dots)).astype(BF)
        dq = jnp.dot(grad_scores, k_ref[...], preferred_element_type=F32) * scale
        o_ref[at, :HD] = turned(
            dq, keep_ref[at, :], up_ref[at, :], down_ref[at, :], -1.0
        ).astype(BF)
        dk = contract(grad_scores, q, 0, 0)
        dv = contract(probs.astype(BF), g, 0, 0)
        if i == 0:
            dk_ref[...] = dk
            dv_ref[...] = dv
        else:
            dk_ref[...] += dk
            dv_ref[...] += dv
    o_ref[:, HD : 2 * HD] = turned(
        dk_ref[...] * scale, keep_ref[...], up_ref[...], down_ref[...], -1.0
    ).astype(BF)
    o_ref[:, 2 * HD :] = dv_ref[...].astype(BF)


def attend_back(qkv, grad_context, log_total, prefix, spots, table):
    length = qkv.shape[0]
    heads = qkv.shape[1] // (3 * HD)
    part = lambda n: pl.BlockSpec((length, HD), lambda h, p: (0, 3 * h + n))
    return pl.pallas_call(
        attend_back_kernel,
        grid_spec=pltpu.PrefetchScalarGridSpec(
            num_scalar_prefetch=1,
            grid=(heads,),
            in_specs=[
                part(0),
                part(1),
                part(2),
                pl.BlockSpec((length, HD), lambda h, p: (0, h)),
                pl.BlockSpec((1, length, 1), lambda h, p: (h, 0, 0)),
                pl.BlockSpec((length, 1), lambda h, p: (0, 0)),
                pl.BlockSpec((1, length), lambda h, p: (0, 0)),
            ]
            + [pl.BlockSpec((length, 128), lambda h, p, k=k: (0, k)) for k in range(3)],
            out_specs=pl.BlockSpec((length, 3 * HD), lambda h, p: (0, h)),
            scratch_shapes=[pltpu.VMEM((length, HD), F32), pltpu.VMEM((length, HD), F32)],
        ),
        out_shape=jax.ShapeDtypeStruct((length, heads * 3 * HD), BF),
        compiler_params=pltpu.CompilerParams(vmem_limit_bytes=48 << 20),
        cost_estimate=SMALL,
        name="attend_back",
    )(prefix, qkv, qkv, qkv, grad_context, log_total, spots[:, None], spots[None, :], table, table, table)


def norm_back_kernel(
    count, grad_qkv_ref, grad_inner_ref, qkv_ref, fc1_ref, gains_ref, *refs
):
    blocks, (o_ref, sums_ref, qkv_sum_ref, inner_sum_ref, rows_ref) = refs[:count], refs[count:]
    step = pl.program_id(0)
    for index, block in enumerate(blocks):

        @pl.when(step == index)
        def _(block=block):
            rows_ref[...] = block[...]

    features = rows_ref[...].astype(F32)
    centered = features - jnp.mean(features, axis=-1, keepdims=True)
    inverse = lax.rsqrt(jnp.mean(centered * centered, axis=-1, keepdims=True) + EPSILON)
    xhat = centered * inverse
    grad_attn = contract(grad_qkv_ref[...], qkv_ref[...], 1, 1)
    grad_mlp = contract(grad_inner_ref[...], fc1_ref[...], 1, 1)
    gain_a, gain_m = gains_ref[0:1, :].astype(F32), gains_ref[2:3, :].astype(F32)
    gained = grad_attn * gain_a + grad_mlp * gain_m
    o_ref[...] = inverse * (
        gained
        - jnp.mean(gained, axis=-1, keepdims=True)
        - xhat * jnp.mean(gained * xhat, axis=-1, keepdims=True)
    )
    pairs = (
        (sums_ref, 0, grad_attn * xhat),
        (sums_ref, 1, grad_attn),
        (sums_ref, 2, grad_mlp * xhat),
        (sums_ref, 3, grad_mlp),
        (qkv_sum_ref, 0, grad_qkv_ref[...].astype(F32)),
        (inner_sum_ref, 0, grad_inner_ref[...].astype(F32)),
    )
    for ref, row, values in pairs:
        total = jnp.sum(values, axis=0, keepdims=True)

        @pl.when(step == 0)
        def _(ref=ref, row=row, total=total):
            ref[row : row + 1, :] = total

        @pl.when(step > 0)
        def _(ref=ref, row=row, total=total):
            ref[row : row + 1, :] += total


def norm_back(grad_qkv, grad_inner, qkv_weight, fc1_weight, gains, blocks, skip):
    count = len(blocks)
    rows, width = blocks[0].shape
    each = lambda a: pl.BlockSpec((rows, a.shape[1]), lambda i: (i + skip, 0))
    full = lambda a: pl.BlockSpec(a.shape, lambda i: (0, 0), pipeline_mode=pl.Buffered(1))
    sums = [(8, width), (8, grad_qkv.shape[1]), (8, grad_inner.shape[1])]
    return pl.pallas_call(
        functools.partial(norm_back_kernel, count),
        grid=(count,),
        in_specs=[each(grad_qkv), each(grad_inner), full(qkv_weight), full(fc1_weight)]
        + [full(gains)]
        + [full(b) for b in blocks],
        out_specs=[pl.BlockSpec((rows, width), lambda i: (i, 0))]
        + [pl.BlockSpec(shape, lambda i: (0, 0)) for shape in sums],
        out_shape=[jax.ShapeDtypeStruct((count * rows, width), F32)]
        + [jax.ShapeDtypeStruct(shape, F32) for shape in sums],
        scratch_shapes=[pltpu.VMEM((rows, width), BF)],
        compiler_params=pltpu.CompilerParams(vmem_limit_bytes=56 << 20),
        cost_estimate=SMALL,
        name="norm_back",
    )(grad_qkv, grad_inner, qkv_weight, fc1_weight, gains, *blocks)


def place_kernel(quarter_ref, *refs):
    pieces, out_ref = refs[-5:-1], refs[-1]
    for index, piece in enumerate(pieces):

        @pl.when(pl.program_id(0) == index)
        def _(piece=piece):
            out_ref[...] = piece[...].astype(F32)


def place_quarters(whole, near, far, shape, axis, offset, quarter):
    rows, columns = near.shape[0] // 2, near.shape[1]
    if axis == 0:
        each, first_row = shape[0] // 4 // rows, offset // rows
        spot = lambda k, q: ((q[0] ^ k) * each + first_row, 0)
    else:
        spot = lambda k, q: (offset // rows, q[0] ^ k)
    first = whole is None
    operands = ([] if first else [whole]) + [near, far, near, far]
    return pl.pallas_call(
        place_kernel,
        grid_spec=pltpu.PrefetchScalarGridSpec(
            num_scalar_prefetch=1,
            grid=(4,),
            in_specs=([] if first else [pl.BlockSpec(memory_space=pl.ANY)])
            + [pl.BlockSpec((rows, columns), lambda k, q, h=h: (h, 0)) for h in (0, 0, 1, 1)],
            out_specs=pl.BlockSpec((rows, columns), spot),
        ),
        out_shape=jax.ShapeDtypeStruct(shape, F32),
        input_output_aliases={} if first else {1: 0},
        compiler_params=pltpu.CompilerParams(vmem_limit_bytes=24 << 20),
        cost_estimate=SMALL,
        name="place_quarters",
    )(quarter.reshape(1), *operands)


def norms_kernel(count, *refs):
    gains_ref, blocks, (attn_ref, mlp_ref) = refs[0], refs[1 : 1 + count], refs[-2:]
    for index, block in enumerate(blocks):

        @pl.when(pl.program_id(0) == index)
        def _(block=block):
            features = block[...].astype(F32)
            average = jnp.mean(features, axis=-1, keepdims=True)
            centered = features - average
            spread = jnp.mean(centered * centered, axis=-1, keepdims=True)
            xhat = centered * lax.rsqrt(spread + EPSILON)
            gain_a, shift_a, gain_m, shift_m = (
                gains_ref[i : i + 1, :].astype(F32) for i in range(4)
            )
            attn_ref[...] = (xhat * gain_a + shift_a).astype(BF)
            mlp_ref[...] = (xhat * gain_m + shift_m).astype(BF)


def both_norms(blocks, gains, total=None, into=()):
    count = len(blocks)
    total = total or count
    skip = total - count if into else 0
    rows, width = blocks[0].shape
    shape = jax.ShapeDtypeStruct((total * rows, width), BF)
    return pl.pallas_call(
        functools.partial(norms_kernel, count),
        grid=(count,),
        in_specs=[pl.BlockSpec(gains.shape, lambda i: (0, 0))]
        + [pl.BlockSpec((rows, width), lambda i: (0, 0))] * count
        + [pl.BlockSpec(memory_space=pl.ANY)] * len(into),
        out_specs=[pl.BlockSpec((rows, width), lambda i: (i + skip, 0))] * 2,
        out_shape=[shape, shape],
        input_output_aliases={1 + count: 0, 2 + count: 1} if into else {},
        compiler_params=pltpu.CompilerParams(vmem_limit_bytes=48 << 20),
        cost_estimate=SMALL,
        name="both_norms",
    )(gains, *blocks, *into)


def outer_kernel(lefts, pieces, outs, _, *refs):
    left_refs, rights = refs[:lefts], refs[lefts : -2 - outs]
    out_refs, (left_ref, joined_ref) = refs[-2 - outs : -2], refs[-2:]

    @pl.when(pl.program_id(0) == 0)
    def _():
        for ref, (row, column) in zip(left_refs, pieces):
            count, width = ref.shape
            step = min(count, 256)
            for start in range(0, count, step):
                left_ref[pl.ds(row, width), pl.ds(column + start, step)] = ref[
                    pl.ds(start, step), :
                ].T

    column = 0
    for ref in rights:
        joined_ref[pl.ds(column, ref.shape[0]), :] = ref[...]
        column += ref.shape[0]
    total = jnp.dot(left_ref[...], joined_ref[...], preferred_element_type=F32).astype(BF)
    row = 0
    for ref in out_refs:
        ref[...] = total[row : row + ref.shape[0], :]
        row += ref.shape[0]


def outer_blocks(lefts, rights, sizes, quarter):
    width = rights[0].shape[1]
    tokens = sum(r.shape[0] for r in rights)
    left = sum(sizes)
    tile = 512
    specs = [
        pl.BlockSpec((a.shape[0], taken), lambda j, q, m=times, o=offset: (0, q[0] * m + o))
        for a, taken, times, offset, _, _ in lefts
    ]
    pieces = [(row, token) for *_, row, token in lefts]
    return pl.pallas_call(
        functools.partial(outer_kernel, len(lefts), pieces, len(sizes)),
        grid_spec=pltpu.PrefetchScalarGridSpec(
            num_scalar_prefetch=1,
            grid=(width // tile,),
            in_specs=specs
            + [pl.BlockSpec((r.shape[0], tile), lambda j, q: (0, j)) for r in rights],
            out_specs=[pl.BlockSpec((size, tile), lambda j, q: (0, j)) for size in sizes],
            scratch_shapes=[pltpu.VMEM((left, tokens), BF), pltpu.VMEM((tokens, tile), BF)],
        ),
        out_shape=[jax.ShapeDtypeStruct((size, width), BF) for size in sizes],
        compiler_params=pltpu.CompilerParams(vmem_limit_bytes=56 << 20),
        cost_estimate=SMALL,
        name="outer_blocks",
    )(quarter.reshape(1), *[a for a, *_ in lefts], *rights)


def back_kernel(weight_ref, slope_ref, *refs):
    blocks, o_ref = refs[:-1], refs[-1]
    for index, block in enumerate(blocks):

        @pl.when(pl.program_id(0) == index)
        def _(block=block):
            o_ref[...] = (contract(block[...], weight_ref[...], 1, 1) * slope_ref[...]).astype(BF)


def back_blocks(blocks, weight, slope):
    rows, width = blocks[0].shape
    units = weight.shape[0]
    count = len(blocks)
    return pl.pallas_call(
        back_kernel,
        grid=(count,),
        in_specs=[
            pl.BlockSpec((units, width), lambda i: (0, 0)),
            pl.BlockSpec((rows, units), lambda i: (i, 0)),
        ]
        + [pl.BlockSpec((rows, width), lambda i: (0, 0))] * count,
        out_specs=pl.BlockSpec((rows, units), lambda i: (i, 0)),
        out_shape=jax.ShapeDtypeStruct((count * rows, units), BF),
        compiler_params=pltpu.CompilerParams(vmem_limit_bytes=56 << 20),
        cost_estimate=SMALL,
        name="back_blocks",
    )(weight, slope, *blocks)


def on_device(
    hidden,
    teacher,
    valid_mask,
    prefix_len,
    ln1_gain,
    ln1_bias,
    ln2_gain,
    ln2_bias,
    qkv_weight,
    qkv_bias,
    out_weight,
    out_bias,
    fc1_weight,
    fc1_bias,
    fc2_weight,
    fc2_bias,
):
    rows = hidden.shape[0]
    dp = lax.axis_size("dp")
    tp = lax.axis_size("tensor")
    ways = tp // 2
    squares = dp // 4
    total_tokens = dp * tp * rows
    heads = qkv_weight.shape[1] // (3 * HD)
    dp_index = lax.axis_index("dp")
    tp_index = lax.axis_index("tensor")
    core, y = tp_index % 2, tp_index // 2
    quarter = dp_index % 4

    def to_core(v):
        return lax.ppermute(v, "tensor", [(t, t ^ 1) for t in range(tp)])

    def from_y(v, step):
        pairs = [(t, ((t // 2 - step) % ways) * 2 + t % 2) for t in range(tp)]
        return lax.ppermute(v, "tensor", pairs)

    def to_y(v, step):
        pairs = [(t, ((t // 2 + step) % ways) * 2 + t % 2) for t in range(tp)]
        return lax.ppermute(v, "tensor", pairs)

    def flip(v, mask):
        return lax.ppermute(v, "dp", [(d, d ^ mask) for d in range(dp)])

    block_ids = [
        ((y + step) % ways) * 2 + (core if mate == 0 else 1 - core)
        for step in range(ways)
        for mate in (0, 1)
    ]

    def gather_near(own):
        over_y = [from_y(own, step) for step in range(1, ways)]
        parts = []
        for block in [own] + over_y:
            parts += [block, to_core(block)]
        return parts, over_y

    def first_far(own):
        return [flip(own, 1), flip(own, 2)]

    def second_far(first, over_y):
        corner = flip(first[1], 1)
        beside = [from_y(first[0], step) for step in range(1, ways)]
        across = [flip(block, 2) for block in over_y]
        return corner, beside, across

    def meet(*trees):
        leaves, shape = jax.tree.flatten(trees)
        return jax.tree.unflatten(shape, lax.optimization_barrier(tuple(leaves)))

    def quarter_of(v, axis, index):
        size = v.shape[axis] // 4
        return lax.dynamic_slice_in_dim(v, index * size, size, axis)

    def swap_quarters(v):
        return [flip(quarter_of(v, 1, quarter ^ mask), mask) for mask in (1, 2, 3)]

    gain_attn = ln1_gain.astype(F32)
    shift_attn = ln1_bias.astype(F32)
    gain_mlp = ln2_gain.astype(F32)
    shift_mlp = ln2_bias.astype(F32)
    gains = jnp.stack([ln1_gain, ln1_bias, ln2_gain, ln2_bias])
    close = 2 * rows

    def units(normed):
        return jnp.dot(normed, fc1_weight, preferred_element_type=F32) + fc1_bias.astype(F32)

    near_blocks, hidden_y = gather_near(hidden)
    first = first_far(hidden)
    norm_attn_own, norm_mlp_own = both_norms(near_blocks[:2], gains)
    pre_own = units(norm_mlp_own)
    active_own = exact_gelu(pre_own)[0].astype(BF)
    mask_f = after(valid_mask, active_own).astype(F32)
    count = jnp.full((8, 128), jnp.sum(mask_f), F32)
    counted = to_core(count)
    table = jnp.concatenate(
        [
            lax.dynamic_slice_in_dim(jnp.asarray(rotary_table(LEN)), b * rows, rows, 0)
            for b in block_ids
        ],
        axis=0,
    )
    spots = jnp.concatenate([b * rows + jnp.arange(rows, dtype=jnp.int32) for b in block_ids])
    active_own, table, spots, counted, first, hidden_y, norm_attn_own = meet(
        active_own, table, spots, counted, first, hidden_y, norm_attn_own
    )
    count = count + counted

    near_blocks = near_blocks[:2]
    for block in hidden_y:
        near_blocks += [block, to_core(block)]
    second = second_far(first, hidden_y)
    counted = flip(count, 1)
    norm_attn_rest, norm_mlp_rest = both_norms(near_blocks[2:], gains)
    qkv_low = project_qkv(norm_attn_own, norm_attn_rest, qkv_weight, qkv_bias, table)
    context, log_total = attend(qkv_low, prefix_len, spots)
    norm_mlp_rest = after(norm_mlp_rest, context)
    context_far = swap_quarters(context)
    pre_rest = units(norm_mlp_rest)
    active_rest = exact_gelu(pre_rest)[0].astype(BF)
    active_rest, context, counted, second, context_far = meet(
        active_rest, context, counted, second, context_far
    )
    count = count + counted

    def branch_rows(context_rows, active_rows):
        return jnp.dot(context_rows, out_weight, preferred_element_type=F32) + jnp.dot(
            active_rows, fc2_weight, preferred_element_type=F32
        )

    def core_total(part):
        blocks = part.reshape(-1, 2, rows, D)
        return blocks[:, 0] + to_core(blocks[:, 1].astype(BF)).astype(F32)

    corner, beside, across = second
    first_mates = [to_core(block) for block in first]
    second_mates = [to_core(block) for block in [corner] + beside + across]
    count = count + flip(count, 2)
    counted = jnp.zeros_like(count)
    bit = 2
    while bit < tp:
        counted = lax.ppermute(count, "tensor", [(t, t ^ bit) for t in range(tp)])
        bit *= 2
        if bit < tp:
            count = count + counted
    part_rest = branch_rows(context[close:], active_rest).reshape(-1, 2, rows, D)
    mates_rest = to_core(part_rest[:, 1].astype(BF))
    part_own = branch_rows(context[:close], after(active_own, part_rest)).reshape(2, rows, D)
    part_own, mates_rest, counted, first_mates, second_mates = meet(
        part_own, mates_rest, counted, first_mates, second_mates
    )
    count = count + counted

    sums = part_rest[:, 0] + mates_rest.astype(F32)
    came = [to_y(sums[step - 1].astype(BF), step) for step in range(1, ways)]
    mates_own = to_core(part_own[1].astype(BF))
    counted = flip(count, 4) if dp > 4 else jnp.zeros_like(count)
    last = [flip(block, 1) for block in across]
    ahead = [first[0]] + beside + [first[1]] + across + [corner]
    mates = (
        [first_mates[0]]
        + second_mates[1:ways]
        + [first_mates[1]]
        + second_mates[ways:]
        + [second_mates[0]]
    )
    far_blocks = [block for pair in zip(ahead, mates) for block in pair]
    norms_far = both_norms(far_blocks, gains, 6 * ways)
    fc2_quarter = quarter_of(after(fc2_weight, norms_far[0]), 0, quarter)
    context_quarter = quarter_of(after(context, norms_far[0]), 1, quarter)
    came, mates_own, counted, norms_far, last, fc2_quarter, context_quarter = meet(
        came, mates_own, counted, norms_far, last, fc2_quarter, context_quarter
    )
    count = count + counted
    mask = 8
    while mask < dp:
        count = count + flip(count, mask)
        mask *= 2
    branch = part_own[0] + mates_own.astype(F32)
    for got in came:
        branch = branch + got.astype(F32)
    output_f = hidden.astype(F32) + branch + out_bias.astype(F32) + fc2_bias.astype(F32)
    mismatch = output_f - teacher.astype(F32)
    scale = 2.0 * total_tokens / count[0, 0]
    grad_out = mask_f[:, None] * mismatch * scale
    grad_low = grad_out.astype(BF)
    grad_out, grad_low, last = meet(grad_out, grad_low, last)

    grad_y = [from_y(grad_low, step) for step in range(1, ways)]
    grad_first = first_far(grad_low)
    grad_mate = to_core(grad_low)
    far_blocks = [block for v in last for block in (v, to_core(v))]
    norm_attn_far, norm_mlp_far = both_norms(far_blocks, gains, 6 * ways, norms_far)
    fc1_quarter = quarter_of(fc1_weight, 1, quarter)
    pre_far = jnp.dot(norm_mlp_far, fc1_quarter, preferred_element_type=F32) + quarter_of(
        fc1_bias, 0, quarter
    ).astype(F32)
    active_far, slope_far = exact_gelu(pre_far)
    active_far = active_far.astype(BF)
    grad_y, grad_first, active_far, grad_mate = meet(grad_y, grad_first, active_far, grad_mate)

    grad_second = second_far(grad_first, grad_y)
    grad_blocks = [grad_low, grad_mate]
    for block in grad_y:
        grad_blocks += [block, to_core(block)]
    grad_near = jnp.concatenate(grad_blocks, axis=0)
    grad_context = contract(grad_near, out_weight, 1, 1).astype(BF)
    grad_qkv = attend_back(qkv_low, grad_context, log_total, prefix_len, spots, table)
    grad_qkv, grad_near, grad_second = meet(grad_qkv, grad_near, grad_second)

    corner, beside, across = grad_second
    grad_last = [flip(block, 1) for block in across]
    ahead = [grad_first[0]] + beside + [grad_first[1]] + across + [corner]
    mates = [to_core(block) for block in ahead]
    swapped_z = flip(quarter_of(grad_qkv, 1, quarter ^ 2), 2)
    hidden_pre = jnp.concatenate([pre_own, pre_rest], axis=0)
    grad_inner = (contract(grad_near, fc2_weight, 1, 1) * exact_gelu(hidden_pre)[1]).astype(BF)
    grad_inner, grad_last, mates, swapped_z = meet(grad_inner, grad_last, mates, swapped_z)

    swapped_x = flip(quarter_of(grad_qkv, 1, quarter ^ 1), 1)
    ahead += grad_last
    mates += [to_core(block) for block in grad_last]
    grad_far = [block for pair in zip(ahead, mates) for block in pair]

    queue = []
    due = {}
    clock, launched = [0], [0]
    results = {}
    token = [grad_near]

    def gate(v):
        return after(v, token[0])

    def flipped(v, mask):
        return v, lambda value: flip(value, mask)

    def travel(low, name, wait):
        mask = 4
        while mask < dp:
            (got,) = yield [flipped(low, mask)], wait
            low = (low.astype(F32) + got.astype(F32)).astype(BF)
            mask, wait = mask * 2, 1
        (across,) = yield [flipped(low, 2)], 1
        near = jnp.concatenate([low, across], axis=0)
        (far,) = yield [flipped(near, 1)], 1
        results.setdefault(name, []).append((near, far))

    def swap_walk(v, into):
        got = yield [flipped(quarter_of(v, 1, quarter ^ 3), 3)], 2
        into.extend(got)

    def last_walk(kept, mates, parts, others, into):
        (got,) = yield [(mates, to_core)], 1
        sums = kept + got.astype(F32)
        total = sums[0]
        for step in range(1, ways):
            (got,) = yield [(sums[step].astype(BF), lambda v, s=step: to_y(v, s))], 1
            total = total + got.astype(F32)
        into["input"] = grad_out + total
        bit = 1
        while bit < tp:
            pairs = [(t, t ^ bit) for t in range(tp)]
            (got,) = yield [(parts, lambda v, p=pairs: lax.ppermute(v, "tensor", p))], 1
            parts = parts + got
            bit *= 2
        parts = jnp.concatenate([parts, others])
        bit = 1
        while bit < dp:
            (got,) = yield [flipped(parts, bit)], 1
            parts = parts + got
            bit *= 2
        into["small"] = parts

    def walk(walker):
        asked = next(walker)
        start(walker, asked, clock[0] - 1)

    def start(walker, asked, now):
        sends, wait = asked
        due.setdefault(now + wait, []).append((walker, [move(v) for v, move in sends]))

    parts_of = {}

    def cut(part, shares):
        unit = part.shape[0] // 16
        edges = [unit * sum(shares[:i]) for i in range(len(shares) + 1)]
        return [lax.slice_in_dim(part, a, b, axis=0) for a, b in zip(edges, edges[1:])]

    def enqueue(name, *units):
        before, _ = parts_of.get(name, (0, 0))
        parts_of[name] = (before + sum(u.shape[0] for u in units), units[0].shape[1])
        queue.extend((unit, name) for unit in units)

    def turn(*others):
        now = clock[0]
        clock[0] = now + 1
        arrived = due.pop(now, [])
        values = [got for _, gots in arrived for got in gots]
        fresh = []
        while queue and launched[0] <= now + 1:
            fresh.append(queue.pop(0) + (max(launched[0] - now, 0) + 1,))
            launched[0] += 1
        tied = list(
            lax.optimization_barrier(tuple(values) + tuple(f[0] for f in fresh) + others)
        )
        token[0] = tied[0]
        asked = []
        for walker, gots in arrived:
            gots = [tied.pop(0) for _ in gots]
            try:
                asked.append((walker, walker.send(gots)))
            except StopIteration:
                pass
        for _, name, wait in fresh:
            walker = travel(tied.pop(0), name, wait)
            asked.append((walker, next(walker)))
        for walker, request in asked:
            start(walker, request, now)
        return tied

    def place_one(whole, near, far, shape, axis, offset):
        rows_here, columns = near.shape[0] // 2, near.shape[1]
        if columns % 128 == 0:
            return place_quarters(whole, near, far, shape, axis, offset, quarter)
        if whole is None:
            whole = jnp.zeros(shape, F32)
        pieces = (near[:rows_here], far[:rows_here], near[rows_here:], far[rows_here:])
        for index, piece in enumerate(pieces):
            spot = quarter ^ index
            start = (
                (spot * (shape[0] // 4) + offset, 0) if axis == 0 else (offset, spot * columns)
            )
            whole = lax.dynamic_update_slice(whole, piece.astype(F32), start)
        return whole

    half = active_far.shape[1] // 2
    rights = [grad_near] + grad_far

    def hidden_lefts(part):
        return [
            (active_own, half, 2, part, 0, 0),
            (active_rest, half, 2, part, 0, close),
            (active_far, half, 0, part, 0, LEN),
        ]

    chunk = half // 2
    kept_columns = context.shape[1] // 4
    enqueue("fc2", *outer_blocks(hidden_lefts(0), rights, [chunk] * 2, quarter))
    turn()
    grad_qkv_far = []
    walk(swap_walk(gate(grad_qkv), grad_qkv_far))
    lefts = hidden_lefts(1)
    for index, piece in enumerate([context_quarter] + context_far):
        lefts.append((piece, kept_columns, 0, 0, half, index * LEN))
    *parts, out_part = outer_blocks(
        lefts, [gate(grad_near)] + rights[1:], [chunk] * 2 + [kept_columns], quarter
    )
    enqueue("fc2", *parts)
    enqueue("out", out_part)
    (swapped_x,) = turn(swapped_x)
    grad_inner_far = back_blocks([gate(grad_far[0])] + grad_far[1:], fc2_quarter, slope_far)
    (grad_inner_far,) = turn(grad_inner_far)
    inner_quarter = gate(quarter_of(grad_inner, 1, quarter))
    fc1_part = (
        contract(norm_mlp_own, inner_quarter[:close], 0, 0)
        + contract(norm_mlp_rest, inner_quarter[close:], 0, 0)
        + contract(norm_mlp_far, grad_inner_far, 0, 0)
    )
    (fc1_part,) = turn(fc1_part.astype(BF))
    enqueue("fc1", *cut(fc1_part, [4, 4, 4, 4]))
    def norm_back_part(part):
        made = norm_back(
            gate(grad_qkv),
            grad_inner,
            qkv_weight,
            fc1_weight,
            gains,
            near_blocks[part * ways : (part + 1) * ways],
            part * ways,
        )
        return turn(*made)

    first_part, second_part = norm_back_part(0), norm_back_part(1)
    sums, qkv_sum, inner_sum = (a + b for a, b in zip(first_part[1:], second_part[1:]))
    blocks = [v.reshape(-1, 2, rows, D) for v in (first_part[0], second_part[0])]
    kept = jnp.concatenate([v[:, 0] for v in blocks], axis=0)
    mates = jnp.concatenate([v[:, 1].astype(BF) for v in blocks], axis=0)
    grad_later = gate(grad_out)
    bias_part = jnp.sum(grad_later, axis=0)
    error_part = jnp.sum(grad_later * grad_later) / (scale * scale)
    tensor_parts = jnp.concatenate(
        [sums[:4].reshape(-1), bias_part, jnp.full((D,), error_part, F32)]
    )
    fc1_bias_part, qkv_bias_part = inner_sum[0], qkv_sum[0]
    others = jnp.concatenate([fc1_bias_part, qkv_bias_part])
    outcome = {}
    qkv_quarter = gate(quarter_of(grad_qkv, 1, quarter))
    qkv_part = (
        contract(norm_attn_own, qkv_quarter[:close], 0, 0)
        + contract(norm_attn_rest, qkv_quarter[close:], 0, 0)
        + contract(norm_attn_far, jnp.concatenate([swapped_x, swapped_z, *grad_qkv_far], axis=0), 0, 0)
    )
    qkv_part, mates, tensor_parts = turn(qkv_part.astype(BF), mates, tensor_parts)
    walk(last_walk(kept, mates, tensor_parts, others, outcome))
    enqueue("qkv", *cut(qkv_part, [4, 4, 4, 2, 1, 1]))
    axes = {"fc2": 0, "out": 0, "fc1": 1, "qkv": 1}
    placed = {name: (None, 0, 0) for name in axes}

    def place(name):
        whole, done, offset = placed[name]
        pieces = results[name][done]
        lengths, columns = parts_of[name]
        shape = (4 * lengths, columns) if axes[name] == 0 else (lengths, 4 * columns)
        whole = place_one(whole, *pieces, shape, axes[name], offset)
        placed[name] = (whole, done + 1, offset + pieces[0].shape[0] // 2)

    while queue or due:
        ready = []
        for name in axes:
            if len(ready) < 2 and len(results.get(name, [])) > placed[name][1]:
                place(name)
                ready.append(name)
        wholes = turn(*[placed[name][0] for name in ready])
        for name, whole in zip(ready, wholes):
            placed[name] = (whole,) + placed[name][1:]
    for name in axes:
        while len(results[name]) > placed[name][1]:
            place(name)
    input_grad = outcome["input"]
    small = outcome["small"]
    vectors = small[: 6 * D].reshape(6, D)
    fc1_bias_grad = small[6 * D : 6 * D + fc1_bias_part.shape[0]]
    qkv_bias_grad = small[6 * D + fc1_bias_part.shape[0] :]
    loss_value = vectors[5, 0] / (count[0, 0] * D)
    fc2_weight_grad, out_weight_grad = placed["fc2"][0], placed["out"][0]
    fc1_weight_grad, qkv_weight_grad = placed["fc1"][0], placed["qkv"][0]
    return (
        output_f.astype(BF),
        loss_value,
        input_grad,
        vectors[0],
        vectors[1],
        vectors[2],
        vectors[3],
        qkv_weight_grad,
        qkv_bias_grad,
        out_weight_grad,
        vectors[4],
        fc1_weight_grad,
        fc1_bias_grad,
        fc2_weight_grad,
        vectors[4],
    )


def solution(mesh):
    tokens = P(("dp", "tensor"), None)
    columns, lanes, down, whole = P(None, "tensor"), P("tensor"), P("tensor", None), P()
    in_specs = (
        tokens,
        tokens,
        P(("dp", "tensor")),
        P("dp"),
        whole,
        whole,
        whole,
        whole,
        columns,
        lanes,
        down,
        whole,
        columns,
        lanes,
        down,
        whole,
    )
    out_specs = (
        tokens,
        whole,
        tokens,
        whole,
        whole,
        whole,
        whole,
        columns,
        lanes,
        down,
        whole,
        columns,
        lanes,
        down,
        whole,
    )
    return jax.shard_map(
        on_device, mesh=mesh, in_specs=in_specs, out_specs=out_specs, check_vma=False
    )
```
